32 devices in a mesh: fsdp: 8 (over y, x, core), seq: 4 (over z).
Axes of the slice: x: 2, y: 2, z: 4, core: 2. Of those that a mesh axis runs over, the one named last changes fastest.
Arguments:
- inputs: bfloat16 [8, 1024, 2048], P('fsdp', 'seq'), may hold values from -6 to 6
- cotangent: bfloat16 [8, 1024, 2048], P('fsdp', 'seq'), may hold values from -6 to 6
- doc_lengths: int32 [8, 8], P('fsdp'), may hold values from 1 to 512, 1024 in all within a row
- projection_weight: float32 [2048, 4096], P(('fsdp', 'seq'))
- projection_moment: float32 [2048, 4096], P(('fsdp', 'seq')), may hold values from -256 to 256
- projection_second: float32 [2048, 4096], P(('fsdp', 'seq')), may hold values from 1024 to 8192
- out_weight: float32 [2048, 2048], P(('fsdp', 'seq'))
- out_moment: float32 [2048, 2048], P(('fsdp', 'seq')), may hold values from -56 to 56
- out_second: float32 [2048, 2048], P(('fsdp', 'seq')), may hold values from 40.96 to 327.68
- ffn_weight: float32 [2048, 12288], P(('fsdp', 'seq'))
- ffn_moment: float32 [2048, 12288], P(('fsdp', 'seq')), may hold values from -256 to 256
- ffn_second: float32 [2048, 12288], P(('fsdp', 'seq')), may hold values from 1024 to 8192
- down_weight: float32 [6144, 2048], P(('fsdp', 'seq'))
- down_moment: float32 [6144, 2048], P(('fsdp', 'seq')), may hold values from -256 to 256
- down_second: float32 [6144, 2048], P(('fsdp', 'seq')), may hold values from 1024 to 8192
- head_gate: float32 [2048, 16], replicated, may hold values from -0.125 to 0.125
- gate_moment: float32 [2048, 16], replicated, may hold values from -2560 to 2560
- gate_second: float32 [2048, 16], replicated, may hold values from 98304 to 819200
- norm_gains: float32 [2, 2048], replicated, may hold values from 0.5 to 1.5
- gains_moment: float32 [2, 2048], replicated, may hold values from -512 to 512
- gains_second: float32 [2, 2048], replicated, may hold values from 4096 to 32768
- qk_gains: float32 [2, 128], replicated, may hold values from 0.5 to 1.5
- qk_moment: float32 [2, 128], replicated, may hold values from -1024 to 1024
- qk_second: float32 [2, 128], replicated, may hold values from 16384 to 131072
Outputs:
- result: bfloat16 [8, 1024, 2048], P('fsdp', 'seq')
- input_grad: float32 [8, 1024, 2048], P('fsdp', 'seq')
- projection_weight_next: float32 [2048, 4096], P(('fsdp', 'seq'))
- projection_moment_next: float32 [2048, 4096], P(('fsdp', 'seq'))
- projection_second_next: float32 [2048, 4096], P(('fsdp', 'seq'))
- qkv_copy: bfloat16 [2048, 4096], P(('fsdp', 'seq'))
- out_new: float32 [2048, 2048], P(('fsdp', 'seq'))
- out_moment_new: float32 [2048, 2048], P(('fsdp', 'seq'))
- out_second_new: float32 [2048, 2048], P(('fsdp', 'seq'))
- out_copy: bfloat16 [2048, 2048], P(('fsdp', 'seq'))
- ffn_new: float32 [2048, 12288], P(('fsdp', 'seq'))
- ffn_moment_new: float32 [2048, 12288], P(('fsdp', 'seq'))
- ffn_second_new: float32 [2048, 12288], P(('fsdp', 'seq'))
- ffn_copy: bfloat16 [2048, 12288], P(('fsdp', 'seq'))
- down_new: float32 [6144, 2048], P(('fsdp', 'seq'))
- down_moment_new: float32 [6144, 2048], P(('fsdp', 'seq'))
- down_second_new: float32 [6144, 2048], P(('fsdp', 'seq'))
- down_copy: bfloat16 [6144, 2048], P(('fsdp', 'seq'))
- head_gate_new: float32 [2048, 16], replicated
- gate_moment_new: float32 [2048, 16], replicated
- gate_second_new: float32 [2048, 16], replicated
- gains_new: float32 [2, 2048], replicated
- gains_moment_new: float32 [2, 2048], replicated
- gains_second_new: float32 [2, 2048], replicated
- qk_new: float32 [2, 128], replicated
- qk_moment_new: float32 [2, 128], replicated
- qk_second_new: float32 [2, 128], replicated
- lamb_norms: float32 [2, 7], replicated
The draws below stay inside these ranges and needn't reach their ends.
Inputs may be any that keep to these rules, and one draw needn't show every extreme that they name: `doc_lengths`: each row's 8 lengths sum to 1024; in every row the longest document has exactly 512 tokens.
All inputs are finite; a program needn't handle non-finite values.
Results may differ from the reference program's by a relative error of at most 0.013.
The reference program's roundings to bfloat16 on the way count: a program that leaves them out, or rounds other values in their place, can miss the bound.
Values may be sent and summed in bfloat16 or wider, within the bound.
A program may use at most 320 MiB of HBM per device.

```python
import math
import jax
import jax.numpy as jnp
import numpy as np
from jax import lax

MODEL_WIDTH = 2048
QUERY_HEADS = 16
KEY_VALUE_HEADS = 8
HEAD_WIDTH = 128
FF = 6144
ROW_TOKENS = 1024
DOCS = 8
STEP = 3
DOC_MOST = 512
QUERY_BLOCK = 512
ROWS = 8
TOKENS = 8192
QKV = 4096


def matrix_scaled(key, rows, columns, fan_in):
    key_base, key_rows, key_cols = jax.random.split(key, 3)
    base = jax.random.normal(key_base, (rows, columns), jnp.float32)
    row_scale = jnp.exp(jax.random.uniform(key_rows, (rows, 1), jnp.float32, -1.15, 1.15))
    col_scale = jnp.exp(jax.random.uniform(key_cols, (1, columns), jnp.float32, -0.35, 0.35))
    return base * row_scale * col_scale * (1.0 / (2.33 * fan_in)) ** 0.5


def draw_projection_weight(key, part):
    return matrix_scaled(key, MODEL_WIDTH, (QUERY_HEADS + 2 * KEY_VALUE_HEADS) * HEAD_WIDTH, MODEL_WIDTH)


def draw_out_weight(key, part):
    return matrix_scaled(key, QUERY_HEADS * HEAD_WIDTH, MODEL_WIDTH, max(1, QUERY_HEADS * HEAD_WIDTH // 128))


def draw_ffn_weight(key, part):
    return matrix_scaled(key, MODEL_WIDTH, 2 * FF, MODEL_WIDTH)


def draw_down_weight(key, part):
    return matrix_scaled(key, FF, MODEL_WIDTH, FF)


def block_levels(own_key, shape, shards, least, high):
    def one(axis_at, parts):
        steps = jax.random.uniform(jax.random.fold_in(jax.random.fold_in(own_key, 6), axis_at), (parts,), jnp.float32, least / len(shards), high / len(shards))
        return jnp.repeat(jnp.exp(steps), shape[axis_at] // parts).reshape((-1,) + (1,) * (len(shape) - axis_at - 1))

    factor_of = one(*shards[0])
    for cut in shards[1:]:
        factor_of = factor_of * one(*cut)
    return factor_of


def profile(count, total, bound, lean):
    weights = [(1 << 20) // math.isqrt(standing ** lean) + 1 for standing in range(2, count + 1)]
    rest, given = total - bound - (count - 1), [1] * (count - 1)
    while rest > 0:
        candidates = [i for i in range(count - 1) if given[i] < bound]
        pool, left = sum([weights[i] for i in candidates]), rest
        for i in candidates:
            addition = min(bound - given[i], max(1, left * weights[i] // pool), rest)
            given[i] = given[i] + addition
            rest = rest - addition
    return np.array([bound] + given)


def uneven_parts(rng, amount, total, bound, skew):
    if amount == 2:
        one = jax.random.randint(rng, (), max(1, total - bound), min(bound, total - 1) + 1)
        return jnp.stack([one, total - one])
    tallies = jnp.asarray(profile(amount, total, bound, skew), jnp.int32)
    twos = (amount - 1) // 2
    giver, sink = tallies[1:1 + 2 * twos:2], tallies[2:2 + 2 * twos:2]
    room = jnp.minimum(giver - 1, bound - sink)
    passed = jax.random.randint(jax.random.fold_in(rng, 1), (twos,), 0, 1 << 20) % (room + 1)
    tallies = tallies.at[1:1 + 2 * twos:2].set(giver - passed).at[2:2 + 2 * twos:2].set(sink + passed)
    return tallies[jax.random.permutation(jax.random.fold_in(rng, 2), amount)]


def centred(key, shape, spread, most, cuts=(), held_as=jnp.bfloat16):
    array = jax.random.normal(key, shape, jnp.float32) * spread
    if len(cuts) > 0:
        array = block_levels(key, shape, cuts, -0.22, 0.18) * array
    return jnp.clip(array, min=-most, max=most).astype(held_as)


def setup_inputs(seed: int = 0) -> dict:
    splits = jax.random.split(jax.random.key(seed), 25)
    inputs = centred(splits[0], (ROWS, ROW_TOKENS, MODEL_WIDTH), 1.0, 6.0, ((0, 8), (1, 4)))
    cotangent = centred(splits[1], (ROWS, ROW_TOKENS, MODEL_WIDTH), 1.0, 6.0, ((0, 8), (1, 4)))
    doc_lengths = jax.vmap(lambda own: uneven_parts(own, DOCS, ROW_TOKENS, DOC_MOST, 2))(jax.random.split(splits[2], ROWS)).reshape((ROWS, DOCS)).astype(jnp.int32)
    projection_weight = draw_projection_weight(jax.random.fold_in(splits[24], 71), 0)
    projection_moment = centred(splits[4], (MODEL_WIDTH, QKV), (0.5 * TOKENS ** 0.5), 256.0, ((0, 32),), jnp.float32)
    projection_second = jnp.clip(jnp.exp(math.log(8192.0) - 2.0794415 * jax.random.uniform(splits[5], (MODEL_WIDTH, QKV), jnp.float32) ** block_levels(splits[5], (MODEL_WIDTH, QKV), ((0, 32),), -0.2, 0.2)), 1024.0, 8192.0)
    out_weight = draw_out_weight(jax.random.fold_in(splits[24], 71), 0)
    out_moment = centred(splits[7], (QUERY_HEADS * HEAD_WIDTH, MODEL_WIDTH), (0.1 * TOKENS ** 0.5), 56.0, ((0, 32),), jnp.float32)
    out_second = jnp.clip(jnp.exp(math.log(327.68) - 2.0794415 * jax.random.uniform(splits[8], (QUERY_HEADS * HEAD_WIDTH, MODEL_WIDTH), jnp.float32) ** block_levels(splits[8], (QUERY_HEADS * HEAD_WIDTH, MODEL_WIDTH), ((0, 32),), -0.2, 0.2)), 40.96, 327.68)
    ffn_weight = draw_ffn_weight(jax.random.fold_in(splits[24], 71), 0)
    ffn_moment = centred(splits[10], (MODEL_WIDTH, 2 * FF), (0.5 * TOKENS ** 0.5), 256.0, ((0, 32),), jnp.float32)
    ffn_second = jnp.clip(jnp.exp(math.log(8192.0) - 2.0794415 * jax.random.uniform(splits[11], (MODEL_WIDTH, 2 * FF), jnp.float32) ** block_levels(splits[11], (MODEL_WIDTH, 2 * FF), ((0, 32),), -0.2, 0.2)), 1024.0, 8192.0)
    down_weight = draw_down_weight(jax.random.fold_in(splits[24], 71), 0)
    down_moment = centred(splits[13], (FF, MODEL_WIDTH), (0.5 * TOKENS ** 0.5), 256.0, ((0, 32),), jnp.float32)
    down_second = jnp.clip(jnp.exp(math.log(8192.0) - 2.0794415 * jax.random.uniform(splits[14], (FF, MODEL_WIDTH), jnp.float32) ** block_levels(splits[14], (FF, MODEL_WIDTH), ((0, 32),), -0.2, 0.2)), 1024.0, 8192.0)
    head_gate = centred(splits[15], (MODEL_WIDTH, QUERY_HEADS), MODEL_WIDTH ** -0.5, 0.125, (), jnp.float32)
    gate_moment = centred(splits[16], (MODEL_WIDTH, QUERY_HEADS), (5.0 * TOKENS ** 0.5), 2560.0, (), jnp.float32)
    gate_second = jnp.clip(jnp.exp(jax.random.uniform(splits[17], (MODEL_WIDTH, QUERY_HEADS), jnp.float32, math.log(98304.0), math.log(819200.0))), 98304.0, 819200.0)
    norm_gains = jnp.clip(1.0 + 0.1 * jax.random.normal(splits[18], (2, MODEL_WIDTH), jnp.float32), 0.5, 1.5)
    gains_moment = centred(splits[19], (2, MODEL_WIDTH), (TOKENS ** 0.5), 512.0, (), jnp.float32)
    gains_second = jnp.clip(jnp.exp(jax.random.uniform(splits[20], (2, MODEL_WIDTH), jnp.float32, math.log(4096.0), math.log(32768.0))), 4096.0, 32768.0)
    qk_gains = jnp.clip(1.0 + 0.1 * jax.random.normal(splits[21], (2, HEAD_WIDTH), jnp.float32), 0.5, 1.5)
    qk_moment = centred(splits[22], (2, HEAD_WIDTH), (0.5 * (QUERY_HEADS * TOKENS) ** 0.5), 1024.0, (), jnp.float32)
    qk_second = jnp.clip(jnp.exp(jax.random.uniform(splits[23], (2, HEAD_WIDTH), jnp.float32, math.log(16384.0), math.log(131072.0))), 16384.0, 131072.0)
    return dict(inputs=inputs, cotangent=cotangent, doc_lengths=doc_lengths, projection_weight=projection_weight, projection_moment=projection_moment, projection_second=projection_second, out_weight=out_weight, out_moment=out_moment, out_second=out_second, ffn_weight=ffn_weight, ffn_moment=ffn_moment, ffn_second=ffn_second, down_weight=down_weight, down_moment=down_moment, down_second=down_second, head_gate=head_gate, gate_moment=gate_moment, gate_second=gate_second, norm_gains=norm_gains, gains_moment=gains_moment, gains_second=gains_second, qk_gains=qk_gains, qk_moment=qk_moment, qk_second=qk_second)


@jax.custom_vjp
def low(v):
    return lax.optimization_barrier(v.astype(jnp.bfloat16)).astype(jnp.float32)

@jax.custom_vjp
def low_back(v):
    return v

def low_keep(v):
    return (low(v), None)

def low_pass(kept, grad):
    return (grad,)

def back_keep(v):
    return (v, None)

def back_low(kept, grad):
    return (low(grad),)
low.defvjp(low_keep, low_pass)
low_back.defvjp(back_keep, back_low)
NORM_EPS = 1e-06
ADAM_EPS = 1e-06
RATE = 0.3
DECAY = 0.01
BETA = 0.5
THETA = 1000000.0
NEGATIVE = -1e+30
HIGHEST = lax.Precision.HIGHEST

def hdot(left, right):
    return jnp.dot(left, right, precision=HIGHEST, preferred_element_type=jnp.float32)

def rms_apply(value_rows, gain):
    return value_rows * lax.rsqrt(lax.optimization_barrier(jnp.mean(value_rows * value_rows, axis=-1, keepdims=True)) + NORM_EPS) * gain

def doc_tables(lengths):
    ends = jnp.cumsum(lengths).astype(jnp.int32)
    starts = (ends - lengths).astype(jnp.int32)
    place = jnp.arange(ROW_TOKENS, dtype=jnp.int32)
    inside = (place[:, None] >= starts[None, :]) & (place[:, None] < ends[None, :])
    labels = jnp.arange(lengths.shape[0], dtype=jnp.int32)
    segment = lax.optimization_barrier(jnp.sum(jnp.where(inside, labels[None, :], 0), axis=1)).astype(jnp.int32)
    position = (place - lax.optimization_barrier(jnp.sum(jnp.where(inside, starts[None, :], 0), axis=1))).astype(jnp.int32)
    return (segment, position)

def rotate(value_rows, position, sign):
    half = value_rows.shape[-1] // 2
    rates = THETA ** (-jnp.arange(half, dtype=jnp.float32) * 2.0 / value_rows.shape[-1])
    angle = position.astype(jnp.float32)[:, None] * rates[None, :]
    cosine = jnp.cos(angle)[:, None, :]
    sine = sign * jnp.sin(angle)[:, None, :]
    former = value_rows[..., :half]
    latter = value_rows[..., half:]
    return jnp.concatenate([former * cosine - latter * sine, latter * cosine + former * sine], axis=-1)

def attention(query_rows, keys, values, segment):
    param_group = QUERY_HEADS // KEY_VALUE_HEADS
    score_blocks = ROW_TOKENS // QUERY_BLOCK
    reshaped_rows = query_rows.reshape(score_blocks, QUERY_BLOCK, KEY_VALUE_HEADS, param_group, HEAD_WIDTH)
    columns = jnp.arange(ROW_TOKENS, dtype=jnp.int32)

    def one_block(index):
        start = (index * QUERY_BLOCK).astype(jnp.int32)
        rows_q = lax.dynamic_index_in_dim(reshaped_rows, index, 0, keepdims=False)
        seg_rows = lax.dynamic_slice_in_dim(segment, start, QUERY_BLOCK, 0)
        scores = jnp.einsum('qhgd,khd->hgqk', rows_q, keys, precision=HIGHEST) * HEAD_WIDTH ** (-0.5)
        scores = low_back(scores)
        rows = start + jnp.arange(QUERY_BLOCK, dtype=jnp.int32)
        allowed = (seg_rows[:, None] == segment[None, :]) & (columns[None, :] <= rows[:, None])
        scores = jnp.where(allowed[None, None], scores, NEGATIVE)
        shifted = scores - lax.optimization_barrier(jnp.max(scores, axis=-1, keepdims=True))
        powers = jnp.exp(shifted)
        softened = low(powers / lax.optimization_barrier(jnp.sum(powers, axis=-1, keepdims=True)))
        return jnp.einsum('hgqk,khd->qhgd', softened, values, precision=HIGHEST)
    outputs = lax.map(jax.checkpoint(one_block), jnp.arange(score_blocks, dtype=jnp.int32))
    return outputs.reshape(ROW_TOKENS, QUERY_HEADS, HEAD_WIDTH)

def layer(inputs, params, segment, position):
    projection_weight, out_weight, ffn_weight, down_weight, head_gate, norm_gains, qk_gains = params
    normed = low(rms_apply(inputs, norm_gains[0]))
    projected_rows = low(low_back(hdot(normed, low(projection_weight))))
    query = projected_rows[:, :QUERY_HEADS * HEAD_WIDTH].reshape(ROW_TOKENS, QUERY_HEADS, HEAD_WIDTH)
    key = projected_rows[:, QUERY_HEADS * HEAD_WIDTH:(QUERY_HEADS + KEY_VALUE_HEADS) * HEAD_WIDTH].reshape(ROW_TOKENS, KEY_VALUE_HEADS, HEAD_WIDTH)
    value_rows = projected_rows[:, (QUERY_HEADS + KEY_VALUE_HEADS) * HEAD_WIDTH:].reshape(ROW_TOKENS, KEY_VALUE_HEADS, HEAD_WIDTH)
    query = low(rotate(rms_apply(query, qk_gains[0]), position, 1.0))
    key = low(rotate(rms_apply(key, qk_gains[1]), position, 1.0))
    attended = low(low_back(attention(query, key, value_rows, segment)))
    gate = jax.nn.sigmoid(low_back(hdot(normed, low(head_gate))))
    gated = low((attended * gate[:, :, None]).reshape(ROW_TOKENS, QUERY_HEADS * HEAD_WIDTH))
    middle = inputs + low_back(hdot(gated, low(out_weight)))
    normed2 = low(rms_apply(middle, norm_gains[1]))
    both = low_back(hdot(normed2, low(ffn_weight)))
    inner = both[:, :FF]
    hidden = low(inner * jax.nn.sigmoid(inner) * both[:, FF:])
    return middle + low_back(hdot(hidden, low(down_weight)))

def moments(weight, moment, second, gradient):
    moment_new = BETA * moment + (1.0 - BETA) * gradient
    second_new = BETA * second + (1.0 - BETA) * gradient * gradient
    correction = 1.0 - BETA ** STEP
    update = moment_new / correction / (jnp.sqrt(second_new / correction) + ADAM_EPS) + DECAY * weight
    return (moment_new, second_new, update)

def trust_groups(weight, moment, second, gradient, widths):
    moment_new, second_new, update = moments(weight, moment, second, gradient)
    weight_norms = []
    update_norms = []
    factors = []
    lower = 0
    for width in widths:
        upper = lower + width
        weight_norm = jnp.sqrt(jnp.sum(weight[:, lower:upper] * weight[:, lower:upper]))
        update_norm = jnp.sqrt(jnp.sum(update[:, lower:upper] * update[:, lower:upper]))
        weight_norms.append(weight_norm)
        update_norms.append(update_norm)
        factors.append(jnp.broadcast_to(weight_norm / update_norm, (width,)))
        lower = upper
    new = weight - RATE * jnp.concatenate(factors)[None, :] * update
    return (new, moment_new, second_new, weight_norms, update_norms)

def row_update(weight, moment, second, gradient):
    moment_new, second_new, update = moments(weight, moment, second, gradient)
    trust = jnp.sqrt(lax.optimization_barrier(jnp.sum(weight * weight, axis=-1, keepdims=True))) / jnp.sqrt(lax.optimization_barrier(jnp.sum(update * update, axis=-1, keepdims=True)))
    return (weight - RATE * trust * update, moment_new, second_new)

def whole_update(weight, moment, second, gradient):
    moment_new, second_new, update = moments(weight, moment, second, gradient)
    trust = jnp.sqrt(jnp.sum(weight * weight)) / jnp.sqrt(jnp.sum(update * update))
    return (weight - RATE * trust * update, moment_new, second_new)

def reference(inputs, cotangent, doc_lengths, projection_weight, projection_moment, projection_second, out_weight, out_moment, out_second, ffn_weight, ffn_moment, ffn_second, down_weight, down_moment, down_second, head_gate, gate_moment, gate_second, norm_gains, gains_moment, gains_second, qk_gains, qk_moment, qk_second):
    segments, positions = jax.vmap(doc_tables)(doc_lengths)
    params = (projection_weight, out_weight, ffn_weight, down_weight, head_gate, norm_gains, qk_gains)

    def per_row(totals, row):
        row_inputs, row_cotangent, segment, position = row

        def forward(values_in, weights):
            return layer(values_in, weights, segment, position)
        output, pullback = jax.vjp(forward, row_inputs.astype(jnp.float32), params)
        row_grad, weight_grads = pullback(row_cotangent.astype(jnp.float32))
        totals = jax.tree.map(lambda left, right: left + right, totals, weight_grads)
        return (totals, (output.astype(jnp.bfloat16), row_grad))
    zeros = jax.tree.map(jnp.zeros_like, params)
    grads, (result, input_grad) = lax.scan(per_row, zeros, (inputs, cotangent, segments, positions))
    projection_gradient, out_grad, ffn_grad, down_grad, gate_grad, gains_grad, qk_grad = grads
    projection_weight_next, projection_moment_next, projection_second_next, projection_norms, projection_updates = trust_groups(projection_weight, projection_moment, projection_second, projection_gradient, (QUERY_HEADS * HEAD_WIDTH, KEY_VALUE_HEADS * HEAD_WIDTH, KEY_VALUE_HEADS * HEAD_WIDTH))
    out_new, out_moment_new, out_second_new, norms_out, updates_out = trust_groups(out_weight, out_moment, out_second, out_grad, (MODEL_WIDTH,))
    ffn_new, ffn_moment_new, ffn_second_new, norms_ffn, updates_ffn = trust_groups(ffn_weight, ffn_moment, ffn_second, ffn_grad, (FF, FF))
    down_new, down_moment_new, down_second_new, norms_down, updates_down = trust_groups(down_weight, down_moment, down_second, down_grad, (MODEL_WIDTH,))
    head_gate_new, gate_moment_new, gate_second_new = whole_update(head_gate, gate_moment, gate_second, gate_grad)
    gains_new, gains_moment_new, gains_second_new = row_update(norm_gains, gains_moment, gains_second, gains_grad)
    qk_new, qk_moment_new, qk_second_new = row_update(qk_gains, qk_moment, qk_second, qk_grad)
    lamb_norms = jnp.stack([jnp.stack(projection_norms + norms_out + norms_ffn + norms_down), jnp.stack(projection_updates + updates_out + updates_ffn + updates_down)])
    return (result, input_grad, projection_weight_next, projection_moment_next, projection_second_next, projection_weight_next.astype(jnp.bfloat16), out_new, out_moment_new, out_second_new, out_new.astype(jnp.bfloat16), ffn_new, ffn_moment_new, ffn_second_new, ffn_new.astype(jnp.bfloat16), down_new, down_moment_new, down_second_new, down_new.astype(jnp.bfloat16), head_gate_new, gate_moment_new, gate_second_new, gains_new, gains_moment_new, gains_second_new, qk_new, qk_moment_new, qk_second_new, lamb_norms)
```

```python
import jax
import jax.numpy as jnp
from jax import lax
from jax.sharding import Mesh
from jax.sharding import PartitionSpec as P

MODEL_WIDTH = 2048
QUERY_HEADS = 16
KEY_VALUE_HEADS = 8
HEAD_WIDTH = 128
FF = 6144
ROW_TOKENS = 1024
STEP = 3
DOC_MOST = 512
TEAM_SIZE = 8
TEAM = ("t2", "t1", "t0")
DEPTH = ("spare", "seq")


NORM_EPS = 1e-06
ADAM_EPS = 1e-06
RATE = 0.3
DECAY = 0.01
BETA = 0.5
THETA = 1000000.0
NEGATIVE = -1e30


def rms_apply(value_rows, gain):
    return (
        value_rows
        * lax.rsqrt(jnp.mean(value_rows * value_rows, axis=-1, keepdims=True) + NORM_EPS)
        * gain
    )


def rms_back(value_rows, gain, gradient):
    scale = lax.rsqrt(jnp.mean(value_rows * value_rows, axis=-1, keepdims=True) + NORM_EPS)
    scaled = gradient * gain
    inner = jnp.mean(scaled * value_rows, axis=-1, keepdims=True)
    grad_value = scale * scaled - value_rows * scale * scale * scale * inner
    grad_gain = gradient * value_rows * scale
    return (grad_value, grad_gain)


def dot_t(left, right):
    return lax.dot_general(
        left, right, (((1,), (1,)), ((), ())), preferred_element_type=jnp.float32
    )


def dot_tokens(left, right):
    return lax.dot_general(
        left, right, (((0,), (0,)), ((), ())), preferred_element_type=jnp.float32
    )


def rotary_tables(position, width):
    half = width // 2
    rates = THETA ** (-jnp.arange(half, dtype=jnp.float32) * 2.0 / width)
    angle = position.astype(jnp.float32)[..., None] * rates
    return (jnp.cos(angle), jnp.sin(angle))


def rotate(value_rows, cosine, sine):
    half = value_rows.shape[-1] // 2
    former = value_rows[..., :half]
    latter = value_rows[..., half:]
    return jnp.concatenate(
        [former * cosine - latter * sine, latter * cosine + former * sine], axis=-1
    )


def doc_tables(lengths, place):
    ends = jnp.cumsum(lengths, axis=1)
    starts = ends - lengths
    inside = (place[None, :, None] >= starts[:, None, :]) & (place[None, :, None] < ends[:, None, :])
    labels = jnp.arange(lengths.shape[1], dtype=jnp.int32)
    segment = jnp.sum(jnp.where(inside, labels[None, None, :] + 1, 0), axis=2) - 1
    position = place[None, :] - jnp.sum(jnp.where(inside, starts[:, None, :], 0), axis=2)
    return (segment, position)


def gather_team(value_rows):
    return lax.all_gather(value_rows, TEAM, axis=0, tiled=True)


def scatter_team(value_rows):
    return lax.psum_scatter(value_rows, TEAM, scatter_dimension=0, tiled=True)


def team_exchange(blocks):
    return lax.all_to_all(blocks, TEAM, split_axis=0, concat_axis=0, tiled=True)


def shift_seq(value_rows, distance):
    count = lax.axis_size("seq")
    pairs = [(i, i + distance) for i in range(count) if 0 <= i + distance < count]
    return lax.ppermute(value_rows, "seq", pairs)


def team_columns(matrix, widths):
    pieces = []
    lower = 0
    for width in widths:
        piece = matrix[:, lower : lower + width]
        pieces.append(piece.reshape(matrix.shape[0], TEAM_SIZE, width // TEAM_SIZE))
        lower = lower + width
    return jnp.concatenate(pieces, axis=2).transpose(1, 0, 2)


def whole_columns(blocks, widths):
    pieces = []
    lower = 0
    for width in widths:
        share = width // TEAM_SIZE
        piece = blocks[:, :, lower : lower + share]
        pieces.append(piece.transpose(1, 0, 2).reshape(blocks.shape[1], width))
        lower = lower + share
    return jnp.concatenate(pieces, axis=1)


def gather_columns(matrix, widths):
    blocks = team_exchange(team_columns(matrix, widths))
    whole = lax.all_gather(blocks, DEPTH, axis=0, tiled=False)
    return whole.transpose(1, 0, 2, 3).reshape(-1, blocks.shape[2])


def scatter_columns(gradient, rows, widths):
    depth = gradient.shape[0] // (TEAM_SIZE * rows)
    ordered = gradient.astype(jnp.bfloat16).reshape(TEAM_SIZE, depth, rows, -1).transpose(1, 0, 2, 3)
    mine = lax.psum_scatter(
        ordered.reshape(gradient.shape), DEPTH, scatter_dimension=0, tiled=True
    ).reshape(TEAM_SIZE, rows, -1)
    return whole_columns(team_exchange(mine), widths).astype(jnp.float32)


def gather_rows(matrix):
    return lax.all_gather(matrix, DEPTH, axis=0, tiled=True)


def scatter_rows(gradient):
    return lax.psum_scatter(
        gradient.astype(jnp.bfloat16), DEPTH, scatter_dimension=0, tiled=True
    ).astype(jnp.float32)


def moments(weight, moment, second, gradient):
    moment_new = BETA * moment + (1.0 - BETA) * gradient
    second_new = BETA * second + (1.0 - BETA) * gradient * gradient
    correction = 1.0 - BETA**STEP
    update = (
        moment_new / correction / (jnp.sqrt(second_new / correction) + ADAM_EPS) + DECAY * weight
    )
    return (moment_new, second_new, update)


def group_squares(matrix, widths):
    sums = []
    lower = 0
    for width in widths:
        piece = matrix[:, lower : lower + width]
        sums.append(jnp.sum(piece * piece))
        lower = lower + width
    return jnp.stack(sums)


def apply_trust(weight, update, trust, widths):
    factors = [jnp.broadcast_to(trust[index], (width,)) for index, width in enumerate(widths)]
    return weight - RATE * jnp.concatenate(factors)[None, :] * update


def row_update(weight, moment, second, gradient):
    moment_new, second_new, update = moments(weight, moment, second, gradient)
    trust = jnp.sqrt(jnp.sum(weight * weight, axis=-1, keepdims=True)) / jnp.sqrt(
        jnp.sum(update * update, axis=-1, keepdims=True)
    )
    return (weight - RATE * trust * update, moment_new, second_new)


def whole_update(weight, moment, second, gradient):
    moment_new, second_new, update = moments(weight, moment, second, gradient)
    trust = jnp.sqrt(jnp.sum(weight * weight)) / jnp.sqrt(jnp.sum(update * update))
    return (weight - RATE * trust * update, moment_new, second_new)


def shards(
    inputs,
    cotangent,
    doc_lengths,
    projection_weight,
    projection_moment,
    projection_second,
    out_weight,
    out_moment,
    out_second,
    ffn_weight,
    ffn_moment,
    ffn_second,
    down_weight,
    down_moment,
    down_second,
    head_gate,
    gate_moment,
    gate_second,
    norm_gains,
    gains_moment,
    gains_second,
    qk_gains,
    qk_moment,
    qk_second,
):
    rows_dev, local_len, width = inputs.shape
    bf16 = jnp.bfloat16
    team = lax.axis_index(TEAM)
    place_seq = lax.axis_index("seq")
    group_heads = QUERY_HEADS // KEY_VALUE_HEADS
    window = -(-(DOC_MOST - 1) // local_len)
    window = min(window, lax.axis_size("seq") - 1)
    query_cols = QUERY_HEADS * HEAD_WIDTH
    key_value_columns = KEY_VALUE_HEADS * HEAD_WIDTH
    widths_qkv = (query_cols, key_value_columns, key_value_columns)
    widths_ffn = (FF, FF)
    own_query = query_cols // TEAM_SIZE
    own_key = key_value_columns // TEAM_SIZE
    own_ff = FF // TEAM_SIZE
    scale = HEAD_WIDTH ** (-0.5)
    weight_squares = jnp.concatenate(
        [
            group_squares(projection_weight, widths_qkv),
            group_squares(out_weight, (MODEL_WIDTH,)),
            group_squares(ffn_weight, widths_ffn),
            group_squares(down_weight, (MODEL_WIDTH,)),
        ]
    )
    own_qkv = gather_columns(projection_weight.astype(bf16), widths_qkv)
    own_out = gather_rows(out_weight.astype(bf16))
    own_ffn = gather_columns(ffn_weight.astype(bf16), widths_ffn)
    own_down = gather_rows(down_weight.astype(bf16))
    own_gate = lax.dynamic_slice_in_dim(
        head_gate.astype(bf16), team * group_heads, group_heads, 1
    )
    lengths = lax.all_gather(doc_lengths, TEAM, axis=0, tiled=True)
    place = place_seq * local_len + jnp.arange(local_len, dtype=jnp.int32)
    key_place = (place_seq - window) * local_len + jnp.arange(
        (window + 1) * local_len, dtype=jnp.int32
    )
    segment, position = doc_tables(lengths, place)
    key_segment, _ = doc_tables(lengths, key_place)
    cosine, sine = rotary_tables(position, HEAD_WIDTH)
    allowed = (segment[:, :, None] == key_segment[:, None, :]) & (
        key_place[None, None, :] <= place[None, :, None]
    )
    inputs_flat = inputs[0].astype(jnp.float32)
    normed = rms_apply(inputs_flat, norm_gains[0]).astype(bf16)
    normed_all = gather_team(normed)
    projected = jnp.dot(normed_all, own_qkv, preferred_element_type=jnp.float32).astype(bf16)
    gate = jax.nn.sigmoid(jnp.dot(normed_all, own_gate, preferred_element_type=jnp.float32))
    gate = gate.reshape(TEAM_SIZE, local_len, group_heads)
    query_raw = (
        projected[:, :own_query]
        .reshape(TEAM_SIZE, local_len, group_heads, HEAD_WIDTH)
        .astype(jnp.float32)
    )
    key_raw = (
        projected[:, own_query : own_query + own_key]
        .reshape(TEAM_SIZE, local_len, HEAD_WIDTH)
        .astype(jnp.float32)
    )
    value = projected[:, own_query + own_key :].reshape(TEAM_SIZE, local_len, HEAD_WIDTH)
    query_rot = rotate(
        rms_apply(query_raw, qk_gains[0]), cosine[:, :, None], sine[:, :, None]
    ).astype(bf16)
    key_rot = rotate(rms_apply(key_raw, qk_gains[1]), cosine, sine).astype(bf16)
    pair = jnp.concatenate([key_rot, value], axis=2)
    blocks = [shift_seq(pair, distance) for distance in range(window, 0, -1)] + [pair]
    pair_window = jnp.concatenate(blocks, axis=1)
    keys = pair_window[:, :, :HEAD_WIDTH]
    values = pair_window[:, :, HEAD_WIDTH:]
    scores = (
        jnp.einsum("bqgd,bkd->bgqk", query_rot, keys, preferred_element_type=jnp.float32) * scale
    )
    scores = jnp.where(allowed[:, None], scores, NEGATIVE)
    top = jnp.max(scores, axis=-1, keepdims=True)
    powers = jnp.exp(scores - top)
    probs = powers / jnp.sum(powers, axis=-1, keepdims=True)
    low_probs = probs.astype(bf16)
    attended = jnp.einsum(
        "bgqk,bkd->bqgd", low_probs, values, preferred_element_type=jnp.float32
    ).astype(bf16)
    attended_wide = attended.astype(jnp.float32)
    gated = (attended_wide * gate[..., None]).astype(bf16).reshape(-1, own_query)
    middle = inputs_flat + scatter_team(
        jnp.dot(gated, own_out, preferred_element_type=jnp.float32).astype(bf16)
    ).astype(jnp.float32)
    normed2 = rms_apply(middle, norm_gains[1]).astype(bf16)
    normed2_all = gather_team(normed2)
    both = jnp.dot(normed2_all, own_ffn, preferred_element_type=jnp.float32)
    inner = both[:, :own_ff]
    up_part = both[:, own_ff:]
    sigma_inner = jax.nn.sigmoid(inner)
    hidden = (inner * sigma_inner * up_part).astype(bf16)
    final = middle + scatter_team(
        jnp.dot(hidden, own_down, preferred_element_type=jnp.float32).astype(bf16)
    ).astype(jnp.float32)
    result = final.astype(bf16).reshape(inputs.shape)
    grad_final = cotangent[0].astype(jnp.float32)
    grad_all = gather_team(cotangent[0])
    grad_hidden = dot_t(grad_all, own_down)
    grad_inner = grad_hidden * up_part * sigma_inner * (1.0 + inner * (1.0 - sigma_inner))
    grad_up = grad_hidden * inner * sigma_inner
    grad_both = jnp.concatenate([grad_inner, grad_up], axis=1).astype(bf16)
    down_grad = scatter_rows(dot_tokens(hidden, grad_all))
    ffn_grad = scatter_columns(
        dot_tokens(normed2_all, grad_both), ffn_weight.shape[0], widths_ffn
    )
    grad_normed2 = scatter_team(dot_t(grad_both, own_ffn).astype(bf16)).astype(jnp.float32)
    grad_mid_part, gain_mid = rms_back(middle, norm_gains[1], grad_normed2)
    grad_middle = grad_final + grad_mid_part
    grad_middle_all = gather_team(grad_middle.astype(bf16))
    out_grad = scatter_rows(dot_tokens(gated, grad_middle_all))
    grad_gated = dot_t(grad_middle_all, own_out).reshape(attended.shape)
    grad_attended = (grad_gated * gate[..., None]).astype(bf16)
    grad_gate_pre = (
        (jnp.sum(grad_gated * attended_wide, axis=-1) * gate * (1.0 - gate))
        .astype(bf16)
        .reshape(-1, group_heads)
    )
    grad_probs = jnp.einsum(
        "bqgd,bkd->bgqk", grad_attended, values, preferred_element_type=jnp.float32
    )
    grad_scores = (
        probs * (grad_probs - jnp.sum(probs * grad_probs, axis=-1, keepdims=True))
    ).astype(bf16)
    grad_values = jnp.einsum(
        "bgqk,bqgd->bkd", low_probs, grad_attended, preferred_element_type=jnp.float32
    )
    grad_query_rot = (
        jnp.einsum("bgqk,bkd->bqgd", grad_scores, keys, preferred_element_type=jnp.float32) * scale
    )
    grad_keys = (
        jnp.einsum("bgqk,bqgd->bkd", grad_scores, query_rot, preferred_element_type=jnp.float32)
        * scale
    )
    grad_pair = jnp.concatenate([grad_keys, grad_values], axis=2)
    grad_own = grad_pair[:, window * local_len :]
    for distance in range(1, window + 1):
        lower = (window - distance) * local_len
        grad_own = grad_own + shift_seq(
            grad_pair[:, lower : lower + local_len].astype(bf16), -distance
        ).astype(jnp.float32)
    grad_query_raw, gain_query = rms_back(
        query_raw, qk_gains[0], rotate(grad_query_rot, cosine[:, :, None], -sine[:, :, None])
    )
    grad_key_raw, gain_key = rms_back(
        key_raw, qk_gains[1], rotate(grad_own[:, :, :HEAD_WIDTH], cosine, -sine)
    )
    qk_local = jnp.stack([jnp.sum(gain_query, axis=(0, 1, 2)), jnp.sum(gain_key, axis=(0, 1))])
    grad_projected = jnp.concatenate(
        [
            grad_query_raw.reshape(-1, own_query),
            grad_key_raw.reshape(-1, own_key),
            grad_own[:, :, HEAD_WIDTH:].reshape(-1, own_key),
        ],
        axis=1,
    ).astype(bf16)
    grad_normed = scatter_team(
        (dot_t(grad_projected, own_qkv) + dot_t(grad_gate_pre, own_gate)).astype(bf16)
    ).astype(jnp.float32)
    grad_in_part, gain_in = rms_back(inputs_flat, norm_gains[0], grad_normed)
    input_grad = (grad_middle + grad_in_part).reshape(inputs.shape)
    projection_gradient = scatter_columns(
        dot_tokens(normed_all, grad_projected), projection_weight.shape[0], widths_qkv
    )
    gains_local = jnp.stack([jnp.sum(gain_in, axis=0), jnp.sum(gain_mid, axis=0)])
    gate_local = lax.dynamic_update_slice_in_dim(
        jnp.zeros((QUERY_HEADS, MODEL_WIDTH), jnp.float32),
        dot_tokens(grad_gate_pre, normed_all),
        team * group_heads,
        0,
    )
    projection_moment_next, projection_second_next, qkv_update = moments(
        projection_weight, projection_moment, projection_second, projection_gradient
    )
    out_moment_new, out_second_new, out_update = moments(
        out_weight, out_moment, out_second, out_grad
    )
    ffn_moment_new, ffn_second_new, ffn_update = moments(
        ffn_weight, ffn_moment, ffn_second, ffn_grad
    )
    down_moment_new, down_second_new, down_update = moments(
        down_weight, down_moment, down_second, down_grad
    )
    update_squares = jnp.concatenate(
        [
            group_squares(qkv_update, widths_qkv),
            group_squares(out_update, (MODEL_WIDTH,)),
            group_squares(ffn_update, widths_ffn),
            group_squares(down_update, (MODEL_WIDTH,)),
        ]
    )
    gains_grad, qk_grad, gate_grad, weight_totals, update_totals = lax.psum(
        (gains_local, qk_local, gate_local, weight_squares, update_squares), TEAM + DEPTH
    )
    weight_norms = jnp.sqrt(weight_totals)
    update_norms = jnp.sqrt(update_totals)
    trust = weight_norms / update_norms
    projection_weight_next = apply_trust(projection_weight, qkv_update, trust[0:3], widths_qkv)
    out_new = apply_trust(out_weight, out_update, trust[3:4], (MODEL_WIDTH,))
    ffn_new = apply_trust(ffn_weight, ffn_update, trust[4:6], widths_ffn)
    down_new = apply_trust(down_weight, down_update, trust[6:7], (MODEL_WIDTH,))
    head_gate_new, gate_moment_new, gate_second_new = whole_update(
        head_gate, gate_moment, gate_second, gate_grad.T
    )
    gains_new, gains_moment_new, gains_second_new = row_update(
        norm_gains, gains_moment, gains_second, gains_grad
    )
    qk_new, qk_moment_new, qk_second_new = row_update(qk_gains, qk_moment, qk_second, qk_grad)
    lamb_norms = jnp.stack([weight_norms, update_norms])
    return (
        result,
        input_grad,
        projection_weight_next,
        projection_moment_next,
        projection_second_next,
        projection_weight_next.astype(jnp.bfloat16),
        out_new,
        out_moment_new,
        out_second_new,
        out_new.astype(jnp.bfloat16),
        ffn_new,
        ffn_moment_new,
        ffn_second_new,
        ffn_new.astype(jnp.bfloat16),
        down_new,
        down_moment_new,
        down_second_new,
        down_new.astype(jnp.bfloat16),
        head_gate_new,
        gate_moment_new,
        gate_second_new,
        gains_new,
        gains_moment_new,
        gains_second_new,
        qk_new,
        qk_moment_new,
        qk_second_new,
        lamb_norms,
    )


def solution(mesh):
    mesh = Mesh(
        mesh.devices.reshape(2, 2, 2, mesh.shape["fsdp"] // TEAM_SIZE, mesh.shape["seq"]),
        TEAM + DEPTH,
    )
    rows = TEAM + DEPTH[:1]
    in_specs = (
        P(rows, "seq", None),
        P(rows, "seq", None),
        P(rows, None),
        P(TEAM + DEPTH, None),
        P(TEAM + DEPTH, None),
        P(TEAM + DEPTH, None),
        P(TEAM + DEPTH, None),
        P(TEAM + DEPTH, None),
        P(TEAM + DEPTH, None),
        P(TEAM + DEPTH, None),
        P(TEAM + DEPTH, None),
        P(TEAM + DEPTH, None),
        P(TEAM + DEPTH, None),
        P(TEAM + DEPTH, None),
        P(TEAM + DEPTH, None),
        P(),
        P(),
        P(),
        P(),
        P(),
        P(),
        P(),
        P(),
        P(),
    )
    out_specs = (
        P(rows, "seq", None),
        P(rows, "seq", None),
        P(TEAM + DEPTH, None),
        P(TEAM + DEPTH, None),
        P(TEAM + DEPTH, None),
        P(TEAM + DEPTH, None),
        P(TEAM + DEPTH, None),
        P(TEAM + DEPTH, None),
        P(TEAM + DEPTH, None),
        P(TEAM + DEPTH, None),
        P(TEAM + DEPTH, None),
        P(TEAM + DEPTH, None),
        P(TEAM + DEPTH, None),
        P(TEAM + DEPTH, None),
        P(TEAM + DEPTH, None),
        P(TEAM + DEPTH, None),
        P(TEAM + DEPTH, None),
        P(TEAM + DEPTH, None),
        P(),
        P(),
        P(),
        P(),
        P(),
        P(),
        P(),
        P(),
        P(),
        P(),
    )
    return jax.shard_map(shards, mesh=mesh, in_specs=in_specs, out_specs=out_specs, check_vma=False)
```

```python
import functools

import jax
import jax.numpy as jnp
from jax import lax
from jax.experimental import pallas as pl
from jax.experimental.pallas import tpu as pltpu
from jax.sharding import Mesh
from jax.sharding import PartitionSpec as P

MODEL_WIDTH = 2048
QUERY_HEADS = 16
KEY_VALUE_HEADS = 8
HEAD_WIDTH = 128
FF = 6144
ROW_TOKENS = 1024
STEP = 3
DOC_MOST = 512
TEAM_SIZE = 8
TEAM = ("t2", "t1", "t0")
DEPTH = ("spare", "seq")
LANES = 128
VMEM_BYTES = 48 << 20
GATHER_COST = 250
SCATTER_COST = 320


NORM_EPS = 1e-06
ADAM_EPS = 1e-06
RATE = 0.3
DECAY = 0.01
BETA = 0.5
THETA = 1000000.0
NEGATIVE = -1e30


def rms_apply(value_rows, gain):
    return (
        value_rows
        * lax.rsqrt(jnp.mean(value_rows * value_rows, axis=-1, keepdims=True) + NORM_EPS)
        * gain
    )


def rms_back(value_rows, gain, gradient):
    scale = lax.rsqrt(jnp.mean(value_rows * value_rows, axis=-1, keepdims=True) + NORM_EPS)
    scaled = gradient * gain
    inner = jnp.mean(scaled * value_rows, axis=-1, keepdims=True)
    grad_value = scale * scaled - value_rows * scale * scale * scale * inner
    grad_gain = gradient * value_rows * scale
    return (grad_value, grad_gain)


def dot_t(left, right):
    return lax.dot_general(
        left, right, (((1,), (1,)), ((), ())), preferred_element_type=jnp.float32
    )


def dot_tokens(left, right):
    return lax.dot_general(
        left, right, (((0,), (0,)), ((), ())), preferred_element_type=jnp.float32
    )


def rotary_tables(position, width):
    half = width // 2
    rates = THETA ** (-jnp.arange(half, dtype=jnp.float32) * 2.0 / width)
    angle = position.astype(jnp.float32)[..., None] * rates
    return (jnp.cos(angle), jnp.sin(angle))


def rotate(value_rows, cosine, sine):
    half = value_rows.shape[-1] // 2
    former = value_rows[..., :half]
    latter = value_rows[..., half:]
    return jnp.concatenate(
        [former * cosine - latter * sine, latter * cosine + former * sine], axis=-1
    )


def doc_tables(lengths, place):
    ends = jnp.cumsum(lengths, axis=1)
    starts = ends - lengths
    inside = (place[None, :, None] >= starts[:, None, :]) & (place[None, :, None] < ends[:, None, :])
    labels = jnp.arange(lengths.shape[1], dtype=jnp.int32)
    segment = jnp.sum(jnp.where(inside, labels[None, None, :] + 1, 0), axis=2) - 1
    position = place[None, :] - jnp.sum(jnp.where(inside, starts[:, None, :], 0), axis=2)
    return (segment, position)


def team_place():
    return tuple(lax.axis_index(axis) for axis in TEAM)


def greet_team(place):
    barrier = pltpu.get_barrier_semaphore()
    for axis, index in zip(TEAM, place):
        pl.semaphore_signal(
            barrier, inc=1, device_id={axis: 1 - index}, device_id_type=pl.DeviceIdType.MESH
        )
    pl.semaphore_wait(barrier, len(TEAM))


def member(place, flips):
    index = 0
    for own, flip in zip(place, flips):
        index = index * 2 + (1 - own if flip else own)
    return index


def gather_kernel(count, *refs):
    owns, alls = refs[:count], refs[count : 2 * count]
    own_sem, send_sem, recv_sem = refs[2 * count :]
    place = team_place()
    greet_team(place)
    me = member(place, (0, 0, 0))
    beside = member(place, (0, 1, 0))
    above = member(place, (1, 0, 0))
    across = member(place, (1, 1, 0))
    copies = [{} for _ in range(count)]
    keeps = []

    def send(item, number, axis, source, target):
        copy = pltpu.make_async_remote_copy(
            src_ref=source,
            dst_ref=target,
            send_sem=send_sem.at[item, number],
            recv_sem=recv_sem.at[item, number],
            device_id={TEAM[axis]: 1 - place[axis]},
            device_id_type=pl.DeviceIdType.MESH,
        )
        copy.start()
        copies[item][number] = copy

    def halves(item):
        half = owns[item].shape[0] // 2
        return pl.ds(0, half), pl.ds(half, half)

    for item in range(count):
        target = alls[item].at[me]
        send(item, 0, 1, owns[item], target)
        send(item, 1, 0, owns[item], target)
        send(item, 2, 2, owns[item], target)
        keeps.append(pltpu.make_async_copy(owns[item], target, own_sem.at[item]))
        keeps[item].start()
    for item in range(count):
        upper, lower = halves(item)
        copies[item][0].wait_recv()
        block = alls[item].at[beside]
        send(item, 3, 0, block.at[upper], block.at[upper])
        send(item, 4, 2, block, block)
        copies[item][1].wait_recv()
        block = alls[item].at[above]
        send(item, 5, 1, block.at[lower], block.at[lower])
        send(item, 6, 2, block, block)
    for item in range(count):
        upper, lower = halves(item)
        block = alls[item].at[across]
        copies[item][3].wait_recv()
        send(item, 7, 2, block.at[upper], block.at[upper])
        copies[item][5].wait_recv()
        send(item, 8, 2, block.at[lower], block.at[lower])
    for item in range(count):
        for number in (2, 4, 6, 7, 8):
            copies[item][number].wait_recv()
        for number in range(9):
            copies[item][number].wait_send()
        keeps[item].wait()


def gather_team(arrays, collective_id):
    count = len(arrays)
    gathered = pl.pallas_call(
        functools.partial(gather_kernel, count),
        out_shape=[jax.ShapeDtypeStruct((TEAM_SIZE,) + own.shape, own.dtype) for own in arrays],
        in_specs=[pl.BlockSpec(memory_space=pl.ANY)] * count,
        out_specs=[pl.BlockSpec(memory_space=pl.ANY)] * count,
        scratch_shapes=[
            pltpu.SemaphoreType.DMA((count,)),
            pltpu.SemaphoreType.DMA((count, 9)),
            pltpu.SemaphoreType.DMA((count, 9)),
        ],
        compiler_params=pltpu.CompilerParams(collective_id=collective_id, has_side_effects=True),
        cost_estimate=pl.CostEstimate(
            flops=0,
            bytes_accessed=sum(GATHER_COST * own.shape[0] * own.shape[1] for own in arrays),
            transcendentals=0,
        ),
    )(*arrays)
    return [
        whole.reshape(TEAM_SIZE * own.shape[0], own.shape[1])
        for whole, own in zip(gathered, arrays)
    ]


def scatter_kernel(
    product, left_ref, right_ref, sum_ref, own, out_near, in_near, out_far, in_half, in_full,
    send_sem, recv_sem,
):
    place = team_place()
    greet_team(place)
    rows = sum_ref.shape[0]
    half = rows // 2
    upper, lower = pl.ds(0, half), pl.ds(half, half)

    def send(number, axis, source, target):
        copy = pltpu.make_async_remote_copy(
            src_ref=source,
            dst_ref=target,
            send_sem=send_sem.at[number],
            recv_sem=recv_sem.at[number],
            device_id={TEAM[axis]: 1 - place[axis]},
            device_id_type=pl.DeviceIdType.MESH,
        )
        copy.start()
        return copy

    flips = ((1, 1), (0, 1), (1, 0), (0, 0))
    near, far = [], {}

    def begin(turn):
        first, second = flips[turn]
        product(left_ref, right_ref, member(place, (first, second, 1)), out_near.at[turn])
        near.append(send(turn, 2, out_near.at[turn], in_near.at[turn]))
        product(left_ref, right_ref, member(place, (first, second, 0)), own.at[turn])

    def join(turn):
        near[turn].wait_recv()
        return own[turn] + in_near[turn].astype(jnp.float32)

    begin(0)
    begin(1)
    out_far[0] = join(0).astype(jnp.bfloat16)
    far[4] = send(4, 1, out_far.at[0, upper], in_half.at[0])
    far[5] = send(5, 0, out_far.at[0, lower], in_half.at[1])
    begin(2)
    own[1] = join(1)
    out_far[1, upper] = own[1, upper].astype(jnp.bfloat16)
    far[6] = send(6, 1, out_far.at[1, upper], in_full.at[0, upper])
    begin(3)
    own[2] = join(2)
    out_far[2, lower] = own[2, lower].astype(jnp.bfloat16)
    far[7] = send(7, 0, out_far.at[2, lower], in_full.at[1, lower])
    sum_ref[...] = join(3)
    far[5].wait_recv()
    out_far[1, lower] = (own[1, lower] + in_half[1].astype(jnp.float32)).astype(jnp.bfloat16)
    far[8] = send(8, 1, out_far.at[1, lower], in_full.at[0, lower])
    far[4].wait_recv()
    out_far[2, upper] = (own[2, upper] + in_half[0].astype(jnp.float32)).astype(jnp.bfloat16)
    far[9] = send(9, 0, out_far.at[2, upper], in_full.at[1, upper])
    far[6].wait_recv()
    far[7].wait_recv()
    far[8].wait_recv()
    far[9].wait_recv()
    sum_ref[...] = (
        sum_ref[...] + in_full[0].astype(jnp.float32) + in_full[1].astype(jnp.float32)
    )
    for copy in near + [far[number] for number in range(4, 10)]:
        copy.wait_send()


def product_rows(left_ref, right_ref, block, target):
    tile = 512

    def one(step, carry):
        columns = pl.ds(pl.multiple_of(step * tile, tile), tile)
        target[:, columns] = jnp.dot(
            left_ref[block], right_ref[:, columns], preferred_element_type=jnp.float32
        ).astype(target.dtype)
        return carry

    lax.fori_loop(0, target.shape[1] // tile, one, 0)


def product_back(left_ref, right_ref, block, target):
    parts, _, rows, depth = right_ref.shape
    tile = parts * rows

    def one(step, carry):
        columns = pl.ds(pl.multiple_of(step * tile, tile), tile)
        target[:, columns] = dot_t(
            left_ref[block], right_ref[:, step].reshape(tile, depth)
        ).astype(target.dtype)
        return carry

    lax.fori_loop(0, target.shape[1] // tile, one, 0)


def scatter_team(product, left, right, collective_id):
    rows = left.shape[0] // TEAM_SIZE
    depth = left.shape[1]
    width = MODEL_WIDTH
    return pl.pallas_call(
        functools.partial(scatter_kernel, product),
        out_shape=jax.ShapeDtypeStruct((rows, width), jnp.float32),
        in_specs=[pl.BlockSpec(memory_space=pltpu.VMEM)] * 2,
        out_specs=pl.BlockSpec(memory_space=pltpu.VMEM),
        scratch_shapes=[
            pltpu.VMEM((4, rows, width), jnp.float32),
            pltpu.VMEM((4, rows, width), jnp.bfloat16),
            pltpu.VMEM((4, rows, width), jnp.bfloat16),
            pltpu.VMEM((3, rows, width), jnp.bfloat16),
            pltpu.VMEM((2, rows // 2, width), jnp.bfloat16),
            pltpu.VMEM((2, rows, width), jnp.bfloat16),
            pltpu.SemaphoreType.DMA((10,)),
            pltpu.SemaphoreType.DMA((10,)),
        ],
        compiler_params=pltpu.CompilerParams(
            collective_id=collective_id, has_side_effects=True, vmem_limit_bytes=VMEM_BYTES
        ),
        cost_estimate=pl.CostEstimate(
            flops=2 * left.shape[0] * depth * width,
            bytes_accessed=SCATTER_COST * rows * width,
            transcendentals=0,
        ),
    )(left.reshape(TEAM_SIZE, rows, depth), right)


def total_kernel(own_ref, sum_ref, stage, landed, slots, send_sem, recv_sem):
    place = team_place()
    barrier = pltpu.get_barrier_semaphore()
    others = []
    for axis in DEPTH:
        count, index = lax.axis_size(axis), lax.axis_index(axis)
        for distance in range(1, count):
            others.append((axis, lax.rem(index + distance, count)))
    for axis, index in list(zip(TEAM, (1 - own for own in place))) + others:
        pl.semaphore_signal(
            barrier, inc=1, device_id={axis: index}, device_id_type=pl.DeviceIdType.MESH
        )
    pl.semaphore_wait(barrier, len(TEAM) + len(others))
    copies = []

    def send(source, target, axis, index):
        copy = pltpu.make_async_remote_copy(
            src_ref=source,
            dst_ref=target,
            send_sem=send_sem.at[len(copies)],
            recv_sem=recv_sem.at[len(copies)],
            device_id={axis: index},
            device_id_type=pl.DeviceIdType.MESH,
        )
        copy.start()
        copies.append(copy)

    stage[0] = own_ref[...]
    for turn in range(len(TEAM)):
        send(stage.at[turn], landed.at[turn], TEAM[-1 - turn], 1 - place[-1 - turn])
        copies[turn].wait_recv()
        stage[turn + 1] = stage[turn] + landed[turn]
    turn = len(TEAM)
    first = 0
    for axis in DEPTH:
        count, index = lax.axis_size(axis), lax.axis_index(axis)
        slots[first + index] = stage[turn]
        begun = len(copies)
        for distance in range(1, count):
            send(
                stage.at[turn], slots.at[first + index], axis, lax.rem(index + distance, count)
            )
        for copy in copies[begun:]:
            copy.wait_recv()
        total = slots[first]
        for item in range(1, count):
            total = total + slots[first + item]
        turn, first = turn + 1, first + count
        stage[turn] = total
    sum_ref[...] = stage[turn]
    for copy in copies:
        copy.wait_send()


def total_all(values, collective_id):
    sizes = [lax.axis_size(axis) for axis in DEPTH]
    copies = len(TEAM) + sum(sizes) - len(sizes)
    return pl.pallas_call(
        total_kernel,
        out_shape=jax.ShapeDtypeStruct(values.shape, values.dtype),
        in_specs=[pl.BlockSpec(memory_space=pltpu.VMEM)],
        out_specs=pl.BlockSpec(memory_space=pltpu.VMEM),
        scratch_shapes=[
            pltpu.VMEM((len(TEAM) + len(DEPTH) + 1,) + values.shape, values.dtype),
            pltpu.VMEM((len(TEAM),) + values.shape, values.dtype),
            pltpu.VMEM((sum(sizes),) + values.shape, values.dtype),
            pltpu.SemaphoreType.DMA((copies,)),
            pltpu.SemaphoreType.DMA((copies,)),
        ],
        compiler_params=pltpu.CompilerParams(collective_id=collective_id, has_side_effects=True),
    )(values)


def team_exchange(blocks):
    return lax.all_to_all(blocks, TEAM, split_axis=0, concat_axis=0, tiled=True)


def shift_seq(value_rows, distance):
    count = lax.axis_size("seq")
    pairs = [(i, i + distance) for i in range(count) if 0 <= i + distance < count]
    return lax.ppermute(value_rows, "seq", pairs)


def team_columns(matrix, widths):
    pieces = []
    lower = 0
    for width in widths:
        piece = matrix[:, lower : lower + width]
        pieces.append(piece.reshape(matrix.shape[0], TEAM_SIZE, width // TEAM_SIZE))
        lower = lower + width
    return jnp.concatenate(pieces, axis=2).transpose(1, 0, 2)


def whole_columns(blocks, widths):
    pieces = []
    lower = 0
    for width in widths:
        share = width // TEAM_SIZE
        piece = blocks[:, :, lower : lower + share]
        pieces.append(piece.transpose(1, 0, 2).reshape(blocks.shape[1], width))
        lower = lower + share
    return jnp.concatenate(pieces, axis=1)


def gather_columns(matrix, widths):
    blocks = team_exchange(team_columns(matrix, widths))
    return lax.all_gather(blocks, DEPTH, axis=0, tiled=False)


def in_order(parts):
    return parts.transpose(1, 0, 2, 3).reshape(-1, parts.shape[3])


def scatter_columns(gradient, rows, widths):
    depth = gradient.shape[0] // (TEAM_SIZE * rows)
    ordered = gradient.astype(jnp.bfloat16).reshape(TEAM_SIZE, depth, rows, -1).transpose(1, 0, 2, 3)
    mine = lax.psum_scatter(
        ordered.reshape(gradient.shape), DEPTH, scatter_dimension=0, tiled=True
    ).reshape(TEAM_SIZE, rows, -1)
    return whole_columns(team_exchange(mine), widths).astype(jnp.float32)


def gather_rows(matrix):
    return lax.all_gather(matrix, DEPTH, axis=0, tiled=True)


def scatter_rows(gradient):
    return lax.psum_scatter(
        gradient.astype(jnp.bfloat16), DEPTH, scatter_dimension=0, tiled=True
    ).astype(jnp.float32)


def moments(weight, moment, second, gradient):
    moment_new = BETA * moment + (1.0 - BETA) * gradient
    second_new = BETA * second + (1.0 - BETA) * gradient * gradient
    correction = 1.0 - BETA**STEP
    update = (
        moment_new / correction / (jnp.sqrt(second_new / correction) + ADAM_EPS) + DECAY * weight
    )
    return (moment_new, second_new, update)


def group_squares(matrix, widths):
    sums = []
    lower = 0
    for width in widths:
        piece = matrix[:, lower : lower + width]
        sums.append(jnp.sum(piece * piece))
        lower = lower + width
    return jnp.stack(sums)


def apply_trust(weight, update, trust, widths):
    factors = [jnp.broadcast_to(trust[index], (width,)) for index, width in enumerate(widths)]
    return weight - RATE * jnp.concatenate(factors)[None, :] * update


def row_update(weight, moment, second, gradient):
    moment_new, second_new, update = moments(weight, moment, second, gradient)
    trust = jnp.sqrt(jnp.sum(weight * weight, axis=-1, keepdims=True)) / jnp.sqrt(
        jnp.sum(update * update, axis=-1, keepdims=True)
    )
    return (weight - RATE * trust * update, moment_new, second_new)


def whole_update(weight, moment, second, gradient):
    moment_new, second_new, update = moments(weight, moment, second, gradient)
    trust = jnp.sqrt(jnp.sum(weight * weight)) / jnp.sqrt(jnp.sum(update * update))
    return (weight - RATE * trust * update, moment_new, second_new)


def shards(
    inputs,
    cotangent,
    doc_lengths,
    projection_weight,
    projection_moment,
    projection_second,
    out_weight,
    out_moment,
    out_second,
    ffn_weight,
    ffn_moment,
    ffn_second,
    down_weight,
    down_moment,
    down_second,
    head_gate,
    gate_moment,
    gate_second,
    norm_gains,
    gains_moment,
    gains_second,
    qk_gains,
    qk_moment,
    qk_second,
):
    rows_dev, local_len, width = inputs.shape
    bf16 = jnp.bfloat16
    team = lax.axis_index(TEAM)
    place_seq = lax.axis_index("seq")
    group_heads = QUERY_HEADS // KEY_VALUE_HEADS
    window = -(-(DOC_MOST - 1) // local_len)
    window = min(window, lax.axis_size("seq") - 1)
    query_cols = QUERY_HEADS * HEAD_WIDTH
    key_value_columns = KEY_VALUE_HEADS * HEAD_WIDTH
    widths_qkv = (query_cols, key_value_columns, key_value_columns)
    widths_ffn = (FF, FF)
    own_query = query_cols // TEAM_SIZE
    own_key = key_value_columns // TEAM_SIZE
    own_ff = FF // TEAM_SIZE
    scale = HEAD_WIDTH ** (-0.5)
    weight_squares = jnp.concatenate(
        [
            group_squares(projection_weight, widths_qkv),
            group_squares(out_weight, (MODEL_WIDTH,)),
            group_squares(ffn_weight, widths_ffn),
            group_squares(down_weight, (MODEL_WIDTH,)),
        ]
    )
    own_qkv = gather_columns(projection_weight.astype(bf16), widths_qkv)
    own_out = gather_rows(out_weight.astype(bf16))
    own_ffn = gather_columns(ffn_weight.astype(bf16), widths_ffn)
    own_down = gather_rows(down_weight.astype(bf16))
    own_gate = lax.dynamic_slice_in_dim(head_gate.astype(bf16), team * group_heads, group_heads, 1)
    own_gate = jnp.pad(own_gate, ((0, 0), (0, LANES - group_heads)))
    gate_parts = own_gate.reshape(TEAM_SIZE, own_qkv.shape[0], own_qkv.shape[2], LANES)
    own_qkv = jnp.concatenate([own_qkv, gate_parts.transpose(1, 0, 2, 3)], axis=3)
    lengths = lax.all_gather(doc_lengths, TEAM, axis=0, tiled=True)
    place = place_seq * local_len + jnp.arange(local_len, dtype=jnp.int32)
    key_place = (place_seq - window) * local_len + jnp.arange(
        (window + 1) * local_len, dtype=jnp.int32
    )
    segment, position = doc_tables(lengths, place)
    key_segment, _ = doc_tables(lengths, key_place)
    cosine, sine = rotary_tables(position, HEAD_WIDTH)
    allowed = (segment[:, :, None] == key_segment[:, None, :]) & (
        key_place[None, None, :] <= place[None, :, None]
    )
    inputs_flat = inputs[0].astype(jnp.float32)
    normed = rms_apply(inputs_flat, norm_gains[0]).astype(bf16)
    normed_all, grad_all = gather_team([normed, cotangent[0]], 0)
    products = jnp.dot(normed_all, in_order(own_qkv), preferred_element_type=jnp.float32)
    projected = products[:, : own_query + 2 * own_key].astype(bf16)
    gate = jax.nn.sigmoid(products[:, own_query + 2 * own_key :][:, :group_heads])
    gate = gate.reshape(TEAM_SIZE, local_len, group_heads)
    query_raw = (
        projected[:, :own_query]
        .reshape(TEAM_SIZE, local_len, group_heads, HEAD_WIDTH)
        .astype(jnp.float32)
    )
    key_raw = (
        projected[:, own_query : own_query + own_key]
        .reshape(TEAM_SIZE, local_len, HEAD_WIDTH)
        .astype(jnp.float32)
    )
    value = projected[:, own_query + own_key : own_query + 2 * own_key].reshape(TEAM_SIZE, local_len, HEAD_WIDTH)
    query_rot = rotate(
        rms_apply(query_raw, qk_gains[0]), cosine[:, :, None], sine[:, :, None]
    ).astype(bf16)
    key_rot = rotate(rms_apply(key_raw, qk_gains[1]), cosine, sine).astype(bf16)
    pair = jnp.concatenate([key_rot, value], axis=2)
    blocks = [shift_seq(pair, distance) for distance in range(window, 0, -1)] + [pair]
    pair_window = jnp.concatenate(blocks, axis=1)
    keys = pair_window[:, :, :HEAD_WIDTH]
    values = pair_window[:, :, HEAD_WIDTH:]
    scores = (
        jnp.einsum("bqgd,bkd->bgqk", query_rot, keys, preferred_element_type=jnp.float32) * scale
    )
    scores = jnp.where(allowed[:, None], scores, NEGATIVE)
    top = jnp.max(scores, axis=-1, keepdims=True)
    powers = jnp.exp(scores - top)
    probs = powers / jnp.sum(powers, axis=-1, keepdims=True)
    low_probs = probs.astype(bf16)
    attended = jnp.einsum(
        "bgqk,bkd->bqgd", low_probs, values, preferred_element_type=jnp.float32
    ).astype(bf16)
    attended_wide = attended.astype(jnp.float32)
    gated = (attended_wide * gate[..., None]).astype(bf16).reshape(-1, own_query)
    middle = inputs_flat + scatter_team(product_rows, gated, own_out, 1)
    normed2 = rms_apply(middle, norm_gains[1]).astype(bf16)
    normed2_all = gather_team([normed2], 2)[0]
    both = jnp.dot(normed2_all, in_order(own_ffn), preferred_element_type=jnp.float32)
    inner = both[:, :own_ff]
    up_part = both[:, own_ff:]
    sigma_inner = jax.nn.sigmoid(inner)
    hidden = (inner * sigma_inner * up_part).astype(bf16)
    final = middle + scatter_team(product_rows, hidden, own_down, 3)
    result = final.astype(bf16).reshape(inputs.shape)
    grad_final = cotangent[0].astype(jnp.float32)
    grad_hidden = dot_t(grad_all, own_down)
    grad_inner = grad_hidden * up_part * sigma_inner * (1.0 + inner * (1.0 - sigma_inner))
    grad_up = grad_hidden * inner * sigma_inner
    grad_both = jnp.concatenate([grad_inner, grad_up], axis=1).astype(bf16)
    down_grad = scatter_rows(dot_tokens(hidden, grad_all))
    ffn_grad = scatter_columns(
        dot_tokens(normed2_all, grad_both), ffn_weight.shape[0], widths_ffn
    )
    grad_normed2 = scatter_team(product_back, grad_both, own_ffn, 4)
    grad_mid_part, gain_mid = rms_back(middle, norm_gains[1], grad_normed2)
    grad_middle = grad_final + grad_mid_part
    grad_middle_all = gather_team([grad_middle.astype(bf16)], 5)[0]
    out_grad = scatter_rows(dot_tokens(gated, grad_middle_all))
    grad_gated = dot_t(grad_middle_all, own_out).reshape(attended.shape)
    grad_attended = (grad_gated * gate[..., None]).astype(bf16)
    grad_gate_pre = (
        (jnp.sum(grad_gated * attended_wide, axis=-1) * gate * (1.0 - gate))
        .astype(bf16)
        .reshape(-1, group_heads)
    )
    grad_probs = jnp.einsum(
        "bqgd,bkd->bgqk", grad_attended, values, preferred_element_type=jnp.float32
    )
    grad_scores = (
        probs * (grad_probs - jnp.sum(probs * grad_probs, axis=-1, keepdims=True))
    ).astype(bf16)
    grad_values = jnp.einsum(
        "bgqk,bqgd->bkd", low_probs, grad_attended, preferred_element_type=jnp.float32
    )
    grad_query_rot = (
        jnp.einsum("bgqk,bkd->bqgd", grad_scores, keys, preferred_element_type=jnp.float32) * scale
    )
    grad_keys = (
        jnp.einsum("bgqk,bqgd->bkd", grad_scores, query_rot, preferred_element_type=jnp.float32)
        * scale
    )
    grad_pair = jnp.concatenate([grad_keys, grad_values], axis=2)
    grad_own = grad_pair[:, window * local_len :]
    for distance in range(1, window + 1):
        lower = (window - distance) * local_len
        grad_own = grad_own + shift_seq(
            grad_pair[:, lower : lower + local_len].astype(bf16), -distance
        ).astype(jnp.float32)
    grad_query_raw, gain_query = rms_back(
        query_raw, qk_gains[0], rotate(grad_query_rot, cosine[:, :, None], -sine[:, :, None])
    )
    grad_key_raw, gain_key = rms_back(
        key_raw, qk_gains[1], rotate(grad_own[:, :, :HEAD_WIDTH], cosine, -sine)
    )
    qk_local = jnp.stack([jnp.sum(gain_query, axis=(0, 1, 2)), jnp.sum(gain_key, axis=(0, 1))])
    grad_projected = jnp.concatenate(
        [
            grad_query_raw.reshape(-1, own_query),
            grad_key_raw.reshape(-1, own_key),
            grad_own[:, :, HEAD_WIDTH:].reshape(-1, own_key),
        ],
        axis=1,
    ).astype(bf16)
    grad_products = jnp.concatenate(
        [grad_projected, jnp.pad(grad_gate_pre, ((0, 0), (0, LANES - group_heads)))], axis=1
    )
    grad_normed = scatter_team(product_back, grad_products, own_qkv, 6)
    grad_in_part, gain_in = rms_back(inputs_flat, norm_gains[0], grad_normed)
    input_grad = (grad_middle + grad_in_part).reshape(inputs.shape)
    products_grad = dot_tokens(normed_all, grad_products)
    projection_gradient = scatter_columns(
        products_grad[:, : own_query + 2 * own_key], projection_weight.shape[0], widths_qkv
    )
    gains_local = jnp.stack([jnp.sum(gain_in, axis=0), jnp.sum(gain_mid, axis=0)])
    gate_local = lax.dynamic_update_slice_in_dim(
        jnp.zeros((QUERY_HEADS, MODEL_WIDTH), jnp.float32),
        products_grad[:, own_query + 2 * own_key :][:, :group_heads].T,
        team * group_heads,
        0,
    )
    projection_moment_next, projection_second_next, qkv_update = moments(
        projection_weight, projection_moment, projection_second, projection_gradient
    )
    out_moment_new, out_second_new, out_update = moments(
        out_weight, out_moment, out_second, out_grad
    )
    ffn_moment_new, ffn_second_new, ffn_update = moments(
        ffn_weight, ffn_moment, ffn_second, ffn_grad
    )
    down_moment_new, down_second_new, down_update = moments(
        down_weight, down_moment, down_second, down_grad
    )
    update_squares = jnp.concatenate(
        [
            group_squares(qkv_update, widths_qkv),
            group_squares(out_update, (MODEL_WIDTH,)),
            group_squares(ffn_update, widths_ffn),
            group_squares(down_update, (MODEL_WIDTH,)),
        ]
    )
    groups = weight_squares.shape[0]
    small = jnp.concatenate([qk_local.reshape(-1), weight_squares, update_squares])
    totals = total_all(
        jnp.concatenate(
            [
                gate_local,
                gains_local,
                jnp.pad(small, (0, MODEL_WIDTH - small.shape[0]))[None],
                jnp.zeros((5, MODEL_WIDTH), jnp.float32),
            ]
        ),
        7,
    )
    gate_grad = totals[:QUERY_HEADS]
    gains_grad = totals[QUERY_HEADS : QUERY_HEADS + 2]
    small = totals[QUERY_HEADS + 2]
    qk_grad = small[: 2 * HEAD_WIDTH].reshape(2, HEAD_WIDTH)
    weight_totals = small[2 * HEAD_WIDTH : 2 * HEAD_WIDTH + groups]
    update_totals = small[2 * HEAD_WIDTH + groups : 2 * HEAD_WIDTH + 2 * groups]
    weight_norms = jnp.sqrt(weight_totals)
    update_norms = jnp.sqrt(update_totals)
    trust = weight_norms / update_norms
    projection_weight_next = apply_trust(projection_weight, qkv_update, trust[0:3], widths_qkv)
    out_new = apply_trust(out_weight, out_update, trust[3:4], (MODEL_WIDTH,))
    ffn_new = apply_trust(ffn_weight, ffn_update, trust[4:6], widths_ffn)
    down_new = apply_trust(down_weight, down_update, trust[6:7], (MODEL_WIDTH,))
    head_gate_new, gate_moment_new, gate_second_new = whole_update(
        head_gate, gate_moment, gate_second, gate_grad.T
    )
    gains_new, gains_moment_new, gains_second_new = row_update(
        norm_gains, gains_moment, gains_second, gains_grad
    )
    qk_new, qk_moment_new, qk_second_new = row_update(qk_gains, qk_moment, qk_second, qk_grad)
    lamb_norms = jnp.stack([weight_norms, update_norms])
    return (
        result,
        input_grad,
        projection_weight_next,
        projection_moment_next,
        projection_second_next,
        projection_weight_next.astype(jnp.bfloat16),
        out_new,
        out_moment_new,
        out_second_new,
        out_new.astype(jnp.bfloat16),
        ffn_new,
        ffn_moment_new,
        ffn_second_new,
        ffn_new.astype(jnp.bfloat16),
        down_new,
        down_moment_new,
        down_second_new,
        down_new.astype(jnp.bfloat16),
        head_gate_new,
        gate_moment_new,
        gate_second_new,
        gains_new,
        gains_moment_new,
        gains_second_new,
        qk_new,
        qk_moment_new,
        qk_second_new,
        lamb_norms,
    )


def solution(mesh):
    mesh = Mesh(
        mesh.devices.reshape(2, 2, 2, mesh.shape["fsdp"] // TEAM_SIZE, mesh.shape["seq"]),
        TEAM + DEPTH,
    )
    rows = TEAM + DEPTH[:1]
    in_specs = (
        P(rows, "seq", None),
        P(rows, "seq", None),
        P(rows, None),
        P(TEAM + DEPTH, None),
        P(TEAM + DEPTH, None),
        P(TEAM + DEPTH, None),
        P(TEAM + DEPTH, None),
        P(TEAM + DEPTH, None),
        P(TEAM + DEPTH, None),
        P(TEAM + DEPTH, None),
        P(TEAM + DEPTH, None),
        P(TEAM + DEPTH, None),
        P(TEAM + DEPTH, None),
        P(TEAM + DEPTH, None),
        P(TEAM + DEPTH, None),
        P(),
        P(),
        P(),
        P(),
        P(),
        P(),
        P(),
        P(),
        P(),
    )
    out_specs = (
        P(rows, "seq", None),
        P(rows, "seq", None),
        P(TEAM + DEPTH, None),
        P(TEAM + DEPTH, None),
        P(TEAM + DEPTH, None),
        P(TEAM + DEPTH, None),
        P(TEAM + DEPTH, None),
        P(TEAM + DEPTH, None),
        P(TEAM + DEPTH, None),
        P(TEAM + DEPTH, None),
        P(TEAM + DEPTH, None),
        P(TEAM + DEPTH, None),
        P(TEAM + DEPTH, None),
        P(TEAM + DEPTH, None),
        P(TEAM + DEPTH, None),
        P(TEAM + DEPTH, None),
        P(TEAM + DEPTH, None),
        P(TEAM + DEPTH, None),
        P(),
        P(),
        P(),
        P(),
        P(),
        P(),
        P(),
        P(),
        P(),
        P(),
    )
    return jax.shard_map(shards, mesh=mesh, in_specs=in_specs, out_specs=out_specs, check_vma=False)
```

```python
import functools

import jax
import jax.numpy as jnp
from jax import lax
from jax.experimental import pallas as pl
from jax.experimental.pallas import tpu as pltpu
from jax.sharding import Mesh
from jax.sharding import PartitionSpec as P

MODEL_WIDTH = 2048
QUERY_HEADS = 16
KEY_VALUE_HEADS = 8
HEAD_WIDTH = 128
FF = 6144
ROW_TOKENS = 1024
STEP = 3
DOC_MOST = 512
TEAM_SIZE = 8
TEAM = ("t2", "t1", "t0")
DEPTH = ("spare", "seq")
LANES = 128
SUBLANES = 8
VMEM_BYTES = 48 << 20
GATHER_COST = 250
SCATTER_COST = 320
ATTEND_COST = 50


NORM_EPS = 1e-06
ADAM_EPS = 1e-06
RATE = 0.3
DECAY = 0.01
BETA = 0.5
THETA = 1000000.0
NEGATIVE = -1e30


def rms_apply(value_rows, gain):
    return (
        value_rows
        * lax.rsqrt(jnp.mean(value_rows * value_rows, axis=-1, keepdims=True) + NORM_EPS)
        * gain
    )


def rms_back(value_rows, gain, gradient):
    scale = lax.rsqrt(jnp.mean(value_rows * value_rows, axis=-1, keepdims=True) + NORM_EPS)
    scaled = gradient * gain
    inner = jnp.mean(scaled * value_rows, axis=-1, keepdims=True)
    grad_value = scale * scaled - value_rows * scale * scale * scale * inner
    grad_gain = gradient * value_rows * scale
    return (grad_value, grad_gain)


def dot_t(left, right):
    return lax.dot_general(
        left, right, (((1,), (1,)), ((), ())), preferred_element_type=jnp.float32
    )


def low_tokens(left, right):
    return dot_tokens(left, right).astype(jnp.bfloat16)


def dot_tokens(left, right):
    return lax.dot_general(
        left, right, (((0,), (0,)), ((), ())), preferred_element_type=jnp.float32
    )


def rotary_tables(position, width):
    half = width // 2
    rates = THETA ** (-jnp.arange(half, dtype=jnp.float32) * 2.0 / width)
    angle = position.astype(jnp.float32)[..., None] * rates
    cosine, sine = jnp.cos(angle), jnp.sin(angle)
    return (
        jnp.concatenate([cosine, cosine], axis=-1),
        jnp.concatenate([-sine, sine], axis=-1),
    )


def positions(lengths, place):
    ends = jnp.cumsum(lengths, axis=1)
    starts = ends - lengths
    inside = (place[None, :, None] >= starts[:, None, :]) & (place[None, :, None] < ends[:, None, :])
    return place[None, :] - jnp.sum(jnp.where(inside, starts[:, None, :], 0), axis=2)


def team_place():
    return tuple(lax.axis_index(axis) for axis in TEAM)


def greet_team(place):
    barrier = pltpu.get_barrier_semaphore()
    for axis, index in zip(TEAM, place):
        pl.semaphore_signal(
            barrier, inc=1, device_id={axis: 1 - index}, device_id_type=pl.DeviceIdType.MESH
        )
    pl.semaphore_wait(barrier, len(TEAM))


def member(place, flips):
    index = 0
    for own, flip in zip(place, flips):
        index = index * 2 + (1 - own if flip else own)
    return index


def gather_kernel(count, *refs):
    owns, alls = refs[:count], refs[count : 2 * count]
    own_sem, send_sem, recv_sem = refs[2 * count :]
    place = team_place()
    greet_team(place)
    me = member(place, (0, 0, 0))
    beside = member(place, (0, 1, 0))
    above = member(place, (1, 0, 0))
    across = member(place, (1, 1, 0))
    copies = [{} for _ in range(count)]
    keeps = []

    def send(item, number, axis, source, target):
        copy = pltpu.make_async_remote_copy(
            src_ref=source,
            dst_ref=target,
            send_sem=send_sem.at[item, number],
            recv_sem=recv_sem.at[item, number],
            device_id={TEAM[axis]: 1 - place[axis]},
            device_id_type=pl.DeviceIdType.MESH,
        )
        copy.start()
        copies[item][number] = copy

    def halves(item):
        half = owns[item].shape[0] // 2
        return pl.ds(0, half), pl.ds(half, half)

    for item in range(count):
        target = alls[item].at[me]
        send(item, 0, 1, owns[item], target)
        send(item, 1, 0, owns[item], target)
        send(item, 2, 2, owns[item], target)
        keeps.append(pltpu.make_async_copy(owns[item], target, own_sem.at[item]))
        keeps[item].start()
    for item in range(count):
        upper, lower = halves(item)
        copies[item][0].wait_recv()
        block = alls[item].at[beside]
        send(item, 3, 0, block.at[upper], block.at[upper])
        send(item, 4, 2, block, block)
        copies[item][1].wait_recv()
        block = alls[item].at[above]
        send(item, 5, 1, block.at[lower], block.at[lower])
        send(item, 6, 2, block, block)
    for item in range(count):
        upper, lower = halves(item)
        block = alls[item].at[across]
        copies[item][3].wait_recv()
        send(item, 7, 2, block.at[upper], block.at[upper])
        copies[item][5].wait_recv()
        send(item, 8, 2, block.at[lower], block.at[lower])
    for item in range(count):
        for number in (2, 4, 6, 7, 8):
            copies[item][number].wait_recv()
        for number in range(9):
            copies[item][number].wait_send()
        keeps[item].wait()


def gather_team(arrays, collective_id):
    count = len(arrays)
    gathered = pl.pallas_call(
        functools.partial(gather_kernel, count),
        out_shape=[jax.ShapeDtypeStruct((TEAM_SIZE,) + own.shape, own.dtype) for own in arrays],
        in_specs=[pl.BlockSpec(memory_space=pl.ANY)] * count,
        out_specs=[pl.BlockSpec(memory_space=pl.ANY)] * count,
        scratch_shapes=[
            pltpu.SemaphoreType.DMA((count,)),
            pltpu.SemaphoreType.DMA((count, 9)),
            pltpu.SemaphoreType.DMA((count, 9)),
        ],
        compiler_params=pltpu.CompilerParams(collective_id=collective_id, has_side_effects=True),
        cost_estimate=pl.CostEstimate(
            flops=0,
            bytes_accessed=sum(GATHER_COST * own.shape[0] * own.shape[1] for own in arrays),
            transcendentals=0,
        ),
    )(*arrays)
    return [
        whole.reshape(TEAM_SIZE * own.shape[0], own.shape[1])
        for whole, own in zip(gathered, arrays)
    ]


def scatter_kernel(
    product, left_ref, right_ref, sum_ref, own, out_near, in_near, out_far, in_half, in_full,
    send_sem, recv_sem,
):
    place = team_place()
    greet_team(place)
    rows = sum_ref.shape[0]
    half = rows // 2
    upper, lower = pl.ds(0, half), pl.ds(half, half)

    def send(number, axis, source, target):
        copy = pltpu.make_async_remote_copy(
            src_ref=source,
            dst_ref=target,
            send_sem=send_sem.at[number],
            recv_sem=recv_sem.at[number],
            device_id={TEAM[axis]: 1 - place[axis]},
            device_id_type=pl.DeviceIdType.MESH,
        )
        copy.start()
        return copy

    flips = ((1, 1), (0, 1), (1, 0), (0, 0))
    near, far = [], {}

    def begin(turn):
        first, second = flips[turn]
        product(left_ref, right_ref, member(place, (first, second, 1)), out_near.at[turn])
        near.append(send(turn, 2, out_near.at[turn], in_near.at[turn]))
        product(left_ref, right_ref, member(place, (first, second, 0)), own.at[turn])

    def join(turn):
        near[turn].wait_recv()
        return own[turn] + in_near[turn].astype(jnp.float32)

    begin(0)
    begin(1)
    out_far[0] = join(0).astype(jnp.bfloat16)
    far[4] = send(4, 1, out_far.at[0, upper], in_half.at[0])
    far[5] = send(5, 0, out_far.at[0, lower], in_half.at[1])
    begin(2)
    own[1] = join(1)
    out_far[1, upper] = own[1, upper].astype(jnp.bfloat16)
    far[6] = send(6, 1, out_far.at[1, upper], in_full.at[0, upper])
    begin(3)
    own[2] = join(2)
    out_far[2, lower] = own[2, lower].astype(jnp.bfloat16)
    far[7] = send(7, 0, out_far.at[2, lower], in_full.at[1, lower])
    sum_ref[...] = join(3)
    far[5].wait_recv()
    out_far[1, lower] = (own[1, lower] + in_half[1].astype(jnp.float32)).astype(jnp.bfloat16)
    far[8] = send(8, 1, out_far.at[1, lower], in_full.at[0, lower])
    far[4].wait_recv()
    out_far[2, upper] = (own[2, upper] + in_half[0].astype(jnp.float32)).astype(jnp.bfloat16)
    far[9] = send(9, 0, out_far.at[2, upper], in_full.at[1, upper])
    far[6].wait_recv()
    far[7].wait_recv()
    far[8].wait_recv()
    far[9].wait_recv()
    sum_ref[...] = (
        sum_ref[...] + in_full[0].astype(jnp.float32) + in_full[1].astype(jnp.float32)
    )
    for copy in near + [far[number] for number in range(4, 10)]:
        copy.wait_send()


def product_rows(left_ref, right_ref, block, target):
    tile = 512

    def one(step, carry):
        columns = pl.ds(pl.multiple_of(step * tile, tile), tile)
        target[:, columns] = jnp.dot(
            left_ref[block], right_ref[:, columns], preferred_element_type=jnp.float32
        ).astype(target.dtype)
        return carry

    lax.fori_loop(0, target.shape[1] // tile, one, 0)


def product_back(left_ref, right_ref, block, target):
    parts, _, rows, depth = right_ref.shape
    tile = parts * rows

    def one(step, carry):
        columns = pl.ds(pl.multiple_of(step * tile, tile), tile)
        target[:, columns] = dot_t(
            left_ref[block], right_ref[:, step].reshape(tile, depth)
        ).astype(target.dtype)
        return carry

    lax.fori_loop(0, target.shape[1] // tile, one, 0)


def scatter_team(product, left, right, collective_id):
    rows = left.shape[0] // TEAM_SIZE
    depth = left.shape[1]
    width = MODEL_WIDTH
    return pl.pallas_call(
        functools.partial(scatter_kernel, product),
        out_shape=jax.ShapeDtypeStruct((rows, width), jnp.float32),
        in_specs=[pl.BlockSpec(memory_space=pltpu.VMEM)] * 2,
        out_specs=pl.BlockSpec(memory_space=pltpu.VMEM),
        scratch_shapes=[
            pltpu.VMEM((4, rows, width), jnp.float32),
            pltpu.VMEM((4, rows, width), jnp.bfloat16),
            pltpu.VMEM((4, rows, width), jnp.bfloat16),
            pltpu.VMEM((3, rows, width), jnp.bfloat16),
            pltpu.VMEM((2, rows // 2, width), jnp.bfloat16),
            pltpu.VMEM((2, rows, width), jnp.bfloat16),
            pltpu.SemaphoreType.DMA((10,)),
            pltpu.SemaphoreType.DMA((10,)),
        ],
        compiler_params=pltpu.CompilerParams(
            collective_id=collective_id, has_side_effects=True, vmem_limit_bytes=VMEM_BYTES
        ),
        cost_estimate=pl.CostEstimate(
            flops=2 * left.shape[0] * depth * width,
            bytes_accessed=SCATTER_COST * rows * width,
            transcendentals=0,
        ),
    )(left.reshape(TEAM_SIZE, rows, depth), right)


def total_kernel(own_ref, sum_ref, stage, landed, slots, send_sem, recv_sem):
    place = team_place()
    barrier = pltpu.get_barrier_semaphore()
    others = []
    for axis in DEPTH:
        count, index = lax.axis_size(axis), lax.axis_index(axis)
        for distance in range(1, count):
            others.append((axis, lax.rem(index + distance, count)))
    for axis, index in list(zip(TEAM, (1 - own for own in place))) + others:
        pl.semaphore_signal(
            barrier, inc=1, device_id={axis: index}, device_id_type=pl.DeviceIdType.MESH
        )
    pl.semaphore_wait(barrier, len(TEAM) + len(others))
    copies = []

    def send(source, target, axis, index):
        copy = pltpu.make_async_remote_copy(
            src_ref=source,
            dst_ref=target,
            send_sem=send_sem.at[len(copies)],
            recv_sem=recv_sem.at[len(copies)],
            device_id={axis: index},
            device_id_type=pl.DeviceIdType.MESH,
        )
        copy.start()
        copies.append(copy)

    stage[0] = own_ref[...]
    for turn in range(len(TEAM)):
        send(stage.at[turn], landed.at[turn], TEAM[-1 - turn], 1 - place[-1 - turn])
        copies[turn].wait_recv()
        stage[turn + 1] = stage[turn] + landed[turn]
    turn = len(TEAM)
    first = 0
    for axis in DEPTH:
        count, index = lax.axis_size(axis), lax.axis_index(axis)
        slots[first + index] = stage[turn]
        begun = len(copies)
        for distance in range(1, count):
            send(
                stage.at[turn], slots.at[first + index], axis, lax.rem(index + distance, count)
            )
        for copy in copies[begun:]:
            copy.wait_recv()
        total = slots[first]
        for item in range(1, count):
            total = total + slots[first + item]
        turn, first = turn + 1, first + count
        stage[turn] = total
    sum_ref[...] = stage[turn]
    for copy in copies:
        copy.wait_send()


def total_all(values, collective_id):
    sizes = [lax.axis_size(axis) for axis in DEPTH]
    copies = len(TEAM) + sum(sizes) - len(sizes)
    return pl.pallas_call(
        total_kernel,
        out_shape=jax.ShapeDtypeStruct(values.shape, values.dtype),
        in_specs=[pl.BlockSpec(memory_space=pltpu.VMEM)],
        out_specs=pl.BlockSpec(memory_space=pltpu.VMEM),
        scratch_shapes=[
            pltpu.VMEM((len(TEAM) + len(DEPTH) + 1,) + values.shape, values.dtype),
            pltpu.VMEM((len(TEAM),) + values.shape, values.dtype),
            pltpu.VMEM((sum(sizes),) + values.shape, values.dtype),
            pltpu.SemaphoreType.DMA((copies,)),
            pltpu.SemaphoreType.DMA((copies,)),
        ],
        compiler_params=pltpu.CompilerParams(collective_id=collective_id, has_side_effects=True),
    )(values)


def team_exchange(blocks):
    return lax.all_to_all(blocks, TEAM, split_axis=0, concat_axis=0, tiled=True)


def turn_half(value_rows):
    return pltpu.roll(value_rows, value_rows.shape[-1] // 2, value_rows.ndim - 1)


def norm_turn(value_rows, gain, cosine, sine):
    scaled = rms_apply(value_rows, gain)
    return scaled * cosine + turn_half(scaled) * sine


def norm_turn_back(value_rows, gain, cosine, sine, gradient):
    turned = gradient * cosine + turn_half(gradient * sine)
    return rms_back(value_rows, gain, turned)


def greet_line():
    index, count = lax.axis_index("seq"), lax.axis_size("seq")
    barrier = pltpu.get_barrier_semaphore()

    @pl.when(index > 0)
    def _():
        pl.semaphore_signal(
            barrier, inc=1, device_id={"seq": index - 1}, device_id_type=pl.DeviceIdType.MESH
        )

    @pl.when(index < count - 1)
    def _():
        pl.semaphore_signal(
            barrier, inc=1, device_id={"seq": index + 1}, device_id_type=pl.DeviceIdType.MESH
        )

    inside = (index > 0) & (index < count - 1)

    @pl.when(inside)
    def _():
        pl.semaphore_wait(barrier, 2)

    @pl.when(jnp.logical_not(inside))
    def _():
        pl.semaphore_wait(barrier, 1)

    return index, count


def attend_kernel(
    window, scale, rows_ref, weight_ref, gains_ref, cosine_ref, sine_ref, start_ref,
    raw_ref, query_ref, pair_ref, stats_ref, across_ref, attended_ref, gated_ref,
    weight, pairs, send_sem, recv_sem,
):
    count_rows, length, _ = rows_ref.shape
    query_cols = query_ref.shape[2]
    heads = query_cols // HEAD_WIDTH
    keys_at = pl.ds(0, HEAD_WIDTH)
    values_at = pl.ds(HEAD_WIDTH, HEAD_WIDTH)
    index, count = greet_line()

    def hop(turn, row):
        return pltpu.make_async_remote_copy(
            src_ref=pairs.at[window - turn + 1, row],
            dst_ref=pairs.at[window - turn, row],
            send_sem=send_sem.at[turn - 1, row],
            recv_sem=recv_sem.at[turn - 1, row],
            device_id={"seq": lax.rem(index + 1, count)},
            device_id_type=pl.DeviceIdType.MESH,
        )

    parts, _, part_rows, width = weight_ref.shape
    block = parts * part_rows
    for step in range(TEAM_SIZE):
        weight[pl.ds(step * block, block), :] = weight_ref[:, step].reshape(block, width)

    def project(row, carry):
        products = jnp.dot(rows_ref[row], weight[...], preferred_element_type=jnp.float32)
        raw = products[:, : query_cols + 2 * HEAD_WIDTH].astype(jnp.bfloat16)
        raw_ref[row] = raw
        cosine, sine = cosine_ref[row], sine_ref[row]
        key = norm_turn(
            raw[:, query_cols : query_cols + HEAD_WIDTH].astype(jnp.float32),
            gains_ref[1:2], cosine, sine,
        )
        pairs[window, row, :, keys_at] = key.astype(jnp.bfloat16)
        pairs[window, row, :, values_at] = raw[:, query_cols + HEAD_WIDTH :]

        @pl.when(index < count - 1)
        def _():
            hop(1, row).start()

        for head in range(heads):
            columns = slice(head * HEAD_WIDTH, (head + 1) * HEAD_WIDTH)
            query_ref[row, :, columns] = norm_turn(
                raw[:, columns].astype(jnp.float32), gains_ref[0:1], cosine, sine
            ).astype(jnp.bfloat16)
        stats_ref[row] = jax.nn.sigmoid(products[:, query_cols + 2 * HEAD_WIDTH :])
        return carry

    lax.fori_loop(0, count_rows, project, 0)

    @pl.when(index == 0)
    def _():
        for slot in range(window):
            pairs[slot] = jnp.zeros_like(pairs[slot])

    for turn in range(2, window + 1):

        def forward(row, carry):
            @pl.when(index > 0)
            def _():
                hop(turn - 1, row).wait_recv()

            @pl.when(index < count - 1)
            def _():
                hop(turn, row).start()

            return carry

        lax.fori_loop(0, count_rows, forward, 0)

    places = lax.broadcasted_iota(jnp.int32, (length, (window + 1) * length), 1)
    latest = window * length + lax.broadcasted_iota(jnp.int32, places.shape, 0)
    lane = lax.broadcasted_iota(jnp.int32, (length, LANES), 1)

    def attend(row, carry):
        @pl.when(index > 0)
        def _():
            hop(window, row).wait_recv()

        allowed = (places >= start_ref[row]) & (places <= latest)
        keys = pairs[:, row, :, keys_at].reshape(-1, HEAD_WIDTH)
        values = pairs[:, row, :, values_at].reshape(-1, HEAD_WIDTH)
        stats = stats_ref[row]
        for head in range(heads):
            columns = slice(head * HEAD_WIDTH, (head + 1) * HEAD_WIDTH)
            scores = dot_t(query_ref[row, :, columns], keys) * scale
            scores = jnp.where(allowed, scores, NEGATIVE)
            top = jnp.max(scores, axis=1, keepdims=True)
            powers = jnp.exp(scores - top)
            total = jnp.sum(powers, axis=1, keepdims=True)
            low_probs = (powers * (1.0 / total)).astype(jnp.bfloat16)
            output = jnp.dot(low_probs, values, preferred_element_type=jnp.float32)
            output = output.astype(jnp.bfloat16)
            attended_ref[row, :, columns] = output
            gated_ref[row, :, columns] = (
                output.astype(jnp.float32) * stats[:, head : head + 1]
            ).astype(jnp.bfloat16)
            stats = jnp.where(lane == heads + head, top + jnp.log(total), stats)
        stats_ref[row] = stats
        across_ref[row] = stats.T[:SUBLANES]
        pair_ref[:, row] = pairs[:, row]
        return carry

    lax.fori_loop(0, count_rows, attend, 0)

    @pl.when(index < count - 1)
    def _():
        for turn in range(1, window + 1):

            def finish(row, carry):
                hop(turn, row).wait_send()
                return carry

            lax.fori_loop(0, count_rows, finish, 0)


def attend(normed_rows, own_qkv, gains, cosine, sine, starts, window, collective_id):
    rows, length, _ = normed_rows.shape
    width = own_qkv.shape[3]
    query_cols = width - 2 * HEAD_WIDTH - LANES
    bf16 = jnp.bfloat16
    vmem = pl.BlockSpec(memory_space=pltpu.VMEM)
    return pl.pallas_call(
        functools.partial(attend_kernel, window, HEAD_WIDTH ** (-0.5)),
        out_shape=[
            jax.ShapeDtypeStruct((rows, length, query_cols + 2 * HEAD_WIDTH), bf16),
            jax.ShapeDtypeStruct((rows, length, query_cols), bf16),
            jax.ShapeDtypeStruct((window + 1, rows, length, 2 * HEAD_WIDTH), bf16),
            jax.ShapeDtypeStruct((rows, length, LANES), jnp.float32),
            jax.ShapeDtypeStruct((rows, SUBLANES, length), jnp.float32),
            jax.ShapeDtypeStruct((rows, length, query_cols), bf16),
            jax.ShapeDtypeStruct((rows, length, query_cols), bf16),
        ],
        in_specs=[vmem] * 6,
        out_specs=[vmem] * 7,
        scratch_shapes=[
            pltpu.VMEM((MODEL_WIDTH, width), bf16),
            pltpu.VMEM((window + 1, rows, length, 2 * HEAD_WIDTH), bf16),
            pltpu.SemaphoreType.DMA((window, rows)),
            pltpu.SemaphoreType.DMA((window, rows)),
        ],
        compiler_params=pltpu.CompilerParams(
            collective_id=collective_id, has_side_effects=True, vmem_limit_bytes=VMEM_BYTES
        ),
        cost_estimate=pl.CostEstimate(
            flops=2 * rows * length * MODEL_WIDTH * width,
            bytes_accessed=ATTEND_COST * rows * length * MODEL_WIDTH,
            transcendentals=0,
        ),
    )(normed_rows, own_qkv, gains, cosine, sine, starts)


def attend_back_kernel(
    window, scale, rows_ref, weight_ref, gains_ref, cosine_ref, sine_ref, start_ref,
    raw_ref, query_ref, pair_ref, stats_ref, across_ref, attended_ref,
    products_ref, gain_ref,
    parts, outs, ins, send_sem, recv_sem,
):
    count_rows, length, _ = rows_ref.shape
    query_cols = query_ref.shape[2]
    heads = query_cols // HEAD_WIDTH
    keys_at = pl.ds(0, HEAD_WIDTH)
    values_at = pl.ds(HEAD_WIDTH, HEAD_WIDTH)
    index, count = greet_line()
    lag = 2

    def hop(turn, row):
        return pltpu.make_async_remote_copy(
            src_ref=outs.at[turn - 1, row],
            dst_ref=ins.at[turn - 1, row],
            send_sem=send_sem.at[turn - 1, row],
            recv_sem=recv_sem.at[turn - 1, row],
            device_id={"seq": lax.rem(index + count - 1, count)},
            device_id_type=pl.DeviceIdType.MESH,
        )

    keys_total = (window + 1) * length
    places = lax.broadcasted_iota(jnp.int32, (keys_total, length), 0)
    latest = window * length + lax.broadcasted_iota(jnp.int32, places.shape, 1)
    lane = lax.broadcasted_iota(jnp.int32, (length, LANES), 1)
    gain_ref[...] = jnp.zeros_like(gain_ref)

    @pl.when(index == count - 1)
    def _():
        ins[...] = jnp.zeros_like(ins)

    def compute(row):
        grad_gated = dot_t(rows_ref[row], weight_ref[...])
        keys = pair_ref[:, row, :, keys_at].reshape(-1, HEAD_WIDTH)
        values = pair_ref[:, row, :, values_at].reshape(-1, HEAD_WIDTH)
        allowed = (places >= start_ref[row]) & (places <= latest)
        cosine, sine = cosine_ref[row], sine_ref[row]
        grad_pre = jnp.zeros((length, LANES), jnp.float32)
        grad_keys = jnp.zeros((keys_total, HEAD_WIDTH), jnp.float32)
        grad_values = jnp.zeros((keys_total, HEAD_WIDTH), jnp.float32)
        for head in range(heads):
            columns = slice(head * HEAD_WIDTH, (head + 1) * HEAD_WIDTH)
            gate = stats_ref[row, :, head : head + 1]
            own = grad_gated[:, columns]
            grad_out = (own * gate).astype(jnp.bfloat16)
            grad_gate = jnp.sum(
                own * attended_ref[row, :, columns].astype(jnp.float32), axis=1, keepdims=True
            )
            grad_pre = jnp.where(lane == head, grad_gate * gate * (1.0 - gate), grad_pre)
            query = query_ref[row, :, columns]
            scores = jnp.where(allowed, dot_t(keys, query) * scale, NEGATIVE)
            probs = jnp.exp(scores - across_ref[row, heads + head : heads + head + 1])
            grad_probs = dot_t(values, grad_out)
            inner = jnp.sum(probs * grad_probs, axis=0, keepdims=True)
            grad_scores = (probs * (grad_probs - inner)).astype(jnp.bfloat16)
            grad_values = grad_values + jnp.dot(
                probs.astype(jnp.bfloat16), grad_out, preferred_element_type=jnp.float32
            )
            grad_keys = grad_keys + jnp.dot(
                grad_scores, query, preferred_element_type=jnp.float32
            )
            grad_query = dot_tokens(grad_scores, keys) * scale
            grad_raw, gain = norm_turn_back(
                raw_ref[row, :, columns].astype(jnp.float32), gains_ref[0:1], cosine, sine,
                grad_query,
            )
            products_ref[row, :, columns] = grad_raw.astype(jnp.bfloat16)
            gain_ref[0:1] += jnp.sum(gain, axis=0, keepdims=True)
        products_ref[row, :, query_cols + 2 * HEAD_WIDTH :] = grad_pre.astype(jnp.bfloat16)
        parts[:, row, :, keys_at] = (grad_keys * scale).reshape(window + 1, length, HEAD_WIDTH)
        parts[:, row, :, values_at] = grad_values.reshape(window + 1, length, HEAD_WIDTH)

    def finish(row):
        grad_pair = parts[window, row] + ins[window - 1, row].astype(jnp.float32)
        grad_raw, gain = norm_turn_back(
            raw_ref[row, :, query_cols : query_cols + HEAD_WIDTH].astype(jnp.float32),
            gains_ref[1:2], cosine_ref[row], sine_ref[row], grad_pair[:, :HEAD_WIDTH],
        )
        products_ref[row, :, query_cols : query_cols + HEAD_WIDTH] = grad_raw.astype(jnp.bfloat16)
        products_ref[row, :, query_cols + HEAD_WIDTH : query_cols + 2 * HEAD_WIDTH] = grad_pair[
            :, HEAD_WIDTH:
        ].astype(jnp.bfloat16)
        gain_ref[1:2] += jnp.sum(gain, axis=0, keepdims=True)

    def step(turn_row, carry):
        @pl.when(turn_row < count_rows)
        def _():
            compute(turn_row)

        for turn in range(1, window + 2):
            row = turn_row - lag * (turn - 1)

            @pl.when((row >= 0) & (row < count_rows))
            def _():
                if turn > 1:

                    @pl.when(index < count - 1)
                    def _():
                        hop(turn - 1, row).wait_recv()

                if turn == window + 1:
                    finish(row)
                else:
                    part = parts[turn - 1, row]
                    if turn > 1:
                        part = part + ins[turn - 2, row].astype(jnp.float32)
                    outs[turn - 1, row] = part.astype(jnp.bfloat16)

                    @pl.when(index > 0)
                    def _():
                        hop(turn, row).start()

        return carry

    lax.fori_loop(0, count_rows + lag * window, step, 0)

    @pl.when(index > 0)
    def _():
        for turn in range(1, window + 1):

            def done(row, carry):
                hop(turn, row).wait_send()
                return carry

            lax.fori_loop(0, count_rows, done, 0)


def attend_back(
    grad_rows, own_out, gains, cosine, sine, starts, saved, window, collective_id
):
    rows, length, _ = grad_rows.shape
    query_cols = own_out.shape[0]
    width = query_cols + 2 * HEAD_WIDTH + LANES
    bf16 = jnp.bfloat16
    vmem = pl.BlockSpec(memory_space=pltpu.VMEM)
    return pl.pallas_call(
        functools.partial(attend_back_kernel, window, HEAD_WIDTH ** (-0.5)),
        out_shape=[
            jax.ShapeDtypeStruct((rows, length, width), bf16),
            jax.ShapeDtypeStruct((SUBLANES, HEAD_WIDTH), jnp.float32),
        ],
        in_specs=[vmem] * 12,
        out_specs=[vmem] * 2,
        scratch_shapes=[
            pltpu.VMEM((window + 1, rows, length, 2 * HEAD_WIDTH), jnp.float32),
            pltpu.VMEM((window, rows, length, 2 * HEAD_WIDTH), bf16),
            pltpu.VMEM((window, rows, length, 2 * HEAD_WIDTH), bf16),
            pltpu.SemaphoreType.DMA((window, rows)),
            pltpu.SemaphoreType.DMA((window, rows)),
        ],
        compiler_params=pltpu.CompilerParams(
            collective_id=collective_id, has_side_effects=True, vmem_limit_bytes=VMEM_BYTES
        ),
        cost_estimate=pl.CostEstimate(
            flops=2 * rows * length * MODEL_WIDTH * query_cols,
            bytes_accessed=ATTEND_COST * rows * length * MODEL_WIDTH,
            transcendentals=0,
        ),
    )(grad_rows, own_out, gains, cosine, sine, starts, *saved)


def team_columns(matrix, widths):
    pieces = []
    lower = 0
    for width in widths:
        piece = matrix[:, lower : lower + width]
        pieces.append(piece.reshape(matrix.shape[0], TEAM_SIZE, width // TEAM_SIZE))
        lower = lower + width
    return jnp.concatenate(pieces, axis=2).transpose(1, 0, 2)


def whole_columns(blocks, widths):
    pieces = []
    lower = 0
    for width in widths:
        share = width // TEAM_SIZE
        piece = blocks[:, :, lower : lower + share]
        pieces.append(piece.transpose(1, 0, 2).reshape(blocks.shape[1], width))
        lower = lower + share
    return jnp.concatenate(pieces, axis=1)


def gather_columns(matrix, widths):
    blocks = team_exchange(team_columns(matrix, widths))
    return lax.all_gather(blocks, DEPTH, axis=0, tiled=False)


def in_order(parts):
    return parts.transpose(1, 0, 2, 3).reshape(-1, parts.shape[3])


def scatter_parts(gradient, rows):
    depth = gradient.shape[0] // (TEAM_SIZE * rows)
    ordered = gradient.reshape(TEAM_SIZE, depth, rows, -1).transpose(1, 0, 2, 3)
    return lax.psum_scatter(
        ordered.reshape(gradient.shape), DEPTH, scatter_dimension=0, tiled=True
    ).reshape(TEAM_SIZE, rows, -1)


def own_rows(parts, widths):
    return whole_columns(team_exchange(parts), widths).astype(jnp.float32)


def gather_rows(matrix):
    return lax.all_gather(matrix, DEPTH, axis=0, tiled=True)


def scatter_rows(gradient):
    return lax.psum_scatter(gradient, DEPTH, scatter_dimension=0, tiled=True)


def moments(weight, moment, second, gradient):
    moment_new = BETA * moment + (1.0 - BETA) * gradient
    second_new = BETA * second + (1.0 - BETA) * gradient * gradient
    correction = 1.0 - BETA**STEP
    update = (
        moment_new / correction / (jnp.sqrt(second_new / correction) + ADAM_EPS) + DECAY * weight
    )
    return (moment_new, second_new, update)


def group_squares(matrix, widths):
    sums = []
    lower = 0
    for width in widths:
        piece = matrix[:, lower : lower + width]
        sums.append(jnp.sum(piece * piece))
        lower = lower + width
    return sums


def apply_trust(weight, update, trust, widths):
    factors = [jnp.broadcast_to(trust[index], (width,)) for index, width in enumerate(widths)]
    return weight - RATE * jnp.concatenate(factors)[None, :] * update


def row_update(weight, moment, second, gradient):
    moment_new, second_new, update = moments(weight, moment, second, gradient)
    trust = jnp.sqrt(jnp.sum(weight * weight, axis=-1, keepdims=True)) / jnp.sqrt(
        jnp.sum(update * update, axis=-1, keepdims=True)
    )
    return (weight - RATE * trust * update, moment_new, second_new)


def whole_update(weight, moment, second, gradient):
    moment_new, second_new, update = moments(weight, moment, second, gradient)
    trust = jnp.sqrt(jnp.sum(weight * weight)) / jnp.sqrt(jnp.sum(update * update))
    return (weight - RATE * trust * update, moment_new, second_new)


def shards(
    inputs,
    cotangent,
    doc_lengths,
    projection_weight,
    projection_moment,
    projection_second,
    out_weight,
    out_moment,
    out_second,
    ffn_weight,
    ffn_moment,
    ffn_second,
    down_weight,
    down_moment,
    down_second,
    head_gate,
    gate_moment,
    gate_second,
    norm_gains,
    gains_moment,
    gains_second,
    qk_gains,
    qk_moment,
    qk_second,
):
    rows_dev, local_len, width = inputs.shape
    bf16 = jnp.bfloat16
    team = lax.axis_index(TEAM)
    place_seq = lax.axis_index("seq")
    group_heads = QUERY_HEADS // KEY_VALUE_HEADS
    window = -(-(DOC_MOST - 1) // local_len)
    window = min(window, lax.axis_size("seq") - 1)
    query_cols = QUERY_HEADS * HEAD_WIDTH
    key_value_columns = KEY_VALUE_HEADS * HEAD_WIDTH
    widths_qkv = (query_cols, key_value_columns, key_value_columns)
    widths_ffn = (FF, FF)
    own_query = query_cols // TEAM_SIZE
    own_key = key_value_columns // TEAM_SIZE
    own_ff = FF // TEAM_SIZE
    weight_squares = (
        group_squares(projection_weight, widths_qkv)
        + group_squares(out_weight, (MODEL_WIDTH,))
        + group_squares(ffn_weight, widths_ffn)
        + group_squares(down_weight, (MODEL_WIDTH,))
    )
    own_qkv = gather_columns(projection_weight.astype(bf16), widths_qkv)
    own_out = gather_rows(out_weight.astype(bf16))
    own_ffn = gather_columns(ffn_weight.astype(bf16), widths_ffn)
    own_down = gather_rows(down_weight.astype(bf16))
    own_gate = lax.dynamic_slice_in_dim(head_gate.astype(bf16), team * group_heads, group_heads, 1)
    own_gate = jnp.pad(own_gate, ((0, 0), (0, LANES - group_heads)))
    gate_parts = own_gate.reshape(TEAM_SIZE, own_qkv.shape[0], own_qkv.shape[2], LANES)
    own_qkv = jnp.concatenate([own_qkv, gate_parts.transpose(1, 0, 2, 3)], axis=3)
    lengths = lax.all_gather(doc_lengths, TEAM, axis=0, tiled=True)
    place = place_seq * local_len + jnp.arange(local_len, dtype=jnp.int32)
    position = positions(lengths, place)
    cosine, sine = rotary_tables(position, HEAD_WIDTH)
    starts = window * local_len + jnp.arange(local_len, dtype=jnp.int32)[None, :] - position
    inputs_flat = inputs[0].astype(jnp.float32)
    normed = rms_apply(inputs_flat, norm_gains[0]).astype(bf16)
    normed_all, grad_all = gather_team([normed, cotangent[0]], 0)
    raw, query_rot, pairs, stats, across, attended, gated = attend(
        normed_all.reshape(TEAM_SIZE, local_len, MODEL_WIDTH),
        own_qkv,
        qk_gains,
        cosine,
        sine,
        starts[:, :, None],
        window,
        8,
    )
    gated = gated.reshape(-1, own_query)
    middle = inputs_flat + scatter_team(product_rows, gated, own_out, 1)
    normed2 = rms_apply(middle, norm_gains[1]).astype(bf16)
    normed2_all = gather_team([normed2], 2)[0]
    both = jnp.dot(normed2_all, in_order(own_ffn), preferred_element_type=jnp.float32)
    inner = both[:, :own_ff]
    up_part = both[:, own_ff:]
    sigma_inner = jax.nn.sigmoid(inner)
    hidden = (inner * sigma_inner * up_part).astype(bf16)
    grad_final = cotangent[0].astype(jnp.float32)
    grad_hidden = dot_t(grad_all, own_down)
    grad_inner = grad_hidden * up_part * sigma_inner * (1.0 + inner * (1.0 - sigma_inner))
    grad_up = grad_hidden * inner * sigma_inner
    grad_both = jnp.concatenate([grad_inner, grad_up], axis=1).astype(bf16)
    down_part, grad_both = lax.optimization_barrier((low_tokens(hidden, grad_all), grad_both))
    down_sum = scatter_rows(down_part)
    grad_normed2 = scatter_team(product_back, grad_both, own_ffn, 4)
    grad_mid_part, gain_mid = rms_back(middle, norm_gains[1], grad_normed2)
    grad_middle = grad_final + grad_mid_part
    ffn_part, grad_low, down_sum = lax.optimization_barrier(
        (low_tokens(normed2_all, grad_both), grad_middle.astype(bf16), down_sum)
    )
    ffn_sum = scatter_parts(ffn_part, ffn_weight.shape[0])
    down_grad = down_sum.astype(jnp.float32)
    grad_middle_all = gather_team([grad_low], 5)[0]
    grad_products, gain_sums = attend_back(
        grad_middle_all.reshape(TEAM_SIZE, local_len, MODEL_WIDTH),
        own_out,
        qk_gains,
        cosine,
        sine,
        starts[:, None, :],
        (raw, query_rot, pairs, stats, across, attended),
        window,
        9,
    )
    qk_local = gain_sums[:2]
    grad_products = grad_products.reshape(-1, grad_products.shape[2])
    products_grad = dot_tokens(normed_all, grad_products)
    out_part, projection_part, grad_products, ffn_sum = lax.optimization_barrier(
        (
            low_tokens(gated, grad_middle_all),
            products_grad[:, : own_query + 2 * own_key].astype(bf16),
            grad_products,
            ffn_sum,
        )
    )
    ffn_grad = own_rows(ffn_sum, widths_ffn)
    out_grad = scatter_rows(out_part).astype(jnp.float32)
    projection_gradient = own_rows(
        scatter_parts(projection_part, projection_weight.shape[0]), widths_qkv
    )
    grad_normed = scatter_team(product_back, grad_products, own_qkv, 6)
    late_hidden, grad_normed = lax.optimization_barrier((hidden, grad_normed))
    final = middle + scatter_team(product_rows, late_hidden, own_down, 3)
    result = final.astype(bf16).reshape(inputs.shape)
    grad_in_part, gain_in = rms_back(inputs_flat, norm_gains[0], grad_normed)
    input_grad = (grad_middle + grad_in_part).reshape(inputs.shape)
    gains_local = jnp.stack([jnp.sum(gain_in, axis=0), jnp.sum(gain_mid, axis=0)])
    gate_local = lax.dynamic_update_slice_in_dim(
        jnp.zeros((QUERY_HEADS, MODEL_WIDTH), jnp.float32),
        products_grad[:, own_query + 2 * own_key :][:, :group_heads].T,
        team * group_heads,
        0,
    )
    projection_moment_next, projection_second_next, qkv_update = moments(
        projection_weight, projection_moment, projection_second, projection_gradient
    )
    out_moment_new, out_second_new, out_update = moments(
        out_weight, out_moment, out_second, out_grad
    )
    ffn_moment_new, ffn_second_new, ffn_update = moments(
        ffn_weight, ffn_moment, ffn_second, ffn_grad
    )
    down_moment_new, down_second_new, down_update = moments(
        down_weight, down_moment, down_second, down_grad
    )
    update_squares = (
        group_squares(qkv_update, widths_qkv)
        + group_squares(out_update, (MODEL_WIDTH,))
        + group_squares(ffn_update, widths_ffn)
        + group_squares(down_update, (MODEL_WIDTH,))
    )
    groups = len(weight_squares)
    lane = jnp.arange(MODEL_WIDTH, dtype=jnp.int32)
    small = jnp.pad(qk_local.reshape(-1), (0, MODEL_WIDTH - 2 * HEAD_WIDTH))
    for number, square in enumerate(weight_squares + update_squares):
        small = small + jnp.where(lane == 2 * HEAD_WIDTH + number, square, 0.0)
    totals = total_all(
        jnp.concatenate(
            [
                gate_local,
                gains_local,
                small[None],
                jnp.zeros((5, MODEL_WIDTH), jnp.float32),
            ]
        ),
        7,
    )
    gate_grad = totals[:QUERY_HEADS]
    gains_grad = totals[QUERY_HEADS : QUERY_HEADS + 2]
    small = totals[QUERY_HEADS + 2]
    qk_grad = small[: 2 * HEAD_WIDTH].reshape(2, HEAD_WIDTH)
    weight_totals = small[2 * HEAD_WIDTH : 2 * HEAD_WIDTH + groups]
    update_totals = small[2 * HEAD_WIDTH + groups : 2 * HEAD_WIDTH + 2 * groups]
    weight_norms = jnp.sqrt(weight_totals)
    update_norms = jnp.sqrt(update_totals)
    trust = weight_norms / update_norms
    projection_weight_next = apply_trust(projection_weight, qkv_update, trust[0:3], widths_qkv)
    out_new = apply_trust(out_weight, out_update, trust[3:4], (MODEL_WIDTH,))
    ffn_new = apply_trust(ffn_weight, ffn_update, trust[4:6], widths_ffn)
    down_new = apply_trust(down_weight, down_update, trust[6:7], (MODEL_WIDTH,))
    head_gate_new, gate_moment_new, gate_second_new = whole_update(
        head_gate, gate_moment, gate_second, gate_grad.T
    )
    gains_new, gains_moment_new, gains_second_new = row_update(
        norm_gains, gains_moment, gains_second, gains_grad
    )
    qk_new, qk_moment_new, qk_second_new = row_update(qk_gains, qk_moment, qk_second, qk_grad)
    lamb_norms = jnp.stack([weight_norms, update_norms])
    return (
        result,
        input_grad,
        projection_weight_next,
        projection_moment_next,
        projection_second_next,
        projection_weight_next.astype(jnp.bfloat16),
        out_new,
        out_moment_new,
        out_second_new,
        out_new.astype(jnp.bfloat16),
        ffn_new,
        ffn_moment_new,
        ffn_second_new,
        ffn_new.astype(jnp.bfloat16),
        down_new,
        down_moment_new,
        down_second_new,
        down_new.astype(jnp.bfloat16),
        head_gate_new,
        gate_moment_new,
        gate_second_new,
        gains_new,
        gains_moment_new,
        gains_second_new,
        qk_new,
        qk_moment_new,
        qk_second_new,
        lamb_norms,
    )


def solution(mesh):
    mesh = Mesh(
        mesh.devices.reshape(2, 2, 2, mesh.shape["fsdp"] // TEAM_SIZE, mesh.shape["seq"]),
        TEAM + DEPTH,
    )
    rows = TEAM + DEPTH[:1]
    in_specs = (
        P(rows, "seq", None),
        P(rows, "seq", None),
        P(rows, None),
        P(TEAM + DEPTH, None),
        P(TEAM + DEPTH, None),
        P(TEAM + DEPTH, None),
        P(TEAM + DEPTH, None),
        P(TEAM + DEPTH, None),
        P(TEAM + DEPTH, None),
        P(TEAM + DEPTH, None),
        P(TEAM + DEPTH, None),
        P(TEAM + DEPTH, None),
        P(TEAM + DEPTH, None),
        P(TEAM + DEPTH, None),
        P(TEAM + DEPTH, None),
        P(),
        P(),
        P(),
        P(),
        P(),
        P(),
        P(),
        P(),
        P(),
    )
    out_specs = (
        P(rows, "seq", None),
        P(rows, "seq", None),
        P(TEAM + DEPTH, None),
        P(TEAM + DEPTH, None),
        P(TEAM + DEPTH, None),
        P(TEAM + DEPTH, None),
        P(TEAM + DEPTH, None),
        P(TEAM + DEPTH, None),
        P(TEAM + DEPTH, None),
        P(TEAM + DEPTH, None),
        P(TEAM + DEPTH, None),
        P(TEAM + DEPTH, None),
        P(TEAM + DEPTH, None),
        P(TEAM + DEPTH, None),
        P(TEAM + DEPTH, None),
        P(TEAM + DEPTH, None),
        P(TEAM + DEPTH, None),
        P(TEAM + DEPTH, None),
        P(),
        P(),
        P(),
        P(),
        P(),
        P(),
        P(),
        P(),
        P(),
        P(),
    )
    return jax.shard_map(shards, mesh=mesh, in_specs=in_specs, out_specs=out_specs, check_vma=False)
```

```python
import functools

import jax
import jax.numpy as jnp
from jax import lax
from jax.experimental import pallas as pl
from jax.experimental.pallas import tpu as pltpu
from jax.sharding import Mesh
from jax.sharding import PartitionSpec as P

MODEL_WIDTH = 2048
QUERY_HEADS = 16
KEY_VALUE_HEADS = 8
HEAD_WIDTH = 128
FF = 6144
ROW_TOKENS = 1024
STEP = 3
DOC_MOST = 512
TEAM_SIZE = 8
TEAM = ("t2", "t1", "t0")
DEPTH = ("spare", "seq")
LANES = 128
SUBLANES = 8
VMEM_BYTES = 48 << 20
GATHER_COST = 250
SCATTER_COST = 320
ATTEND_COST = 50


NORM_EPS = 1e-06
ADAM_EPS = 1e-06
RATE = 0.3
DECAY = 0.01
BETA = 0.5
THETA = 1000000.0
NEGATIVE = -1e30


def rms_apply(value_rows, gain):
    return (
        value_rows
        * lax.rsqrt(jnp.mean(value_rows * value_rows, axis=-1, keepdims=True) + NORM_EPS)
        * gain
    )


def rms_back(value_rows, gain, gradient):
    scale = lax.rsqrt(jnp.mean(value_rows * value_rows, axis=-1, keepdims=True) + NORM_EPS)
    scaled = gradient * gain
    inner = jnp.mean(scaled * value_rows, axis=-1, keepdims=True)
    grad_value = scale * scaled - value_rows * scale * scale * scale * inner
    grad_gain = gradient * value_rows * scale
    return (grad_value, grad_gain)


def dot_t(left, right):
    return lax.dot_general(
        left, right, (((1,), (1,)), ((), ())), preferred_element_type=jnp.float32
    )


def low_tokens(left, right):
    return dot_tokens(left, right).astype(jnp.bfloat16)


def dot_tokens(left, right):
    return lax.dot_general(
        left, right, (((0,), (0,)), ((), ())), preferred_element_type=jnp.float32
    )


def rotary_tables(position, width):
    half = width // 2
    rates = THETA ** (-jnp.arange(half, dtype=jnp.float32) * 2.0 / width)
    angle = position.astype(jnp.float32)[..., None] * rates
    cosine, sine = jnp.cos(angle), jnp.sin(angle)
    return (
        jnp.concatenate([cosine, cosine], axis=-1),
        jnp.concatenate([-sine, sine], axis=-1),
    )


def positions(lengths, place):
    ends = jnp.cumsum(lengths, axis=1)
    starts = ends - lengths
    inside = (place[None, :, None] >= starts[:, None, :]) & (place[None, :, None] < ends[:, None, :])
    return place[None, :] - jnp.sum(jnp.where(inside, starts[:, None, :], 0), axis=2)


def team_place():
    return tuple(lax.axis_index(axis) for axis in TEAM)


def greet_team(place):
    barrier = pltpu.get_barrier_semaphore()
    for axis, index in zip(TEAM, place):
        pl.semaphore_signal(
            barrier, inc=1, device_id={axis: 1 - index}, device_id_type=pl.DeviceIdType.MESH
        )
    pl.semaphore_wait(barrier, len(TEAM))


def member(place, flips):
    index = 0
    for own, flip in zip(place, flips):
        index = index * 2 + (1 - own if flip else own)
    return index


def gather_kernel(count, *refs):
    owns, alls = refs[:count], refs[count : 2 * count]
    own_sem, send_sem, recv_sem = refs[2 * count :]
    place = team_place()
    greet_team(place)
    me = member(place, (0, 0, 0))
    beside = member(place, (0, 1, 0))
    above = member(place, (1, 0, 0))
    across = member(place, (1, 1, 0))
    copies = [{} for _ in range(count)]
    keeps = []

    def send(item, number, axis, source, target):
        copy = pltpu.make_async_remote_copy(
            src_ref=source,
            dst_ref=target,
            send_sem=send_sem.at[item, number],
            recv_sem=recv_sem.at[item, number],
            device_id={TEAM[axis]: 1 - place[axis]},
            device_id_type=pl.DeviceIdType.MESH,
        )
        copy.start()
        copies[item][number] = copy

    def halves(item):
        half = owns[item].shape[0] // 2
        return pl.ds(0, half), pl.ds(half, half)

    for item in range(count):
        target = alls[item].at[me]
        send(item, 0, 1, owns[item], target)
        send(item, 1, 0, owns[item], target)
        send(item, 2, 2, owns[item], target)
        keeps.append(pltpu.make_async_copy(owns[item], target, own_sem.at[item]))
        keeps[item].start()
    for item in range(count):
        upper, lower = halves(item)
        copies[item][0].wait_recv()
        block = alls[item].at[beside]
        send(item, 3, 0, block.at[upper], block.at[upper])
        send(item, 4, 2, block, block)
        copies[item][1].wait_recv()
        block = alls[item].at[above]
        send(item, 5, 1, block.at[lower], block.at[lower])
        send(item, 6, 2, block, block)
    for item in range(count):
        upper, lower = halves(item)
        block = alls[item].at[across]
        copies[item][3].wait_recv()
        send(item, 7, 2, block.at[upper], block.at[upper])
        copies[item][5].wait_recv()
        send(item, 8, 2, block.at[lower], block.at[lower])
    for item in range(count):
        for number in (2, 4, 6, 7, 8):
            copies[item][number].wait_recv()
        for number in range(9):
            copies[item][number].wait_send()
        keeps[item].wait()


def gather_team(arrays, collective_id):
    count = len(arrays)
    gathered = pl.pallas_call(
        functools.partial(gather_kernel, count),
        out_shape=[jax.ShapeDtypeStruct((TEAM_SIZE,) + own.shape, own.dtype) for own in arrays],
        in_specs=[pl.BlockSpec(memory_space=pl.ANY)] * count,
        out_specs=[pl.BlockSpec(memory_space=pl.ANY)] * count,
        scratch_shapes=[
            pltpu.SemaphoreType.DMA((count,)),
            pltpu.SemaphoreType.DMA((count, 9)),
            pltpu.SemaphoreType.DMA((count, 9)),
        ],
        compiler_params=pltpu.CompilerParams(collective_id=collective_id, has_side_effects=True),
        cost_estimate=pl.CostEstimate(
            flops=0,
            bytes_accessed=sum(GATHER_COST * own.shape[0] * own.shape[1] for own in arrays),
            transcendentals=0,
        ),
    )(*arrays)
    return [
        whole.reshape(TEAM_SIZE * own.shape[0], own.shape[1])
        for whole, own in zip(gathered, arrays)
    ]


def scatter_kernel(product, count, *refs):
    operands = refs[:count]
    sum_ref, own, out_near, in_near, out_far, in_half, in_full, send_sem, recv_sem = refs[count:]
    place = team_place()
    greet_team(place)
    rows = sum_ref.shape[0]
    half = rows // 2
    upper, lower = pl.ds(0, half), pl.ds(half, half)

    def send(number, axis, source, target):
        copy = pltpu.make_async_remote_copy(
            src_ref=source,
            dst_ref=target,
            send_sem=send_sem.at[number],
            recv_sem=recv_sem.at[number],
            device_id={TEAM[axis]: 1 - place[axis]},
            device_id_type=pl.DeviceIdType.MESH,
        )
        copy.start()
        return copy

    flips = ((1, 1), (0, 1), (1, 0), (0, 0))
    near, far = [], {}

    def begin(turn):
        first, second = flips[turn]
        product(operands, member(place, (first, second, 1)), out_near.at[turn])
        near.append(send(turn, 2, out_near.at[turn], in_near.at[turn]))
        product(operands, member(place, (first, second, 0)), own.at[turn])

    def join(turn):
        near[turn].wait_recv()
        return own[turn] + in_near[turn].astype(jnp.float32)

    begin(0)
    begin(1)
    out_far[0] = join(0).astype(jnp.bfloat16)
    far[4] = send(4, 1, out_far.at[0, upper], in_half.at[0])
    far[5] = send(5, 0, out_far.at[0, lower], in_half.at[1])
    begin(2)
    own[1] = join(1)
    out_far[1, upper] = own[1, upper].astype(jnp.bfloat16)
    far[6] = send(6, 1, out_far.at[1, upper], in_full.at[0, upper])
    begin(3)
    own[2] = join(2)
    out_far[2, lower] = own[2, lower].astype(jnp.bfloat16)
    far[7] = send(7, 0, out_far.at[2, lower], in_full.at[1, lower])
    sum_ref[...] = join(3)
    far[5].wait_recv()
    out_far[1, lower] = (own[1, lower] + in_half[1].astype(jnp.float32)).astype(jnp.bfloat16)
    far[8] = send(8, 1, out_far.at[1, lower], in_full.at[0, lower])
    far[4].wait_recv()
    out_far[2, upper] = (own[2, upper] + in_half[0].astype(jnp.float32)).astype(jnp.bfloat16)
    far[9] = send(9, 0, out_far.at[2, upper], in_full.at[1, upper])
    far[6].wait_recv()
    far[7].wait_recv()
    far[8].wait_recv()
    far[9].wait_recv()
    sum_ref[...] = (
        sum_ref[...] + in_full[0].astype(jnp.float32) + in_full[1].astype(jnp.float32)
    )
    for copy in near + [far[number] for number in range(4, 10)]:
        copy.wait_send()


def over_tiles(target, tile, product):
    def one(step, carry):
        columns = pl.ds(pl.multiple_of(step * tile, tile), tile)
        target[:, columns] = product(step, columns).astype(target.dtype)
        return carry

    lax.fori_loop(0, target.shape[1] // tile, one, 0)


def whole_block(ref, step, columns=slice(None)):
    block = ref[:, step, :, columns]
    return block.reshape(block.shape[0] * block.shape[1], block.shape[2])


def product_down(operands, block, target):
    hidden, weight = operands

    def one(step, columns):
        return jnp.dot(hidden[block], weight[:, columns], preferred_element_type=jnp.float32)

    over_tiles(target, 512, one)


def product_out(operands, block, target):
    gated, weight = operands
    depth = gated.shape[2]
    share = pl.ds(weight.shape[3] - depth, depth)

    def one(step, columns):
        return jnp.dot(
            gated[block], whole_block(weight, step, share), preferred_element_type=jnp.float32
        )

    over_tiles(target, target.shape[1] // TEAM_SIZE, one)


def product_ffn_back(operands, block, target):
    grad_inner, grad_up, inner_weight, up_weight = operands

    def one(step, columns):
        return dot_t(grad_inner[block], whole_block(inner_weight, step)) + dot_t(
            grad_up[block], whole_block(up_weight, step)
        )

    over_tiles(target, target.shape[1] // TEAM_SIZE, one)


def product_qkv_back(operands, block, target):
    grad_products, weight, gate_weight = operands
    depth = grad_products.shape[2] - LANES
    share = pl.ds(0, depth)

    def one(step, columns):
        return dot_t(
            grad_products[block, :, share], whole_block(weight, step, share)
        ) + dot_t(grad_products[block, :, pl.ds(depth, LANES)], gate_weight[columns, :])

    over_tiles(target, target.shape[1] // TEAM_SIZE, one)


def scatter_team(product, operands, collective_id):
    rows = operands[0].shape[1]
    depth = sum(left.shape[2] for left in operands if left.shape[:2] == (TEAM_SIZE, rows))
    width = MODEL_WIDTH
    vmem = pl.BlockSpec(memory_space=pltpu.VMEM)
    return pl.pallas_call(
        functools.partial(scatter_kernel, product, len(operands)),
        out_shape=jax.ShapeDtypeStruct((rows, width), jnp.float32),
        in_specs=[vmem] * len(operands),
        out_specs=vmem,
        scratch_shapes=[
            pltpu.VMEM((4, rows, width), jnp.float32),
            pltpu.VMEM((4, rows, width), jnp.bfloat16),
            pltpu.VMEM((4, rows, width), jnp.bfloat16),
            pltpu.VMEM((3, rows, width), jnp.bfloat16),
            pltpu.VMEM((2, rows // 2, width), jnp.bfloat16),
            pltpu.VMEM((2, rows, width), jnp.bfloat16),
            pltpu.SemaphoreType.DMA((10,)),
            pltpu.SemaphoreType.DMA((10,)),
        ],
        compiler_params=pltpu.CompilerParams(
            collective_id=collective_id, has_side_effects=True, vmem_limit_bytes=VMEM_BYTES
        ),
        cost_estimate=pl.CostEstimate(
            flops=2 * TEAM_SIZE * rows * depth * width,
            bytes_accessed=SCATTER_COST * rows * width,
            transcendentals=0,
        ),
    )(*operands)


def ffn_kernel(rows_ref, inner_ref, up_ref, hidden_ref, slope_ref, swish_ref, inner_weight, up_weight):
    @pl.when(pl.program_id(0) == 0)
    def _():
        block = inner_ref.shape[0] * inner_ref.shape[2]
        for step in range(TEAM_SIZE):
            inner_weight[pl.ds(step * block, block), :] = whole_block(inner_ref, step)
            up_weight[pl.ds(step * block, block), :] = whole_block(up_ref, step)

    tile = 256

    def one(step, carry):
        columns = pl.ds(pl.multiple_of(step * tile, tile), tile)
        inner = jnp.dot(rows_ref[0], inner_weight[:, columns], preferred_element_type=jnp.float32)
        up_part = jnp.dot(rows_ref[0], up_weight[:, columns], preferred_element_type=jnp.float32)
        sigma = jax.nn.sigmoid(inner)
        swish = inner * sigma
        hidden_ref[0, :, columns] = (swish * up_part).astype(jnp.bfloat16)
        slope_ref[0, :, columns] = up_part * sigma * (1.0 + inner * (1.0 - sigma))
        swish_ref[0, :, columns] = swish
        return carry

    lax.fori_loop(0, hidden_ref.shape[2] // tile, one, 0)


def ffn_forward(normed_rows, inner_weight, up_weight):
    count, length, depth = normed_rows.shape
    width = inner_weight.shape[3]
    whole = pl.BlockSpec(inner_weight.shape, lambda i: (0, 0, 0, 0), pipeline_mode=pl.Buffered(1))
    out = pl.BlockSpec((1, length, width), lambda i: (i, 0, 0))
    return pl.pallas_call(
        ffn_kernel,
        grid=(count,),
        out_shape=[
            jax.ShapeDtypeStruct((count, length, width), jnp.bfloat16),
            jax.ShapeDtypeStruct((count, length, width), jnp.float32),
            jax.ShapeDtypeStruct((count, length, width), jnp.float32),
        ],
        in_specs=[pl.BlockSpec((1, length, depth), lambda i: (i, 0, 0)), whole, whole],
        out_specs=[out, out, out],
        scratch_shapes=[pltpu.VMEM((depth, width), jnp.bfloat16)] * 2,
        compiler_params=pltpu.CompilerParams(vmem_limit_bytes=VMEM_BYTES),
        cost_estimate=pl.CostEstimate(
            flops=4 * count * length * depth * width,
            bytes_accessed=count * length * (2 * depth + 10 * width),
            transcendentals=count * length * width,
        ),
    )(normed_rows, inner_weight, up_weight)


def ffn_back_kernel(grad_ref, weight_ref, slope_ref, swish_ref, inner_ref, up_ref):
    tile = 256

    def one(step, carry):
        columns = pl.ds(pl.multiple_of(step * tile, tile), tile)
        grad_hidden = dot_t(grad_ref[0], weight_ref[columns, :])
        inner_ref[0, :, columns] = (grad_hidden * slope_ref[0, :, columns]).astype(jnp.bfloat16)
        up_ref[0, :, columns] = (grad_hidden * swish_ref[0, :, columns]).astype(jnp.bfloat16)
        return carry

    lax.fori_loop(0, inner_ref.shape[2] // tile, one, 0)


def ffn_back(grad_rows, down_weight, slope, swish):
    count, length, depth = grad_rows.shape
    width = down_weight.shape[0]
    whole = pl.BlockSpec(down_weight.shape, lambda i: (0, 0), pipeline_mode=pl.Buffered(1))
    part = pl.BlockSpec((1, length, width), lambda i: (i, 0, 0))
    return pl.pallas_call(
        ffn_back_kernel,
        grid=(count,),
        out_shape=[jax.ShapeDtypeStruct((count, length, width), jnp.bfloat16)] * 2,
        in_specs=[pl.BlockSpec((1, length, depth), lambda i: (i, 0, 0)), whole, part, part],
        out_specs=[part, part],
        compiler_params=pltpu.CompilerParams(vmem_limit_bytes=VMEM_BYTES),
        cost_estimate=pl.CostEstimate(
            flops=2 * count * length * depth * width,
            bytes_accessed=count * length * (2 * depth + 12 * width),
            transcendentals=0,
        ),
    )(grad_rows, down_weight, slope, swish)


def weight_kernel(left_ref, right_ref, part_ref):
    depth, _, rows, width = part_ref.shape
    part = dot_tokens(left_ref[...], right_ref[...])
    part_ref[...] = part.astype(jnp.bfloat16).reshape(depth, 1, rows, width)


def weight_parts(left, right, rows):
    tokens, height = left.shape
    width = right.shape[1]
    depth = height // (TEAM_SIZE * rows)
    return pl.pallas_call(
        weight_kernel,
        grid=(TEAM_SIZE,),
        out_shape=jax.ShapeDtypeStruct((depth, TEAM_SIZE, rows, width), jnp.bfloat16),
        in_specs=[
            pl.BlockSpec((tokens, depth * rows), lambda i: (0, i)),
            pl.BlockSpec((tokens, width), lambda i: (0, 0), pipeline_mode=pl.Buffered(1)),
        ],
        out_specs=pl.BlockSpec((depth, 1, rows, width), lambda i: (0, i, 0, 0)),
        compiler_params=pltpu.CompilerParams(vmem_limit_bytes=VMEM_BYTES),
        cost_estimate=pl.CostEstimate(
            flops=2 * tokens * height * width,
            bytes_accessed=2 * tokens * (height + width) + 2 * height * width,
            transcendentals=0,
        ),
    )(left, right)


def attention_weight_kernel(normed_ref, products_ref, gated_ref, grad_ref, part_ref, gate_ref):
    depth, _, rows, _ = part_ref.shape
    own = products_ref.shape[1] - LANES
    part = dot_tokens(normed_ref[...], products_ref[...])
    gate_ref[...] = part[:, own:]
    part_ref[:, :, :, pl.ds(0, own)] = (
        part[:, :own].astype(jnp.bfloat16).reshape(depth, 1, rows, own)
    )
    share = grad_ref.shape[1]
    part = dot_tokens(gated_ref[...], grad_ref[...])
    part_ref[:, :, :, pl.ds(own, share)] = part.astype(jnp.bfloat16).reshape(depth, 1, rows, share)


def attention_weight_parts(normed, grad_products, gated, grad_middle, rows):
    tokens, height = normed.shape
    width = grad_products.shape[1]
    share = height // TEAM_SIZE
    depth = share // rows
    column = pl.BlockSpec((tokens, share), lambda i: (0, i))

    def whole(array):
        return pl.BlockSpec(array.shape, lambda i: (0, 0), pipeline_mode=pl.Buffered(1))

    return pl.pallas_call(
        attention_weight_kernel,
        grid=(TEAM_SIZE,),
        out_shape=[
            jax.ShapeDtypeStruct((depth, TEAM_SIZE, rows, width - LANES + share), jnp.bfloat16),
            jax.ShapeDtypeStruct((height, LANES), jnp.float32),
        ],
        in_specs=[column, whole(grad_products), whole(gated), column],
        out_specs=[
            pl.BlockSpec((depth, 1, rows, width - LANES + share), lambda i: (0, i, 0, 0)),
            pl.BlockSpec((share, LANES), lambda i: (i, 0)),
        ],
        compiler_params=pltpu.CompilerParams(vmem_limit_bytes=VMEM_BYTES),
        cost_estimate=pl.CostEstimate(
            flops=2 * tokens * height * (width + share),
            bytes_accessed=4 * tokens * height + 3 * height * width,
            transcendentals=0,
        ),
    )(normed, grad_products, gated, grad_middle)


def total_kernel(own_ref, sum_ref, stage, landed, slots, send_sem, recv_sem):
    place = team_place()
    barrier = pltpu.get_barrier_semaphore()
    others = []
    for axis in DEPTH:
        count, index = lax.axis_size(axis), lax.axis_index(axis)
        for distance in range(1, count):
            others.append((axis, lax.rem(index + distance, count)))
    for axis, index in list(zip(TEAM, (1 - own for own in place))) + others:
        pl.semaphore_signal(
            barrier, inc=1, device_id={axis: index}, device_id_type=pl.DeviceIdType.MESH
        )
    pl.semaphore_wait(barrier, len(TEAM) + len(others))
    copies = []

    def send(source, target, axis, index):
        copy = pltpu.make_async_remote_copy(
            src_ref=source,
            dst_ref=target,
            send_sem=send_sem.at[len(copies)],
            recv_sem=recv_sem.at[len(copies)],
            device_id={axis: index},
            device_id_type=pl.DeviceIdType.MESH,
        )
        copy.start()
        copies.append(copy)

    stage[0] = own_ref[...]
    for turn in range(len(TEAM)):
        send(stage.at[turn], landed.at[turn], TEAM[-1 - turn], 1 - place[-1 - turn])
        copies[turn].wait_recv()
        stage[turn + 1] = stage[turn] + landed[turn]
    turn = len(TEAM)
    first = 0
    for axis in DEPTH:
        count, index = lax.axis_size(axis), lax.axis_index(axis)
        slots[first + index] = stage[turn]
        begun = len(copies)
        for distance in range(1, count):
            send(
                stage.at[turn], slots.at[first + index], axis, lax.rem(index + distance, count)
            )
        for copy in copies[begun:]:
            copy.wait_recv()
        total = slots[first]
        for item in range(1, count):
            total = total + slots[first + item]
        turn, first = turn + 1, first + count
        stage[turn] = total
    sum_ref[...] = stage[turn]
    for copy in copies:
        copy.wait_send()


def total_all(values, collective_id):
    sizes = [lax.axis_size(axis) for axis in DEPTH]
    copies = len(TEAM) + sum(sizes) - len(sizes)
    return pl.pallas_call(
        total_kernel,
        out_shape=jax.ShapeDtypeStruct(values.shape, values.dtype),
        in_specs=[pl.BlockSpec(memory_space=pltpu.VMEM)],
        out_specs=pl.BlockSpec(memory_space=pltpu.VMEM),
        scratch_shapes=[
            pltpu.VMEM((len(TEAM) + len(DEPTH) + 1,) + values.shape, values.dtype),
            pltpu.VMEM((len(TEAM),) + values.shape, values.dtype),
            pltpu.VMEM((sum(sizes),) + values.shape, values.dtype),
            pltpu.SemaphoreType.DMA((copies,)),
            pltpu.SemaphoreType.DMA((copies,)),
        ],
        compiler_params=pltpu.CompilerParams(collective_id=collective_id, has_side_effects=True),
    )(values)


def team_exchange(blocks):
    return lax.all_to_all(blocks, TEAM, split_axis=0, concat_axis=0, tiled=True)


def turn_half(value_rows):
    return pltpu.roll(value_rows, value_rows.shape[-1] // 2, value_rows.ndim - 1)


def norm_turn(value_rows, gain, cosine, sine):
    scaled = rms_apply(value_rows, gain)
    return scaled * cosine + turn_half(scaled) * sine


def norm_turn_back(value_rows, gain, cosine, sine, gradient):
    turned = gradient * cosine + turn_half(gradient * sine)
    return rms_back(value_rows, gain, turned)


def greet_line():
    index, count = lax.axis_index("seq"), lax.axis_size("seq")
    barrier = pltpu.get_barrier_semaphore()

    @pl.when(index > 0)
    def _():
        pl.semaphore_signal(
            barrier, inc=1, device_id={"seq": index - 1}, device_id_type=pl.DeviceIdType.MESH
        )

    @pl.when(index < count - 1)
    def _():
        pl.semaphore_signal(
            barrier, inc=1, device_id={"seq": index + 1}, device_id_type=pl.DeviceIdType.MESH
        )

    inside = (index > 0) & (index < count - 1)

    @pl.when(inside)
    def _():
        pl.semaphore_wait(barrier, 2)

    @pl.when(jnp.logical_not(inside))
    def _():
        pl.semaphore_wait(barrier, 1)

    return index, count


def attend_kernel(
    window, scale, rows_ref, weight_ref, gate_ref, gains_ref, cosine_ref, sine_ref, start_ref,
    raw_ref, query_ref, pair_ref, stats_ref, across_ref, attended_ref, gated_ref,
    weight, pairs, send_sem, recv_sem,
):
    count_rows, length, _ = rows_ref.shape
    query_cols = query_ref.shape[2]
    heads = query_cols // HEAD_WIDTH
    keys_at = pl.ds(0, HEAD_WIDTH)
    values_at = pl.ds(HEAD_WIDTH, HEAD_WIDTH)
    index, count = greet_line()

    def hop(turn, row):
        return pltpu.make_async_remote_copy(
            src_ref=pairs.at[window - turn + 1, row],
            dst_ref=pairs.at[window - turn, row],
            send_sem=send_sem.at[turn - 1, row],
            recv_sem=recv_sem.at[turn - 1, row],
            device_id={"seq": lax.rem(index + 1, count)},
            device_id_type=pl.DeviceIdType.MESH,
        )

    block = weight_ref.shape[0] * weight_ref.shape[2]
    own = raw_ref.shape[2]
    for step in range(TEAM_SIZE):
        weight[pl.ds(step * block, block), pl.ds(0, own)] = whole_block(
            weight_ref, step, pl.ds(0, own)
        )
    weight[:, pl.ds(own, LANES)] = gate_ref[...]

    def project(row, carry):
        products = jnp.dot(rows_ref[row], weight[...], preferred_element_type=jnp.float32)
        raw = products[:, : query_cols + 2 * HEAD_WIDTH].astype(jnp.bfloat16)
        raw_ref[row] = raw
        cosine, sine = cosine_ref[row], sine_ref[row]
        key = norm_turn(
            raw[:, query_cols : query_cols + HEAD_WIDTH].astype(jnp.float32),
            gains_ref[1:2], cosine, sine,
        )
        pairs[window, row, :, keys_at] = key.astype(jnp.bfloat16)
        pairs[window, row, :, values_at] = raw[:, query_cols + HEAD_WIDTH :]

        @pl.when(index < count - 1)
        def _():
            hop(1, row).start()

        for head in range(heads):
            columns = slice(head * HEAD_WIDTH, (head + 1) * HEAD_WIDTH)
            query_ref[row, :, columns] = norm_turn(
                raw[:, columns].astype(jnp.float32), gains_ref[0:1], cosine, sine
            ).astype(jnp.bfloat16)
        stats_ref[row] = jax.nn.sigmoid(products[:, query_cols + 2 * HEAD_WIDTH :])
        return carry

    lax.fori_loop(0, count_rows, project, 0)

    @pl.when(index == 0)
    def _():
        for slot in range(window):
            pairs[slot] = jnp.zeros_like(pairs[slot])

    for turn in range(2, window + 1):

        def forward(row, carry):
            @pl.when(index > 0)
            def _():
                hop(turn - 1, row).wait_recv()

            @pl.when(index < count - 1)
            def _():
                hop(turn, row).start()

            return carry

        lax.fori_loop(0, count_rows, forward, 0)

    places = lax.broadcasted_iota(jnp.int32, (length, (window + 1) * length), 1)
    latest = window * length + lax.broadcasted_iota(jnp.int32, places.shape, 0)
    lane = lax.broadcasted_iota(jnp.int32, (length, LANES), 1)

    def attend(row, carry):
        @pl.when(index > 0)
        def _():
            hop(window, row).wait_recv()

        allowed = (places >= start_ref[row]) & (places <= latest)
        keys = pairs[:, row, :, keys_at].reshape(-1, HEAD_WIDTH)
        values = pairs[:, row, :, values_at].reshape(-1, HEAD_WIDTH)
        stats = stats_ref[row]
        for head in range(heads):
            columns = slice(head * HEAD_WIDTH, (head + 1) * HEAD_WIDTH)
            scores = dot_t(query_ref[row, :, columns], keys) * scale
            scores = jnp.where(allowed, scores, NEGATIVE)
            top = jnp.max(scores, axis=1, keepdims=True)
            powers = jnp.exp(scores - top)
            total = jnp.sum(powers, axis=1, keepdims=True)
            low_probs = (powers * (1.0 / total)).astype(jnp.bfloat16)
            output = jnp.dot(low_probs, values, preferred_element_type=jnp.float32)
            output = output.astype(jnp.bfloat16)
            attended_ref[row, :, columns] = output
            gated_ref[row, :, columns] = (
                output.astype(jnp.float32) * stats[:, head : head + 1]
            ).astype(jnp.bfloat16)
            stats = jnp.where(lane == heads + head, top + jnp.log(total), stats)
        stats_ref[row] = stats
        across_ref[row] = stats.T[:SUBLANES]
        pair_ref[:, row] = pairs[:, row]
        return carry

    lax.fori_loop(0, count_rows, attend, 0)

    @pl.when(index < count - 1)
    def _():
        for turn in range(1, window + 1):

            def finish(row, carry):
                hop(turn, row).wait_send()
                return carry

            lax.fori_loop(0, count_rows, finish, 0)


def attend(
    normed_rows, own_attention, own_gate, gains, cosine, sine, starts, query_cols, window, collective_id
):
    rows, length, _ = normed_rows.shape
    width = query_cols + 2 * HEAD_WIDTH + LANES
    bf16 = jnp.bfloat16
    vmem = pl.BlockSpec(memory_space=pltpu.VMEM)
    return pl.pallas_call(
        functools.partial(attend_kernel, window, HEAD_WIDTH ** (-0.5)),
        out_shape=[
            jax.ShapeDtypeStruct((rows, length, query_cols + 2 * HEAD_WIDTH), bf16),
            jax.ShapeDtypeStruct((rows, length, query_cols), bf16),
            jax.ShapeDtypeStruct((window + 1, rows, length, 2 * HEAD_WIDTH), bf16),
            jax.ShapeDtypeStruct((rows, length, LANES), jnp.float32),
            jax.ShapeDtypeStruct((rows, SUBLANES, length), jnp.float32),
            jax.ShapeDtypeStruct((rows, length, query_cols), bf16),
            jax.ShapeDtypeStruct((rows, length, query_cols), bf16),
        ],
        in_specs=[vmem] * 7,
        out_specs=[vmem] * 7,
        scratch_shapes=[
            pltpu.VMEM((MODEL_WIDTH, width), bf16),
            pltpu.VMEM((window + 1, rows, length, 2 * HEAD_WIDTH), bf16),
            pltpu.SemaphoreType.DMA((window, rows)),
            pltpu.SemaphoreType.DMA((window, rows)),
        ],
        compiler_params=pltpu.CompilerParams(
            collective_id=collective_id, has_side_effects=True, vmem_limit_bytes=VMEM_BYTES
        ),
        cost_estimate=pl.CostEstimate(
            flops=2 * rows * length * MODEL_WIDTH * width,
            bytes_accessed=ATTEND_COST * rows * length * MODEL_WIDTH,
            transcendentals=0,
        ),
    )(normed_rows, own_attention, own_gate, gains, cosine, sine, starts)


def attend_back_kernel(
    window, scale, rows_ref, weight_ref, gains_ref, cosine_ref, sine_ref, start_ref,
    raw_ref, query_ref, pair_ref, stats_ref, across_ref, attended_ref,
    products_ref, gain_ref,
    weight, parts, outs, ins, send_sem, recv_sem,
):
    count_rows, length, _ = rows_ref.shape
    query_cols = query_ref.shape[2]
    heads = query_cols // HEAD_WIDTH
    keys_at = pl.ds(0, HEAD_WIDTH)
    values_at = pl.ds(HEAD_WIDTH, HEAD_WIDTH)
    index, count = greet_line()
    lag = 2

    def hop(turn, row):
        return pltpu.make_async_remote_copy(
            src_ref=outs.at[turn - 1, row],
            dst_ref=ins.at[turn - 1, row],
            send_sem=send_sem.at[turn - 1, row],
            recv_sem=recv_sem.at[turn - 1, row],
            device_id={"seq": lax.rem(index + count - 1, count)},
            device_id_type=pl.DeviceIdType.MESH,
        )

    keys_total = (window + 1) * length
    places = lax.broadcasted_iota(jnp.int32, (keys_total, length), 0)
    latest = window * length + lax.broadcasted_iota(jnp.int32, places.shape, 1)
    lane = lax.broadcasted_iota(jnp.int32, (length, LANES), 1)
    gain_ref[...] = jnp.zeros_like(gain_ref)
    share = weight_ref.shape[3] - query_cols
    for step in range(TEAM_SIZE):
        weight[:, pl.ds(step * query_cols, query_cols)] = whole_block(
            weight_ref, step, pl.ds(share, query_cols)
        )

    @pl.when(index == count - 1)
    def _():
        ins[...] = jnp.zeros_like(ins)

    def compute(row):
        grad_gated = dot_t(rows_ref[row], weight[...])
        keys = pair_ref[:, row, :, keys_at].reshape(-1, HEAD_WIDTH)
        values = pair_ref[:, row, :, values_at].reshape(-1, HEAD_WIDTH)
        allowed = (places >= start_ref[row]) & (places <= latest)
        cosine, sine = cosine_ref[row], sine_ref[row]
        grad_pre = jnp.zeros((length, LANES), jnp.float32)
        grad_keys = jnp.zeros((keys_total, HEAD_WIDTH), jnp.float32)
        grad_values = jnp.zeros((keys_total, HEAD_WIDTH), jnp.float32)
        for head in range(heads):
            columns = slice(head * HEAD_WIDTH, (head + 1) * HEAD_WIDTH)
            gate = stats_ref[row, :, head : head + 1]
            own = grad_gated[:, columns]
            grad_out = (own * gate).astype(jnp.bfloat16)
            grad_gate = jnp.sum(
                own * attended_ref[row, :, columns].astype(jnp.float32), axis=1, keepdims=True
            )
            grad_pre = jnp.where(lane == head, grad_gate * gate * (1.0 - gate), grad_pre)
            query = query_ref[row, :, columns]
            scores = jnp.where(allowed, dot_t(keys, query) * scale, NEGATIVE)
            probs = jnp.exp(scores - across_ref[row, heads + head : heads + head + 1])
            grad_probs = dot_t(values, grad_out)
            inner = jnp.sum(probs * grad_probs, axis=0, keepdims=True)
            grad_scores = (probs * (grad_probs - inner)).astype(jnp.bfloat16)
            grad_values = grad_values + jnp.dot(
                probs.astype(jnp.bfloat16), grad_out, preferred_element_type=jnp.float32
            )
            grad_keys = grad_keys + jnp.dot(
                grad_scores, query, preferred_element_type=jnp.float32
            )
            grad_query = dot_tokens(grad_scores, keys) * scale
            grad_raw, gain = norm_turn_back(
                raw_ref[row, :, columns].astype(jnp.float32), gains_ref[0:1], cosine, sine,
                grad_query,
            )
            products_ref[row, :, columns] = grad_raw.astype(jnp.bfloat16)
            gain_ref[0:1] += jnp.sum(gain, axis=0, keepdims=True)
        products_ref[row, :, query_cols + 2 * HEAD_WIDTH :] = grad_pre.astype(jnp.bfloat16)
        parts[:, row, :, keys_at] = (grad_keys * scale).reshape(window + 1, length, HEAD_WIDTH)
        parts[:, row, :, values_at] = grad_values.reshape(window + 1, length, HEAD_WIDTH)

    def finish(row):
        grad_pair = parts[window, row] + ins[window - 1, row].astype(jnp.float32)
        grad_raw, gain = norm_turn_back(
            raw_ref[row, :, query_cols : query_cols + HEAD_WIDTH].astype(jnp.float32),
            gains_ref[1:2], cosine_ref[row], sine_ref[row], grad_pair[:, :HEAD_WIDTH],
        )
        products_ref[row, :, query_cols : query_cols + HEAD_WIDTH] = grad_raw.astype(jnp.bfloat16)
        products_ref[row, :, query_cols + HEAD_WIDTH : query_cols + 2 * HEAD_WIDTH] = grad_pair[
            :, HEAD_WIDTH:
        ].astype(jnp.bfloat16)
        gain_ref[1:2] += jnp.sum(gain, axis=0, keepdims=True)

    def step(turn_row, carry):
        @pl.when(turn_row < count_rows)
        def _():
            compute(turn_row)

        for turn in range(1, window + 2):
            row = turn_row - lag * (turn - 1)

            @pl.when((row >= 0) & (row < count_rows))
            def _():
                if turn > 1:

                    @pl.when(index < count - 1)
                    def _():
                        hop(turn - 1, row).wait_recv()

                if turn == window + 1:
                    finish(row)
                else:
                    part = parts[turn - 1, row]
                    if turn > 1:
                        part = part + ins[turn - 2, row].astype(jnp.float32)
                    outs[turn - 1, row] = part.astype(jnp.bfloat16)

                    @pl.when(index > 0)
                    def _():
                        hop(turn, row).start()

        return carry

    lax.fori_loop(0, count_rows + lag * window, step, 0)

    @pl.when(index > 0)
    def _():
        for turn in range(1, window + 1):

            def done(row, carry):
                hop(turn, row).wait_send()
                return carry

            lax.fori_loop(0, count_rows, done, 0)


def attend_back(
    grad_rows, own_attention, gains, cosine, sine, starts, saved, window, collective_id
):
    rows, length, _ = grad_rows.shape
    query_cols = saved[1].shape[2]
    width = query_cols + 2 * HEAD_WIDTH + LANES
    bf16 = jnp.bfloat16
    vmem = pl.BlockSpec(memory_space=pltpu.VMEM)
    return pl.pallas_call(
        functools.partial(attend_back_kernel, window, HEAD_WIDTH ** (-0.5)),
        out_shape=[
            jax.ShapeDtypeStruct((rows, length, width), bf16),
            jax.ShapeDtypeStruct((SUBLANES, HEAD_WIDTH), jnp.float32),
        ],
        in_specs=[vmem] * 12,
        out_specs=[vmem] * 2,
        scratch_shapes=[
            pltpu.VMEM((query_cols, MODEL_WIDTH), bf16),
            pltpu.VMEM((window + 1, rows, length, 2 * HEAD_WIDTH), jnp.float32),
            pltpu.VMEM((window, rows, length, 2 * HEAD_WIDTH), bf16),
            pltpu.VMEM((window, rows, length, 2 * HEAD_WIDTH), bf16),
            pltpu.SemaphoreType.DMA((window, rows)),
            pltpu.SemaphoreType.DMA((window, rows)),
        ],
        compiler_params=pltpu.CompilerParams(
            collective_id=collective_id, has_side_effects=True, vmem_limit_bytes=VMEM_BYTES
        ),
        cost_estimate=pl.CostEstimate(
            flops=2 * rows * length * MODEL_WIDTH * query_cols,
            bytes_accessed=ATTEND_COST * rows * length * MODEL_WIDTH,
            transcendentals=0,
        ),
    )(grad_rows, own_attention, gains, cosine, sine, starts, *saved)


def team_columns(matrix, widths):
    pieces = []
    lower = 0
    for width in widths:
        piece = matrix[:, lower : lower + width]
        pieces.append(piece.reshape(matrix.shape[0], TEAM_SIZE, width // TEAM_SIZE))
        lower = lower + width
    return jnp.concatenate(pieces, axis=2).transpose(1, 0, 2)


def whole_columns(blocks, widths):
    pieces = []
    lower = 0
    for width in widths:
        share = width // TEAM_SIZE
        piece = blocks[:, :, lower : lower + share]
        pieces.append(piece.transpose(1, 0, 2).reshape(blocks.shape[1], width))
        lower = lower + share
    return jnp.concatenate(pieces, axis=1)


def gather_parts(blocks):
    return lax.all_gather(blocks, DEPTH, axis=0, tiled=False)


def scatter_parts(parts):
    depth, team, rows, width = parts.shape
    return lax.psum_scatter(
        parts.reshape(depth * team * rows, width), DEPTH, scatter_dimension=0, tiled=True
    ).reshape(team, rows, width)


def own_rows(parts, widths):
    return whole_columns(team_exchange(parts), widths).astype(jnp.float32)


def gather_rows(matrix):
    return lax.all_gather(matrix, DEPTH, axis=0, tiled=True)


def scatter_rows(gradient):
    return lax.psum_scatter(gradient, DEPTH, scatter_dimension=0, tiled=True)


def moments(weight, moment, second, gradient):
    moment_new = BETA * moment + (1.0 - BETA) * gradient
    second_new = BETA * second + (1.0 - BETA) * gradient * gradient
    correction = 1.0 - BETA**STEP
    update = (
        moment_new / correction / (jnp.sqrt(second_new / correction) + ADAM_EPS) + DECAY * weight
    )
    return (moment_new, second_new, update)


def group_squares(matrix, widths):
    sums = []
    lower = 0
    for width in widths:
        piece = matrix[:, lower : lower + width]
        sums.append(jnp.sum(piece * piece))
        lower = lower + width
    return sums


def apply_trust(weight, update, trust, widths):
    factors = [jnp.broadcast_to(trust[index], (width,)) for index, width in enumerate(widths)]
    return weight - RATE * jnp.concatenate(factors)[None, :] * update


def row_update(weight, moment, second, gradient):
    moment_new, second_new, update = moments(weight, moment, second, gradient)
    trust = jnp.sqrt(jnp.sum(weight * weight, axis=-1, keepdims=True)) / jnp.sqrt(
        jnp.sum(update * update, axis=-1, keepdims=True)
    )
    return (weight - RATE * trust * update, moment_new, second_new)


def whole_update(weight, moment, second, gradient):
    moment_new, second_new, update = moments(weight, moment, second, gradient)
    trust = jnp.sqrt(jnp.sum(weight * weight)) / jnp.sqrt(jnp.sum(update * update))
    return (weight - RATE * trust * update, moment_new, second_new)


def shards(
    inputs,
    cotangent,
    doc_lengths,
    projection_weight,
    projection_moment,
    projection_second,
    out_weight,
    out_moment,
    out_second,
    ffn_weight,
    ffn_moment,
    ffn_second,
    down_weight,
    down_moment,
    down_second,
    head_gate,
    gate_moment,
    gate_second,
    norm_gains,
    gains_moment,
    gains_second,
    qk_gains,
    qk_moment,
    qk_second,
):
    rows_dev, local_len, width = inputs.shape
    bf16 = jnp.bfloat16
    team = lax.axis_index(TEAM)
    place_seq = lax.axis_index("seq")
    group_heads = QUERY_HEADS // KEY_VALUE_HEADS
    window = -(-(DOC_MOST - 1) // local_len)
    window = min(window, lax.axis_size("seq") - 1)
    query_cols = QUERY_HEADS * HEAD_WIDTH
    key_value_columns = KEY_VALUE_HEADS * HEAD_WIDTH
    widths_qkv = (query_cols, key_value_columns, key_value_columns)
    widths_ffn = (FF, FF)
    own_query = query_cols // TEAM_SIZE
    own_key = key_value_columns // TEAM_SIZE
    own_ff = FF // TEAM_SIZE
    weight_squares = (
        group_squares(projection_weight, widths_qkv)
        + group_squares(out_weight, (MODEL_WIDTH,))
        + group_squares(ffn_weight, widths_ffn)
        + group_squares(down_weight, (MODEL_WIDTH,))
    )
    own_gate = lax.dynamic_slice_in_dim(head_gate.astype(bf16), team * group_heads, group_heads, 1)
    own_gate = jnp.pad(own_gate, ((0, 0), (0, LANES - group_heads)))
    own_attention = gather_parts(
        jnp.concatenate(
            [
                team_exchange(team_columns(projection_weight.astype(bf16), widths_qkv)),
                team_columns(out_weight.astype(bf16), (MODEL_WIDTH,)),
            ],
            axis=2,
        )
    )
    ffn_blocks = team_exchange(team_columns(ffn_weight.astype(bf16), widths_ffn))
    own_inner = gather_parts(ffn_blocks[:, :, :own_ff])
    lengths = lax.all_gather(doc_lengths, TEAM, axis=0, tiled=True)
    place = place_seq * local_len + jnp.arange(local_len, dtype=jnp.int32)
    position = positions(lengths, place)
    cosine, sine = rotary_tables(position, HEAD_WIDTH)
    starts = window * local_len + jnp.arange(local_len, dtype=jnp.int32)[None, :] - position
    inputs_flat = inputs[0].astype(jnp.float32)
    normed = rms_apply(inputs_flat, norm_gains[0]).astype(bf16)
    normed_all, grad_all = gather_team([normed, cotangent[0]], 0)
    raw, query_rot, pairs, stats, across, attended, gated = attend(
        normed_all.reshape(TEAM_SIZE, local_len, MODEL_WIDTH),
        own_attention,
        own_gate,
        qk_gains,
        cosine,
        sine,
        starts[:, :, None],
        own_query,
        window,
        8,
    )
    gated, up_blocks, low_down = lax.optimization_barrier(
        (gated, ffn_blocks[:, :, own_ff:], down_weight.astype(bf16))
    )
    own_up = gather_parts(up_blocks)
    own_down = gather_rows(low_down)
    middle = inputs_flat + scatter_team(product_out, [gated, own_attention], 1)
    normed2 = rms_apply(middle, norm_gains[1]).astype(bf16)
    normed2_all = gather_team([normed2], 2)[0]
    hidden, slope, swish = ffn_forward(
        normed2_all.reshape(TEAM_SIZE, local_len, MODEL_WIDTH), own_inner, own_up
    )
    grad_final = cotangent[0].astype(jnp.float32)
    down_part, own_down = lax.optimization_barrier(
        (low_tokens(hidden.reshape(-1, own_ff), grad_all), own_down)
    )
    grad_inner, grad_up = ffn_back(
        grad_all.reshape(TEAM_SIZE, local_len, MODEL_WIDTH), own_down, slope, swish
    )
    down_sum = scatter_rows(down_part)
    grad_normed2 = scatter_team(product_ffn_back, [grad_inner, grad_up, own_inner, own_up], 4)
    grad_mid_part, gain_mid = rms_back(middle, norm_gains[1], grad_normed2)
    grad_middle = grad_final + grad_mid_part
    inner_part, grad_low, down_sum = lax.optimization_barrier(
        (
            weight_parts(normed2_all, grad_inner.reshape(-1, own_ff), ffn_weight.shape[0]),
            grad_middle.astype(bf16),
            down_sum,
        )
    )
    inner_sum = scatter_parts(inner_part)
    down_grad = down_sum.astype(jnp.float32)
    grad_middle_all = gather_team([grad_low], 5)[0]
    grad_products, gain_sums = attend_back(
        grad_middle_all.reshape(TEAM_SIZE, local_len, MODEL_WIDTH),
        own_attention,
        qk_gains,
        cosine,
        sine,
        starts[:, None, :],
        (raw, query_rot, pairs, stats, across, attended),
        window,
        9,
    )
    qk_local = gain_sums[:2]
    grad_products = grad_products.reshape(-1, grad_products.shape[2])
    attention_part, gate_part = attention_weight_parts(
        normed_all, grad_products, gated.reshape(-1, own_query), grad_middle_all, out_weight.shape[0]
    )
    up_part = weight_parts(normed2_all, grad_up.reshape(-1, own_ff), ffn_weight.shape[0])
    attention_part, up_part, grad_products, inner_sum = lax.optimization_barrier(
        (attention_part, up_part, grad_products, inner_sum)
    )
    up_sum = scatter_parts(up_part)
    grad_normed = scatter_team(
        product_qkv_back,
        [grad_products.reshape(TEAM_SIZE, local_len, -1), own_attention, own_gate],
        6,
    )
    late_hidden, grad_normed, up_sum, attention_part = lax.optimization_barrier(
        (hidden, grad_normed, up_sum, attention_part)
    )
    attention_sum = scatter_parts(attention_part)
    own_projection = own_query + 2 * own_key
    out_grad = whole_columns(attention_sum[:, :, own_projection:], (MODEL_WIDTH,)).astype(
        jnp.float32
    )
    projection_gradient = own_rows(attention_sum[:, :, :own_projection], widths_qkv)
    ffn_grad = own_rows(jnp.concatenate([inner_sum, up_sum], axis=2), widths_ffn)
    final = middle + scatter_team(product_down, [late_hidden, own_down], 3)
    result = final.astype(bf16).reshape(inputs.shape)
    grad_in_part, gain_in = rms_back(inputs_flat, norm_gains[0], grad_normed)
    input_grad = (grad_middle + grad_in_part).reshape(inputs.shape)
    gains_local = jnp.stack([jnp.sum(gain_in, axis=0), jnp.sum(gain_mid, axis=0)])
    gate_local = lax.dynamic_update_slice_in_dim(
        jnp.zeros((QUERY_HEADS, MODEL_WIDTH), jnp.float32),
        gate_part[:, :group_heads].T,
        team * group_heads,
        0,
    )
    projection_moment_next, projection_second_next, qkv_update = moments(
        projection_weight, projection_moment, projection_second, projection_gradient
    )
    out_moment_new, out_second_new, out_update = moments(
        out_weight, out_moment, out_second, out_grad
    )
    ffn_moment_new, ffn_second_new, ffn_update = moments(
        ffn_weight, ffn_moment, ffn_second, ffn_grad
    )
    down_moment_new, down_second_new, down_update = moments(
        down_weight, down_moment, down_second, down_grad
    )
    update_squares = (
        group_squares(qkv_update, widths_qkv)
        + group_squares(out_update, (MODEL_WIDTH,))
        + group_squares(ffn_update, widths_ffn)
        + group_squares(down_update, (MODEL_WIDTH,))
    )
    groups = len(weight_squares)
    lane = jnp.arange(MODEL_WIDTH, dtype=jnp.int32)
    small = jnp.pad(qk_local.reshape(-1), (0, MODEL_WIDTH - 2 * HEAD_WIDTH))
    for number, square in enumerate(weight_squares + update_squares):
        small = small + jnp.where(lane == 2 * HEAD_WIDTH + number, square, 0.0)
    totals = total_all(
        jnp.concatenate(
            [
                gate_local,
                gains_local,
                small[None],
                jnp.zeros((5, MODEL_WIDTH), jnp.float32),
            ]
        ),
        7,
    )
    gate_grad = totals[:QUERY_HEADS]
    gains_grad = totals[QUERY_HEADS : QUERY_HEADS + 2]
    small = totals[QUERY_HEADS + 2]
    qk_grad = small[: 2 * HEAD_WIDTH].reshape(2, HEAD_WIDTH)
    weight_totals = small[2 * HEAD_WIDTH : 2 * HEAD_WIDTH + groups]
    update_totals = small[2 * HEAD_WIDTH + groups : 2 * HEAD_WIDTH + 2 * groups]
    weight_norms = jnp.sqrt(weight_totals)
    update_norms = jnp.sqrt(update_totals)
    trust = weight_norms / update_norms
    projection_weight_next = apply_trust(projection_weight, qkv_update, trust[0:3], widths_qkv)
    out_new = apply_trust(out_weight, out_update, trust[3:4], (MODEL_WIDTH,))
    ffn_new = apply_trust(ffn_weight, ffn_update, trust[4:6], widths_ffn)
    down_new = apply_trust(down_weight, down_update, trust[6:7], (MODEL_WIDTH,))
    head_gate_new, gate_moment_new, gate_second_new = whole_update(
        head_gate, gate_moment, gate_second, gate_grad.T
    )
    gains_new, gains_moment_new, gains_second_new = row_update(
        norm_gains, gains_moment, gains_second, gains_grad
    )
    qk_new, qk_moment_new, qk_second_new = row_update(qk_gains, qk_moment, qk_second, qk_grad)
    lamb_norms = jnp.stack([weight_norms, update_norms])
    return (
        result,
        input_grad,
        projection_weight_next,
        projection_moment_next,
        projection_second_next,
        projection_weight_next.astype(jnp.bfloat16),
        out_new,
        out_moment_new,
        out_second_new,
        out_new.astype(jnp.bfloat16),
        ffn_new,
        ffn_moment_new,
        ffn_second_new,
        ffn_new.astype(jnp.bfloat16),
        down_new,
        down_moment_new,
        down_second_new,
        down_new.astype(jnp.bfloat16),
        head_gate_new,
        gate_moment_new,
        gate_second_new,
        gains_new,
        gains_moment_new,
        gains_second_new,
        qk_new,
        qk_moment_new,
        qk_second_new,
        lamb_norms,
    )


def solution(mesh):
    mesh = Mesh(
        mesh.devices.reshape(2, 2, 2, mesh.shape["fsdp"] // TEAM_SIZE, mesh.shape["seq"]),
        TEAM + DEPTH,
    )
    rows = TEAM + DEPTH[:1]
    in_specs = (
        P(rows, "seq", None),
        P(rows, "seq", None),
        P(rows, None),
        P(TEAM + DEPTH, None),
        P(TEAM + DEPTH, None),
        P(TEAM + DEPTH, None),
        P(TEAM + DEPTH, None),
        P(TEAM + DEPTH, None),
        P(TEAM + DEPTH, None),
        P(TEAM + DEPTH, None),
        P(TEAM + DEPTH, None),
        P(TEAM + DEPTH, None),
        P(TEAM + DEPTH, None),
        P(TEAM + DEPTH, None),
        P(TEAM + DEPTH, None),
        P(),
        P(),
        P(),
        P(),
        P(),
        P(),
        P(),
        P(),
        P(),
    )
    out_specs = (
        P(rows, "seq", None),
        P(rows, "seq", None),
        P(TEAM + DEPTH, None),
        P(TEAM + DEPTH, None),
        P(TEAM + DEPTH, None),
        P(TEAM + DEPTH, None),
        P(TEAM + DEPTH, None),
        P(TEAM + DEPTH, None),
        P(TEAM + DEPTH, None),
        P(TEAM + DEPTH, None),
        P(TEAM + DEPTH, None),
        P(TEAM + DEPTH, None),
        P(TEAM + DEPTH, None),
        P(TEAM + DEPTH, None),
        P(TEAM + DEPTH, None),
        P(TEAM + DEPTH, None),
        P(TEAM + DEPTH, None),
        P(TEAM + DEPTH, None),
        P(),
        P(),
        P(),
        P(),
        P(),
        P(),
        P(),
        P(),
        P(),
        P(),
    )
    return jax.shard_map(shards, mesh=mesh, in_specs=in_specs, out_specs=out_specs, check_vma=False)
```

```python
import functools

import jax
import jax.numpy as jnp
from jax import lax
from jax.experimental import pallas as pl
from jax.experimental.pallas import tpu as pltpu
from jax.sharding import Mesh
from jax.sharding import PartitionSpec as P

MODEL_WIDTH = 2048
QUERY_HEADS = 16
KEY_VALUE_HEADS = 8
HEAD_WIDTH = 128
FF = 6144
ROW_TOKENS = 1024
STEP = 3
DOC_MOST = 512
TEAM_SIZE = 8
TEAM = ("t2", "t1", "t0")
DEPTH = ("spare", "seq")
LANES = 128
SUBLANES = 8
VMEM_BYTES = 48 << 20
GATHER_VMEM = 32 << 20
TOTAL_COST = 30000
GATHER_COST = 250
SCATTER_COST = 320
ATTEND_COST = 50


NORM_EPS = 1e-06
ADAM_EPS = 1e-06
RATE = 0.3
DECAY = 0.01
BETA = 0.5
THETA = 1000000.0
NEGATIVE = -1e30


def rms_apply(value_rows, gain):
    return (
        value_rows
        * lax.rsqrt(jnp.mean(value_rows * value_rows, axis=-1, keepdims=True) + NORM_EPS)
        * gain
    )


def rms_back(value_rows, gain, gradient):
    scale = lax.rsqrt(jnp.mean(value_rows * value_rows, axis=-1, keepdims=True) + NORM_EPS)
    scaled = gradient * gain
    inner = jnp.mean(scaled * value_rows, axis=-1, keepdims=True)
    grad_value = scale * scaled - value_rows * scale * scale * scale * inner
    grad_gain = gradient * value_rows * scale
    return (grad_value, grad_gain)


def dot_t(left, right):
    return lax.dot_general(
        left, right, (((1,), (1,)), ((), ())), preferred_element_type=jnp.float32
    )


def low_tokens(left, right):
    return dot_tokens(left, right).astype(jnp.bfloat16)


def dot_tokens(left, right):
    return lax.dot_general(
        left, right, (((0,), (0,)), ((), ())), preferred_element_type=jnp.float32
    )


def rotary_tables(position, width):
    half = width // 2
    rates = THETA ** (-jnp.arange(half, dtype=jnp.float32) * 2.0 / width)
    angle = position.astype(jnp.float32)[..., None] * rates
    cosine, sine = jnp.cos(angle), jnp.sin(angle)
    return (
        jnp.concatenate([cosine, cosine], axis=-1),
        jnp.concatenate([-sine, sine], axis=-1),
    )


def positions(lengths, place):
    ends = jnp.cumsum(lengths, axis=1)
    starts = ends - lengths
    inside = (place[None, :, None] >= starts[:, None, :]) & (place[None, :, None] < ends[:, None, :])
    return place[None, :] - jnp.sum(jnp.where(inside, starts[:, None, :], 0), axis=2)


def team_place():
    return tuple(lax.axis_index(axis) for axis in TEAM)


def greet_team(place):
    barrier = pltpu.get_barrier_semaphore()
    for axis, index in zip(TEAM, place):
        pl.semaphore_signal(
            barrier, inc=1, device_id={axis: 1 - index}, device_id_type=pl.DeviceIdType.MESH
        )
    pl.semaphore_wait(barrier, len(TEAM))


def member(place, flips):
    index = 0
    for own, flip in zip(place, flips):
        index = index * 2 + (1 - own if flip else own)
    return index


def gather_kernel(count, work, *refs):
    given, made = (work[1], work[2]) if work else (0, 0)
    owns, operands = refs[:count], refs[count : count + given]
    alls = refs[count + given : 2 * count + given]
    results = refs[2 * count + given : 2 * count + given + made]
    own_sem, send_sem, recv_sem = refs[2 * count + given + made :]
    place = team_place()
    greet_team(place)
    me = member(place, (0, 0, 0))
    beside = member(place, (0, 1, 0))
    above = member(place, (1, 0, 0))
    across = member(place, (1, 1, 0))
    copies = [{} for _ in range(count)]
    keeps = []

    def send(item, number, axis, source, target):
        copy = pltpu.make_async_remote_copy(
            src_ref=source,
            dst_ref=target,
            send_sem=send_sem.at[item, number],
            recv_sem=recv_sem.at[item, number],
            device_id={TEAM[axis]: 1 - place[axis]},
            device_id_type=pl.DeviceIdType.MESH,
        )
        copy.start()
        copies[item][number] = copy

    def halves(item):
        half = owns[item].shape[0] // 2
        return pl.ds(0, half), pl.ds(half, half)

    for item in range(count):
        target = alls[item].at[me]
        send(item, 0, 1, owns[item], target)
        send(item, 1, 0, owns[item], target)
        send(item, 2, 2, owns[item], target)
        keeps.append(pltpu.make_async_copy(owns[item], target, own_sem.at[item]))
        keeps[item].start()
    if work:
        work[0](*operands, *results)
    for item in range(count):
        upper, lower = halves(item)
        copies[item][0].wait_recv()
        block = alls[item].at[beside]
        send(item, 3, 0, block.at[upper], block.at[upper])
        send(item, 4, 2, block, block)
        copies[item][1].wait_recv()
        block = alls[item].at[above]
        send(item, 5, 1, block.at[lower], block.at[lower])
        send(item, 6, 2, block, block)
    for item in range(count):
        upper, lower = halves(item)
        block = alls[item].at[across]
        copies[item][3].wait_recv()
        send(item, 7, 2, block.at[upper], block.at[upper])
        copies[item][5].wait_recv()
        send(item, 8, 2, block.at[lower], block.at[lower])
    for item in range(count):
        for number in (2, 4, 6, 7, 8):
            copies[item][number].wait_recv()
        for number in range(9):
            copies[item][number].wait_send()
        keeps[item].wait()


def gather_team(arrays, collective_id, work=None, operands=(), results=()):
    count = len(arrays)
    anywhere = pl.BlockSpec(memory_space=pl.ANY)
    out_shape = [jax.ShapeDtypeStruct((TEAM_SIZE,) + own.shape, own.dtype) for own in arrays]
    gathered = pl.pallas_call(
        functools.partial(
            gather_kernel, count, (work, len(operands), len(results)) if work else None
        ),
        out_shape=out_shape + list(results),
        in_specs=[anywhere] * (count + len(operands)),
        out_specs=[anywhere] * (count + len(results)),
        scratch_shapes=[
            pltpu.SemaphoreType.DMA((count,)),
            pltpu.SemaphoreType.DMA((count, 9)),
            pltpu.SemaphoreType.DMA((count, 9)),
        ],
        compiler_params=pltpu.CompilerParams(
            collective_id=collective_id, has_side_effects=True, vmem_limit_bytes=GATHER_VMEM
        ),
        cost_estimate=pl.CostEstimate(
            flops=0,
            bytes_accessed=sum(GATHER_COST * own.shape[0] * own.shape[1] for own in arrays),
            transcendentals=0,
        ),
    )(*arrays, *operands)
    return [
        whole.reshape(TEAM_SIZE * own.shape[0], own.shape[1])
        for whole, own in zip(gathered, arrays)
    ] + list(gathered[count:])


def scatter_kernel(product, count, work, *refs):
    given, made = (work[1], work[2]) if work else (0, 0)
    operands, extra = refs[:count], refs[count : count + given]
    sum_ref = refs[count + given]
    results = refs[count + given + 1 : count + given + 1 + made]
    own, out_near, in_near, out_far, in_half, in_full, send_sem, recv_sem = refs[
        count + given + 1 + made :
    ]
    place = team_place()
    greet_team(place)
    rows = sum_ref.shape[0]
    half = rows // 2
    upper, lower = pl.ds(0, half), pl.ds(half, half)

    def send(number, axis, source, target):
        copy = pltpu.make_async_remote_copy(
            src_ref=source,
            dst_ref=target,
            send_sem=send_sem.at[number],
            recv_sem=recv_sem.at[number],
            device_id={TEAM[axis]: 1 - place[axis]},
            device_id_type=pl.DeviceIdType.MESH,
        )
        copy.start()
        return copy

    flips = ((1, 1), (0, 1), (1, 0), (0, 0))
    near, far = [], {}
    is_first = place[2] == 0

    def begin(turn):
        first, second = flips[turn]
        pair = member(place[:2], (first, second))

        def one(step, columns):
            both = product(operands, pair, step, columns)
            former, latter = both[:rows], both[rows:]
            out_near[turn, :, columns] = jnp.where(is_first, latter, former).astype(jnp.bfloat16)
            own[turn, :, columns] = jnp.where(is_first, former, latter)

        over_tiles(sum_ref.shape[1], one)
        near.append(send(turn, 2, out_near.at[turn], in_near.at[turn]))

    def join(turn):
        near[turn].wait_recv()
        return own[turn] + in_near[turn].astype(jnp.float32)

    begin(0)
    begin(1)
    out_far[0] = join(0).astype(jnp.bfloat16)
    far[4] = send(4, 1, out_far.at[0, upper], in_half.at[0])
    far[5] = send(5, 0, out_far.at[0, lower], in_half.at[1])
    begin(2)
    own[1] = join(1)
    out_far[1, upper] = own[1, upper].astype(jnp.bfloat16)
    far[6] = send(6, 1, out_far.at[1, upper], in_full.at[0, upper])
    begin(3)
    own[2] = join(2)
    out_far[2, lower] = own[2, lower].astype(jnp.bfloat16)
    far[7] = send(7, 0, out_far.at[2, lower], in_full.at[1, lower])
    sum_ref[...] = join(3)
    far[5].wait_recv()
    out_far[1, lower] = (own[1, lower] + in_half[1].astype(jnp.float32)).astype(jnp.bfloat16)
    far[8] = send(8, 1, out_far.at[1, lower], in_full.at[0, lower])
    far[4].wait_recv()
    out_far[2, upper] = (own[2, upper] + in_half[0].astype(jnp.float32)).astype(jnp.bfloat16)
    far[9] = send(9, 0, out_far.at[2, upper], in_full.at[1, upper])
    if work:
        work[0](*extra, *results)
    far[6].wait_recv()
    far[7].wait_recv()
    far[8].wait_recv()
    far[9].wait_recv()
    sum_ref[...] = (
        sum_ref[...] + in_full[0].astype(jnp.float32) + in_full[1].astype(jnp.float32)
    )
    for copy in near + [far[number] for number in range(4, 10)]:
        copy.wait_send()


def over_tiles(width, one):
    tile = width // TEAM_SIZE

    def body(step, carry):
        one(step, pl.ds(pl.multiple_of(step * tile, tile), tile))
        return carry

    lax.fori_loop(0, TEAM_SIZE, body, 0)


def whole_block(ref, step, columns=slice(None)):
    block = ref[:, step, :, columns]
    return block.reshape(block.shape[0] * block.shape[1], block.shape[2])


def product_down(operands, pair, step, columns):
    hidden, weight = operands
    return jnp.dot(hidden[pair], weight[:, columns], preferred_element_type=jnp.float32)


def product_out(operands, pair, step, columns):
    gated, weight = operands
    depth = gated.shape[2]
    share = pl.ds(weight.shape[3] - depth, depth)
    return jnp.dot(
        gated[pair], whole_block(weight, step, share), preferred_element_type=jnp.float32
    )


def product_ffn_back(operands, pair, step, columns):
    grad_inner, grad_up, inner_weight, up_weight = operands
    return dot_t(grad_inner[pair], whole_block(inner_weight, step)) + dot_t(
        grad_up[pair], whole_block(up_weight, step)
    )


def product_qkv_back(operands, pair, step, columns):
    grad_products, weight, gate_weight = operands
    depth = grad_products.shape[2] - LANES
    share = pl.ds(0, depth)
    return dot_t(grad_products[pair, :, share], whole_block(weight, step, share)) + dot_t(
        grad_products[pair, :, pl.ds(depth, LANES)], gate_weight[columns, :]
    )


def scatter_team(
    product, lefts, rights, collective_id, work=None, operands=(), results=()
):
    rows = lefts[0].shape[0] // TEAM_SIZE
    depth = sum(left.shape[1] for left in lefts)
    width = MODEL_WIDTH
    paired = [left.reshape(TEAM_SIZE // 2, 2 * rows, left.shape[1]) for left in lefts]
    vmem = pl.BlockSpec(memory_space=pltpu.VMEM)
    anywhere = pl.BlockSpec(memory_space=pl.ANY)
    count = len(lefts) + len(rights)
    summed = pl.pallas_call(
        functools.partial(
            scatter_kernel, product, count, (work, len(operands), len(results)) if work else None
        ),
        out_shape=[jax.ShapeDtypeStruct((rows, width), jnp.float32)] + list(results),
        in_specs=[vmem] * count + [anywhere] * len(operands),
        out_specs=[vmem] + [anywhere] * len(results),
        scratch_shapes=[
            pltpu.VMEM((4, rows, width), jnp.float32),
            pltpu.VMEM((4, rows, width), jnp.bfloat16),
            pltpu.VMEM((4, rows, width), jnp.bfloat16),
            pltpu.VMEM((3, rows, width), jnp.bfloat16),
            pltpu.VMEM((2, rows // 2, width), jnp.bfloat16),
            pltpu.VMEM((2, rows, width), jnp.bfloat16),
            pltpu.SemaphoreType.DMA((10,)),
            pltpu.SemaphoreType.DMA((10,)),
        ],
        compiler_params=pltpu.CompilerParams(
            collective_id=collective_id, has_side_effects=True, vmem_limit_bytes=VMEM_BYTES
        ),
        cost_estimate=pl.CostEstimate(
            flops=2 * TEAM_SIZE * rows * depth * width,
            bytes_accessed=SCATTER_COST * rows * width,
            transcendentals=0,
        ),
    )(*paired, *rights, *operands)
    return summed if work else summed[0]


def ffn_kernel(rows_ref, inner_ref, up_ref, hidden_ref, slope_ref, swish_ref, inner_weight, up_weight):
    @pl.when(pl.program_id(0) == 0)
    def _():
        block = inner_ref.shape[0] * inner_ref.shape[2]
        for step in range(TEAM_SIZE):
            inner_weight[pl.ds(step * block, block), :] = whole_block(inner_ref, step)
            up_weight[pl.ds(step * block, block), :] = whole_block(up_ref, step)

    tile = 256

    def one(step, carry):
        columns = pl.ds(pl.multiple_of(step * tile, tile), tile)
        inner = jnp.dot(rows_ref[0], inner_weight[:, columns], preferred_element_type=jnp.float32)
        up_part = jnp.dot(rows_ref[0], up_weight[:, columns], preferred_element_type=jnp.float32)
        sigma = jax.nn.sigmoid(inner)
        swish = inner * sigma
        hidden_ref[0, :, columns] = (swish * up_part).astype(jnp.bfloat16)
        slope_ref[0, :, columns] = up_part * sigma * (1.0 + inner * (1.0 - sigma))
        swish_ref[0, :, columns] = swish
        return carry

    lax.fori_loop(0, hidden_ref.shape[2] // tile, one, 0)


def ffn_forward(normed_rows, inner_weight, up_weight):
    count, length, depth = normed_rows.shape
    width = inner_weight.shape[3]
    whole = pl.BlockSpec(inner_weight.shape, lambda i: (0, 0, 0, 0), pipeline_mode=pl.Buffered(1))
    out = pl.BlockSpec((1, length, width), lambda i: (i, 0, 0))
    return pl.pallas_call(
        ffn_kernel,
        grid=(count,),
        out_shape=[
            jax.ShapeDtypeStruct((count, length, width), jnp.bfloat16),
            jax.ShapeDtypeStruct((count, length, width), jnp.float32),
            jax.ShapeDtypeStruct((count, length, width), jnp.float32),
        ],
        in_specs=[pl.BlockSpec((1, length, depth), lambda i: (i, 0, 0)), whole, whole],
        out_specs=[out, out, out],
        scratch_shapes=[pltpu.VMEM((depth, width), jnp.bfloat16)] * 2,
        compiler_params=pltpu.CompilerParams(vmem_limit_bytes=VMEM_BYTES),
        cost_estimate=pl.CostEstimate(
            flops=4 * count * length * depth * width,
            bytes_accessed=count * length * (2 * depth + 10 * width),
            transcendentals=count * length * width,
        ),
    )(normed_rows, inner_weight, up_weight)


def ffn_back_kernel(grad_ref, weight_ref, slope_ref, swish_ref, inner_ref, up_ref):
    tile = 256

    def one(step, carry):
        columns = pl.ds(pl.multiple_of(step * tile, tile), tile)
        grad_hidden = dot_t(grad_ref[0], weight_ref[columns, :])
        inner_ref[0, :, columns] = (grad_hidden * slope_ref[0, :, columns]).astype(jnp.bfloat16)
        up_ref[0, :, columns] = (grad_hidden * swish_ref[0, :, columns]).astype(jnp.bfloat16)
        return carry

    lax.fori_loop(0, inner_ref.shape[2] // tile, one, 0)


def ffn_back(grad_rows, down_weight, slope, swish):
    count, length, depth = grad_rows.shape
    width = down_weight.shape[0]
    whole = pl.BlockSpec(down_weight.shape, lambda i: (0, 0), pipeline_mode=pl.Buffered(1))
    part = pl.BlockSpec((1, length, width), lambda i: (i, 0, 0))
    return pl.pallas_call(
        ffn_back_kernel,
        grid=(count,),
        out_shape=[jax.ShapeDtypeStruct((count, length, width), jnp.bfloat16)] * 2,
        in_specs=[pl.BlockSpec((1, length, depth), lambda i: (i, 0, 0)), whole, part, part],
        out_specs=[part, part],
        compiler_params=pltpu.CompilerParams(vmem_limit_bytes=VMEM_BYTES),
        cost_estimate=pl.CostEstimate(
            flops=2 * count * length * depth * width,
            bytes_accessed=count * length * (2 * depth + 12 * width),
            transcendentals=0,
        ),
    )(grad_rows, down_weight, slope, swish)


def weight_kernel(left_ref, right_ref, part_ref):
    depth, _, rows, width = part_ref.shape
    part = dot_tokens(left_ref[...], right_ref[...])
    part_ref[...] = part.astype(jnp.bfloat16).reshape(depth, 1, rows, width)


def weight_shape(left, right, rows):
    depth = left.shape[1] // (TEAM_SIZE * rows)
    return jax.ShapeDtypeStruct((depth, TEAM_SIZE, rows, right.shape[1]), jnp.bfloat16)


def weight_specs(left, right, part):
    depth, _, rows, width = part.shape
    return dict(
        grid=(TEAM_SIZE,),
        in_specs=[
            pl.BlockSpec((left.shape[0], depth * rows), lambda i: (0, i)),
            pl.BlockSpec(right.shape, lambda i: (0, 0)),
        ],
        out_specs=[pl.BlockSpec((depth, 1, rows, width), lambda i: (0, i, 0, 0))],
    )


def weight_parts(left, right, rows):
    part = weight_shape(left, right, rows)
    (tokens, height), width = left.shape, right.shape[1]
    return pl.pallas_call(
        weight_kernel,
        out_shape=[part],
        compiler_params=pltpu.CompilerParams(vmem_limit_bytes=VMEM_BYTES),
        cost_estimate=pl.CostEstimate(
            flops=2 * tokens * height * width,
            bytes_accessed=2 * tokens * (height + width) + 2 * height * width,
            transcendentals=0,
        ),
        **weight_specs(left, right, part),
    )(left, right)[0]


def weight_work(left_ref, right_ref, part_ref):
    pltpu.emit_pipeline(weight_kernel, **weight_specs(left_ref, right_ref, part_ref))(
        left_ref, right_ref, part_ref
    )


def attention_weight_kernel(normed_ref, products_ref, gated_ref, grad_ref, part_ref, gate_ref):
    depth, _, rows, _ = part_ref.shape
    own = products_ref.shape[1] - LANES
    part = dot_tokens(normed_ref[...], products_ref[...])
    gate_ref[...] = part[:, own:]
    part_ref[:, :, :, pl.ds(0, own)] = (
        part[:, :own].astype(jnp.bfloat16).reshape(depth, 1, rows, own)
    )
    share = grad_ref.shape[1]
    part = dot_tokens(gated_ref[...], grad_ref[...])
    part_ref[:, :, :, pl.ds(own, share)] = part.astype(jnp.bfloat16).reshape(depth, 1, rows, share)


def attention_weight_work(*refs):
    normed, products, gated, grad, part, gate = refs
    depth, _, rows, width = part.shape
    share = depth * rows
    column = pl.BlockSpec((normed.shape[0], share), lambda i: (0, i))
    pltpu.emit_pipeline(
        attention_weight_kernel,
        grid=(TEAM_SIZE,),
        in_specs=[
            column,
            pl.BlockSpec(products.shape, lambda i: (0, 0)),
            pl.BlockSpec(gated.shape, lambda i: (0, 0)),
            column,
        ],
        out_specs=[
            pl.BlockSpec((depth, 1, rows, width), lambda i: (0, i, 0, 0)),
            pl.BlockSpec((share, LANES), lambda i: (i, 0)),
        ],
    )(*refs)


def attention_weight_shapes(normed, grad_products, rows):
    height, width = normed.shape[1], grad_products.shape[1]
    share = height // TEAM_SIZE
    return [
        jax.ShapeDtypeStruct((share // rows, TEAM_SIZE, rows, width - LANES + share), jnp.bfloat16),
        jax.ShapeDtypeStruct((height, LANES), jnp.float32),
    ]


def exchange_all(own, line, team, team_sems, line_sems):
    place = team_place()
    me = member(place, (0, 0, 0))
    barrier = pltpu.get_barrier_semaphore()
    flips = [(step // 4, step // 2 % 2, step % 2) for step in range(1, TEAM_SIZE)]
    targets = []
    for flip in flips:
        targets.append(
            {axis: 1 - at if turn else at for axis, at, turn in zip(TEAM, place, flip)}
        )
    sizes = [lax.axis_size(axis) for axis in DEPTH]
    spots = [lax.axis_index(axis) for axis in DEPTH]
    depth = sizes[0] * sizes[1]
    spot = spots[0] * sizes[1] + spots[1]
    line_targets = []
    for step in range(1, depth):
        other = lax.rem(spot + step, depth)
        line_targets.append({DEPTH[0]: other // sizes[1], DEPTH[1]: lax.rem(other, sizes[1])})
    for target in targets + line_targets:
        pl.semaphore_signal(
            barrier, inc=1, device_id=target, device_id_type=pl.DeviceIdType.MESH
        )
    pl.semaphore_wait(barrier, len(targets) + len(line_targets))

    def send(source, target, sems, number, device):
        copy = pltpu.make_async_remote_copy(
            src_ref=source,
            dst_ref=target,
            send_sem=sems.at[0, number],
            recv_sem=sems.at[1, number],
            device_id=device,
            device_id_type=pl.DeviceIdType.MESH,
        )
        copy.start()
        return copy

    line[spot] = own[...]
    copies = [
        send(own, line.at[spot], line_sems, number, device)
        for number, device in enumerate(line_targets)
    ]
    for copy in copies:
        copy.wait_recv()
    total = line[0]
    for step in range(1, depth):
        total = total + line[step]
    team[me] = total
    more = [
        send(team.at[me], team.at[me], team_sems, number, device)
        for number, device in enumerate(targets)
    ]
    for copy in more:
        copy.wait_recv()
    for copy in copies + more:
        copy.wait_send()


def exchange_scratch(rows, width):
    depth = lax.axis_size(DEPTH[0]) * lax.axis_size(DEPTH[1])
    return [
        pltpu.VMEM((rows, width), jnp.float32),
        pltpu.VMEM((depth, rows, width), jnp.float32),
        pltpu.VMEM((TEAM_SIZE, rows, width), jnp.float32),
        pltpu.SemaphoreType.DMA((2, TEAM_SIZE - 1)),
        pltpu.SemaphoreType.DMA((2, max(depth - 1, 1))),
    ]


def squares_row(squares, shape):
    lane = lax.broadcasted_iota(jnp.int32, shape, 1)
    row = jnp.zeros(shape, jnp.float32)
    for number, square in enumerate(squares):
        row = jnp.where(lane == number, square[0, 0], row)
    return row


def gains_kernel(count, gate_ref, first_ref, second_ref, qk_ref, *refs):
    squares = refs[:count]
    gate_out, gains_out, small_out, own, line, team, team_sems, line_sems = refs[count:]
    heads = gate_ref.shape[0]
    own[...] = jnp.zeros_like(own)
    own[0:heads] = gate_ref[...]
    own[heads : heads + 1] = first_ref[...]
    own[heads + 1 : heads + 2] = second_ref[...]
    for row in range(2):
        own[heads + 2 : heads + 3, pl.ds(row * HEAD_WIDTH, HEAD_WIDTH)] = qk_ref[row : row + 1]
    own[heads + 2 : heads + 3, pl.ds(2 * HEAD_WIDTH, LANES)] = squares_row(squares, (1, LANES))
    exchange_all(own, line, team, team_sems, line_sems)
    total = team[0, heads:]
    for step in range(1, TEAM_SIZE):
        total = total + team[step, heads:]
    gains_out[...] = total[:2]
    small_out[...] = total[2:3, : 2 * HEAD_WIDTH + LANES]
    for step in range(TEAM_SIZE):
        gate_out[step * heads : (step + 1) * heads] = team[step, :heads]


def total_gains(gate, gains, qk_gains, squares, collective_id):
    heads = gate.shape[0]
    vmem = pl.BlockSpec(memory_space=pltpu.VMEM)
    scalar = pl.BlockSpec(memory_space=pltpu.SMEM)
    width = gate.shape[1]
    return pl.pallas_call(
        functools.partial(gains_kernel, len(squares)),
        out_shape=[
            jax.ShapeDtypeStruct((TEAM_SIZE * heads, width), jnp.float32),
            jax.ShapeDtypeStruct((2, width), jnp.float32),
            jax.ShapeDtypeStruct((1, 2 * HEAD_WIDTH + LANES), jnp.float32),
        ],
        in_specs=[vmem] * 4 + [scalar] * len(squares),
        out_specs=[vmem] * 3,
        scratch_shapes=exchange_scratch(SUBLANES, width),
        compiler_params=pltpu.CompilerParams(collective_id=collective_id, has_side_effects=True),
        cost_estimate=pl.CostEstimate(
            flops=0, bytes_accessed=TOTAL_COST * width, transcendentals=0
        ),
    )(gate, gains[0][None], gains[1][None], qk_gains, *[square.reshape(1, 1) for square in squares])


def norms_kernel(count, weights_ref, *refs):
    squares = refs[:count]
    norms_out, own, line, team, team_sems, line_sems = refs[count:]
    own[...] = squares_row(squares, own.shape)
    exchange_all(own, line, team, team_sems, line_sems)
    total = team[0]
    for step in range(1, TEAM_SIZE):
        total = total + team[step]
    weight_norm = jnp.sqrt(weights_ref[...])
    update_norm = jnp.sqrt(total[0:1])
    lane = lax.broadcasted_iota(jnp.int32, update_norm.shape, 1)
    norms_out[0:1] = weight_norm
    norms_out[1:2] = update_norm
    norms_out[2:3] = weight_norm / jnp.where(lane < count, update_norm, 1.0)
    norms_out[3:] = jnp.zeros_like(norms_out[3:])


def total_norms(weight_squares, squares, collective_id):
    vmem = pl.BlockSpec(memory_space=pltpu.VMEM)
    scalar = pl.BlockSpec(memory_space=pltpu.SMEM)
    return pl.pallas_call(
        functools.partial(norms_kernel, len(squares)),
        out_shape=jax.ShapeDtypeStruct((SUBLANES, LANES), jnp.float32),
        in_specs=[vmem] + [scalar] * len(squares),
        out_specs=vmem,
        scratch_shapes=exchange_scratch(SUBLANES, LANES),
        compiler_params=pltpu.CompilerParams(collective_id=collective_id, has_side_effects=True),
    )(weight_squares, *[square.reshape(1, 1) for square in squares])


def team_exchange(blocks):
    return lax.all_to_all(blocks, TEAM, split_axis=0, concat_axis=0, tiled=True)


def turn_half(value_rows):
    return pltpu.roll(value_rows, value_rows.shape[-1] // 2, value_rows.ndim - 1)


def norm_turn(value_rows, gain, cosine, sine):
    scaled = rms_apply(value_rows, gain)
    return scaled * cosine + turn_half(scaled) * sine


def norm_turn_back(value_rows, gain, cosine, sine, gradient):
    turned = gradient * cosine + turn_half(gradient * sine)
    return rms_back(value_rows, gain, turned)


def greet_line():
    index, count = lax.axis_index("seq"), lax.axis_size("seq")
    barrier = pltpu.get_barrier_semaphore()

    @pl.when(index > 0)
    def _():
        pl.semaphore_signal(
            barrier, inc=1, device_id={"seq": index - 1}, device_id_type=pl.DeviceIdType.MESH
        )

    @pl.when(index < count - 1)
    def _():
        pl.semaphore_signal(
            barrier, inc=1, device_id={"seq": index + 1}, device_id_type=pl.DeviceIdType.MESH
        )

    inside = (index > 0) & (index < count - 1)

    @pl.when(inside)
    def _():
        pl.semaphore_wait(barrier, 2)

    @pl.when(jnp.logical_not(inside))
    def _():
        pl.semaphore_wait(barrier, 1)

    return index, count


def attend_kernel(
    window, scale, rows_ref, weight_ref, gate_ref, gains_ref, cosine_ref, sine_ref, start_ref,
    raw_ref, query_ref, pair_ref, stats_ref, across_ref, attended_ref, gated_ref,
    weight, pairs, send_sem, recv_sem,
):
    count_rows, length, _ = rows_ref.shape
    query_cols = query_ref.shape[2]
    heads = query_cols // HEAD_WIDTH
    keys_at = pl.ds(0, HEAD_WIDTH)
    values_at = pl.ds(HEAD_WIDTH, HEAD_WIDTH)
    index, count = greet_line()

    def hop(turn, row):
        return pltpu.make_async_remote_copy(
            src_ref=pairs.at[window - turn + 1, row],
            dst_ref=pairs.at[window - turn, row],
            send_sem=send_sem.at[turn - 1, row],
            recv_sem=recv_sem.at[turn - 1, row],
            device_id={"seq": lax.rem(index + 1, count)},
            device_id_type=pl.DeviceIdType.MESH,
        )

    block = weight_ref.shape[0] * weight_ref.shape[2]
    own = raw_ref.shape[2]
    for step in range(TEAM_SIZE):
        weight[pl.ds(step * block, block), pl.ds(0, own)] = whole_block(
            weight_ref, step, pl.ds(0, own)
        )
    weight[:, pl.ds(own, LANES)] = gate_ref[...]

    def project(row, carry):
        products = jnp.dot(rows_ref[row], weight[...], preferred_element_type=jnp.float32)
        raw = products[:, : query_cols + 2 * HEAD_WIDTH].astype(jnp.bfloat16)
        raw_ref[row] = raw
        cosine, sine = cosine_ref[row], sine_ref[row]
        key = norm_turn(
            raw[:, query_cols : query_cols + HEAD_WIDTH].astype(jnp.float32),
            gains_ref[1:2], cosine, sine,
        )
        pairs[window, row, :, keys_at] = key.astype(jnp.bfloat16)
        pairs[window, row, :, values_at] = raw[:, query_cols + HEAD_WIDTH :]

        @pl.when(index < count - 1)
        def _():
            hop(1, row).start()

        for head in range(heads):
            columns = slice(head * HEAD_WIDTH, (head + 1) * HEAD_WIDTH)
            query_ref[row, :, columns] = norm_turn(
                raw[:, columns].astype(jnp.float32), gains_ref[0:1], cosine, sine
            ).astype(jnp.bfloat16)
        stats_ref[row] = jax.nn.sigmoid(products[:, query_cols + 2 * HEAD_WIDTH :])
        return carry

    lax.fori_loop(0, count_rows, project, 0)

    @pl.when(index == 0)
    def _():
        for slot in range(window):
            pairs[slot] = jnp.zeros_like(pairs[slot])

    for turn in range(2, window + 1):

        def forward(row, carry):
            @pl.when(index > 0)
            def _():
                hop(turn - 1, row).wait_recv()

            @pl.when(index < count - 1)
            def _():
                hop(turn, row).start()

            return carry

        lax.fori_loop(0, count_rows, forward, 0)

    places = lax.broadcasted_iota(jnp.int32, (length, (window + 1) * length), 1)
    latest = window * length + lax.broadcasted_iota(jnp.int32, places.shape, 0)
    lane = lax.broadcasted_iota(jnp.int32, (length, LANES), 1)

    def attend(row, carry):
        @pl.when(index > 0)
        def _():
            hop(window, row).wait_recv()

        allowed = (places >= start_ref[row]) & (places <= latest)
        keys = pairs[:, row, :, keys_at].reshape(-1, HEAD_WIDTH)
        values = pairs[:, row, :, values_at].reshape(-1, HEAD_WIDTH)
        stats = stats_ref[row]
        for head in range(heads):
            columns = slice(head * HEAD_WIDTH, (head + 1) * HEAD_WIDTH)
            scores = dot_t(query_ref[row, :, columns], keys) * scale
            scores = jnp.where(allowed, scores, NEGATIVE)
            top = jnp.max(scores, axis=1, keepdims=True)
            powers = jnp.exp(scores - top)
            total = jnp.sum(powers, axis=1, keepdims=True)
            low_probs = (powers * (1.0 / total)).astype(jnp.bfloat16)
            output = jnp.dot(low_probs, values, preferred_element_type=jnp.float32)
            output = output.astype(jnp.bfloat16)
            attended_ref[row, :, columns] = output
            gated_ref[row, :, columns] = (
                output.astype(jnp.float32) * stats[:, head : head + 1]
            ).astype(jnp.bfloat16)
            stats = jnp.where(lane == heads + head, top + jnp.log(total), stats)
        stats_ref[row] = stats
        across_ref[row] = stats.T[:SUBLANES]
        pair_ref[:, row] = pairs[:, row]
        return carry

    lax.fori_loop(0, count_rows, attend, 0)

    @pl.when(index < count - 1)
    def _():
        for turn in range(1, window + 1):

            def finish(row, carry):
                hop(turn, row).wait_send()
                return carry

            lax.fori_loop(0, count_rows, finish, 0)


def attend(
    normed_rows, own_attention, own_gate, gains, cosine, sine, starts, query_cols, window, collective_id
):
    rows, length, _ = normed_rows.shape
    width = query_cols + 2 * HEAD_WIDTH + LANES
    bf16 = jnp.bfloat16
    vmem = pl.BlockSpec(memory_space=pltpu.VMEM)
    return pl.pallas_call(
        functools.partial(attend_kernel, window, HEAD_WIDTH ** (-0.5)),
        out_shape=[
            jax.ShapeDtypeStruct((rows, length, query_cols + 2 * HEAD_WIDTH), bf16),
            jax.ShapeDtypeStruct((rows, length, query_cols), bf16),
            jax.ShapeDtypeStruct((window + 1, rows, length, 2 * HEAD_WIDTH), bf16),
            jax.ShapeDtypeStruct((rows, length, LANES), jnp.float32),
            jax.ShapeDtypeStruct((rows, SUBLANES, length), jnp.float32),
            jax.ShapeDtypeStruct((rows, length, query_cols), bf16),
            jax.ShapeDtypeStruct((rows, length, query_cols), bf16),
        ],
        in_specs=[vmem] * 7,
        out_specs=[vmem] * 7,
        scratch_shapes=[
            pltpu.VMEM((MODEL_WIDTH, width), bf16),
            pltpu.VMEM((window + 1, rows, length, 2 * HEAD_WIDTH), bf16),
            pltpu.SemaphoreType.DMA((window, rows)),
            pltpu.SemaphoreType.DMA((window, rows)),
        ],
        compiler_params=pltpu.CompilerParams(
            collective_id=collective_id, has_side_effects=True, vmem_limit_bytes=VMEM_BYTES
        ),
        cost_estimate=pl.CostEstimate(
            flops=2 * rows * length * MODEL_WIDTH * width,
            bytes_accessed=ATTEND_COST * rows * length * MODEL_WIDTH,
            transcendentals=0,
        ),
    )(normed_rows, own_attention, own_gate, gains, cosine, sine, starts)


def attend_back_kernel(
    window, scale, rows_ref, weight_ref, gains_ref, cosine_ref, sine_ref, start_ref,
    raw_ref, query_ref, pair_ref, stats_ref, across_ref, attended_ref,
    products_ref, gain_ref,
    weight, parts, outs, ins, send_sem, recv_sem,
):
    count_rows, length, _ = rows_ref.shape
    query_cols = query_ref.shape[2]
    heads = query_cols // HEAD_WIDTH
    keys_at = pl.ds(0, HEAD_WIDTH)
    values_at = pl.ds(HEAD_WIDTH, HEAD_WIDTH)
    index, count = greet_line()
    lag = 2

    def hop(turn, row):
        return pltpu.make_async_remote_copy(
            src_ref=outs.at[turn - 1, row],
            dst_ref=ins.at[turn - 1, row],
            send_sem=send_sem.at[turn - 1, row],
            recv_sem=recv_sem.at[turn - 1, row],
            device_id={"seq": lax.rem(index + count - 1, count)},
            device_id_type=pl.DeviceIdType.MESH,
        )

    keys_total = (window + 1) * length
    places = lax.broadcasted_iota(jnp.int32, (keys_total, length), 0)
    latest = window * length + lax.broadcasted_iota(jnp.int32, places.shape, 1)
    lane = lax.broadcasted_iota(jnp.int32, (length, LANES), 1)
    gain_ref[...] = jnp.zeros_like(gain_ref)
    share = weight_ref.shape[3] - query_cols
    for step in range(TEAM_SIZE):
        weight[:, pl.ds(step * query_cols, query_cols)] = whole_block(
            weight_ref, step, pl.ds(share, query_cols)
        )

    @pl.when(index == count - 1)
    def _():
        ins[...] = jnp.zeros_like(ins)

    def compute(row):
        grad_gated = dot_t(rows_ref[row], weight[...])
        keys = pair_ref[:, row, :, keys_at].reshape(-1, HEAD_WIDTH)
        values = pair_ref[:, row, :, values_at].reshape(-1, HEAD_WIDTH)
        allowed = (places >= start_ref[row]) & (places <= latest)
        cosine, sine = cosine_ref[row], sine_ref[row]
        grad_pre = jnp.zeros((length, LANES), jnp.float32)
        grad_keys = jnp.zeros((keys_total, HEAD_WIDTH), jnp.float32)
        grad_values = jnp.zeros((keys_total, HEAD_WIDTH), jnp.float32)
        for head in range(heads):
            columns = slice(head * HEAD_WIDTH, (head + 1) * HEAD_WIDTH)
            gate = stats_ref[row, :, head : head + 1]
            own = grad_gated[:, columns]
            grad_out = (own * gate).astype(jnp.bfloat16)
            grad_gate = jnp.sum(
                own * attended_ref[row, :, columns].astype(jnp.float32), axis=1, keepdims=True
            )
            grad_pre = jnp.where(lane == head, grad_gate * gate * (1.0 - gate), grad_pre)
            query = query_ref[row, :, columns]
            scores = jnp.where(allowed, dot_t(keys, query) * scale, NEGATIVE)
            probs = jnp.exp(scores - across_ref[row, heads + head : heads + head + 1])
            grad_probs = dot_t(values, grad_out)
            inner = jnp.sum(probs * grad_probs, axis=0, keepdims=True)
            grad_scores = (probs * (grad_probs - inner)).astype(jnp.bfloat16)
            grad_values = grad_values + jnp.dot(
                probs.astype(jnp.bfloat16), grad_out, preferred_element_type=jnp.float32
            )
            grad_keys = grad_keys + jnp.dot(
                grad_scores, query, preferred_element_type=jnp.float32
            )
            grad_query = dot_tokens(grad_scores, keys) * scale
            grad_raw, gain = norm_turn_back(
                raw_ref[row, :, columns].astype(jnp.float32), gains_ref[0:1], cosine, sine,
                grad_query,
            )
            products_ref[row, :, columns] = grad_raw.astype(jnp.bfloat16)
            gain_ref[0:1] += jnp.sum(gain, axis=0, keepdims=True)
        products_ref[row, :, query_cols + 2 * HEAD_WIDTH :] = grad_pre.astype(jnp.bfloat16)
        parts[:, row, :, keys_at] = (grad_keys * scale).reshape(window + 1, length, HEAD_WIDTH)
        parts[:, row, :, values_at] = grad_values.reshape(window + 1, length, HEAD_WIDTH)

    def finish(row):
        grad_pair = parts[window, row] + ins[window - 1, row].astype(jnp.float32)
        grad_raw, gain = norm_turn_back(
            raw_ref[row, :, query_cols : query_cols + HEAD_WIDTH].astype(jnp.float32),
            gains_ref[1:2], cosine_ref[row], sine_ref[row], grad_pair[:, :HEAD_WIDTH],
        )
        products_ref[row, :, query_cols : query_cols + HEAD_WIDTH] = grad_raw.astype(jnp.bfloat16)
        products_ref[row, :, query_cols + HEAD_WIDTH : query_cols + 2 * HEAD_WIDTH] = grad_pair[
            :, HEAD_WIDTH:
        ].astype(jnp.bfloat16)
        gain_ref[1:2] += jnp.sum(gain, axis=0, keepdims=True)

    def step(turn_row, carry):
        @pl.when(turn_row < count_rows)
        def _():
            compute(turn_row)

        for turn in range(1, window + 2):
            row = turn_row - lag * (turn - 1)

            @pl.when((row >= 0) & (row < count_rows))
            def _():
                if turn > 1:

                    @pl.when(index < count - 1)
                    def _():
                        hop(turn - 1, row).wait_recv()

                if turn == window + 1:
                    finish(row)
                else:
                    part = parts[turn - 1, row]
                    if turn > 1:
                        part = part + ins[turn - 2, row].astype(jnp.float32)
                    outs[turn - 1, row] = part.astype(jnp.bfloat16)

                    @pl.when(index > 0)
                    def _():
                        hop(turn, row).start()

        return carry

    lax.fori_loop(0, count_rows + lag * window, step, 0)

    @pl.when(index > 0)
    def _():
        for turn in range(1, window + 1):

            def done(row, carry):
                hop(turn, row).wait_send()
                return carry

            lax.fori_loop(0, count_rows, done, 0)


def attend_back(
    grad_rows, own_attention, gains, cosine, sine, starts, saved, window, collective_id
):
    rows, length, _ = grad_rows.shape
    query_cols = saved[1].shape[2]
    width = query_cols + 2 * HEAD_WIDTH + LANES
    bf16 = jnp.bfloat16
    vmem = pl.BlockSpec(memory_space=pltpu.VMEM)
    return pl.pallas_call(
        functools.partial(attend_back_kernel, window, HEAD_WIDTH ** (-0.5)),
        out_shape=[
            jax.ShapeDtypeStruct((rows, length, width), bf16),
            jax.ShapeDtypeStruct((SUBLANES, HEAD_WIDTH), jnp.float32),
        ],
        in_specs=[vmem] * 12,
        out_specs=[vmem] * 2,
        scratch_shapes=[
            pltpu.VMEM((query_cols, MODEL_WIDTH), bf16),
            pltpu.VMEM((window + 1, rows, length, 2 * HEAD_WIDTH), jnp.float32),
            pltpu.VMEM((window, rows, length, 2 * HEAD_WIDTH), bf16),
            pltpu.VMEM((window, rows, length, 2 * HEAD_WIDTH), bf16),
            pltpu.SemaphoreType.DMA((window, rows)),
            pltpu.SemaphoreType.DMA((window, rows)),
        ],
        compiler_params=pltpu.CompilerParams(
            collective_id=collective_id, has_side_effects=True, vmem_limit_bytes=VMEM_BYTES
        ),
        cost_estimate=pl.CostEstimate(
            flops=2 * rows * length * MODEL_WIDTH * query_cols,
            bytes_accessed=ATTEND_COST * rows * length * MODEL_WIDTH,
            transcendentals=0,
        ),
    )(grad_rows, own_attention, gains, cosine, sine, starts, *saved)


def team_columns(matrix, widths):
    pieces = []
    lower = 0
    for width in widths:
        piece = matrix[:, lower : lower + width]
        pieces.append(piece.reshape(matrix.shape[0], TEAM_SIZE, width // TEAM_SIZE))
        lower = lower + width
    return jnp.concatenate(pieces, axis=2).transpose(1, 0, 2)


def whole_columns(blocks, widths):
    pieces = []
    lower = 0
    for width in widths:
        share = width // TEAM_SIZE
        piece = blocks[:, :, lower : lower + share]
        pieces.append(piece.transpose(1, 0, 2).reshape(blocks.shape[1], width))
        lower = lower + share
    return jnp.concatenate(pieces, axis=1)


def gather_parts(blocks):
    return lax.all_gather(blocks, DEPTH, axis=0, tiled=False)


def scatter_parts(parts):
    depth, team, rows, width = parts.shape
    return lax.psum_scatter(
        parts.reshape(depth * team * rows, width), DEPTH, scatter_dimension=0, tiled=True
    ).reshape(team, rows, width)


def own_rows(parts, widths):
    return whole_columns(team_exchange(parts), widths).astype(jnp.float32)


def gather_rows(matrix):
    return lax.all_gather(matrix, DEPTH, axis=0, tiled=True)


def scatter_rows(gradient):
    return lax.psum_scatter(gradient, DEPTH, scatter_dimension=0, tiled=True)


def moments(weight, moment, second, gradient):
    moment_new = BETA * moment + (1.0 - BETA) * gradient
    second_new = BETA * second + (1.0 - BETA) * gradient * gradient
    correction = 1.0 - BETA**STEP
    update = (
        moment_new / correction / (jnp.sqrt(second_new / correction) + ADAM_EPS) + DECAY * weight
    )
    return (moment_new, second_new, update)


def group_squares(matrix, widths):
    sums = []
    lower = 0
    for width in widths:
        piece = matrix[:, lower : lower + width]
        sums.append(jnp.sum(piece * piece))
        lower = lower + width
    return sums


def apply_trust(weight, update, trust, widths):
    column = lax.broadcasted_iota(jnp.int32, (1, weight.shape[1]), 1)
    factor = trust[0]
    lower = 0
    for index, width in enumerate(widths[:-1]):
        lower = lower + width
        factor = jnp.where(column < lower, factor, trust[index + 1])
    return weight - RATE * factor * update


def row_update(weight, moment, second, gradient):
    moment_new, second_new, update = moments(weight, moment, second, gradient)
    trust = jnp.sqrt(jnp.sum(weight * weight, axis=-1, keepdims=True)) / jnp.sqrt(
        jnp.sum(update * update, axis=-1, keepdims=True)
    )
    return (weight - RATE * trust * update, moment_new, second_new)


def whole_update(weight, moment, second, gradient):
    moment_new, second_new, update = moments(weight, moment, second, gradient)
    trust = jnp.sqrt(jnp.sum(weight * weight)) / jnp.sqrt(jnp.sum(update * update))
    return (weight - RATE * trust * update, moment_new, second_new)


def shards(
    inputs,
    cotangent,
    doc_lengths,
    projection_weight,
    projection_moment,
    projection_second,
    out_weight,
    out_moment,
    out_second,
    ffn_weight,
    ffn_moment,
    ffn_second,
    down_weight,
    down_moment,
    down_second,
    head_gate,
    gate_moment,
    gate_second,
    norm_gains,
    gains_moment,
    gains_second,
    qk_gains,
    qk_moment,
    qk_second,
):
    rows_dev, local_len, width = inputs.shape
    bf16 = jnp.bfloat16
    team = lax.axis_index(TEAM)
    place_seq = lax.axis_index("seq")
    group_heads = QUERY_HEADS // KEY_VALUE_HEADS
    window = -(-(DOC_MOST - 1) // local_len)
    window = min(window, lax.axis_size("seq") - 1)
    query_cols = QUERY_HEADS * HEAD_WIDTH
    key_value_columns = KEY_VALUE_HEADS * HEAD_WIDTH
    widths_qkv = (query_cols, key_value_columns, key_value_columns)
    widths_ffn = (FF, FF)
    own_query = query_cols // TEAM_SIZE
    own_key = key_value_columns // TEAM_SIZE
    own_ff = FF // TEAM_SIZE
    weight_squares = (
        group_squares(projection_weight, widths_qkv)
        + group_squares(out_weight, (MODEL_WIDTH,))
        + group_squares(ffn_weight, widths_ffn)
        + group_squares(down_weight, (MODEL_WIDTH,))
    )
    own_gate = lax.dynamic_slice_in_dim(head_gate.astype(bf16), team * group_heads, group_heads, 1)
    own_gate = jnp.pad(own_gate, ((0, 0), (0, LANES - group_heads)))
    own_attention = gather_parts(
        jnp.concatenate(
            [
                team_exchange(team_columns(projection_weight.astype(bf16), widths_qkv)),
                team_columns(out_weight.astype(bf16), (MODEL_WIDTH,)),
            ],
            axis=2,
        )
    )
    ffn_blocks = team_exchange(team_columns(ffn_weight.astype(bf16), widths_ffn))
    own_inner = gather_parts(ffn_blocks[:, :, :own_ff])
    lengths = lax.all_gather(doc_lengths, TEAM, axis=0, tiled=True)
    place = place_seq * local_len + jnp.arange(local_len, dtype=jnp.int32)
    position = positions(lengths, place)
    cosine, sine = rotary_tables(position, HEAD_WIDTH)
    starts = window * local_len + jnp.arange(local_len, dtype=jnp.int32)[None, :] - position
    inputs_flat = inputs[0].astype(jnp.float32)
    normed = rms_apply(inputs_flat, norm_gains[0]).astype(bf16)
    normed_all, grad_all = gather_team([normed, cotangent[0]], 0)
    raw, query_rot, pairs, stats, across, attended, gated = attend(
        normed_all.reshape(TEAM_SIZE, local_len, MODEL_WIDTH),
        own_attention,
        own_gate,
        qk_gains,
        cosine,
        sine,
        starts[:, :, None],
        own_query,
        window,
        8,
    )
    gated, up_blocks, low_down = lax.optimization_barrier(
        (gated, ffn_blocks[:, :, own_ff:], down_weight.astype(bf16))
    )
    own_up = gather_parts(up_blocks)
    own_down = gather_rows(low_down)
    middle = inputs_flat + scatter_team(product_out, [gated.reshape(-1, own_query)], [own_attention], 1)
    normed2 = rms_apply(middle, norm_gains[1]).astype(bf16)
    normed2_all = gather_team([normed2], 2)[0]
    hidden, slope, swish = ffn_forward(
        normed2_all.reshape(TEAM_SIZE, local_len, MODEL_WIDTH), own_inner, own_up
    )
    grad_final = cotangent[0].astype(jnp.float32)
    down_part, own_down = lax.optimization_barrier(
        (low_tokens(hidden.reshape(-1, own_ff), grad_all), own_down)
    )
    grad_inner, grad_up = ffn_back(
        grad_all.reshape(TEAM_SIZE, local_len, MODEL_WIDTH), own_down, slope, swish
    )
    grad_inner, grad_up = grad_inner.reshape(-1, own_ff), grad_up.reshape(-1, own_ff)
    inner_part, grad_inner = lax.optimization_barrier(
        (weight_parts(normed2_all, grad_inner, ffn_weight.shape[0]), grad_inner)
    )
    down_sum = scatter_rows(down_part)
    grad_normed2 = scatter_team(
        product_ffn_back, [grad_inner, grad_up], [own_inner, own_up], 4
    )
    grad_mid_part, gain_mid = rms_back(middle, norm_gains[1], grad_normed2)
    grad_middle = grad_final + grad_mid_part
    grad_low, down_sum = lax.optimization_barrier((grad_middle.astype(bf16), down_sum))
    inner_sum = scatter_parts(inner_part)
    down_grad = down_sum.astype(jnp.float32)
    grad_middle_all, up_part = gather_team(
        [grad_low],
        5,
        weight_work,
        (normed2_all, grad_up),
        (weight_shape(normed2_all, grad_up, ffn_weight.shape[0]),),
    )
    grad_products, gain_sums = attend_back(
        grad_middle_all.reshape(TEAM_SIZE, local_len, MODEL_WIDTH),
        own_attention,
        qk_gains,
        cosine,
        sine,
        starts[:, None, :],
        (raw, query_rot, pairs, stats, across, attended),
        window,
        9,
    )
    grad_products = grad_products.reshape(-1, grad_products.shape[2])
    up_part, grad_products, inner_sum = lax.optimization_barrier(
        (up_part, grad_products, inner_sum)
    )
    up_sum = scatter_parts(up_part)
    grad_normed, attention_part, gate_part = scatter_team(
        product_qkv_back,
        [grad_products],
        [own_attention, own_gate],
        6,
        attention_weight_work,
        (normed_all, grad_products, gated.reshape(-1, own_query), grad_middle_all),
        attention_weight_shapes(normed_all, grad_products, out_weight.shape[0]),
    )
    late_hidden, grad_normed = lax.optimization_barrier((hidden, grad_normed))
    attention_sum = scatter_parts(attention_part)
    final = middle + scatter_team(product_down, [late_hidden.reshape(-1, own_ff)], [own_down], 3)
    result = final.astype(bf16).reshape(inputs.shape)
    grad_in_part, gain_in = rms_back(inputs_flat, norm_gains[0], grad_normed)
    input_grad = (grad_middle + grad_in_part).reshape(inputs.shape)
    ffn_rows = team_exchange(jnp.concatenate([inner_sum, up_sum], axis=2))
    gate_part, ffn_rows = lax.optimization_barrier((gate_part, ffn_rows))
    ffn_grad = whole_columns(ffn_rows, widths_ffn).astype(jnp.float32)
    gate_grad, gains_grad, small_sums = total_gains(
        gate_part[:, :group_heads].T,
        (jnp.sum(gain_in, axis=0), jnp.sum(gain_mid, axis=0)),
        gain_sums,
        weight_squares,
        7,
    )
    attention_sum, small_sums = lax.optimization_barrier((attention_sum, small_sums))
    own_projection = own_query + 2 * own_key
    out_grad = whole_columns(attention_sum[:, :, own_projection:], (MODEL_WIDTH,)).astype(
        jnp.float32
    )
    projection_gradient = own_rows(attention_sum[:, :, :own_projection], widths_qkv)
    qk_grad = small_sums[0, : 2 * HEAD_WIDTH].reshape(2, HEAD_WIDTH)
    projection_moment_next, projection_second_next, qkv_update = moments(
        projection_weight, projection_moment, projection_second, projection_gradient
    )
    out_moment_new, out_second_new, out_update = moments(
        out_weight, out_moment, out_second, out_grad
    )
    ffn_moment_new, ffn_second_new, ffn_update = moments(
        ffn_weight, ffn_moment, ffn_second, ffn_grad
    )
    down_moment_new, down_second_new, down_update = moments(
        down_weight, down_moment, down_second, down_grad
    )
    update_squares = (
        group_squares(qkv_update, widths_qkv)
        + group_squares(out_update, (MODEL_WIDTH,))
        + group_squares(ffn_update, widths_ffn)
        + group_squares(down_update, (MODEL_WIDTH,))
    )
    norms = total_norms(small_sums[:, 2 * HEAD_WIDTH :], update_squares, 10)
    trust = norms[2]
    projection_weight_next = apply_trust(projection_weight, qkv_update, trust[0:3], widths_qkv)
    out_new = apply_trust(out_weight, out_update, trust[3:4], (MODEL_WIDTH,))
    ffn_new = apply_trust(ffn_weight, ffn_update, trust[4:6], widths_ffn)
    down_new = apply_trust(down_weight, down_update, trust[6:7], (MODEL_WIDTH,))
    head_gate_new, gate_moment_new, gate_second_new = whole_update(
        head_gate, gate_moment, gate_second, gate_grad.T
    )
    gains_new, gains_moment_new, gains_second_new = row_update(
        norm_gains, gains_moment, gains_second, gains_grad
    )
    qk_new, qk_moment_new, qk_second_new = row_update(qk_gains, qk_moment, qk_second, qk_grad)
    lamb_norms = norms[:2, : len(update_squares)]
    return (
        result,
        input_grad,
        projection_weight_next,
        projection_moment_next,
        projection_second_next,
        projection_weight_next.astype(jnp.bfloat16),
        out_new,
        out_moment_new,
        out_second_new,
        out_new.astype(jnp.bfloat16),
        ffn_new,
        ffn_moment_new,
        ffn_second_new,
        ffn_new.astype(jnp.bfloat16),
        down_new,
        down_moment_new,
        down_second_new,
        down_new.astype(jnp.bfloat16),
        head_gate_new,
        gate_moment_new,
        gate_second_new,
        gains_new,
        gains_moment_new,
        gains_second_new,
        qk_new,
        qk_moment_new,
        qk_second_new,
        lamb_norms,
    )


def solution(mesh):
    mesh = Mesh(
        mesh.devices.reshape(2, 2, 2, mesh.shape["fsdp"] // TEAM_SIZE, mesh.shape["seq"]),
        TEAM + DEPTH,
    )
    rows = TEAM + DEPTH[:1]
    in_specs = (
        P(rows, "seq", None),
        P(rows, "seq", None),
        P(rows, None),
        P(TEAM + DEPTH, None),
        P(TEAM + DEPTH, None),
        P(TEAM + DEPTH, None),
        P(TEAM + DEPTH, None),
        P(TEAM + DEPTH, None),
        P(TEAM + DEPTH, None),
        P(TEAM + DEPTH, None),
        P(TEAM + DEPTH, None),
        P(TEAM + DEPTH, None),
        P(TEAM + DEPTH, None),
        P(TEAM + DEPTH, None),
        P(TEAM + DEPTH, None),
        P(),
        P(),
        P(),
        P(),
        P(),
        P(),
        P(),
        P(),
        P(),
    )
    out_specs = (
        P(rows, "seq", None),
        P(rows, "seq", None),
        P(TEAM + DEPTH, None),
        P(TEAM + DEPTH, None),
        P(TEAM + DEPTH, None),
        P(TEAM + DEPTH, None),
        P(TEAM + DEPTH, None),
        P(TEAM + DEPTH, None),
        P(TEAM + DEPTH, None),
        P(TEAM + DEPTH, None),
        P(TEAM + DEPTH, None),
        P(TEAM + DEPTH, None),
        P(TEAM + DEPTH, None),
        P(TEAM + DEPTH, None),
        P(TEAM + DEPTH, None),
        P(TEAM + DEPTH, None),
        P(TEAM + DEPTH, None),
        P(TEAM + DEPTH, None),
        P(),
        P(),
        P(),
        P(),
        P(),
        P(),
        P(),
        P(),
        P(),
        P(),
    )
    return jax.shard_map(shards, mesh=mesh, in_specs=in_specs, out_specs=out_specs, check_vma=False)
```

```python
import functools

import jax
import jax.numpy as jnp
from jax import lax
from jax.experimental import pallas as pl
from jax.experimental.pallas import tpu as pltpu
from jax.sharding import Mesh
from jax.sharding import PartitionSpec as P

MODEL_WIDTH = 2048
QUERY_HEADS = 16
KEY_VALUE_HEADS = 8
HEAD_WIDTH = 128
FF = 6144
ROW_TOKENS = 1024
STEP = 3
DOC_MOST = 512
TEAM_SIZE = 8
TEAM = ("t2", "t1", "t0")
DEPTH = ("spare", "seq")
LANES = 128
SUBLANES = 8
VMEM_BYTES = 48 << 20
GATHER_VMEM = 32 << 20
LAMB_COST = 70
GATHER_COST = 250
SCATTER_COST = 320
ATTEND_COST = 50


NORM_EPS = 1e-06
ADAM_EPS = 1e-06
RATE = 0.3
DECAY = 0.01
BETA = 0.5
THETA = 1000000.0
NEGATIVE = -1e30


def rms_apply(value_rows, gain):
    return (
        value_rows
        * lax.rsqrt(jnp.mean(value_rows * value_rows, axis=-1, keepdims=True) + NORM_EPS)
        * gain
    )


def rms_back(value_rows, gain, gradient):
    scale = lax.rsqrt(jnp.mean(value_rows * value_rows, axis=-1, keepdims=True) + NORM_EPS)
    scaled = gradient * gain
    inner = jnp.mean(scaled * value_rows, axis=-1, keepdims=True)
    grad_value = scale * scaled - value_rows * scale * scale * scale * inner
    grad_gain = gradient * value_rows * scale
    return (grad_value, grad_gain)


def dot_t(left, right):
    return lax.dot_general(
        left, right, (((1,), (1,)), ((), ())), preferred_element_type=jnp.float32
    )


def low_tokens(left, right):
    return dot_tokens(left, right).astype(jnp.bfloat16)


def dot_tokens(left, right):
    return lax.dot_general(
        left, right, (((0,), (0,)), ((), ())), preferred_element_type=jnp.float32
    )


def moments(weight, moment, second, gradient):
    moment_new = BETA * moment + (1.0 - BETA) * gradient
    second_new = BETA * second + (1.0 - BETA) * gradient * gradient
    correction = 1.0 - BETA**STEP
    update = (
        moment_new / correction / (jnp.sqrt(second_new / correction) + ADAM_EPS) + DECAY * weight
    )
    return (moment_new, second_new, update)


def rotary_tables(position, width):
    half = width // 2
    rates = THETA ** (-jnp.arange(half, dtype=jnp.float32) * 2.0 / width)
    angle = position.astype(jnp.float32)[..., None] * rates
    cosine, sine = jnp.cos(angle), jnp.sin(angle)
    return (
        jnp.concatenate([cosine, cosine], axis=-1),
        jnp.concatenate([-sine, sine], axis=-1),
    )


def positions(lengths, place):
    ends = jnp.cumsum(lengths, axis=1)
    starts = ends - lengths
    inside = (place[None, :, None] >= starts[:, None, :]) & (place[None, :, None] < ends[:, None, :])
    return place[None, :] - jnp.sum(jnp.where(inside, starts[:, None, :], 0), axis=2)


def team_place():
    return tuple(lax.axis_index(axis) for axis in TEAM)


def greet_team(place):
    barrier = pltpu.get_barrier_semaphore()
    for axis, index in zip(TEAM, place):
        pl.semaphore_signal(
            barrier, inc=1, device_id={axis: 1 - index}, device_id_type=pl.DeviceIdType.MESH
        )
    pl.semaphore_wait(barrier, len(TEAM))


def member(place, flips):
    index = 0
    for own, flip in zip(place, flips):
        index = index * 2 + (1 - own if flip else own)
    return index


def gather_kernel(count, work, *refs):
    given, made = (work[1], work[2]) if work else (0, 0)
    owns, operands = refs[:count], refs[count : count + given]
    alls = refs[count + given : 2 * count + given]
    results = refs[2 * count + given : 2 * count + given + made]
    own_sem, send_sem, recv_sem = refs[2 * count + given + made :]
    place = team_place()
    greet_team(place)
    me = member(place, (0, 0, 0))
    beside = member(place, (0, 1, 0))
    above = member(place, (1, 0, 0))
    across = member(place, (1, 1, 0))
    copies = [{} for _ in range(count)]
    keeps = []

    def send(item, number, axis, source, target):
        copy = pltpu.make_async_remote_copy(
            src_ref=source,
            dst_ref=target,
            send_sem=send_sem.at[item, number],
            recv_sem=recv_sem.at[item, number],
            device_id={TEAM[axis]: 1 - place[axis]},
            device_id_type=pl.DeviceIdType.MESH,
        )
        copy.start()
        copies[item][number] = copy

    def halves(item):
        half = owns[item].shape[0] // 2
        return pl.ds(0, half), pl.ds(half, half)

    for item in range(count):
        target = alls[item].at[me]
        send(item, 0, 1, owns[item], target)
        send(item, 1, 0, owns[item], target)
        send(item, 2, 2, owns[item], target)
        keeps.append(pltpu.make_async_copy(owns[item], target, own_sem.at[item]))
        keeps[item].start()
    if work:
        work[0](*operands, *results)
    for item in range(count):
        upper, lower = halves(item)
        copies[item][0].wait_recv()
        block = alls[item].at[beside]
        send(item, 3, 0, block.at[upper], block.at[upper])
        send(item, 4, 2, block, block)
        copies[item][1].wait_recv()
        block = alls[item].at[above]
        send(item, 5, 1, block.at[lower], block.at[lower])
        send(item, 6, 2, block, block)
    for item in range(count):
        upper, lower = halves(item)
        block = alls[item].at[across]
        copies[item][3].wait_recv()
        send(item, 7, 2, block.at[upper], block.at[upper])
        copies[item][5].wait_recv()
        send(item, 8, 2, block.at[lower], block.at[lower])
    for item in range(count):
        for number in (2, 4, 6, 7, 8):
            copies[item][number].wait_recv()
        for number in range(9):
            copies[item][number].wait_send()
        keeps[item].wait()


def gather_team(arrays, collective_id, work=None, operands=(), results=()):
    count = len(arrays)
    anywhere = pl.BlockSpec(memory_space=pl.ANY)
    out_shape = [jax.ShapeDtypeStruct((TEAM_SIZE,) + own.shape, own.dtype) for own in arrays]
    gathered = pl.pallas_call(
        functools.partial(
            gather_kernel, count, (work, len(operands), len(results)) if work else None
        ),
        out_shape=out_shape + list(results),
        in_specs=[anywhere] * (count + len(operands)),
        out_specs=[anywhere] * (count + len(results)),
        scratch_shapes=[
            pltpu.SemaphoreType.DMA((count,)),
            pltpu.SemaphoreType.DMA((count, 9)),
            pltpu.SemaphoreType.DMA((count, 9)),
        ],
        compiler_params=pltpu.CompilerParams(
            collective_id=collective_id, has_side_effects=True, vmem_limit_bytes=GATHER_VMEM
        ),
        cost_estimate=pl.CostEstimate(
            flops=0,
            bytes_accessed=sum(GATHER_COST * own.shape[0] * own.shape[1] for own in arrays),
            transcendentals=0,
        ),
    )(*arrays, *operands)
    return [
        whole.reshape(TEAM_SIZE * own.shape[0], own.shape[1])
        for whole, own in zip(gathered, arrays)
    ] + list(gathered[count:])


def scatter_kernel(product, count, work, *refs):
    given, made = (work[1], work[2]) if work else (0, 0)
    operands, extra = refs[:count], refs[count : count + given]
    sum_ref = refs[count + given]
    results = refs[count + given + 1 : count + given + 1 + made]
    own, out_near, in_near, out_far, in_half, in_full, send_sem, recv_sem = refs[
        count + given + 1 + made :
    ]
    place = team_place()
    greet_team(place)
    rows = sum_ref.shape[0]
    half = rows // 2
    upper, lower = pl.ds(0, half), pl.ds(half, half)

    def send(number, axis, source, target):
        copy = pltpu.make_async_remote_copy(
            src_ref=source,
            dst_ref=target,
            send_sem=send_sem.at[number],
            recv_sem=recv_sem.at[number],
            device_id={TEAM[axis]: 1 - place[axis]},
            device_id_type=pl.DeviceIdType.MESH,
        )
        copy.start()
        return copy

    flips = ((1, 1), (0, 1), (1, 0), (0, 0))
    near, far = [], {}
    is_first = place[2] == 0

    def begin(turn):
        first, second = flips[turn]
        pair = member(place[:2], (first, second))

        def one(step, columns):
            both = product(operands, pair, step, columns)
            former, latter = both[:rows], both[rows:]
            out_near[turn, :, columns] = jnp.where(is_first, latter, former).astype(jnp.bfloat16)
            own[turn, :, columns] = jnp.where(is_first, former, latter)

        over_tiles(sum_ref.shape[1], one)
        near.append(send(turn, 2, out_near.at[turn], in_near.at[turn]))

    def join(turn):
        near[turn].wait_recv()
        return own[turn] + in_near[turn].astype(jnp.float32)

    begin(0)
    begin(1)
    out_far[0] = join(0).astype(jnp.bfloat16)
    far[4] = send(4, 1, out_far.at[0, upper], in_half.at[0])
    far[5] = send(5, 0, out_far.at[0, lower], in_half.at[1])
    begin(2)
    own[1] = join(1)
    out_far[1, upper] = own[1, upper].astype(jnp.bfloat16)
    far[6] = send(6, 1, out_far.at[1, upper], in_full.at[0, upper])
    begin(3)
    own[2] = join(2)
    out_far[2, lower] = own[2, lower].astype(jnp.bfloat16)
    far[7] = send(7, 0, out_far.at[2, lower], in_full.at[1, lower])
    sum_ref[...] = join(3)
    far[5].wait_recv()
    out_far[1, lower] = (own[1, lower] + in_half[1].astype(jnp.float32)).astype(jnp.bfloat16)
    far[8] = send(8, 1, out_far.at[1, lower], in_full.at[0, lower])
    far[4].wait_recv()
    out_far[2, upper] = (own[2, upper] + in_half[0].astype(jnp.float32)).astype(jnp.bfloat16)
    far[9] = send(9, 0, out_far.at[2, upper], in_full.at[1, upper])
    if work:
        work[0](*extra, *results)
    far[6].wait_recv()
    far[7].wait_recv()
    far[8].wait_recv()
    far[9].wait_recv()
    sum_ref[...] = (
        sum_ref[...] + in_full[0].astype(jnp.float32) + in_full[1].astype(jnp.float32)
    )
    for copy in near + [far[number] for number in range(4, 10)]:
        copy.wait_send()


def over_tiles(width, one):
    tile = width // TEAM_SIZE

    def body(step, carry):
        one(step, pl.ds(pl.multiple_of(step * tile, tile), tile))
        return carry

    lax.fori_loop(0, TEAM_SIZE, body, 0)


def whole_block(ref, step, columns=slice(None)):
    block = ref[:, step, :, columns]
    return block.reshape(block.shape[0] * block.shape[1], block.shape[2])


def product_down(operands, pair, step, columns):
    hidden, weight = operands
    return jnp.dot(hidden[pair], weight[:, columns], preferred_element_type=jnp.float32)


def product_out(operands, pair, step, columns):
    gated, weight = operands
    depth = gated.shape[2]
    share = pl.ds(weight.shape[3] - depth, depth)
    return jnp.dot(
        gated[pair], whole_block(weight, step, share), preferred_element_type=jnp.float32
    )


def product_ffn_back(operands, pair, step, columns):
    grad_inner, grad_up, inner_weight, up_weight = operands
    return dot_t(grad_inner[pair], whole_block(inner_weight, step)) + dot_t(
        grad_up[pair], whole_block(up_weight, step)
    )


def product_qkv_back(operands, pair, step, columns):
    grad_products, weight, gate_weight = operands
    depth = grad_products.shape[2] - LANES
    share = pl.ds(0, depth)
    return dot_t(grad_products[pair, :, share], whole_block(weight, step, share)) + dot_t(
        grad_products[pair, :, pl.ds(depth, LANES)], gate_weight[columns, :]
    )


def scatter_team(
    product, lefts, rights, collective_id, work=None, operands=(), results=()
):
    rows = lefts[0].shape[0] // TEAM_SIZE
    depth = sum(left.shape[1] for left in lefts)
    width = MODEL_WIDTH
    paired = [left.reshape(TEAM_SIZE // 2, 2 * rows, left.shape[1]) for left in lefts]
    vmem = pl.BlockSpec(memory_space=pltpu.VMEM)
    anywhere = pl.BlockSpec(memory_space=pl.ANY)
    count = len(lefts) + len(rights)
    summed = pl.pallas_call(
        functools.partial(
            scatter_kernel, product, count, (work, len(operands), len(results)) if work else None
        ),
        out_shape=[jax.ShapeDtypeStruct((rows, width), jnp.float32)] + list(results),
        in_specs=[vmem] * count + [anywhere] * len(operands),
        out_specs=[vmem] + [anywhere] * len(results),
        scratch_shapes=[
            pltpu.VMEM((4, rows, width), jnp.float32),
            pltpu.VMEM((4, rows, width), jnp.bfloat16),
            pltpu.VMEM((4, rows, width), jnp.bfloat16),
            pltpu.VMEM((3, rows, width), jnp.bfloat16),
            pltpu.VMEM((2, rows // 2, width), jnp.bfloat16),
            pltpu.VMEM((2, rows, width), jnp.bfloat16),
            pltpu.SemaphoreType.DMA((10,)),
            pltpu.SemaphoreType.DMA((10,)),
        ],
        compiler_params=pltpu.CompilerParams(
            collective_id=collective_id, has_side_effects=True, vmem_limit_bytes=VMEM_BYTES
        ),
        cost_estimate=pl.CostEstimate(
            flops=2 * TEAM_SIZE * rows * depth * width,
            bytes_accessed=SCATTER_COST * rows * width,
            transcendentals=0,
        ),
    )(*paired, *rights, *operands)
    return summed if work else summed[0]


def ffn_kernel(rows_ref, inner_ref, up_ref, hidden_ref, slope_ref, swish_ref, inner_weight, up_weight):
    @pl.when(pl.program_id(0) == 0)
    def _():
        block = inner_ref.shape[0] * inner_ref.shape[2]
        for step in range(TEAM_SIZE):
            inner_weight[pl.ds(step * block, block), :] = whole_block(inner_ref, step)
            up_weight[pl.ds(step * block, block), :] = whole_block(up_ref, step)

    tile = 256

    def one(step, carry):
        columns = pl.ds(pl.multiple_of(step * tile, tile), tile)
        inner = jnp.dot(rows_ref[0], inner_weight[:, columns], preferred_element_type=jnp.float32)
        up_part = jnp.dot(rows_ref[0], up_weight[:, columns], preferred_element_type=jnp.float32)
        sigma = jax.nn.sigmoid(inner)
        swish = inner * sigma
        hidden_ref[0, :, columns] = (swish * up_part).astype(jnp.bfloat16)
        slope_ref[0, :, columns] = up_part * sigma * (1.0 + inner * (1.0 - sigma))
        swish_ref[0, :, columns] = swish
        return carry

    lax.fori_loop(0, hidden_ref.shape[2] // tile, one, 0)


def ffn_forward(normed_rows, inner_weight, up_weight):
    count, length, depth = normed_rows.shape
    width = inner_weight.shape[3]
    whole = pl.BlockSpec(inner_weight.shape, lambda i: (0, 0, 0, 0), pipeline_mode=pl.Buffered(1))
    out = pl.BlockSpec((1, length, width), lambda i: (i, 0, 0))
    return pl.pallas_call(
        ffn_kernel,
        grid=(count,),
        out_shape=[
            jax.ShapeDtypeStruct((count, length, width), jnp.bfloat16),
            jax.ShapeDtypeStruct((count, length, width), jnp.float32),
            jax.ShapeDtypeStruct((count, length, width), jnp.float32),
        ],
        in_specs=[pl.BlockSpec((1, length, depth), lambda i: (i, 0, 0)), whole, whole],
        out_specs=[out, out, out],
        scratch_shapes=[pltpu.VMEM((depth, width), jnp.bfloat16)] * 2,
        compiler_params=pltpu.CompilerParams(vmem_limit_bytes=VMEM_BYTES),
        cost_estimate=pl.CostEstimate(
            flops=4 * count * length * depth * width,
            bytes_accessed=count * length * (2 * depth + 10 * width),
            transcendentals=count * length * width,
        ),
    )(normed_rows, inner_weight, up_weight)


def ffn_back_kernel(grad_ref, weight_ref, slope_ref, swish_ref, inner_ref, up_ref):
    tile = 256

    def one(step, carry):
        columns = pl.ds(pl.multiple_of(step * tile, tile), tile)
        grad_hidden = dot_t(grad_ref[0], weight_ref[columns, :])
        inner_ref[0, :, columns] = (grad_hidden * slope_ref[0, :, columns]).astype(jnp.bfloat16)
        up_ref[0, :, columns] = (grad_hidden * swish_ref[0, :, columns]).astype(jnp.bfloat16)
        return carry

    lax.fori_loop(0, inner_ref.shape[2] // tile, one, 0)


def ffn_back(grad_rows, down_weight, slope, swish):
    count, length, depth = grad_rows.shape
    width = down_weight.shape[0]
    whole = pl.BlockSpec(down_weight.shape, lambda i: (0, 0), pipeline_mode=pl.Buffered(1))
    part = pl.BlockSpec((1, length, width), lambda i: (i, 0, 0))
    return pl.pallas_call(
        ffn_back_kernel,
        grid=(count,),
        out_shape=[jax.ShapeDtypeStruct((count, length, width), jnp.bfloat16)] * 2,
        in_specs=[pl.BlockSpec((1, length, depth), lambda i: (i, 0, 0)), whole, part, part],
        out_specs=[part, part],
        compiler_params=pltpu.CompilerParams(vmem_limit_bytes=VMEM_BYTES),
        cost_estimate=pl.CostEstimate(
            flops=2 * count * length * depth * width,
            bytes_accessed=count * length * (2 * depth + 12 * width),
            transcendentals=0,
        ),
    )(grad_rows, down_weight, slope, swish)


def weight_kernel(left_ref, right_ref, part_ref):
    depth, _, rows, width = part_ref.shape
    part = dot_tokens(left_ref[...], right_ref[...])
    part_ref[...] = part.astype(jnp.bfloat16).reshape(depth, 1, rows, width)


def weight_shape(left, right, rows):
    depth = left.shape[1] // (TEAM_SIZE * rows)
    return jax.ShapeDtypeStruct((depth, TEAM_SIZE, rows, right.shape[1]), jnp.bfloat16)


def weight_specs(left, right, part):
    depth, _, rows, width = part.shape
    return dict(
        grid=(TEAM_SIZE,),
        in_specs=[
            pl.BlockSpec((left.shape[0], depth * rows), lambda i: (0, i)),
            pl.BlockSpec(right.shape, lambda i: (0, 0)),
        ],
        out_specs=[pl.BlockSpec((depth, 1, rows, width), lambda i: (0, i, 0, 0))],
    )


def weight_parts(left, right, rows):
    part = weight_shape(left, right, rows)
    (tokens, height), width = left.shape, right.shape[1]
    return pl.pallas_call(
        weight_kernel,
        out_shape=[part],
        compiler_params=pltpu.CompilerParams(vmem_limit_bytes=VMEM_BYTES),
        cost_estimate=pl.CostEstimate(
            flops=2 * tokens * height * width,
            bytes_accessed=2 * tokens * (height + width) + 2 * height * width,
            transcendentals=0,
        ),
        **weight_specs(left, right, part),
    )(left, right)[0]


def weight_work(left_ref, right_ref, part_ref):
    pltpu.emit_pipeline(weight_kernel, **weight_specs(left_ref, right_ref, part_ref))(
        left_ref, right_ref, part_ref
    )


def attention_weight_kernel(normed_ref, products_ref, gated_ref, grad_ref, part_ref, gate_ref):
    depth, _, rows, _ = part_ref.shape
    own = products_ref.shape[1] - LANES
    part = dot_tokens(normed_ref[...], products_ref[...])
    gate_ref[...] = part[:, own:]
    part_ref[:, :, :, pl.ds(0, own)] = (
        part[:, :own].astype(jnp.bfloat16).reshape(depth, 1, rows, own)
    )
    share = grad_ref.shape[1]
    part = dot_tokens(gated_ref[...], grad_ref[...])
    part_ref[:, :, :, pl.ds(own, share)] = part.astype(jnp.bfloat16).reshape(depth, 1, rows, share)


def attention_weight_work(*refs):
    normed, products, gated, grad, part, gate = refs
    depth, _, rows, width = part.shape
    share = depth * rows
    column = pl.BlockSpec((normed.shape[0], share), lambda i: (0, i))
    pltpu.emit_pipeline(
        attention_weight_kernel,
        grid=(TEAM_SIZE,),
        in_specs=[
            column,
            pl.BlockSpec(products.shape, lambda i: (0, 0)),
            pl.BlockSpec(gated.shape, lambda i: (0, 0)),
            column,
        ],
        out_specs=[
            pl.BlockSpec((depth, 1, rows, width), lambda i: (0, i, 0, 0)),
            pl.BlockSpec((share, LANES), lambda i: (i, 0)),
        ],
    )(*refs)


def attention_weight_shapes(normed, grad_products, rows):
    height, width = normed.shape[1], grad_products.shape[1]
    share = height // TEAM_SIZE
    return [
        jax.ShapeDtypeStruct((share // rows, TEAM_SIZE, rows, width - LANES + share), jnp.bfloat16),
        jax.ShapeDtypeStruct((height, LANES), jnp.float32),
    ]


def greet_all():
    place = team_place()
    barrier = pltpu.get_barrier_semaphore()
    flips = [(step // 4, step // 2 % 2, step % 2) for step in range(1, TEAM_SIZE)]
    team = [
        (
            member(place, flip),
            {axis: 1 - at if turn else at for axis, at, turn in zip(TEAM, place, flip)},
        )
        for flip in flips
    ]
    sizes = [lax.axis_size(axis) for axis in DEPTH]
    depth = sizes[0] * sizes[1]
    spot = lax.axis_index(DEPTH[0]) * sizes[1] + lax.axis_index(DEPTH[1])
    line = []
    for step in range(1, depth):
        other = lax.rem(spot + step, depth)
        line.append({DEPTH[0]: other // sizes[1], DEPTH[1]: lax.rem(other, sizes[1])})
    for target in [device for _, device in team] + line:
        pl.semaphore_signal(
            barrier, inc=1, device_id=target, device_id_type=pl.DeviceIdType.MESH
        )
    pl.semaphore_wait(barrier, len(team) + len(line))
    return member(place, (0, 0, 0)), team, spot, line


def push(source, target, sems, number, device):
    copy = pltpu.make_async_remote_copy(
        src_ref=source,
        dst_ref=target,
        send_sem=sems.at[0, number],
        recv_sem=sems.at[1, number],
        device_id=device,
        device_id_type=pl.DeviceIdType.MESH,
    )
    copy.start()
    return copy


def begin_line(own, slots, sems, spot, line):
    slots[spot] = own[...]
    return [
        push(own, slots.at[spot], sems, number, device) for number, device in enumerate(line)
    ]


def begin_team(copies, slots, team_slots, sems, me, team):
    for copy in copies:
        copy.wait_recv()
    total = slots[0]
    for step in range(1, slots.shape[0]):
        total = total + slots[step]
    team_slots[me] = total
    return [
        push(team_slots.at[me], team_slots.at[me], sems, number, device)
        for number, (_, device) in enumerate(team)
    ]


def begin_blocks(parts, landed, columns, sems, first, me, team):
    landed[me] = parts[me, :, columns]
    return [
        push(parts.at[index, :, columns], landed.at[me], sems, first + number, device)
        for number, (index, device) in enumerate(team)
    ]


def depth_size():
    return lax.axis_size(DEPTH[0]) * lax.axis_size(DEPTH[1])


def lane_squares(piece):
    total = jnp.sum(piece * piece, axis=0, keepdims=True)
    lanes = total[:, :LANES]
    for first in range(LANES, total.shape[1], LANES):
        lanes = lanes + total[:, first : first + LANES]
    return lanes


def in_lanes(values, shape):
    lane = lax.broadcasted_iota(jnp.int32, shape, 1)
    row = jnp.zeros(shape, jnp.float32)
    for number, value in enumerate(values):
        row = jnp.where(lane == number, jnp.sum(value, axis=1, keepdims=True), row)
    return row


def update_columns(columns, gradient, state, results, update_ref):
    weight = state[0][:, columns]
    moment, second, update = moments(
        weight, state[1][:, columns], state[2][:, columns], gradient.astype(jnp.float32)
    )
    results[0][:, columns] = moment
    results[1][:, columns] = second
    update_ref[:, columns] = update
    return lane_squares(weight), lane_squares(update)


def at_columns(first, width):
    return pl.ds(pl.multiple_of(first, width if width < LANES else LANES), width)


def ffn_lamb_kernel(
    inner_ref, up_ref, down_ref, *refs
):
    state, down_state = refs[0:3], refs[3:6]
    results, update, down_results, down_update, squares_ref = (
        refs[6:8], refs[8], refs[9:11], refs[11], refs[12]
    )
    inner_in, up_in, inner_sems, up_sems = refs[13:]
    me, team, _, _ = greet_all()
    width = inner_ref.shape[2]
    every = pl.ds(0, width)
    copies = begin_blocks(inner_ref, inner_in, every, inner_sems, 0, me, team)
    more = begin_blocks(up_ref, up_in, every, up_sems, 0, me, team)
    zero = jnp.zeros((1, LANES), jnp.float32)
    share = down_ref.shape[1] // TEAM_SIZE

    def down(step, sums):
        columns = at_columns(step * share, share)
        found = update_columns(
            columns, down_ref[:, columns], down_state, down_results, down_update
        )
        return tuple(old + new for old, new in zip(sums, found))

    down_sums = lax.fori_loop(0, TEAM_SIZE, down, (zero, zero))
    for copy in copies:
        copy.wait_recv()

    def inner(step, sums):
        columns = at_columns(step * width, width)
        found = update_columns(columns, inner_in[step], state, results, update)
        return tuple(old + new for old, new in zip(sums, found))

    inner_sums = lax.fori_loop(0, TEAM_SIZE, inner, (zero, zero))
    for copy in more:
        copy.wait_recv()

    def up(step, sums):
        columns = at_columns((TEAM_SIZE + step) * width, width)
        found = update_columns(columns, up_in[step], state, results, update)
        return tuple(old + new for old, new in zip(sums, found))

    up_sums = lax.fori_loop(0, TEAM_SIZE, up, (zero, zero))
    squares_ref[...] = jnp.zeros_like(squares_ref)
    squares_ref[0:1] = in_lanes(
        [inner_sums[0], up_sums[0], down_sums[0], inner_sums[1], up_sums[1], down_sums[1]],
        (1, LANES),
    )
    for copy in copies + more:
        copy.wait_send()


def ffn_lamb(inner_sum, up_sum, down_sum, state, down_state, collective_id):
    vmem = pl.BlockSpec(memory_space=pltpu.VMEM)
    like = [jax.ShapeDtypeStruct(state[0].shape, jnp.float32)] * 3
    like_down = [jax.ShapeDtypeStruct(down_state[0].shape, jnp.float32)] * 3
    return pl.pallas_call(
        ffn_lamb_kernel,
        out_shape=like + like_down + [jax.ShapeDtypeStruct((SUBLANES, LANES), jnp.float32)],
        in_specs=[vmem] * 9,
        out_specs=[vmem] * 7,
        scratch_shapes=[
            pltpu.VMEM(inner_sum.shape, jnp.bfloat16),
            pltpu.VMEM(up_sum.shape, jnp.bfloat16),
            pltpu.SemaphoreType.DMA((2, TEAM_SIZE - 1)),
            pltpu.SemaphoreType.DMA((2, TEAM_SIZE - 1)),
        ],
        compiler_params=pltpu.CompilerParams(
            collective_id=collective_id, has_side_effects=True, vmem_limit_bytes=VMEM_BYTES
        ),
        cost_estimate=pl.CostEstimate(
            flops=0, bytes_accessed=LAMB_COST * state[0].size, transcendentals=0
        ),
    )(inner_sum, up_sum, down_sum, *state, *down_state)


def small_update(state, gradient, results, by_row):
    weight = state[0][...]
    moment, second, update = moments(weight, state[1][...], state[2][...], gradient)
    ratio = jnp.sum(weight * weight, axis=1, keepdims=True)
    size = jnp.sum(update * update, axis=1, keepdims=True)
    if not by_row:
        ratio = jnp.sum(ratio, axis=0, keepdims=True)
        size = jnp.sum(size, axis=0, keepdims=True)
    results[0][...] = weight - RATE * (jnp.sqrt(ratio) / jnp.sqrt(size)) * update
    results[1][...] = moment
    results[2][...] = second


def lamb_kernel(*refs):
    (
        attention_ref, gate_ref, first_ref, second_ref, qk_ref, squares_ref,
        ffn_ref, ffn_step_ref, down_ref, down_step_ref,
    ) = refs[:10]
    state, out_state, gate_state, gains_state, qk_state = (
        refs[10:13], refs[13:16], refs[16:19], refs[19:22], refs[22:25]
    )
    (
        new, copy_out, out_new, out_copy, ffn_new, ffn_copy, down_new, down_copy, norms_ref,
    ) = (refs[25], refs[28], refs[29], refs[32], refs[33], refs[34], refs[35], refs[36], refs[37])
    results, out_results = refs[26:28], refs[30:32]
    gate_results, gains_results, qk_results = refs[38:41], refs[41:44], refs[44:47]
    (
        landed, step, out_step, ffn, ffn_step, down, down_step,
        own, line_slots, team_slots, tile, tile_line, tile_team,
        load_sems, block_sems, line_sems, team_sems, tile_line_sems, tile_team_sems,
    ) = refs[47:]
    loads = [
        pltpu.make_async_copy(source, target, load_sems.at[number])
        for number, (source, target) in enumerate(
            ((ffn_ref, ffn), (ffn_step_ref, ffn_step), (down_ref, down), (down_step_ref, down_step))
        )
    ]
    for load in loads:
        load.start()
    me, team, spot, line = greet_all()
    heads = gate_ref.shape[0]
    share = landed.shape[2]
    blocks = begin_blocks(attention_ref, landed, pl.ds(0, share), block_sems, 0, me, team)
    own[...] = jnp.zeros_like(own)
    own[0:heads] = gate_ref[...]
    own[heads : heads + 1] = first_ref[...]
    own[heads + 1 : heads + 2] = second_ref[...]
    for row in range(2):
        own[heads + 2 : heads + 3, pl.ds(row * HEAD_WIDTH, HEAD_WIDTH)] = qk_ref[row : row + 1]
    along = begin_line(own, line_slots, line_sems, spot, line)
    zero = jnp.zeros((1, LANES), jnp.float32)
    out_width = out_state[0].shape[1] // TEAM_SIZE
    query_width = share - 2 * HEAD_WIDTH

    def out(turn, sums):
        columns = at_columns(turn * out_width, out_width)
        found = update_columns(
            columns, attention_ref[turn, :, pl.ds(share, out_width)], out_state, out_results,
            out_step,
        )
        return tuple(old + now for old, now in zip(sums, found))

    out_sums = lax.fori_loop(0, TEAM_SIZE, out, (zero, zero))
    across = begin_team(along, line_slots, team_slots, team_sems, me, team)
    for copy in blocks:
        copy.wait_recv()

    def projection(turn, sums):
        found = ()
        for first, start, width in (
            (turn * query_width, 0, query_width),
            (TEAM_SIZE * query_width + turn * HEAD_WIDTH, query_width, HEAD_WIDTH),
            (
                TEAM_SIZE * (query_width + HEAD_WIDTH) + turn * HEAD_WIDTH,
                query_width + HEAD_WIDTH,
                HEAD_WIDTH,
            ),
        ):
            found = found + update_columns(
                at_columns(first, width), landed[turn, :, pl.ds(start, width)], state, results,
                step,
            )
        return tuple(old + now for old, now in zip(sums, found))

    sums = lax.fori_loop(0, TEAM_SIZE, projection, (zero,) * 6)
    known = squares_ref[0:1]
    tile[...] = jnp.zeros_like(tile)
    tile[0:1] = in_lanes(
        [sums[0], sums[2], sums[4], out_sums[0]]
        + [known[:, number : number + 1] for number in range(3)]
        + [sums[1], sums[3], sums[5], out_sums[1]]
        + [known[:, number : number + 1] for number in range(3, 6)],
        (1, LANES),
    )
    tile_along = begin_line(tile, tile_line, tile_line_sems, spot, line)
    tile_across = begin_team(tile_along, tile_line, tile_team, tile_team_sems, me, team)
    for copy in across:
        copy.wait_recv()
    total = team_slots[0, heads:]
    for turn in range(1, TEAM_SIZE):
        total = total + team_slots[turn, heads:]
    gate_total = jnp.concatenate([team_slots[turn, :heads] for turn in range(TEAM_SIZE)], axis=0)
    small_update(gate_state, gate_total, gate_results, False)
    small_update(gains_state, total[:2], gains_results, True)
    qk_total = jnp.concatenate(
        [total[2:3, :HEAD_WIDTH], total[2:3, HEAD_WIDTH : 2 * HEAD_WIDTH]], axis=0
    )
    small_update(qk_state, qk_total, qk_results, True)
    for copy in tile_across:
        copy.wait_recv()
    total = tile_team[0, 0:1]
    for turn in range(1, TEAM_SIZE):
        total = total + tile_team[turn, 0:1]
    norms = jnp.sqrt(total)
    groups = 7
    weight_norms = [norms[:, number : number + 1] for number in range(groups)]
    update_norms = [norms[:, groups + number : groups + number + 1] for number in range(groups)]
    rates = [RATE * (former / latter) for former, latter in zip(weight_norms, update_norms)]
    norms_ref[...] = jnp.zeros_like(norms_ref)
    norms_ref[0:1] = in_lanes(weight_norms, (1, LANES))
    norms_ref[1:2] = in_lanes(update_norms, (1, LANES))

    def apply(weight, update, target, low_target, first, width, turns, rate):
        def one(turn, carry):
            columns = at_columns(first + turn * width, width)
            value = weight[:, columns] - rate * update[:, columns]
            target[:, columns] = value
            low_target[:, columns] = value.astype(jnp.bfloat16)
            return carry

        lax.fori_loop(0, turns, one, 0)

    lower = 0
    for number, width in enumerate((query_width, HEAD_WIDTH, HEAD_WIDTH)):
        apply(state[0], step, new, copy_out, lower, width, TEAM_SIZE, rates[number])
        lower = lower + TEAM_SIZE * width
    apply(out_state[0], out_step, out_new, out_copy, 0, out_width, TEAM_SIZE, rates[3])
    for load in loads:
        load.wait()
    width = ffn.shape[1] // (2 * TEAM_SIZE)
    apply(ffn, ffn_step, ffn_new, ffn_copy, 0, width, TEAM_SIZE, rates[4])
    apply(ffn, ffn_step, ffn_new, ffn_copy, TEAM_SIZE * width, width, TEAM_SIZE, rates[5])
    width = down.shape[1] // TEAM_SIZE
    apply(down, down_step, down_new, down_copy, 0, width, TEAM_SIZE, rates[6])
    for copy in blocks + along + across + tile_along + tile_across:
        copy.wait_send()


def lamb(
    attention_sum, gate_part, gains, qk_gains, squares, ffn, down, state, out_state, gate_state,
    gains_state, qk_state, collective_id,
):
    vmem = pl.BlockSpec(memory_space=pltpu.VMEM)
    anywhere = pl.BlockSpec(memory_space=pl.ANY)

    def shape(array, kind=jnp.float32):
        return jax.ShapeDtypeStruct(array.shape, kind)

    def four(array):
        return [shape(array)] * 3 + [shape(array, jnp.bfloat16)]

    def two(array):
        return [shape(array), shape(array, jnp.bfloat16)]

    team, rows, _ = attention_sum.shape
    share = state[0].shape[1] // TEAM_SIZE
    depth = depth_size()
    width = gate_part.shape[1]
    out_shape = (
        four(state[0]) + four(out_state[0]) + two(ffn[0]) + two(down[0])
        + [jax.ShapeDtypeStruct((SUBLANES, LANES), jnp.float32)]
        + [shape(gate_state[0])] * 3 + [shape(gains_state[0])] * 3 + [shape(qk_state[0])] * 3
    )
    return pl.pallas_call(
        lamb_kernel,
        out_shape=out_shape,
        in_specs=[vmem] * 6 + [anywhere] * 4 + [vmem] * 15,
        out_specs=[vmem] * len(out_shape),
        scratch_shapes=[
            pltpu.VMEM((team, rows, share), jnp.bfloat16),
            pltpu.VMEM(state[0].shape, jnp.float32),
            pltpu.VMEM(out_state[0].shape, jnp.float32),
            pltpu.VMEM(ffn[0].shape, jnp.float32),
            pltpu.VMEM(ffn[0].shape, jnp.float32),
            pltpu.VMEM(down[0].shape, jnp.float32),
            pltpu.VMEM(down[0].shape, jnp.float32),
            pltpu.VMEM((SUBLANES, width), jnp.float32),
            pltpu.VMEM((depth, SUBLANES, width), jnp.float32),
            pltpu.VMEM((TEAM_SIZE, SUBLANES, width), jnp.float32),
            pltpu.VMEM((SUBLANES, LANES), jnp.float32),
            pltpu.VMEM((depth, SUBLANES, LANES), jnp.float32),
            pltpu.VMEM((TEAM_SIZE, SUBLANES, LANES), jnp.float32),
            pltpu.SemaphoreType.DMA((4,)),
            pltpu.SemaphoreType.DMA((2, TEAM_SIZE - 1)),
            pltpu.SemaphoreType.DMA((2, max(depth - 1, 1))),
            pltpu.SemaphoreType.DMA((2, TEAM_SIZE - 1)),
            pltpu.SemaphoreType.DMA((2, max(depth - 1, 1))),
            pltpu.SemaphoreType.DMA((2, TEAM_SIZE - 1)),
        ],
        compiler_params=pltpu.CompilerParams(
            collective_id=collective_id, has_side_effects=True, vmem_limit_bytes=VMEM_BYTES
        ),
        cost_estimate=pl.CostEstimate(
            flops=0, bytes_accessed=LAMB_COST * ffn[0].size, transcendentals=0
        ),
    )(
        attention_sum, gate_part, gains[0][None], gains[1][None], qk_gains, squares,
        *ffn, *down, *state, *out_state, *gate_state, *gains_state, *qk_state,
    )


def team_exchange(blocks):
    return lax.all_to_all(blocks, TEAM, split_axis=0, concat_axis=0, tiled=True)


def turn_half(value_rows):
    return pltpu.roll(value_rows, value_rows.shape[-1] // 2, value_rows.ndim - 1)


def norm_turn(value_rows, gain, cosine, sine):
    scaled = rms_apply(value_rows, gain)
    return scaled * cosine + turn_half(scaled) * sine


def norm_turn_back(value_rows, gain, cosine, sine, gradient):
    turned = gradient * cosine + turn_half(gradient * sine)
    return rms_back(value_rows, gain, turned)


def greet_line():
    index, count = lax.axis_index("seq"), lax.axis_size("seq")
    barrier = pltpu.get_barrier_semaphore()

    @pl.when(index > 0)
    def _():
        pl.semaphore_signal(
            barrier, inc=1, device_id={"seq": index - 1}, device_id_type=pl.DeviceIdType.MESH
        )

    @pl.when(index < count - 1)
    def _():
        pl.semaphore_signal(
            barrier, inc=1, device_id={"seq": index + 1}, device_id_type=pl.DeviceIdType.MESH
        )

    inside = (index > 0) & (index < count - 1)

    @pl.when(inside)
    def _():
        pl.semaphore_wait(barrier, 2)

    @pl.when(jnp.logical_not(inside))
    def _():
        pl.semaphore_wait(barrier, 1)

    return index, count


def attend_kernel(
    window, scale, rows_ref, weight_ref, gate_ref, gains_ref, cosine_ref, sine_ref, start_ref,
    raw_ref, query_ref, pair_ref, stats_ref, across_ref, attended_ref, gated_ref,
    weight, pairs, send_sem, recv_sem,
):
    count_rows, length, _ = rows_ref.shape
    query_cols = query_ref.shape[2]
    heads = query_cols // HEAD_WIDTH
    keys_at = pl.ds(0, HEAD_WIDTH)
    values_at = pl.ds(HEAD_WIDTH, HEAD_WIDTH)
    index, count = greet_line()

    def hop(turn, row):
        return pltpu.make_async_remote_copy(
            src_ref=pairs.at[window - turn + 1, row],
            dst_ref=pairs.at[window - turn, row],
            send_sem=send_sem.at[turn - 1, row],
            recv_sem=recv_sem.at[turn - 1, row],
            device_id={"seq": lax.rem(index + 1, count)},
            device_id_type=pl.DeviceIdType.MESH,
        )

    block = weight_ref.shape[0] * weight_ref.shape[2]
    own = raw_ref.shape[2]
    for step in range(TEAM_SIZE):
        weight[pl.ds(step * block, block), pl.ds(0, own)] = whole_block(
            weight_ref, step, pl.ds(0, own)
        )
    weight[:, pl.ds(own, LANES)] = gate_ref[...]

    def project(row, carry):
        products = jnp.dot(rows_ref[row], weight[...], preferred_element_type=jnp.float32)
        raw = products[:, : query_cols + 2 * HEAD_WIDTH].astype(jnp.bfloat16)
        raw_ref[row] = raw
        cosine, sine = cosine_ref[row], sine_ref[row]
        key = norm_turn(
            raw[:, query_cols : query_cols + HEAD_WIDTH].astype(jnp.float32),
            gains_ref[1:2], cosine, sine,
        )
        pairs[window, row, :, keys_at] = key.astype(jnp.bfloat16)
        pairs[window, row, :, values_at] = raw[:, query_cols + HEAD_WIDTH :]

        @pl.when(index < count - 1)
        def _():
            hop(1, row).start()

        for head in range(heads):
            columns = slice(head * HEAD_WIDTH, (head + 1) * HEAD_WIDTH)
            query_ref[row, :, columns] = norm_turn(
                raw[:, columns].astype(jnp.float32), gains_ref[0:1], cosine, sine
            ).astype(jnp.bfloat16)
        stats_ref[row] = jax.nn.sigmoid(products[:, query_cols + 2 * HEAD_WIDTH :])
        return carry

    lax.fori_loop(0, count_rows, project, 0)

    @pl.when(index == 0)
    def _():
        for slot in range(window):
            pairs[slot] = jnp.zeros_like(pairs[slot])

    for turn in range(2, window + 1):

        def forward(row, carry):
            @pl.when(index > 0)
            def _():
                hop(turn - 1, row).wait_recv()

            @pl.when(index < count - 1)
            def _():
                hop(turn, row).start()

            return carry

        lax.fori_loop(0, count_rows, forward, 0)

    places = lax.broadcasted_iota(jnp.int32, (length, (window + 1) * length), 1)
    latest = window * length + lax.broadcasted_iota(jnp.int32, places.shape, 0)
    lane = lax.broadcasted_iota(jnp.int32, (length, LANES), 1)

    def attend(row, carry):
        @pl.when(index > 0)
        def _():
            hop(window, row).wait_recv()

        allowed = (places >= start_ref[row]) & (places <= latest)
        keys = pairs[:, row, :, keys_at].reshape(-1, HEAD_WIDTH)
        values = pairs[:, row, :, values_at].reshape(-1, HEAD_WIDTH)
        stats = stats_ref[row]
        for head in range(heads):
            columns = slice(head * HEAD_WIDTH, (head + 1) * HEAD_WIDTH)
            scores = dot_t(query_ref[row, :, columns], keys) * scale
            scores = jnp.where(allowed, scores, NEGATIVE)
            top = jnp.max(scores, axis=1, keepdims=True)
            powers = jnp.exp(scores - top)
            total = jnp.sum(powers, axis=1, keepdims=True)
            low_probs = (powers * (1.0 / total)).astype(jnp.bfloat16)
            output = jnp.dot(low_probs, values, preferred_element_type=jnp.float32)
            output = output.astype(jnp.bfloat16)
            attended_ref[row, :, columns] = output
            gated_ref[row, :, columns] = (
                output.astype(jnp.float32) * stats[:, head : head + 1]
            ).astype(jnp.bfloat16)
            stats = jnp.where(lane == heads + head, top + jnp.log(total), stats)
        stats_ref[row] = stats
        across_ref[row] = stats.T[:SUBLANES]
        pair_ref[:, row] = pairs[:, row]
        return carry

    lax.fori_loop(0, count_rows, attend, 0)

    @pl.when(index < count - 1)
    def _():
        for turn in range(1, window + 1):

            def finish(row, carry):
                hop(turn, row).wait_send()
                return carry

            lax.fori_loop(0, count_rows, finish, 0)


def attend(
    normed_rows, own_attention, own_gate, gains, cosine, sine, starts, query_cols, window, collective_id
):
    rows, length, _ = normed_rows.shape
    width = query_cols + 2 * HEAD_WIDTH + LANES
    bf16 = jnp.bfloat16
    vmem = pl.BlockSpec(memory_space=pltpu.VMEM)
    return pl.pallas_call(
        functools.partial(attend_kernel, window, HEAD_WIDTH ** (-0.5)),
        out_shape=[
            jax.ShapeDtypeStruct((rows, length, query_cols + 2 * HEAD_WIDTH), bf16),
            jax.ShapeDtypeStruct((rows, length, query_cols), bf16),
            jax.ShapeDtypeStruct((window + 1, rows, length, 2 * HEAD_WIDTH), bf16),
            jax.ShapeDtypeStruct((rows, length, LANES), jnp.float32),
            jax.ShapeDtypeStruct((rows, SUBLANES, length), jnp.float32),
            jax.ShapeDtypeStruct((rows, length, query_cols), bf16),
            jax.ShapeDtypeStruct((rows, length, query_cols), bf16),
        ],
        in_specs=[vmem] * 7,
        out_specs=[vmem] * 7,
        scratch_shapes=[
            pltpu.VMEM((MODEL_WIDTH, width), bf16),
            pltpu.VMEM((window + 1, rows, length, 2 * HEAD_WIDTH), bf16),
            pltpu.SemaphoreType.DMA((window, rows)),
            pltpu.SemaphoreType.DMA((window, rows)),
        ],
        compiler_params=pltpu.CompilerParams(
            collective_id=collective_id, has_side_effects=True, vmem_limit_bytes=VMEM_BYTES
        ),
        cost_estimate=pl.CostEstimate(
            flops=2 * rows * length * MODEL_WIDTH * width,
            bytes_accessed=ATTEND_COST * rows * length * MODEL_WIDTH,
            transcendentals=0,
        ),
    )(normed_rows, own_attention, own_gate, gains, cosine, sine, starts)


def attend_back_kernel(
    window, scale, rows_ref, weight_ref, gains_ref, cosine_ref, sine_ref, start_ref,
    raw_ref, query_ref, pair_ref, stats_ref, across_ref, attended_ref,
    products_ref, gain_ref,
    weight, parts, outs, ins, send_sem, recv_sem,
):
    count_rows, length, _ = rows_ref.shape
    query_cols = query_ref.shape[2]
    heads = query_cols // HEAD_WIDTH
    keys_at = pl.ds(0, HEAD_WIDTH)
    values_at = pl.ds(HEAD_WIDTH, HEAD_WIDTH)
    index, count = greet_line()
    lag = 2

    def hop(turn, row):
        return pltpu.make_async_remote_copy(
            src_ref=outs.at[turn - 1, row],
            dst_ref=ins.at[turn - 1, row],
            send_sem=send_sem.at[turn - 1, row],
            recv_sem=recv_sem.at[turn - 1, row],
            device_id={"seq": lax.rem(index + count - 1, count)},
            device_id_type=pl.DeviceIdType.MESH,
        )

    keys_total = (window + 1) * length
    places = lax.broadcasted_iota(jnp.int32, (keys_total, length), 0)
    latest = window * length + lax.broadcasted_iota(jnp.int32, places.shape, 1)
    lane = lax.broadcasted_iota(jnp.int32, (length, LANES), 1)
    gain_ref[...] = jnp.zeros_like(gain_ref)
    share = weight_ref.shape[3] - query_cols
    for step in range(TEAM_SIZE):
        weight[:, pl.ds(step * query_cols, query_cols)] = whole_block(
            weight_ref, step, pl.ds(share, query_cols)
        )

    @pl.when(index == count - 1)
    def _():
        ins[...] = jnp.zeros_like(ins)

    def compute(row):
        grad_gated = dot_t(rows_ref[row], weight[...])
        keys = pair_ref[:, row, :, keys_at].reshape(-1, HEAD_WIDTH)
        values = pair_ref[:, row, :, values_at].reshape(-1, HEAD_WIDTH)
        allowed = (places >= start_ref[row]) & (places <= latest)
        cosine, sine = cosine_ref[row], sine_ref[row]
        grad_pre = jnp.zeros((length, LANES), jnp.float32)
        grad_keys = jnp.zeros((keys_total, HEAD_WIDTH), jnp.float32)
        grad_values = jnp.zeros((keys_total, HEAD_WIDTH), jnp.float32)
        for head in range(heads):
            columns = slice(head * HEAD_WIDTH, (head + 1) * HEAD_WIDTH)
            gate = stats_ref[row, :, head : head + 1]
            own = grad_gated[:, columns]
            grad_out = (own * gate).astype(jnp.bfloat16)
            grad_gate = jnp.sum(
                own * attended_ref[row, :, columns].astype(jnp.float32), axis=1, keepdims=True
            )
            grad_pre = jnp.where(lane == head, grad_gate * gate * (1.0 - gate), grad_pre)
            query = query_ref[row, :, columns]
            scores = jnp.where(allowed, dot_t(keys, query) * scale, NEGATIVE)
            probs = jnp.exp(scores - across_ref[row, heads + head : heads + head + 1])
            grad_probs = dot_t(values, grad_out)
            inner = jnp.sum(probs * grad_probs, axis=0, keepdims=True)
            grad_scores = (probs * (grad_probs - inner)).astype(jnp.bfloat16)
            grad_values = grad_values + jnp.dot(
                probs.astype(jnp.bfloat16), grad_out, preferred_element_type=jnp.float32
            )
            grad_keys = grad_keys + jnp.dot(
                grad_scores, query, preferred_element_type=jnp.float32
            )
            grad_query = dot_tokens(grad_scores, keys) * scale
            grad_raw, gain = norm_turn_back(
                raw_ref[row, :, columns].astype(jnp.float32), gains_ref[0:1], cosine, sine,
                grad_query,
            )
            products_ref[row, :, columns] = grad_raw.astype(jnp.bfloat16)
            gain_ref[0:1] += jnp.sum(gain, axis=0, keepdims=True)
        products_ref[row, :, query_cols + 2 * HEAD_WIDTH :] = grad_pre.astype(jnp.bfloat16)
        parts[:, row, :, keys_at] = (grad_keys * scale).reshape(window + 1, length, HEAD_WIDTH)
        parts[:, row, :, values_at] = grad_values.reshape(window + 1, length, HEAD_WIDTH)

    def finish(row):
        grad_pair = parts[window, row] + ins[window - 1, row].astype(jnp.float32)
        grad_raw, gain = norm_turn_back(
            raw_ref[row, :, query_cols : query_cols + HEAD_WIDTH].astype(jnp.float32),
            gains_ref[1:2], cosine_ref[row], sine_ref[row], grad_pair[:, :HEAD_WIDTH],
        )
        products_ref[row, :, query_cols : query_cols + HEAD_WIDTH] = grad_raw.astype(jnp.bfloat16)
        products_ref[row, :, query_cols + HEAD_WIDTH : query_cols + 2 * HEAD_WIDTH] = grad_pair[
            :, HEAD_WIDTH:
        ].astype(jnp.bfloat16)
        gain_ref[1:2] += jnp.sum(gain, axis=0, keepdims=True)

    def step(turn_row, carry):
        @pl.when(turn_row < count_rows)
        def _():
            compute(turn_row)

        for turn in range(1, window + 2):
            row = turn_row - lag * (turn - 1)

            @pl.when((row >= 0) & (row < count_rows))
            def _():
                if turn > 1:

                    @pl.when(index < count - 1)
                    def _():
                        hop(turn - 1, row).wait_recv()

                if turn == window + 1:
                    finish(row)
                else:
                    part = parts[turn - 1, row]
                    if turn > 1:
                        part = part + ins[turn - 2, row].astype(jnp.float32)
                    outs[turn - 1, row] = part.astype(jnp.bfloat16)

                    @pl.when(index > 0)
                    def _():
                        hop(turn, row).start()

        return carry

    lax.fori_loop(0, count_rows + lag * window, step, 0)

    @pl.when(index > 0)
    def _():
        for turn in range(1, window + 1):

            def done(row, carry):
                hop(turn, row).wait_send()
                return carry

            lax.fori_loop(0, count_rows, done, 0)


def attend_back(
    grad_rows, own_attention, gains, cosine, sine, starts, saved, window, collective_id
):
    rows, length, _ = grad_rows.shape
    query_cols = saved[1].shape[2]
    width = query_cols + 2 * HEAD_WIDTH + LANES
    bf16 = jnp.bfloat16
    vmem = pl.BlockSpec(memory_space=pltpu.VMEM)
    return pl.pallas_call(
        functools.partial(attend_back_kernel, window, HEAD_WIDTH ** (-0.5)),
        out_shape=[
            jax.ShapeDtypeStruct((rows, length, width), bf16),
            jax.ShapeDtypeStruct((SUBLANES, HEAD_WIDTH), jnp.float32),
        ],
        in_specs=[vmem] * 12,
        out_specs=[vmem] * 2,
        scratch_shapes=[
            pltpu.VMEM((query_cols, MODEL_WIDTH), bf16),
            pltpu.VMEM((window + 1, rows, length, 2 * HEAD_WIDTH), jnp.float32),
            pltpu.VMEM((window, rows, length, 2 * HEAD_WIDTH), bf16),
            pltpu.VMEM((window, rows, length, 2 * HEAD_WIDTH), bf16),
            pltpu.SemaphoreType.DMA((window, rows)),
            pltpu.SemaphoreType.DMA((window, rows)),
        ],
        compiler_params=pltpu.CompilerParams(
            collective_id=collective_id, has_side_effects=True, vmem_limit_bytes=VMEM_BYTES
        ),
        cost_estimate=pl.CostEstimate(
            flops=2 * rows * length * MODEL_WIDTH * query_cols,
            bytes_accessed=ATTEND_COST * rows * length * MODEL_WIDTH,
            transcendentals=0,
        ),
    )(grad_rows, own_attention, gains, cosine, sine, starts, *saved)


def team_columns(matrix, widths):
    pieces = []
    lower = 0
    for width in widths:
        piece = matrix[:, lower : lower + width]
        pieces.append(piece.reshape(matrix.shape[0], TEAM_SIZE, width // TEAM_SIZE))
        lower = lower + width
    return jnp.concatenate(pieces, axis=2).transpose(1, 0, 2)


def gather_parts(blocks):
    return lax.all_gather(blocks, DEPTH, axis=0, tiled=False)


def scatter_parts(parts):
    depth, team, rows, width = parts.shape
    return lax.psum_scatter(
        parts.reshape(depth * team * rows, width), DEPTH, scatter_dimension=0, tiled=True
    ).reshape(team, rows, width)


def gather_rows(matrix):
    return lax.all_gather(matrix, DEPTH, axis=0, tiled=True)


def scatter_rows(gradient):
    return lax.psum_scatter(gradient, DEPTH, scatter_dimension=0, tiled=True)


def shards(
    inputs,
    cotangent,
    doc_lengths,
    projection_weight,
    projection_moment,
    projection_second,
    out_weight,
    out_moment,
    out_second,
    ffn_weight,
    ffn_moment,
    ffn_second,
    down_weight,
    down_moment,
    down_second,
    head_gate,
    gate_moment,
    gate_second,
    norm_gains,
    gains_moment,
    gains_second,
    qk_gains,
    qk_moment,
    qk_second,
):
    rows_dev, local_len, width = inputs.shape
    bf16 = jnp.bfloat16
    team = lax.axis_index(TEAM)
    place_seq = lax.axis_index("seq")
    group_heads = QUERY_HEADS // KEY_VALUE_HEADS
    window = -(-(DOC_MOST - 1) // local_len)
    window = min(window, lax.axis_size("seq") - 1)
    query_cols = QUERY_HEADS * HEAD_WIDTH
    key_value_columns = KEY_VALUE_HEADS * HEAD_WIDTH
    widths_qkv = (query_cols, key_value_columns, key_value_columns)
    widths_ffn = (FF, FF)
    own_query = query_cols // TEAM_SIZE
    own_key = key_value_columns // TEAM_SIZE
    own_ff = FF // TEAM_SIZE
    own_gate = lax.dynamic_slice_in_dim(head_gate.astype(bf16), team * group_heads, group_heads, 1)
    own_gate = jnp.pad(own_gate, ((0, 0), (0, LANES - group_heads)))
    own_attention = gather_parts(
        jnp.concatenate(
            [
                team_exchange(team_columns(projection_weight.astype(bf16), widths_qkv)),
                team_columns(out_weight.astype(bf16), (MODEL_WIDTH,)),
            ],
            axis=2,
        )
    )
    ffn_blocks = team_exchange(team_columns(ffn_weight.astype(bf16), widths_ffn))
    own_inner = gather_parts(ffn_blocks[:, :, :own_ff])
    lengths = lax.all_gather(doc_lengths, TEAM, axis=0, tiled=True)
    place = place_seq * local_len + jnp.arange(local_len, dtype=jnp.int32)
    position = positions(lengths, place)
    cosine, sine = rotary_tables(position, HEAD_WIDTH)
    starts = window * local_len + jnp.arange(local_len, dtype=jnp.int32)[None, :] - position
    inputs_flat = inputs[0].astype(jnp.float32)
    normed = rms_apply(inputs_flat, norm_gains[0]).astype(bf16)
    normed_all, grad_all = gather_team([normed, cotangent[0]], 0)
    raw, query_rot, pairs, stats, across, attended, gated = attend(
        normed_all.reshape(TEAM_SIZE, local_len, MODEL_WIDTH),
        own_attention,
        own_gate,
        qk_gains,
        cosine,
        sine,
        starts[:, :, None],
        own_query,
        window,
        8,
    )
    gated, up_blocks, low_down = lax.optimization_barrier(
        (gated, ffn_blocks[:, :, own_ff:], down_weight.astype(bf16))
    )
    own_up = gather_parts(up_blocks)
    own_down = gather_rows(low_down)
    middle = inputs_flat + scatter_team(product_out, [gated.reshape(-1, own_query)], [own_attention], 1)
    normed2 = rms_apply(middle, norm_gains[1]).astype(bf16)
    normed2_all = gather_team([normed2], 2)[0]
    hidden, slope, swish = ffn_forward(
        normed2_all.reshape(TEAM_SIZE, local_len, MODEL_WIDTH), own_inner, own_up
    )
    grad_final = cotangent[0].astype(jnp.float32)
    down_part, own_down = lax.optimization_barrier(
        (low_tokens(hidden.reshape(-1, own_ff), grad_all), own_down)
    )
    grad_inner, grad_up = ffn_back(
        grad_all.reshape(TEAM_SIZE, local_len, MODEL_WIDTH), own_down, slope, swish
    )
    grad_inner, grad_up = grad_inner.reshape(-1, own_ff), grad_up.reshape(-1, own_ff)
    inner_part, grad_inner = lax.optimization_barrier(
        (weight_parts(normed2_all, grad_inner, ffn_weight.shape[0]), grad_inner)
    )
    down_sum = scatter_rows(down_part)
    grad_normed2 = scatter_team(
        product_ffn_back, [grad_inner, grad_up], [own_inner, own_up], 4
    )
    grad_mid_part, gain_mid = rms_back(middle, norm_gains[1], grad_normed2)
    grad_middle = grad_final + grad_mid_part
    grad_low, down_sum = lax.optimization_barrier((grad_middle.astype(bf16), down_sum))
    inner_sum = scatter_parts(inner_part)
    grad_middle_all, up_part = gather_team(
        [grad_low],
        5,
        weight_work,
        (normed2_all, grad_up),
        (weight_shape(normed2_all, grad_up, ffn_weight.shape[0]),),
    )
    grad_products, gain_sums = attend_back(
        grad_middle_all.reshape(TEAM_SIZE, local_len, MODEL_WIDTH),
        own_attention,
        qk_gains,
        cosine,
        sine,
        starts[:, None, :],
        (raw, query_rot, pairs, stats, across, attended),
        window,
        9,
    )
    grad_products = grad_products.reshape(-1, grad_products.shape[2])
    up_part, grad_products, inner_sum = lax.optimization_barrier(
        (up_part, grad_products, inner_sum)
    )
    up_sum = scatter_parts(up_part)
    grad_normed, attention_part, gate_part = scatter_team(
        product_qkv_back,
        [grad_products],
        [own_attention, own_gate],
        6,
        attention_weight_work,
        (normed_all, grad_products, gated.reshape(-1, own_query), grad_middle_all),
        attention_weight_shapes(normed_all, grad_products, out_weight.shape[0]),
    )
    late_hidden, grad_normed = lax.optimization_barrier((hidden, grad_normed))
    attention_sum = scatter_parts(attention_part)
    final = middle + scatter_team(product_down, [late_hidden.reshape(-1, own_ff)], [own_down], 3)
    result = final.astype(bf16).reshape(inputs.shape)
    grad_in_part, gain_in = rms_back(inputs_flat, norm_gains[0], grad_normed)
    input_grad = (grad_middle + grad_in_part).reshape(inputs.shape)
    ffn_moment_new, ffn_second_new, ffn_update, down_moment_new, down_second_new, down_update, squares = (
        ffn_lamb(
            inner_sum,
            up_sum,
            down_sum,
            (ffn_weight, ffn_moment, ffn_second),
            (down_weight, down_moment, down_second),
            7,
        )
    )
    (
        projection_weight_next,
        projection_moment_next,
        projection_second_next,
        qkv_copy,
        out_new,
        out_moment_new,
        out_second_new,
        out_copy,
        ffn_new,
        ffn_copy,
        down_new,
        down_copy,
        norms,
        head_gate_new,
        gate_moment_new,
        gate_second_new,
        gains_new,
        gains_moment_new,
        gains_second_new,
        qk_new,
        qk_moment_new,
        qk_second_new,
    ) = lamb(
        attention_sum,
        gate_part[:, :group_heads].T,
        (jnp.sum(gain_in, axis=0), jnp.sum(gain_mid, axis=0)),
        gain_sums,
        squares,
        (ffn_weight, ffn_update),
        (down_weight, down_update),
        (projection_weight, projection_moment, projection_second),
        (out_weight, out_moment, out_second),
        (head_gate.T, gate_moment.T, gate_second.T),
        (norm_gains, gains_moment, gains_second),
        (qk_gains, qk_moment, qk_second),
        10,
    )
    return (
        result,
        input_grad,
        projection_weight_next,
        projection_moment_next,
        projection_second_next,
        qkv_copy,
        out_new,
        out_moment_new,
        out_second_new,
        out_copy,
        ffn_new,
        ffn_moment_new,
        ffn_second_new,
        ffn_copy,
        down_new,
        down_moment_new,
        down_second_new,
        down_copy,
        head_gate_new.T,
        gate_moment_new.T,
        gate_second_new.T,
        gains_new,
        gains_moment_new,
        gains_second_new,
        qk_new,
        qk_moment_new,
        qk_second_new,
        norms[:2, :7],
    )


def solution(mesh):
    mesh = Mesh(
        mesh.devices.reshape(2, 2, 2, mesh.shape["fsdp"] // TEAM_SIZE, mesh.shape["seq"]),
        TEAM + DEPTH,
    )
    rows = TEAM + DEPTH[:1]
    in_specs = (
        P(rows, "seq", None),
        P(rows, "seq", None),
        P(rows, None),
        P(TEAM + DEPTH, None),
        P(TEAM + DEPTH, None),
        P(TEAM + DEPTH, None),
        P(TEAM + DEPTH, None),
        P(TEAM + DEPTH, None),
        P(TEAM + DEPTH, None),
        P(TEAM + DEPTH, None),
        P(TEAM + DEPTH, None),
        P(TEAM + DEPTH, None),
        P(TEAM + DEPTH, None),
        P(TEAM + DEPTH, None),
        P(TEAM + DEPTH, None),
        P(),
        P(),
        P(),
        P(),
        P(),
        P(),
        P(),
        P(),
        P(),
    )
    out_specs = (
        P(rows, "seq", None),
        P(rows, "seq", None),
        P(TEAM + DEPTH, None),
        P(TEAM + DEPTH, None),
        P(TEAM + DEPTH, None),
        P(TEAM + DEPTH, None),
        P(TEAM + DEPTH, None),
        P(TEAM + DEPTH, None),
        P(TEAM + DEPTH, None),
        P(TEAM + DEPTH, None),
        P(TEAM + DEPTH, None),
        P(TEAM + DEPTH, None),
        P(TEAM + DEPTH, None),
        P(TEAM + DEPTH, None),
        P(TEAM + DEPTH, None),
        P(TEAM + DEPTH, None),
        P(TEAM + DEPTH, None),
        P(TEAM + DEPTH, None),
        P(),
        P(),
        P(),
        P(),
        P(),
        P(),
        P(),
        P(),
        P(),
        P(),
    )
    return jax.shard_map(shards, mesh=mesh, in_specs=in_specs, out_specs=out_specs, check_vma=False)
```

```python
import functools

import jax
import jax.numpy as jnp
from jax import lax
from jax.experimental import pallas as pl
from jax.experimental.pallas import tpu as pltpu
from jax.sharding import Mesh
from jax.sharding import PartitionSpec as P

MODEL_WIDTH = 2048
QUERY_HEADS = 16
KEY_VALUE_HEADS = 8
HEAD_WIDTH = 128
FF = 6144
ROW_TOKENS = 1024
STEP = 3
DOC_MOST = 512
TEAM_SIZE = 8
TEAM = ("t2", "t1", "t0")
DEPTH = ("spare", "seq")
LANES = 128
SUBLANES = 8
VMEM_BYTES = 48 << 20
GATHER_VMEM = 32 << 20
LAMB_COST = 70
GATHER_COST = 250
SCATTER_COST = 320
ATTEND_COST = 50


NORM_EPS = 1e-06
ADAM_EPS = 1e-06
RATE = 0.3
DECAY = 0.01
BETA = 0.5
THETA = 1000000.0
NEGATIVE = -1e30


def rms_apply(value_rows, gain):
    return (
        value_rows
        * lax.rsqrt(jnp.mean(value_rows * value_rows, axis=-1, keepdims=True) + NORM_EPS)
        * gain
    )


def rms_back(value_rows, gain, gradient):
    scale = lax.rsqrt(jnp.mean(value_rows * value_rows, axis=-1, keepdims=True) + NORM_EPS)
    scaled = gradient * gain
    inner = jnp.mean(scaled * value_rows, axis=-1, keepdims=True)
    grad_value = scale * scaled - value_rows * scale * scale * scale * inner
    grad_gain = gradient * value_rows * scale
    return (grad_value, grad_gain)


def dot_t(left, right):
    return lax.dot_general(
        left, right, (((1,), (1,)), ((), ())), preferred_element_type=jnp.float32
    )


def low_tokens(left, right):
    return dot_tokens(left, right).astype(jnp.bfloat16)


def dot_tokens(left, right):
    return lax.dot_general(
        left, right, (((0,), (0,)), ((), ())), preferred_element_type=jnp.float32
    )


def moments(weight, moment, second, gradient):
    moment_new = BETA * moment + (1.0 - BETA) * gradient
    second_new = BETA * second + (1.0 - BETA) * gradient * gradient
    correction = 1.0 - BETA**STEP
    update = (
        moment_new / correction / (jnp.sqrt(second_new / correction) + ADAM_EPS) + DECAY * weight
    )
    return (moment_new, second_new, update)


def rotary_tables(position, width):
    half = width // 2
    rates = THETA ** (-jnp.arange(half, dtype=jnp.float32) * 2.0 / width)
    angle = position.astype(jnp.float32)[..., None] * rates
    cosine, sine = jnp.cos(angle), jnp.sin(angle)
    return (
        jnp.concatenate([cosine, cosine], axis=-1),
        jnp.concatenate([-sine, sine], axis=-1),
    )


def positions(lengths, place):
    ends = jnp.cumsum(lengths, axis=1)
    starts = ends - lengths
    inside = (place[None, :, None] >= starts[:, None, :]) & (place[None, :, None] < ends[:, None, :])
    return place[None, :] - jnp.sum(jnp.where(inside, starts[:, None, :], 0), axis=2)


def team_place():
    return tuple(lax.axis_index(axis) for axis in TEAM)


def greet_team(place):
    barrier = pltpu.get_barrier_semaphore()
    for axis, index in zip(TEAM, place):
        pl.semaphore_signal(
            barrier, inc=1, device_id={axis: 1 - index}, device_id_type=pl.DeviceIdType.MESH
        )
    pl.semaphore_wait(barrier, len(TEAM))


def member(place, flips):
    index = 0
    for own, flip in zip(place, flips):
        index = index * 2 + (1 - own if flip else own)
    return index


def gather_kernel(count, work, *refs):
    given, made = (work[1], work[2]) if work else (0, 0)
    owns, operands = refs[:count], refs[count : count + given]
    alls = refs[count + given : 2 * count + given]
    results = refs[2 * count + given : 2 * count + given + made]
    own_sem, send_sem, recv_sem = refs[2 * count + given + made :]
    place = team_place()
    greet_team(place)
    me = member(place, (0, 0, 0))
    beside = member(place, (0, 1, 0))
    above = member(place, (1, 0, 0))
    across = member(place, (1, 1, 0))
    copies = [{} for _ in range(count)]
    keeps = []

    def send(item, number, axis, source, target):
        copy = pltpu.make_async_remote_copy(
            src_ref=source,
            dst_ref=target,
            send_sem=send_sem.at[item, number],
            recv_sem=recv_sem.at[item, number],
            device_id={TEAM[axis]: 1 - place[axis]},
            device_id_type=pl.DeviceIdType.MESH,
        )
        copy.start()
        copies[item][number] = copy

    def halves(item):
        half = owns[item].shape[0] // 2
        return pl.ds(0, half), pl.ds(half, half)

    for item in range(count):
        target = alls[item].at[me]
        send(item, 0, 1, owns[item], target)
        send(item, 1, 0, owns[item], target)
        send(item, 2, 2, owns[item], target)
        keeps.append(pltpu.make_async_copy(owns[item], target, own_sem.at[item]))
        keeps[item].start()
    if work:
        work[0](*operands, *results)
    for item in range(count):
        upper, lower = halves(item)
        copies[item][0].wait_recv()
        block = alls[item].at[beside]
        send(item, 3, 0, block.at[upper], block.at[upper])
        send(item, 4, 2, block, block)
        copies[item][1].wait_recv()
        block = alls[item].at[above]
        send(item, 5, 1, block.at[lower], block.at[lower])
        send(item, 6, 2, block, block)
    for item in range(count):
        upper, lower = halves(item)
        block = alls[item].at[across]
        copies[item][3].wait_recv()
        send(item, 7, 2, block.at[upper], block.at[upper])
        copies[item][5].wait_recv()
        send(item, 8, 2, block.at[lower], block.at[lower])
    for item in range(count):
        for number in (2, 4, 6, 7, 8):
            copies[item][number].wait_recv()
        for number in range(9):
            copies[item][number].wait_send()
        keeps[item].wait()


def gather_team(arrays, collective_id, work=None, operands=(), results=()):
    count = len(arrays)
    anywhere = pl.BlockSpec(memory_space=pl.ANY)
    out_shape = [jax.ShapeDtypeStruct((TEAM_SIZE,) + own.shape, own.dtype) for own in arrays]
    gathered = pl.pallas_call(
        functools.partial(
            gather_kernel, count, (work, len(operands), len(results)) if work else None
        ),
        out_shape=out_shape + list(results),
        in_specs=[anywhere] * (count + len(operands)),
        out_specs=[anywhere] * (count + len(results)),
        scratch_shapes=[
            pltpu.SemaphoreType.DMA((count,)),
            pltpu.SemaphoreType.DMA((count, 9)),
            pltpu.SemaphoreType.DMA((count, 9)),
        ],
        compiler_params=pltpu.CompilerParams(
            collective_id=collective_id, has_side_effects=True, vmem_limit_bytes=GATHER_VMEM
        ),
        cost_estimate=pl.CostEstimate(
            flops=0,
            bytes_accessed=sum(GATHER_COST * own.shape[0] * own.shape[1] for own in arrays),
            transcendentals=0,
        ),
    )(*arrays, *operands)
    return [
        whole.reshape(TEAM_SIZE * own.shape[0], own.shape[1])
        for whole, own in zip(gathered, arrays)
    ] + list(gathered[count:])


def scatter_kernel(product, count, work, *refs):
    given, made = (work[1], work[2]) if work else (0, 0)
    operands, extra = refs[:count], refs[count : count + given]
    sum_ref = refs[count + given]
    results = refs[count + given + 1 : count + given + 1 + made]
    own, out_near, in_near, out_far, in_half, in_full, send_sem, recv_sem = refs[
        count + given + 1 + made :
    ]
    place = team_place()
    greet_team(place)
    rows = sum_ref.shape[0]
    half = rows // 2
    upper, lower = pl.ds(0, half), pl.ds(half, half)

    def send(number, axis, source, target):
        copy = pltpu.make_async_remote_copy(
            src_ref=source,
            dst_ref=target,
            send_sem=send_sem.at[number],
            recv_sem=recv_sem.at[number],
            device_id={TEAM[axis]: 1 - place[axis]},
            device_id_type=pl.DeviceIdType.MESH,
        )
        copy.start()
        return copy

    flips = ((1, 1), (0, 1), (1, 0), (0, 0))
    near, far = [], {}
    is_first = place[2] == 0

    def begin(turn):
        first, second = flips[turn]
        pair = member(place[:2], (first, second))

        def one(step, columns):
            both = product(operands, pair, step, columns)
            former, latter = both[:rows], both[rows:]
            out_near[turn, :, columns] = jnp.where(is_first, latter, former).astype(jnp.bfloat16)
            own[turn, :, columns] = jnp.where(is_first, former, latter)

        over_tiles(sum_ref.shape[1], one)
        near.append(send(turn, 2, out_near.at[turn], in_near.at[turn]))

    def join(turn):
        near[turn].wait_recv()
        return own[turn] + in_near[turn].astype(jnp.float32)

    begin(0)
    begin(1)
    out_far[0] = join(0).astype(jnp.bfloat16)
    far[4] = send(4, 1, out_far.at[0, upper], in_half.at[0])
    far[5] = send(5, 0, out_far.at[0, lower], in_half.at[1])
    begin(2)
    own[1] = join(1)
    out_far[1, upper] = own[1, upper].astype(jnp.bfloat16)
    far[6] = send(6, 1, out_far.at[1, upper], in_full.at[0, upper])
    begin(3)
    own[2] = join(2)
    out_far[2, lower] = own[2, lower].astype(jnp.bfloat16)
    far[7] = send(7, 0, out_far.at[2, lower], in_full.at[1, lower])
    sum_ref[...] = join(3)
    far[5].wait_recv()
    out_far[1, lower] = (own[1, lower] + in_half[1].astype(jnp.float32)).astype(jnp.bfloat16)
    far[8] = send(8, 1, out_far.at[1, lower], in_full.at[0, lower])
    far[4].wait_recv()
    out_far[2, upper] = (own[2, upper] + in_half[0].astype(jnp.float32)).astype(jnp.bfloat16)
    far[9] = send(9, 0, out_far.at[2, upper], in_full.at[1, upper])
    if work:
        work[0](*extra, *results)
    far[6].wait_recv()
    far[7].wait_recv()
    far[8].wait_recv()
    far[9].wait_recv()
    sum_ref[...] = (
        sum_ref[...] + in_full[0].astype(jnp.float32) + in_full[1].astype(jnp.float32)
    )
    for copy in near + [far[number] for number in range(4, 10)]:
        copy.wait_send()


def over_tiles(width, one):
    tile = width // TEAM_SIZE

    def body(step, carry):
        one(step, pl.ds(pl.multiple_of(step * tile, tile), tile))
        return carry

    lax.fori_loop(0, TEAM_SIZE, body, 0)


def whole_block(ref, step, columns=slice(None)):
    block = ref[:, step, :, columns]
    return block.reshape(block.shape[0] * block.shape[1], block.shape[2])


def product_down(operands, pair, step, columns):
    hidden, weight = operands
    return jnp.dot(hidden[pair], weight[:, columns], preferred_element_type=jnp.float32)


def product_out(operands, pair, step, columns):
    gated, weight = operands
    depth = gated.shape[2]
    share = pl.ds(weight.shape[3] - depth, depth)
    return jnp.dot(
        gated[pair], whole_block(weight, step, share), preferred_element_type=jnp.float32
    )


def product_ffn_back(operands, pair, step, columns):
    grad_inner, grad_up, inner_weight, up_weight = operands
    return dot_t(grad_inner[pair], whole_block(inner_weight, step)) + dot_t(
        grad_up[pair], whole_block(up_weight, step)
    )


def product_qkv_back(operands, pair, step, columns):
    grad_products, weight, gate_weight = operands
    depth = grad_products.shape[2] - LANES
    share = pl.ds(0, depth)
    return dot_t(grad_products[pair, :, share], whole_block(weight, step, share)) + dot_t(
        grad_products[pair, :, pl.ds(depth, LANES)], gate_weight[columns, :]
    )


def scatter_team(
    product, lefts, rights, collective_id, work=None, operands=(), results=()
):
    rows = lefts[0].shape[0] // TEAM_SIZE
    depth = sum(left.shape[1] for left in lefts)
    width = MODEL_WIDTH
    paired = [left.reshape(TEAM_SIZE // 2, 2 * rows, left.shape[1]) for left in lefts]
    vmem = pl.BlockSpec(memory_space=pltpu.VMEM)
    anywhere = pl.BlockSpec(memory_space=pl.ANY)
    count = len(lefts) + len(rights)
    summed = pl.pallas_call(
        functools.partial(
            scatter_kernel, product, count, (work, len(operands), len(results)) if work else None
        ),
        out_shape=[jax.ShapeDtypeStruct((rows, width), jnp.float32)] + list(results),
        in_specs=[vmem] * count + [anywhere] * len(operands),
        out_specs=[vmem] + [anywhere] * len(results),
        scratch_shapes=[
            pltpu.VMEM((4, rows, width), jnp.float32),
            pltpu.VMEM((4, rows, width), jnp.bfloat16),
            pltpu.VMEM((4, rows, width), jnp.bfloat16),
            pltpu.VMEM((3, rows, width), jnp.bfloat16),
            pltpu.VMEM((2, rows // 2, width), jnp.bfloat16),
            pltpu.VMEM((2, rows, width), jnp.bfloat16),
            pltpu.SemaphoreType.DMA((10,)),
            pltpu.SemaphoreType.DMA((10,)),
        ],
        compiler_params=pltpu.CompilerParams(
            collective_id=collective_id, has_side_effects=True, vmem_limit_bytes=VMEM_BYTES
        ),
        cost_estimate=pl.CostEstimate(
            flops=2 * TEAM_SIZE * rows * depth * width,
            bytes_accessed=SCATTER_COST * rows * width,
            transcendentals=0,
        ),
    )(*paired, *rights, *operands)
    return summed if work else summed[0]


def ffn_kernel(rows_ref, inner_ref, up_ref, hidden_ref, slope_ref, swish_ref, inner_weight, up_weight):
    @pl.when(pl.program_id(0) == 0)
    def _():
        block = inner_ref.shape[0] * inner_ref.shape[2]
        for step in range(TEAM_SIZE):
            inner_weight[pl.ds(step * block, block), :] = whole_block(inner_ref, step)
            up_weight[pl.ds(step * block, block), :] = whole_block(up_ref, step)

    tile = 256

    def one(step, carry):
        columns = pl.ds(pl.multiple_of(step * tile, tile), tile)
        inner = jnp.dot(rows_ref[0], inner_weight[:, columns], preferred_element_type=jnp.float32)
        up_part = jnp.dot(rows_ref[0], up_weight[:, columns], preferred_element_type=jnp.float32)
        sigma = jax.nn.sigmoid(inner)
        swish = inner * sigma
        hidden_ref[0, :, columns] = (swish * up_part).astype(jnp.bfloat16)
        slope_ref[0, :, columns] = up_part * sigma * (1.0 + inner * (1.0 - sigma))
        swish_ref[0, :, columns] = swish
        return carry

    lax.fori_loop(0, hidden_ref.shape[2] // tile, one, 0, unroll=True)


def ffn_forward(normed_rows, inner_weight, up_weight):
    count, depth = TEAM_SIZE // 2, normed_rows.shape[1]
    length = normed_rows.shape[0] // count
    width = inner_weight.shape[3]
    whole = pl.BlockSpec(inner_weight.shape, lambda i: (0, 0, 0, 0), pipeline_mode=pl.Buffered(1))
    out = pl.BlockSpec((1, length, width), lambda i: (i, 0, 0))
    return pl.pallas_call(
        ffn_kernel,
        grid=(count,),
        out_shape=[
            jax.ShapeDtypeStruct((count, length, width), jnp.bfloat16),
            jax.ShapeDtypeStruct((count, length, width), jnp.float32),
            jax.ShapeDtypeStruct((count, length, width), jnp.float32),
        ],
        in_specs=[pl.BlockSpec((1, length, depth), lambda i: (i, 0, 0)), whole, whole],
        out_specs=[out, out, out],
        scratch_shapes=[pltpu.VMEM((depth, width), jnp.bfloat16)] * 2,
        compiler_params=pltpu.CompilerParams(vmem_limit_bytes=VMEM_BYTES),
        cost_estimate=pl.CostEstimate(
            flops=4 * count * length * depth * width,
            bytes_accessed=count * length * (2 * depth + 10 * width),
            transcendentals=count * length * width,
        ),
    )(normed_rows.reshape(count, length, depth), inner_weight, up_weight)


def ffn_back_kernel(grad_ref, weight_ref, slope_ref, swish_ref, inner_ref, up_ref):
    tile = 256

    def one(step, carry):
        columns = pl.ds(pl.multiple_of(step * tile, tile), tile)
        grad_hidden = dot_t(grad_ref[0], weight_ref[columns, :])
        inner_ref[0, :, columns] = (grad_hidden * slope_ref[0, :, columns]).astype(jnp.bfloat16)
        up_ref[0, :, columns] = (grad_hidden * swish_ref[0, :, columns]).astype(jnp.bfloat16)
        return carry

    lax.fori_loop(0, inner_ref.shape[2] // tile, one, 0, unroll=True)


def ffn_back(grad_rows, down_weight, slope, swish):
    count, length, width = slope.shape
    depth = grad_rows.shape[1]
    whole = pl.BlockSpec(down_weight.shape, lambda i: (0, 0), pipeline_mode=pl.Buffered(1))
    part = pl.BlockSpec((1, length, width), lambda i: (i, 0, 0))
    return pl.pallas_call(
        ffn_back_kernel,
        grid=(count,),
        out_shape=[jax.ShapeDtypeStruct((count, length, width), jnp.bfloat16)] * 2,
        in_specs=[pl.BlockSpec((1, length, depth), lambda i: (i, 0, 0)), whole, part, part],
        out_specs=[part, part],
        compiler_params=pltpu.CompilerParams(vmem_limit_bytes=VMEM_BYTES),
        cost_estimate=pl.CostEstimate(
            flops=2 * count * length * depth * width,
            bytes_accessed=count * length * (2 * depth + 12 * width),
            transcendentals=0,
        ),
    )(grad_rows.reshape(count, length, depth), down_weight, slope, swish)


def weight_kernel(left_ref, right_ref, part_ref):
    depth, _, rows, width = part_ref.shape
    part = dot_tokens(left_ref[...], right_ref[...])
    part_ref[...] = part.astype(jnp.bfloat16).reshape(depth, 1, rows, width)


def weight_shape(left, right, rows):
    depth = left.shape[1] // (TEAM_SIZE * rows)
    return jax.ShapeDtypeStruct((depth, TEAM_SIZE, rows, right.shape[1]), jnp.bfloat16)


def weight_specs(left, right, part):
    depth, _, rows, width = part.shape
    return dict(
        grid=(TEAM_SIZE,),
        in_specs=[
            pl.BlockSpec((left.shape[0], depth * rows), lambda i: (0, i)),
            pl.BlockSpec(right.shape, lambda i: (0, 0)),
        ],
        out_specs=[pl.BlockSpec((depth, 1, rows, width), lambda i: (0, i, 0, 0))],
    )


def weight_parts(left, right, rows):
    part = weight_shape(left, right, rows)
    (tokens, height), width = left.shape, right.shape[1]
    return pl.pallas_call(
        weight_kernel,
        out_shape=[part],
        compiler_params=pltpu.CompilerParams(vmem_limit_bytes=VMEM_BYTES),
        cost_estimate=pl.CostEstimate(
            flops=2 * tokens * height * width,
            bytes_accessed=2 * tokens * (height + width) + 2 * height * width,
            transcendentals=0,
        ),
        **weight_specs(left, right, part),
    )(left, right)[0]


def weight_work(left_ref, right_ref, part_ref):
    pltpu.emit_pipeline(weight_kernel, **weight_specs(left_ref, right_ref, part_ref))(
        left_ref, right_ref, part_ref
    )


def attention_weight_kernel(normed_ref, products_ref, gated_ref, grad_ref, part_ref, gate_ref):
    depth, _, rows, _ = part_ref.shape
    own = products_ref.shape[1] - LANES
    part = dot_tokens(normed_ref[...], products_ref[...])
    gate_ref[...] = part[:, own:]
    part_ref[:, :, :, pl.ds(0, own)] = (
        part[:, :own].astype(jnp.bfloat16).reshape(depth, 1, rows, own)
    )
    share = grad_ref.shape[1]
    part = dot_tokens(gated_ref[...], grad_ref[...])
    part_ref[:, :, :, pl.ds(own, share)] = part.astype(jnp.bfloat16).reshape(depth, 1, rows, share)


def attention_weight_work(*refs):
    normed, products, gated, grad, part, gate = refs
    depth, _, rows, width = part.shape
    share = depth * rows
    column = pl.BlockSpec((normed.shape[0], share), lambda i: (0, i))
    pltpu.emit_pipeline(
        attention_weight_kernel,
        grid=(TEAM_SIZE,),
        in_specs=[
            column,
            pl.BlockSpec(products.shape, lambda i: (0, 0)),
            pl.BlockSpec(gated.shape, lambda i: (0, 0)),
            column,
        ],
        out_specs=[
            pl.BlockSpec((depth, 1, rows, width), lambda i: (0, i, 0, 0)),
            pl.BlockSpec((share, LANES), lambda i: (i, 0)),
        ],
    )(*refs)


def attention_weight_shapes(normed, grad_products, rows):
    height, width = normed.shape[1], grad_products.shape[1]
    share = height // TEAM_SIZE
    return [
        jax.ShapeDtypeStruct((share // rows, TEAM_SIZE, rows, width - LANES + share), jnp.bfloat16),
        jax.ShapeDtypeStruct((height, LANES), jnp.float32),
    ]


def greet_all():
    place = team_place()
    barrier = pltpu.get_barrier_semaphore()
    flips = [(step // 4, step // 2 % 2, step % 2) for step in range(1, TEAM_SIZE)]
    team = [
        (
            member(place, flip),
            {axis: 1 - at if turn else at for axis, at, turn in zip(TEAM, place, flip)},
        )
        for flip in flips
    ]
    sizes = [lax.axis_size(axis) for axis in DEPTH]
    depth = sizes[0] * sizes[1]
    spot = lax.axis_index(DEPTH[0]) * sizes[1] + lax.axis_index(DEPTH[1])
    line = []
    for step in range(1, depth):
        other = lax.rem(spot + step, depth)
        line.append({DEPTH[0]: other // sizes[1], DEPTH[1]: lax.rem(other, sizes[1])})
    for target in [device for _, device in team] + line:
        pl.semaphore_signal(
            barrier, inc=1, device_id=target, device_id_type=pl.DeviceIdType.MESH
        )
    pl.semaphore_wait(barrier, len(team) + len(line))
    return member(place, (0, 0, 0)), team, spot, line


def push(source, target, sems, number, device):
    copy = pltpu.make_async_remote_copy(
        src_ref=source,
        dst_ref=target,
        send_sem=sems.at[0, number],
        recv_sem=sems.at[1, number],
        device_id=device,
        device_id_type=pl.DeviceIdType.MESH,
    )
    copy.start()
    return copy


def begin_line(own, slots, sems, spot, line):
    slots[spot] = own[...]
    return [
        push(own, slots.at[spot], sems, number, device) for number, device in enumerate(line)
    ]


def begin_team(copies, slots, team_slots, sems, me, team):
    for copy in copies:
        copy.wait_recv()
    total = slots[0]
    for step in range(1, slots.shape[0]):
        total = total + slots[step]
    team_slots[me] = total
    return [
        push(team_slots.at[me], team_slots.at[me], sems, number, device)
        for number, (_, device) in enumerate(team)
    ]


def depth_size():
    return lax.axis_size(DEPTH[0]) * lax.axis_size(DEPTH[1])


def lane_squares(piece):
    total = jnp.sum(piece * piece, axis=0, keepdims=True)
    lanes = total[:, :LANES]
    for first in range(LANES, total.shape[1], LANES):
        lanes = lanes + total[:, first : first + LANES]
    return lanes


def in_lanes(values, shape):
    lane = lax.broadcasted_iota(jnp.int32, shape, 1)
    row = jnp.zeros(shape, jnp.float32)
    for number, value in enumerate(values):
        row = jnp.where(lane == number, jnp.sum(value, axis=1, keepdims=True), row)
    return row


def update_columns(columns, gradient, state, results, update_ref):
    weight = state[0][:, columns]
    moment, second, update = moments(
        weight, state[1][:, columns], state[2][:, columns], gradient.astype(jnp.float32)
    )
    results[0][:, columns] = moment
    results[1][:, columns] = second
    update_ref[:, columns] = update
    return lane_squares(weight), lane_squares(update)


def at_columns(first, width):
    return pl.ds(pl.multiple_of(first, width if width < LANES else LANES), width)


STEPS = 16


def ffn_moments_kernel(rows_ref, down_ref, *refs):
    state, down_state = refs[0:3], refs[3:6]
    results, update, down_results, down_update, squares_ref = (
        refs[6:8], refs[8], refs[9:11], refs[11], refs[12]
    )
    step = pl.program_id(0)

    @pl.when(step == 0)
    def _():
        squares_ref[...] = jnp.zeros_like(squares_ref)

    every = slice(None)
    found = update_columns(every, rows_ref[0], state, results, update)
    group = step // (STEPS // 2)
    squares_ref[pl.ds(group, 1)] += found[0]
    squares_ref[pl.ds(4 + group, 1)] += found[1]
    found = update_columns(every, down_ref[...], down_state, down_results, down_update)
    squares_ref[2:3] += found[0]
    squares_ref[6:7] += found[1]


def ffn_moments(ffn_rows, down_sum, state, down_state):
    team, rows, width = ffn_rows.shape
    half = STEPS // 2

    def column(array):
        return pl.BlockSpec((array.shape[0], array.shape[1] // STEPS), lambda i: (0, i))

    like = [jax.ShapeDtypeStruct(state[0].shape, jnp.float32)] * 3
    like_down = [jax.ShapeDtypeStruct(down_state[0].shape, jnp.float32)] * 3
    return pl.pallas_call(
        ffn_moments_kernel,
        grid=(STEPS,),
        out_shape=like + like_down + [jax.ShapeDtypeStruct((SUBLANES, LANES), jnp.float32)],
        in_specs=[
            pl.BlockSpec((1, rows, width // 2), lambda i: (lax.rem(i, half), 0, i // half)),
            column(down_sum),
        ]
        + [column(array) for array in state + down_state],
        out_specs=[column(array) for array in state + down_state]
        + [pl.BlockSpec((SUBLANES, LANES), lambda i: (0, 0))],
        compiler_params=pltpu.CompilerParams(vmem_limit_bytes=GATHER_VMEM),
        cost_estimate=pl.CostEstimate(
            flops=20 * state[0].size, bytes_accessed=30 * state[0].size, transcendentals=0
        ),
    )(ffn_rows, down_sum, *state, *down_state)


def attention_moments_kernel(rows_ref, attention_ref, *refs):
    state, out_state = refs[0:3], refs[3:6]
    results, step_ref, out_results, out_step_ref, squares_ref = (
        refs[6:8], refs[8], refs[9:11], refs[11], refs[12]
    )
    share = rows_ref.shape[2]
    query_width = share - 2 * HEAD_WIDTH
    out_width = out_state[0].shape[1] // TEAM_SIZE
    zero = jnp.zeros((1, LANES), jnp.float32)

    def one(turn, sums):
        found = ()
        for first, start, width in (
            (turn * query_width, 0, query_width),
            (TEAM_SIZE * query_width + turn * HEAD_WIDTH, query_width, HEAD_WIDTH),
            (
                TEAM_SIZE * (query_width + HEAD_WIDTH) + turn * HEAD_WIDTH,
                query_width + HEAD_WIDTH,
                HEAD_WIDTH,
            ),
        ):
            found = found + update_columns(
                at_columns(first, width), rows_ref[turn, :, pl.ds(start, width)], state, results,
                step_ref,
            )
        found = found + update_columns(
            at_columns(turn * out_width, out_width),
            attention_ref[turn, :, pl.ds(share, out_width)], out_state, out_results, out_step_ref,
        )
        return tuple(old + new for old, new in zip(sums, found))

    sums = lax.fori_loop(0, TEAM_SIZE, one, (zero,) * 8)
    for group in range(4):
        squares_ref[group : group + 1] = sums[2 * group]
        squares_ref[4 + group : 5 + group] = sums[2 * group + 1]


def attention_moments(projection_rows, attention_sum, state, out_state):
    vmem = pl.BlockSpec(memory_space=pltpu.VMEM)
    like = [jax.ShapeDtypeStruct(state[0].shape, jnp.float32)] * 3
    like_out = [jax.ShapeDtypeStruct(out_state[0].shape, jnp.float32)] * 3
    return pl.pallas_call(
        attention_moments_kernel,
        out_shape=like + like_out + [jax.ShapeDtypeStruct((SUBLANES, LANES), jnp.float32)],
        in_specs=[vmem] * 8,
        out_specs=[vmem] * 7,
        compiler_params=pltpu.CompilerParams(vmem_limit_bytes=GATHER_VMEM),
        cost_estimate=pl.CostEstimate(
            flops=20 * state[0].size, bytes_accessed=30 * state[0].size, transcendentals=0
        ),
    )(projection_rows, attention_sum, *state, *out_state)


def totals_kernel(
    gate_ref, first_ref, second_ref, qk_ref, squares_ref, ffn_squares_ref,
    gate_out, gains_out, qk_out, norms_out,
    own, line_slots, team_slots, line_sems, team_sems,
):
    heads = gate_ref.shape[0]
    own[...] = jnp.zeros_like(own)
    own[0:heads] = gate_ref[...]
    own[heads : heads + 1] = first_ref[...]
    own[heads + 1 : heads + 2] = second_ref[...]
    for row in range(2):
        own[heads + 2 : heads + 3, pl.ds(row * HEAD_WIDTH, HEAD_WIDTH)] = qk_ref[row : row + 1]
    rows = [squares_ref[group : group + 1] for group in range(4)]
    rows += [ffn_squares_ref[group : group + 1] for group in range(3)]
    rows += [squares_ref[4 + group : 5 + group] for group in range(4)]
    rows += [ffn_squares_ref[4 + group : 5 + group] for group in range(3)]
    own[heads + 2 : heads + 3, pl.ds(2 * HEAD_WIDTH, LANES)] = in_lanes(rows, (1, LANES))
    me, team, spot, line = greet_all()
    along = begin_line(own, line_slots, line_sems, spot, line)
    across = begin_team(along, line_slots, team_slots, team_sems, me, team)
    for copy in across:
        copy.wait_recv()
    total = team_slots[0, heads:]
    for turn in range(1, TEAM_SIZE):
        total = total + team_slots[turn, heads:]
    gains_out[...] = total[:2]
    for row in range(2):
        qk_out[row : row + 1] = total[2:3, row * HEAD_WIDTH : (row + 1) * HEAD_WIDTH]
    for turn in range(TEAM_SIZE):
        gate_out[turn * heads : (turn + 1) * heads] = team_slots[turn, :heads]
    norms = jnp.sqrt(total[2:3, 2 * HEAD_WIDTH : 2 * HEAD_WIDTH + LANES])
    groups = 7
    weight_norms = [norms[:, number : number + 1] for number in range(groups)]
    update_norms = [norms[:, groups + number : groups + number + 1] for number in range(groups)]
    norms_out[...] = jnp.zeros_like(norms_out)
    norms_out[0:1] = in_lanes(weight_norms, (1, LANES))
    norms_out[1:2] = in_lanes(update_norms, (1, LANES))
    norms_out[2:3] = in_lanes(
        [former / latter for former, latter in zip(weight_norms, update_norms)], (1, LANES)
    )
    for copy in along + across:
        copy.wait_send()


def totals(gate_part, gains, qk_gains, squares, ffn_squares, collective_id):
    vmem = pl.BlockSpec(memory_space=pltpu.VMEM)
    heads, width = gate_part.shape
    depth = depth_size()
    return pl.pallas_call(
        totals_kernel,
        out_shape=[
            jax.ShapeDtypeStruct((TEAM_SIZE * heads, width), jnp.float32),
            jax.ShapeDtypeStruct((2, width), jnp.float32),
            jax.ShapeDtypeStruct((2, HEAD_WIDTH), jnp.float32),
            jax.ShapeDtypeStruct((SUBLANES, LANES), jnp.float32),
        ],
        in_specs=[vmem] * 6,
        out_specs=[vmem] * 4,
        scratch_shapes=[
            pltpu.VMEM((SUBLANES, width), jnp.float32),
            pltpu.VMEM((depth, SUBLANES, width), jnp.float32),
            pltpu.VMEM((TEAM_SIZE, SUBLANES, width), jnp.float32),
            pltpu.SemaphoreType.DMA((2, max(depth - 1, 1))),
            pltpu.SemaphoreType.DMA((2, TEAM_SIZE - 1)),
        ],
        compiler_params=pltpu.CompilerParams(collective_id=collective_id, has_side_effects=True),
    )(gate_part, gains[0][None], gains[1][None], qk_gains, squares, ffn_squares)


def small_update(state, gradient, results, by_row):
    weight = state[0][...]
    moment, second, update = moments(weight, state[1][...], state[2][...], gradient[...])
    ratio = jnp.sum(weight * weight, axis=1, keepdims=True)
    size = jnp.sum(update * update, axis=1, keepdims=True)
    if not by_row:
        ratio = jnp.sum(ratio, axis=0, keepdims=True)
        size = jnp.sum(size, axis=0, keepdims=True)
    results[0][...] = weight - RATE * (jnp.sqrt(ratio) / jnp.sqrt(size)) * update
    results[1][...] = moment
    results[2][...] = second


def apply_kernel(edges, norms_ref, gate_ref, gains_ref, qk_ref, *refs):
    pairs = [refs[2 * number : 2 * number + 2] for number in range(4)]
    states = [refs[8 + 3 * number : 11 + 3 * number] for number in range(3)]
    targets = [refs[17 + 2 * number : 19 + 2 * number] for number in range(4)]
    results = [refs[25 + 3 * number : 28 + 3 * number] for number in range(3)]
    norms_out = refs[34]
    step = pl.program_id(0)

    @pl.when(step == 0)
    def _():
        norms_out[...] = norms_ref[0:2]
        small_update(states[0], gate_ref, results[0], False)
        small_update(states[1], gains_ref, results[1], True)
        small_update(states[2], qk_ref, results[2], True)

    for (weight, update), (new, low_new), (first, uppers) in zip(pairs, targets, edges):
        rate = norms_ref[2:3, first : first + 1]
        for number, upper in enumerate(uppers):
            group = first + number + 1
            rate = jnp.where(step < upper, rate, norms_ref[2:3, group : group + 1])
        value = weight[...] - RATE * rate * update[...]
        new[...] = value
        low_new[...] = value.astype(jnp.bfloat16)


def apply_all(norms, gate_total, gains_total, qk_total, pairs, edges, states):
    def whole(array):
        return pl.BlockSpec(array.shape, lambda i: (0, 0))

    def column(array):
        return pl.BlockSpec((array.shape[0], array.shape[1] // STEPS), lambda i: (0, i))

    small = [array for state in states for array in state]
    operands = [norms, gate_total, gains_total, qk_total]
    targets = []
    for weight, _ in pairs:
        targets.append(jax.ShapeDtypeStruct(weight.shape, jnp.float32))
        targets.append(jax.ShapeDtypeStruct(weight.shape, jnp.bfloat16))
    results = [jax.ShapeDtypeStruct(array.shape, jnp.float32) for array in small]
    results.append(jax.ShapeDtypeStruct((2, norms.shape[1]), jnp.float32))
    return pl.pallas_call(
        functools.partial(apply_kernel, edges),
        grid=(STEPS,),
        out_shape=targets + results,
        in_specs=[whole(array) for array in operands]
        + [column(array) for pair in pairs for array in pair]
        + [whole(array) for array in small],
        out_specs=[column(array) for array in targets] + [whole(array) for array in results],
        compiler_params=pltpu.CompilerParams(vmem_limit_bytes=GATHER_VMEM),
        cost_estimate=pl.CostEstimate(
            flops=4 * pairs[2][0].size, bytes_accessed=30 * pairs[2][0].size, transcendentals=0
        ),
    )(*operands, *[array for pair in pairs for array in pair], *small)


def team_exchange(blocks):
    return lax.all_to_all(blocks, TEAM, split_axis=0, concat_axis=0, tiled=True)


def turn_half(value_rows):
    return pltpu.roll(value_rows, value_rows.shape[-1] // 2, value_rows.ndim - 1)


def norm_turn(value_rows, gain, cosine, sine):
    scaled = rms_apply(value_rows, gain)
    return scaled * cosine + turn_half(scaled) * sine


def norm_turn_back(value_rows, gain, cosine, sine, gradient):
    turned = gradient * cosine + turn_half(gradient * sine)
    return rms_back(value_rows, gain, turned)


def greet_line():
    index, count = lax.axis_index("seq"), lax.axis_size("seq")
    barrier = pltpu.get_barrier_semaphore()

    @pl.when(index > 0)
    def _():
        pl.semaphore_signal(
            barrier, inc=1, device_id={"seq": index - 1}, device_id_type=pl.DeviceIdType.MESH
        )

    @pl.when(index < count - 1)
    def _():
        pl.semaphore_signal(
            barrier, inc=1, device_id={"seq": index + 1}, device_id_type=pl.DeviceIdType.MESH
        )

    inside = (index > 0) & (index < count - 1)

    @pl.when(inside)
    def _():
        pl.semaphore_wait(barrier, 2)

    @pl.when(jnp.logical_not(inside))
    def _():
        pl.semaphore_wait(barrier, 1)

    return index, count


def attend_kernel(
    window, scale, rows_ref, weight_ref, gate_ref, gains_ref, cosine_ref, sine_ref, start_ref,
    raw_ref, query_ref, pair_ref, stats_ref, across_ref, attended_ref, gated_ref,
    weight, pairs, send_sem, recv_sem,
):
    count_rows, length, _ = rows_ref.shape
    query_cols = query_ref.shape[2]
    heads = query_cols // HEAD_WIDTH
    keys_at = pl.ds(0, HEAD_WIDTH)
    values_at = pl.ds(HEAD_WIDTH, HEAD_WIDTH)
    index, count = greet_line()

    def hop(turn, row):
        return pltpu.make_async_remote_copy(
            src_ref=pairs.at[window - turn + 1, row],
            dst_ref=pairs.at[window - turn, row],
            send_sem=send_sem.at[turn - 1, row],
            recv_sem=recv_sem.at[turn - 1, row],
            device_id={"seq": lax.rem(index + 1, count)},
            device_id_type=pl.DeviceIdType.MESH,
        )

    block = weight_ref.shape[0] * weight_ref.shape[2]
    own = raw_ref.shape[2]
    for step in range(TEAM_SIZE):
        weight[pl.ds(step * block, block), pl.ds(0, own)] = whole_block(
            weight_ref, step, pl.ds(0, own)
        )
    weight[:, pl.ds(own, LANES)] = gate_ref[...]

    def project(row, carry):
        products = jnp.dot(rows_ref[row], weight[...], preferred_element_type=jnp.float32)
        raw = products[:, : query_cols + 2 * HEAD_WIDTH].astype(jnp.bfloat16)
        raw_ref[row] = raw
        cosine, sine = cosine_ref[row], sine_ref[row]
        key = norm_turn(
            raw[:, query_cols : query_cols + HEAD_WIDTH].astype(jnp.float32),
            gains_ref[1:2], cosine, sine,
        )
        pairs[window, row, :, keys_at] = key.astype(jnp.bfloat16)
        pairs[window, row, :, values_at] = raw[:, query_cols + HEAD_WIDTH :]

        @pl.when(index < count - 1)
        def _():
            hop(1, row).start()

        for head in range(heads):
            columns = slice(head * HEAD_WIDTH, (head + 1) * HEAD_WIDTH)
            query_ref[row, :, columns] = norm_turn(
                raw[:, columns].astype(jnp.float32), gains_ref[0:1], cosine, sine
            ).astype(jnp.bfloat16)
        stats_ref[row] = jax.nn.sigmoid(products[:, query_cols + 2 * HEAD_WIDTH :])
        return carry

    lax.fori_loop(0, count_rows, project, 0)

    @pl.when(index == 0)
    def _():
        for slot in range(window):
            pairs[slot] = jnp.zeros_like(pairs[slot])

    for turn in range(2, window + 1):

        def forward(row, carry):
            @pl.when(index > 0)
            def _():
                hop(turn - 1, row).wait_recv()

            @pl.when(index < count - 1)
            def _():
                hop(turn, row).start()

            return carry

        lax.fori_loop(0, count_rows, forward, 0)

    places = lax.broadcasted_iota(jnp.int32, (length, (window + 1) * length), 1)
    latest = window * length + lax.broadcasted_iota(jnp.int32, places.shape, 0)
    lane = lax.broadcasted_iota(jnp.int32, (length, LANES), 1)

    def attend(row, carry):
        @pl.when(index > 0)
        def _():
            hop(window, row).wait_recv()

        allowed = (places >= start_ref[row]) & (places <= latest)
        keys = pairs[:, row, :, keys_at].reshape(-1, HEAD_WIDTH)
        values = pairs[:, row, :, values_at].reshape(-1, HEAD_WIDTH)
        stats = stats_ref[row]
        for head in range(heads):
            columns = slice(head * HEAD_WIDTH, (head + 1) * HEAD_WIDTH)
            scores = dot_t(query_ref[row, :, columns], keys) * scale
            scores = jnp.where(allowed, scores, NEGATIVE)
            top = jnp.max(scores, axis=1, keepdims=True)
            powers = jnp.exp(scores - top)
            total = jnp.sum(powers, axis=1, keepdims=True)
            low_probs = (powers * (1.0 / total)).astype(jnp.bfloat16)
            output = jnp.dot(low_probs, values, preferred_element_type=jnp.float32)
            output = output.astype(jnp.bfloat16)
            attended_ref[row, :, columns] = output
            gated_ref[row, :, columns] = (
                output.astype(jnp.float32) * stats[:, head : head + 1]
            ).astype(jnp.bfloat16)
            stats = jnp.where(lane == heads + head, top + jnp.log(total), stats)
        stats_ref[row] = stats
        across_ref[row] = stats.T[:SUBLANES]
        pair_ref[:, row] = pairs[:, row]
        return carry

    lax.fori_loop(0, count_rows, attend, 0)

    @pl.when(index < count - 1)
    def _():
        for turn in range(1, window + 1):

            def finish(row, carry):
                hop(turn, row).wait_send()
                return carry

            lax.fori_loop(0, count_rows, finish, 0)


def attend(
    normed_rows, own_attention, own_gate, gains, cosine, sine, starts, query_cols, window, collective_id
):
    rows, length, _ = normed_rows.shape
    width = query_cols + 2 * HEAD_WIDTH + LANES
    bf16 = jnp.bfloat16
    vmem = pl.BlockSpec(memory_space=pltpu.VMEM)
    return pl.pallas_call(
        functools.partial(attend_kernel, window, HEAD_WIDTH ** (-0.5)),
        out_shape=[
            jax.ShapeDtypeStruct((rows, length, query_cols + 2 * HEAD_WIDTH), bf16),
            jax.ShapeDtypeStruct((rows, length, query_cols), bf16),
            jax.ShapeDtypeStruct((window + 1, rows, length, 2 * HEAD_WIDTH), bf16),
            jax.ShapeDtypeStruct((rows, length, LANES), jnp.float32),
            jax.ShapeDtypeStruct((rows, SUBLANES, length), jnp.float32),
            jax.ShapeDtypeStruct((rows, length, query_cols), bf16),
            jax.ShapeDtypeStruct((rows, length, query_cols), bf16),
        ],
        in_specs=[vmem] * 7,
        out_specs=[vmem] * 7,
        scratch_shapes=[
            pltpu.VMEM((MODEL_WIDTH, width), bf16),
            pltpu.VMEM((window + 1, rows, length, 2 * HEAD_WIDTH), bf16),
            pltpu.SemaphoreType.DMA((window, rows)),
            pltpu.SemaphoreType.DMA((window, rows)),
        ],
        compiler_params=pltpu.CompilerParams(
            collective_id=collective_id, has_side_effects=True, vmem_limit_bytes=VMEM_BYTES
        ),
        cost_estimate=pl.CostEstimate(
            flops=2 * rows * length * MODEL_WIDTH * width,
            bytes_accessed=ATTEND_COST * rows * length * MODEL_WIDTH,
            transcendentals=0,
        ),
    )(normed_rows, own_attention, own_gate, gains, cosine, sine, starts)


def attend_back_kernel(
    window, scale, rows_ref, weight_ref, gains_ref, cosine_ref, sine_ref, start_ref,
    raw_ref, query_ref, pair_ref, stats_ref, across_ref, attended_ref,
    products_ref, gain_ref,
    weight, parts, outs, ins, send_sem, recv_sem,
):
    count_rows, length, _ = rows_ref.shape
    query_cols = query_ref.shape[2]
    heads = query_cols // HEAD_WIDTH
    keys_at = pl.ds(0, HEAD_WIDTH)
    values_at = pl.ds(HEAD_WIDTH, HEAD_WIDTH)
    index, count = greet_line()
    lag = 2

    def hop(turn, row):
        return pltpu.make_async_remote_copy(
            src_ref=outs.at[turn - 1, row],
            dst_ref=ins.at[turn - 1, row],
            send_sem=send_sem.at[turn - 1, row],
            recv_sem=recv_sem.at[turn - 1, row],
            device_id={"seq": lax.rem(index + count - 1, count)},
            device_id_type=pl.DeviceIdType.MESH,
        )

    keys_total = (window + 1) * length
    places = lax.broadcasted_iota(jnp.int32, (keys_total, length), 0)
    latest = window * length + lax.broadcasted_iota(jnp.int32, places.shape, 1)
    lane = lax.broadcasted_iota(jnp.int32, (length, LANES), 1)
    gain_ref[...] = jnp.zeros_like(gain_ref)
    share = weight_ref.shape[3] - query_cols
    for step in range(TEAM_SIZE):
        weight[:, pl.ds(step * query_cols, query_cols)] = whole_block(
            weight_ref, step, pl.ds(share, query_cols)
        )

    @pl.when(index == count - 1)
    def _():
        ins[...] = jnp.zeros_like(ins)

    def compute(row):
        grad_gated = dot_t(rows_ref[row], weight[...])
        keys = pair_ref[:, row, :, keys_at].reshape(-1, HEAD_WIDTH)
        values = pair_ref[:, row, :, values_at].reshape(-1, HEAD_WIDTH)
        allowed = (places >= start_ref[row]) & (places <= latest)
        cosine, sine = cosine_ref[row], sine_ref[row]
        grad_pre = jnp.zeros((length, LANES), jnp.float32)
        grad_keys = jnp.zeros((keys_total, HEAD_WIDTH), jnp.float32)
        grad_values = jnp.zeros((keys_total, HEAD_WIDTH), jnp.float32)
        for head in range(heads):
            columns = slice(head * HEAD_WIDTH, (head + 1) * HEAD_WIDTH)
            gate = stats_ref[row, :, head : head + 1]
            own = grad_gated[:, columns]
            grad_out = (own * gate).astype(jnp.bfloat16)
            grad_gate = jnp.sum(
                own * attended_ref[row, :, columns].astype(jnp.float32), axis=1, keepdims=True
            )
            grad_pre = jnp.where(lane == head, grad_gate * gate * (1.0 - gate), grad_pre)
            query = query_ref[row, :, columns]
            scores = jnp.where(allowed, dot_t(keys, query) * scale, NEGATIVE)
            probs = jnp.exp(scores - across_ref[row, heads + head : heads + head + 1])
            grad_probs = dot_t(values, grad_out)
            inner = jnp.sum(probs * grad_probs, axis=0, keepdims=True)
            grad_scores = (probs * (grad_probs - inner)).astype(jnp.bfloat16)
            grad_values = grad_values + jnp.dot(
                probs.astype(jnp.bfloat16), grad_out, preferred_element_type=jnp.float32
            )
            grad_keys = grad_keys + jnp.dot(
                grad_scores, query, preferred_element_type=jnp.float32
            )
            grad_query = dot_tokens(grad_scores, keys) * scale
            grad_raw, gain = norm_turn_back(
                raw_ref[row, :, columns].astype(jnp.float32), gains_ref[0:1], cosine, sine,
                grad_query,
            )
            products_ref[row, :, columns] = grad_raw.astype(jnp.bfloat16)
            gain_ref[0:1] += jnp.sum(gain, axis=0, keepdims=True)
        products_ref[row, :, query_cols + 2 * HEAD_WIDTH :] = grad_pre.astype(jnp.bfloat16)
        parts[:, row, :, keys_at] = (grad_keys * scale).reshape(window + 1, length, HEAD_WIDTH)
        parts[:, row, :, values_at] = grad_values.reshape(window + 1, length, HEAD_WIDTH)

    def finish(row):
        grad_pair = parts[window, row] + ins[window - 1, row].astype(jnp.float32)
        grad_raw, gain = norm_turn_back(
            raw_ref[row, :, query_cols : query_cols + HEAD_WIDTH].astype(jnp.float32),
            gains_ref[1:2], cosine_ref[row], sine_ref[row], grad_pair[:, :HEAD_WIDTH],
        )
        products_ref[row, :, query_cols : query_cols + HEAD_WIDTH] = grad_raw.astype(jnp.bfloat16)
        products_ref[row, :, query_cols + HEAD_WIDTH : query_cols + 2 * HEAD_WIDTH] = grad_pair[
            :, HEAD_WIDTH:
        ].astype(jnp.bfloat16)
        gain_ref[1:2] += jnp.sum(gain, axis=0, keepdims=True)

    def step(turn_row, carry):
        @pl.when(turn_row < count_rows)
        def _():
            compute(turn_row)

        for turn in range(1, window + 2):
            row = turn_row - lag * (turn - 1)

            @pl.when((row >= 0) & (row < count_rows))
            def _():
                if turn > 1:

                    @pl.when(index < count - 1)
                    def _():
                        hop(turn - 1, row).wait_recv()

                if turn == window + 1:
                    finish(row)
                else:
                    part = parts[turn - 1, row]
                    if turn > 1:
                        part = part + ins[turn - 2, row].astype(jnp.float32)
                    outs[turn - 1, row] = part.astype(jnp.bfloat16)

                    @pl.when(index > 0)
                    def _():
                        hop(turn, row).start()

        return carry

    lax.fori_loop(0, count_rows + lag * window, step, 0)

    @pl.when(index > 0)
    def _():
        for turn in range(1, window + 1):

            def done(row, carry):
                hop(turn, row).wait_send()
                return carry

            lax.fori_loop(0, count_rows, done, 0)


def attend_back(
    grad_rows, own_attention, gains, cosine, sine, starts, saved, window, collective_id
):
    rows, length, _ = grad_rows.shape
    query_cols = saved[1].shape[2]
    width = query_cols + 2 * HEAD_WIDTH + LANES
    bf16 = jnp.bfloat16
    vmem = pl.BlockSpec(memory_space=pltpu.VMEM)
    return pl.pallas_call(
        functools.partial(attend_back_kernel, window, HEAD_WIDTH ** (-0.5)),
        out_shape=[
            jax.ShapeDtypeStruct((rows, length, width), bf16),
            jax.ShapeDtypeStruct((SUBLANES, HEAD_WIDTH), jnp.float32),
        ],
        in_specs=[vmem] * 12,
        out_specs=[vmem] * 2,
        scratch_shapes=[
            pltpu.VMEM((query_cols, MODEL_WIDTH), bf16),
            pltpu.VMEM((window + 1, rows, length, 2 * HEAD_WIDTH), jnp.float32),
            pltpu.VMEM((window, rows, length, 2 * HEAD_WIDTH), bf16),
            pltpu.VMEM((window, rows, length, 2 * HEAD_WIDTH), bf16),
            pltpu.SemaphoreType.DMA((window, rows)),
            pltpu.SemaphoreType.DMA((window, rows)),
        ],
        compiler_params=pltpu.CompilerParams(
            collective_id=collective_id, has_side_effects=True, vmem_limit_bytes=VMEM_BYTES
        ),
        cost_estimate=pl.CostEstimate(
            flops=2 * rows * length * MODEL_WIDTH * query_cols,
            bytes_accessed=ATTEND_COST * rows * length * MODEL_WIDTH,
            transcendentals=0,
        ),
    )(grad_rows, own_attention, gains, cosine, sine, starts, *saved)


def team_columns(matrix, widths):
    pieces = []
    lower = 0
    for width in widths:
        piece = matrix[:, lower : lower + width]
        pieces.append(piece.reshape(matrix.shape[0], TEAM_SIZE, width // TEAM_SIZE))
        lower = lower + width
    return jnp.concatenate(pieces, axis=2).transpose(1, 0, 2)


def gather_parts(blocks):
    return lax.all_gather(blocks, DEPTH, axis=0, tiled=False)


def scatter_parts(parts):
    depth, team, rows, width = parts.shape
    return lax.psum_scatter(
        parts.reshape(depth * team * rows, width), DEPTH, scatter_dimension=0, tiled=True
    ).reshape(team, rows, width)


def gather_rows(matrix):
    return lax.all_gather(matrix, DEPTH, axis=0, tiled=True)


def scatter_rows(gradient):
    return lax.psum_scatter(gradient, DEPTH, scatter_dimension=0, tiled=True)


def shards(
    inputs,
    cotangent,
    doc_lengths,
    projection_weight,
    projection_moment,
    projection_second,
    out_weight,
    out_moment,
    out_second,
    ffn_weight,
    ffn_moment,
    ffn_second,
    down_weight,
    down_moment,
    down_second,
    head_gate,
    gate_moment,
    gate_second,
    norm_gains,
    gains_moment,
    gains_second,
    qk_gains,
    qk_moment,
    qk_second,
):
    rows_dev, local_len, width = inputs.shape
    bf16 = jnp.bfloat16
    team = lax.axis_index(TEAM)
    place_seq = lax.axis_index("seq")
    group_heads = QUERY_HEADS // KEY_VALUE_HEADS
    window = -(-(DOC_MOST - 1) // local_len)
    window = min(window, lax.axis_size("seq") - 1)
    query_cols = QUERY_HEADS * HEAD_WIDTH
    key_value_columns = KEY_VALUE_HEADS * HEAD_WIDTH
    widths_qkv = (query_cols, key_value_columns, key_value_columns)
    widths_ffn = (FF, FF)
    own_query = query_cols // TEAM_SIZE
    own_key = key_value_columns // TEAM_SIZE
    own_ff = FF // TEAM_SIZE
    own_gate = lax.dynamic_slice_in_dim(head_gate.astype(bf16), team * group_heads, group_heads, 1)
    own_gate = jnp.pad(own_gate, ((0, 0), (0, LANES - group_heads)))
    own_attention = gather_parts(
        jnp.concatenate(
            [
                team_exchange(team_columns(projection_weight.astype(bf16), widths_qkv)),
                team_columns(out_weight.astype(bf16), (MODEL_WIDTH,)),
            ],
            axis=2,
        )
    )
    ffn_blocks = team_exchange(team_columns(ffn_weight.astype(bf16), widths_ffn))
    own_inner = gather_parts(ffn_blocks[:, :, :own_ff])
    lengths = lax.all_gather(doc_lengths, TEAM, axis=0, tiled=True)
    place = place_seq * local_len + jnp.arange(local_len, dtype=jnp.int32)
    position = positions(lengths, place)
    cosine, sine = rotary_tables(position, HEAD_WIDTH)
    starts = window * local_len + jnp.arange(local_len, dtype=jnp.int32)[None, :] - position
    inputs_flat = inputs[0].astype(jnp.float32)
    normed = rms_apply(inputs_flat, norm_gains[0]).astype(bf16)
    normed_all, grad_all = gather_team([normed, cotangent[0]], 0)
    raw, query_rot, pairs, stats, across, attended, gated = attend(
        normed_all.reshape(TEAM_SIZE, local_len, MODEL_WIDTH),
        own_attention,
        own_gate,
        qk_gains,
        cosine,
        sine,
        starts[:, :, None],
        own_query,
        window,
        8,
    )
    gated, up_blocks, low_down = lax.optimization_barrier(
        (gated, ffn_blocks[:, :, own_ff:], down_weight.astype(bf16))
    )
    own_up = gather_parts(up_blocks)
    own_down = gather_rows(low_down)
    middle = inputs_flat + scatter_team(product_out, [gated.reshape(-1, own_query)], [own_attention], 1)
    normed2 = rms_apply(middle, norm_gains[1]).astype(bf16)
    normed2_all = gather_team([normed2], 2)[0]
    hidden, slope, swish = ffn_forward(normed2_all, own_inner, own_up)
    grad_final = cotangent[0].astype(jnp.float32)
    down_part, own_down = lax.optimization_barrier(
        (low_tokens(hidden.reshape(-1, own_ff), grad_all), own_down)
    )
    grad_inner, grad_up = ffn_back(grad_all, own_down, slope, swish)
    grad_inner, grad_up = grad_inner.reshape(-1, own_ff), grad_up.reshape(-1, own_ff)
    inner_part, grad_inner = lax.optimization_barrier(
        (weight_parts(normed2_all, grad_inner, ffn_weight.shape[0]), grad_inner)
    )
    down_sum = scatter_rows(down_part)
    grad_normed2 = scatter_team(
        product_ffn_back, [grad_inner, grad_up], [own_inner, own_up], 4
    )
    grad_mid_part, gain_mid = rms_back(middle, norm_gains[1], grad_normed2)
    grad_middle = grad_final + grad_mid_part
    grad_low, down_sum = lax.optimization_barrier((grad_middle.astype(bf16), down_sum))
    inner_sum = scatter_parts(inner_part)
    grad_middle_all, up_part = gather_team(
        [grad_low],
        5,
        weight_work,
        (normed2_all, grad_up),
        (weight_shape(normed2_all, grad_up, ffn_weight.shape[0]),),
    )
    grad_products, gain_sums = attend_back(
        grad_middle_all.reshape(TEAM_SIZE, local_len, MODEL_WIDTH),
        own_attention,
        qk_gains,
        cosine,
        sine,
        starts[:, None, :],
        (raw, query_rot, pairs, stats, across, attended),
        window,
        9,
    )
    grad_products = grad_products.reshape(-1, grad_products.shape[2])
    up_part, grad_products, inner_sum = lax.optimization_barrier(
        (up_part, grad_products, inner_sum)
    )
    up_sum = scatter_parts(up_part)
    grad_normed, attention_part, gate_part = scatter_team(
        product_qkv_back,
        [grad_products],
        [own_attention, own_gate],
        6,
        attention_weight_work,
        (normed_all, grad_products, gated.reshape(-1, own_query), grad_middle_all),
        attention_weight_shapes(normed_all, grad_products, out_weight.shape[0]),
    )
    late_hidden, grad_normed = lax.optimization_barrier((hidden, grad_normed))
    attention_sum = scatter_parts(attention_part)
    final = middle + scatter_team(product_down, [late_hidden.reshape(-1, own_ff)], [own_down], 3)
    result = final.astype(bf16).reshape(inputs.shape)
    grad_in_part, gain_in = rms_back(inputs_flat, norm_gains[0], grad_normed)
    input_grad = (grad_middle + grad_in_part).reshape(inputs.shape)
    ffn_rows = team_exchange(jnp.concatenate([inner_sum, up_sum], axis=2))
    (
        ffn_moment_new,
        ffn_second_new,
        ffn_update,
        down_moment_new,
        down_second_new,
        down_update,
        ffn_squares,
    ) = ffn_moments(
        ffn_rows,
        down_sum,
        (ffn_weight, ffn_moment, ffn_second),
        (down_weight, down_moment, down_second),
    )
    attention_sum, ffn_squares = lax.optimization_barrier((attention_sum, ffn_squares))
    own_projection = own_query + 2 * own_key
    (
        projection_moment_next,
        projection_second_next,
        projection_update,
        out_moment_new,
        out_second_new,
        out_update,
        squares,
    ) = attention_moments(
        team_exchange(attention_sum[:, :, :own_projection]),
        attention_sum,
        (projection_weight, projection_moment, projection_second),
        (out_weight, out_moment, out_second),
    )
    gate_total, gains_total, qk_total, norms = totals(
        gate_part[:, :group_heads].T,
        (jnp.sum(gain_in, axis=0), jnp.sum(gain_mid, axis=0)),
        gain_sums,
        squares,
        ffn_squares,
        10,
    )
    query_steps = STEPS * query_cols // (query_cols + 2 * key_value_columns)
    key_steps = STEPS * key_value_columns // (query_cols + 2 * key_value_columns)
    (
        projection_weight_next,
        qkv_copy,
        out_new,
        out_copy,
        ffn_new,
        ffn_copy,
        down_new,
        down_copy,
        head_gate_new,
        gate_moment_new,
        gate_second_new,
        gains_new,
        gains_moment_new,
        gains_second_new,
        qk_new,
        qk_moment_new,
        qk_second_new,
        norms,
    ) = apply_all(
        norms,
        gate_total,
        gains_total,
        qk_total,
        (
            (projection_weight, projection_update),
            (out_weight, out_update),
            (ffn_weight, ffn_update),
            (down_weight, down_update),
        ),
        (
            (0, (query_steps, query_steps + key_steps)),
            (3, ()),
            (4, (STEPS // 2,)),
            (6, ()),
        ),
        (
            (head_gate.T, gate_moment.T, gate_second.T),
            (norm_gains, gains_moment, gains_second),
            (qk_gains, qk_moment, qk_second),
        ),
    )
    return (
        result,
        input_grad,
        projection_weight_next,
        projection_moment_next,
        projection_second_next,
        qkv_copy,
        out_new,
        out_moment_new,
        out_second_new,
        out_copy,
        ffn_new,
        ffn_moment_new,
        ffn_second_new,
        ffn_copy,
        down_new,
        down_moment_new,
        down_second_new,
        down_copy,
        head_gate_new.T,
        gate_moment_new.T,
        gate_second_new.T,
        gains_new,
        gains_moment_new,
        gains_second_new,
        qk_new,
        qk_moment_new,
        qk_second_new,
        norms[:2, :7],
    )


def solution(mesh):
    mesh = Mesh(
        mesh.devices.reshape(2, 2, 2, mesh.shape["fsdp"] // TEAM_SIZE, mesh.shape["seq"]),
        TEAM + DEPTH,
    )
    rows = TEAM + DEPTH[:1]
    in_specs = (
        P(rows, "seq", None),
        P(rows, "seq", None),
        P(rows, None),
        P(TEAM + DEPTH, None),
        P(TEAM + DEPTH, None),
        P(TEAM + DEPTH, None),
        P(TEAM + DEPTH, None),
        P(TEAM + DEPTH, None),
        P(TEAM + DEPTH, None),
        P(TEAM + DEPTH, None),
        P(TEAM + DEPTH, None),
        P(TEAM + DEPTH, None),
        P(TEAM + DEPTH, None),
        P(TEAM + DEPTH, None),
        P(TEAM + DEPTH, None),
        P(),
        P(),
        P(),
        P(),
        P(),
        P(),
        P(),
        P(),
        P(),
    )
    out_specs = (
        P(rows, "seq", None),
        P(rows, "seq", None),
        P(TEAM + DEPTH, None),
        P(TEAM + DEPTH, None),
        P(TEAM + DEPTH, None),
        P(TEAM + DEPTH, None),
        P(TEAM + DEPTH, None),
        P(TEAM + DEPTH, None),
        P(TEAM + DEPTH, None),
        P(TEAM + DEPTH, None),
        P(TEAM + DEPTH, None),
        P(TEAM + DEPTH, None),
        P(TEAM + DEPTH, None),
        P(TEAM + DEPTH, None),
        P(TEAM + DEPTH, None),
        P(TEAM + DEPTH, None),
        P(TEAM + DEPTH, None),
        P(TEAM + DEPTH, None),
        P(),
        P(),
        P(),
        P(),
        P(),
        P(),
        P(),
        P(),
        P(),
        P(),
    )
    return jax.shard_map(shards, mesh=mesh, in_specs=in_specs, out_specs=out_specs, check_vma=False)
```

```python
import functools

import jax
import jax.numpy as jnp
from jax import lax
from jax.experimental import pallas as pl
from jax.experimental.pallas import tpu as pltpu
from jax.sharding import Mesh
from jax.sharding import PartitionSpec as P

MODEL_WIDTH = 2048
QUERY_HEADS = 16
KEY_VALUE_HEADS = 8
HEAD_WIDTH = 128
FF = 6144
ROW_TOKENS = 1024
STEP = 3
DOC_MOST = 512
TEAM_SIZE = 8
TEAM = ("t2", "t1", "t0")
DEPTH = ("spare", "seq")
LANES = 128
SUBLANES = 8
VMEM_BYTES = 60 << 20
GATHER_VMEM = 60 << 20
LAMB_COST = 70
GATHER_COST = 250
SCATTER_COST = 320
ATTEND_COST = 50


NORM_EPS = 1e-06
ADAM_EPS = 1e-06
RATE = 0.3
DECAY = 0.01
BETA = 0.5
THETA = 1000000.0
NEGATIVE = -1e30


def rms_apply(value_rows, gain):
    return (
        value_rows
        * lax.rsqrt(jnp.mean(value_rows * value_rows, axis=-1, keepdims=True) + NORM_EPS)
        * gain
    )


def rms_back(value_rows, gain, gradient):
    scale = lax.rsqrt(jnp.mean(value_rows * value_rows, axis=-1, keepdims=True) + NORM_EPS)
    scaled = gradient * gain
    inner = jnp.mean(scaled * value_rows, axis=-1, keepdims=True)
    grad_value = scale * scaled - value_rows * scale * scale * scale * inner
    grad_gain = gradient * value_rows * scale
    return (grad_value, grad_gain)


def dot_t(left, right):
    return lax.dot_general(
        left, right, (((1,), (1,)), ((), ())), preferred_element_type=jnp.float32
    )


def low_tokens(left, right):
    return dot_tokens(left, right).astype(jnp.bfloat16)


def dot_tokens(left, right):
    return lax.dot_general(
        left, right, (((0,), (0,)), ((), ())), preferred_element_type=jnp.float32
    )


def moments(weight, moment, second, gradient):
    moment_new = BETA * moment + (1.0 - BETA) * gradient
    second_new = BETA * second + (1.0 - BETA) * gradient * gradient
    correction = 1.0 - BETA**STEP
    update = (
        moment_new / correction / (jnp.sqrt(second_new / correction) + ADAM_EPS) + DECAY * weight
    )
    return (moment_new, second_new, update)


def rotary_tables(position, width):
    half = width // 2
    rates = THETA ** (-jnp.arange(half, dtype=jnp.float32) * 2.0 / width)
    angle = position.astype(jnp.float32)[..., None] * rates
    cosine, sine = jnp.cos(angle), jnp.sin(angle)
    return (
        jnp.concatenate([cosine, cosine], axis=-1),
        jnp.concatenate([-sine, sine], axis=-1),
    )


def positions(lengths, place):
    ends = jnp.cumsum(lengths, axis=1)
    starts = ends - lengths
    inside = (place[None, :, None] >= starts[:, None, :]) & (place[None, :, None] < ends[:, None, :])
    return place[None, :] - jnp.sum(jnp.where(inside, starts[:, None, :], 0), axis=2)


def team_place():
    return tuple(lax.axis_index(axis) for axis in TEAM)


def greet_team(place):
    barrier = pltpu.get_barrier_semaphore()
    for axis, index in zip(TEAM, place):
        pl.semaphore_signal(
            barrier, inc=1, device_id={axis: 1 - index}, device_id_type=pl.DeviceIdType.MESH
        )
    pl.semaphore_wait(barrier, len(TEAM))


def member(place, flips):
    index = 0
    for own, flip in zip(place, flips):
        index = index * 2 + (1 - own if flip else own)
    return index


def gather_kernel(count, work, *refs):
    given, made = (work[1], work[2]) if work else (0, 0)
    owns, operands = refs[:count], refs[count : count + given]
    alls = refs[count + given : 2 * count + given]
    results = refs[2 * count + given : 2 * count + given + made]
    own_sem, send_sem, recv_sem = refs[2 * count + given + made :]
    place = team_place()
    greet_team(place)
    me = member(place, (0, 0, 0))
    beside = member(place, (0, 1, 0))
    above = member(place, (1, 0, 0))
    across = member(place, (1, 1, 0))
    copies = [{} for _ in range(count)]
    keeps = []

    def send(item, number, axis, source, target):
        copy = pltpu.make_async_remote_copy(
            src_ref=source,
            dst_ref=target,
            send_sem=send_sem.at[item, number],
            recv_sem=recv_sem.at[item, number],
            device_id={TEAM[axis]: 1 - place[axis]},
            device_id_type=pl.DeviceIdType.MESH,
        )
        copy.start()
        copies[item][number] = copy

    def halves(item):
        half = owns[item].shape[0] // 2
        return pl.ds(0, half), pl.ds(half, half)

    for item in range(count):
        target = alls[item].at[me]
        send(item, 0, 1, owns[item], target)
        send(item, 1, 0, owns[item], target)
        send(item, 2, 2, owns[item], target)
        keeps.append(pltpu.make_async_copy(owns[item], target, own_sem.at[item]))
        keeps[item].start()
    if work:
        work[0](*operands, *results)
    for item in range(count):
        upper, lower = halves(item)
        copies[item][0].wait_recv()
        block = alls[item].at[beside]
        send(item, 3, 0, block.at[upper], block.at[upper])
        send(item, 4, 2, block, block)
        copies[item][1].wait_recv()
        block = alls[item].at[above]
        send(item, 5, 1, block.at[lower], block.at[lower])
        send(item, 6, 2, block, block)
    for item in range(count):
        upper, lower = halves(item)
        block = alls[item].at[across]
        copies[item][3].wait_recv()
        send(item, 7, 2, block.at[upper], block.at[upper])
        copies[item][5].wait_recv()
        send(item, 8, 2, block.at[lower], block.at[lower])
    for item in range(count):
        for number in (2, 4, 6, 7, 8):
            copies[item][number].wait_recv()
        for number in range(9):
            copies[item][number].wait_send()
        keeps[item].wait()


def gather_team(arrays, collective_id, work=None, operands=(), results=()):
    count = len(arrays)
    anywhere = pl.BlockSpec(memory_space=pl.ANY)
    out_shape = [jax.ShapeDtypeStruct((TEAM_SIZE,) + own.shape, own.dtype) for own in arrays]
    gathered = pl.pallas_call(
        functools.partial(
            gather_kernel, count, (work, len(operands), len(results)) if work else None
        ),
        out_shape=out_shape + list(results),
        in_specs=[anywhere] * (count + len(operands)),
        out_specs=[anywhere] * (count + len(results)),
        scratch_shapes=[
            pltpu.SemaphoreType.DMA((count,)),
            pltpu.SemaphoreType.DMA((count, 9)),
            pltpu.SemaphoreType.DMA((count, 9)),
        ],
        compiler_params=pltpu.CompilerParams(
            collective_id=collective_id, has_side_effects=True, vmem_limit_bytes=GATHER_VMEM
        ),
        cost_estimate=pl.CostEstimate(
            flops=0,
            bytes_accessed=sum(GATHER_COST * own.shape[0] * own.shape[1] for own in arrays),
            transcendentals=0,
        ),
    )(*arrays, *operands)
    return [
        whole.reshape(TEAM_SIZE * own.shape[0], own.shape[1])
        for whole, own in zip(gathered, arrays)
    ] + list(gathered[count:])


def scatter_kernel(product, count, work, *refs):
    given, made = (work[1], work[2]) if work else (0, 0)
    operands, extra = refs[:count], refs[count : count + given]
    sum_ref = refs[count + given]
    results = refs[count + given + 1 : count + given + 1 + made]
    own, out_near, in_near, out_far, in_half, in_full, send_sem, recv_sem = refs[
        count + given + 1 + made :
    ]
    place = team_place()
    greet_team(place)
    rows = sum_ref.shape[0]
    half = rows // 2
    upper, lower = pl.ds(0, half), pl.ds(half, half)

    def send(number, axis, source, target):
        copy = pltpu.make_async_remote_copy(
            src_ref=source,
            dst_ref=target,
            send_sem=send_sem.at[number],
            recv_sem=recv_sem.at[number],
            device_id={TEAM[axis]: 1 - place[axis]},
            device_id_type=pl.DeviceIdType.MESH,
        )
        copy.start()
        return copy

    flips = ((1, 1), (0, 1), (1, 0), (0, 0))
    near, far = [], {}
    is_first = place[2] == 0

    def begin(turn):
        first, second = flips[turn]
        pair = member(place[:2], (first, second))

        def one(step, columns):
            both = product(operands, pair, step, columns)
            former, latter = both[:rows], both[rows:]
            out_near[turn, :, columns] = jnp.where(is_first, latter, former).astype(jnp.bfloat16)
            own[turn, :, columns] = jnp.where(is_first, former, latter)

        over_tiles(sum_ref.shape[1], one)
        near.append(send(turn, 2, out_near.at[turn], in_near.at[turn]))

    def join(turn):
        near[turn].wait_recv()
        return own[turn] + in_near[turn].astype(jnp.float32)

    begin(0)
    begin(1)
    out_far[0] = join(0).astype(jnp.bfloat16)
    far[4] = send(4, 1, out_far.at[0, upper], in_half.at[0])
    far[5] = send(5, 0, out_far.at[0, lower], in_half.at[1])
    begin(2)
    own[1] = join(1)
    out_far[1, upper] = own[1, upper].astype(jnp.bfloat16)
    far[6] = send(6, 1, out_far.at[1, upper], in_full.at[0, upper])
    begin(3)
    own[2] = join(2)
    out_far[2, lower] = own[2, lower].astype(jnp.bfloat16)
    far[7] = send(7, 0, out_far.at[2, lower], in_full.at[1, lower])
    sum_ref[...] = join(3)
    far[5].wait_recv()
    out_far[1, lower] = (own[1, lower] + in_half[1].astype(jnp.float32)).astype(jnp.bfloat16)
    far[8] = send(8, 1, out_far.at[1, lower], in_full.at[0, lower])
    far[4].wait_recv()
    out_far[2, upper] = (own[2, upper] + in_half[0].astype(jnp.float32)).astype(jnp.bfloat16)
    far[9] = send(9, 0, out_far.at[2, upper], in_full.at[1, upper])
    if work:
        work[0](*extra, *results)
    far[6].wait_recv()
    far[7].wait_recv()
    far[8].wait_recv()
    far[9].wait_recv()
    sum_ref[...] = (
        sum_ref[...] + in_full[0].astype(jnp.float32) + in_full[1].astype(jnp.float32)
    )
    for copy in near + [far[number] for number in range(4, 10)]:
        copy.wait_send()


def over_tiles(width, one):
    tile = width // TEAM_SIZE

    def body(step, carry):
        one(step, pl.ds(pl.multiple_of(step * tile, tile), tile))
        return carry

    lax.fori_loop(0, TEAM_SIZE, body, 0)


def whole_block(ref, step, columns=slice(None)):
    block = ref[:, step, :, columns]
    return block.reshape(block.shape[0] * block.shape[1], block.shape[2])


def product_down(operands, pair, step, columns):
    hidden, weight = operands
    return jnp.dot(hidden[pair], weight[:, columns], preferred_element_type=jnp.float32)


def product_out(operands, pair, step, columns):
    gated, weight = operands
    depth = gated.shape[2]
    share = pl.ds(weight.shape[3] - depth, depth)
    return jnp.dot(
        gated[pair], whole_block(weight, step, share), preferred_element_type=jnp.float32
    )


def product_ffn_back(operands, pair, step, columns):
    grad_inner, grad_up, inner_weight, up_weight = operands
    return dot_t(grad_inner[pair], whole_block(inner_weight, step)) + dot_t(
        grad_up[pair], whole_block(up_weight, step)
    )


def product_qkv_back(operands, pair, step, columns):
    grad_products, weight, gate_weight = operands
    depth = grad_products.shape[2] - LANES
    share = pl.ds(0, depth)
    return dot_t(grad_products[pair, :, share], whole_block(weight, step, share)) + dot_t(
        grad_products[pair, :, pl.ds(depth, LANES)], gate_weight[columns, :]
    )


def scatter_team(
    product, lefts, rights, collective_id, work=None, operands=(), results=()
):
    rows = lefts[0].shape[0] // TEAM_SIZE
    depth = sum(left.shape[1] for left in lefts)
    width = MODEL_WIDTH
    paired = [left.reshape(TEAM_SIZE // 2, 2 * rows, left.shape[1]) for left in lefts]
    vmem = pl.BlockSpec(memory_space=pltpu.VMEM)
    anywhere = pl.BlockSpec(memory_space=pl.ANY)
    count = len(lefts) + len(rights)
    summed = pl.pallas_call(
        functools.partial(
            scatter_kernel, product, count, (work, len(operands), len(results)) if work else None
        ),
        out_shape=[jax.ShapeDtypeStruct((rows, width), jnp.float32)] + list(results),
        in_specs=[vmem] * count + [anywhere] * len(operands),
        out_specs=[vmem] + [anywhere] * len(results),
        scratch_shapes=[
            pltpu.VMEM((4, rows, width), jnp.float32),
            pltpu.VMEM((4, rows, width), jnp.bfloat16),
            pltpu.VMEM((4, rows, width), jnp.bfloat16),
            pltpu.VMEM((3, rows, width), jnp.bfloat16),
            pltpu.VMEM((2, rows // 2, width), jnp.bfloat16),
            pltpu.VMEM((2, rows, width), jnp.bfloat16),
            pltpu.SemaphoreType.DMA((10,)),
            pltpu.SemaphoreType.DMA((10,)),
        ],
        compiler_params=pltpu.CompilerParams(
            collective_id=collective_id, has_side_effects=True, vmem_limit_bytes=VMEM_BYTES
        ),
        cost_estimate=pl.CostEstimate(
            flops=2 * TEAM_SIZE * rows * depth * width,
            bytes_accessed=SCATTER_COST * rows * width,
            transcendentals=0,
        ),
    )(*paired, *rights, *operands)
    return summed if work else summed[0]


def ffn_kernel(rows_ref, inner_ref, up_ref, hidden_ref, slope_ref, swish_ref, inner_weight, up_weight):
    @pl.when(pl.program_id(0) == 0)
    def _():
        block = inner_ref.shape[0] * inner_ref.shape[2]
        for step in range(TEAM_SIZE):
            inner_weight[pl.ds(step * block, block), :] = whole_block(inner_ref, step)
            up_weight[pl.ds(step * block, block), :] = whole_block(up_ref, step)

    tile = 256

    def one(step, carry):
        columns = pl.ds(pl.multiple_of(step * tile, tile), tile)
        inner = jnp.dot(rows_ref[0], inner_weight[:, columns], preferred_element_type=jnp.float32)
        up_part = jnp.dot(rows_ref[0], up_weight[:, columns], preferred_element_type=jnp.float32)
        sigma = jax.nn.sigmoid(inner)
        swish = inner * sigma
        hidden_ref[0, :, columns] = (swish * up_part).astype(jnp.bfloat16)
        slope_ref[0, :, columns] = up_part * sigma * (1.0 + inner * (1.0 - sigma))
        swish_ref[0, :, columns] = swish
        return carry

    lax.fori_loop(0, hidden_ref.shape[2] // tile, one, 0, unroll=True)


def ffn_forward(normed_rows, inner_weight, up_weight):
    count, depth = TEAM_SIZE // 2, normed_rows.shape[1]
    length = normed_rows.shape[0] // count
    width = inner_weight.shape[3]
    whole = pl.BlockSpec(inner_weight.shape, lambda i: (0, 0, 0, 0), pipeline_mode=pl.Buffered(1))
    out = pl.BlockSpec((1, length, width), lambda i: (i, 0, 0))
    return pl.pallas_call(
        ffn_kernel,
        grid=(count,),
        out_shape=[
            jax.ShapeDtypeStruct((count, length, width), jnp.bfloat16),
            jax.ShapeDtypeStruct((count, length, width), jnp.float32),
            jax.ShapeDtypeStruct((count, length, width), jnp.float32),
        ],
        in_specs=[pl.BlockSpec((1, length, depth), lambda i: (i, 0, 0)), whole, whole],
        out_specs=[out, out, out],
        scratch_shapes=[pltpu.VMEM((depth, width), jnp.bfloat16)] * 2,
        compiler_params=pltpu.CompilerParams(vmem_limit_bytes=VMEM_BYTES),
        cost_estimate=pl.CostEstimate(
            flops=4 * count * length * depth * width,
            bytes_accessed=count * length * (2 * depth + 10 * width),
            transcendentals=count * length * width,
        ),
    )(normed_rows.reshape(count, length, depth), inner_weight, up_weight)


def ffn_back_kernel(grad_ref, weight_ref, slope_ref, swish_ref, inner_ref, up_ref):
    tile = 256

    def one(step, carry):
        columns = pl.ds(pl.multiple_of(step * tile, tile), tile)
        grad_hidden = dot_t(grad_ref[0], weight_ref[columns, :])
        inner_ref[0, :, columns] = (grad_hidden * slope_ref[0, :, columns]).astype(jnp.bfloat16)
        up_ref[0, :, columns] = (grad_hidden * swish_ref[0, :, columns]).astype(jnp.bfloat16)
        return carry

    lax.fori_loop(0, inner_ref.shape[2] // tile, one, 0, unroll=True)


def ffn_back(grad_rows, down_weight, slope, swish):
    count, length, width = slope.shape
    depth = grad_rows.shape[1]
    whole = pl.BlockSpec(down_weight.shape, lambda i: (0, 0), pipeline_mode=pl.Buffered(1))
    part = pl.BlockSpec((1, length, width), lambda i: (i, 0, 0))
    return pl.pallas_call(
        ffn_back_kernel,
        grid=(count,),
        out_shape=[jax.ShapeDtypeStruct((count, length, width), jnp.bfloat16)] * 2,
        in_specs=[pl.BlockSpec((1, length, depth), lambda i: (i, 0, 0)), whole, part, part],
        out_specs=[part, part],
        compiler_params=pltpu.CompilerParams(vmem_limit_bytes=VMEM_BYTES),
        cost_estimate=pl.CostEstimate(
            flops=2 * count * length * depth * width,
            bytes_accessed=count * length * (2 * depth + 12 * width),
            transcendentals=0,
        ),
    )(grad_rows.reshape(count, length, depth), down_weight, slope, swish)


def weight_kernel(left_ref, right_ref, part_ref):
    depth, _, rows, width = part_ref.shape
    part = dot_tokens(left_ref[...], right_ref[...])
    part_ref[...] = part.astype(jnp.bfloat16).reshape(depth, 1, rows, width)


def weight_shape(left, right, rows):
    depth = left.shape[1] // (TEAM_SIZE * rows)
    return jax.ShapeDtypeStruct((depth, TEAM_SIZE, rows, right.shape[1]), jnp.bfloat16)


def weight_specs(left, right, part):
    depth, _, rows, width = part.shape
    return dict(
        grid=(TEAM_SIZE,),
        in_specs=[
            pl.BlockSpec((left.shape[0], depth * rows), lambda i: (0, i)),
            pl.BlockSpec(right.shape, lambda i: (0, 0)),
        ],
        out_specs=[pl.BlockSpec((depth, 1, rows, width), lambda i: (0, i, 0, 0))],
    )


def weight_parts(left, right, rows):
    part = weight_shape(left, right, rows)
    (tokens, height), width = left.shape, right.shape[1]
    return pl.pallas_call(
        weight_kernel,
        out_shape=[part],
        compiler_params=pltpu.CompilerParams(vmem_limit_bytes=VMEM_BYTES),
        cost_estimate=pl.CostEstimate(
            flops=2 * tokens * height * width,
            bytes_accessed=2 * tokens * (height + width) + 2 * height * width,
            transcendentals=0,
        ),
        **weight_specs(left, right, part),
    )(left, right)[0]


def weight_work(left_ref, right_ref, part_ref):
    pltpu.emit_pipeline(weight_kernel, **weight_specs(left_ref, right_ref, part_ref))(
        left_ref, right_ref, part_ref
    )


def attention_weight_kernel(normed_ref, products_ref, gated_ref, grad_ref, part_ref, gate_ref):
    depth, _, rows, _ = part_ref.shape
    own = products_ref.shape[1] - LANES
    part = dot_tokens(normed_ref[...], products_ref[...])
    gate_ref[...] = part[:, own:].T[:SUBLANES]
    part_ref[:, :, :, pl.ds(0, own)] = (
        part[:, :own].astype(jnp.bfloat16).reshape(depth, 1, rows, own)
    )
    share = grad_ref.shape[1]
    part = dot_tokens(gated_ref[...], grad_ref[...])
    part_ref[:, :, :, pl.ds(own, share)] = part.astype(jnp.bfloat16).reshape(depth, 1, rows, share)


def attention_weight_work(*refs):
    normed, products, gated, grad, part, gate = refs
    depth, _, rows, width = part.shape
    share = depth * rows
    column = pl.BlockSpec((normed.shape[0], share), lambda i: (0, i))
    pltpu.emit_pipeline(
        attention_weight_kernel,
        grid=(TEAM_SIZE,),
        in_specs=[
            column,
            pl.BlockSpec(products.shape, lambda i: (0, 0)),
            pl.BlockSpec(gated.shape, lambda i: (0, 0)),
            column,
        ],
        out_specs=[
            pl.BlockSpec((depth, 1, rows, width), lambda i: (0, i, 0, 0)),
            pl.BlockSpec((SUBLANES, share), lambda i: (0, i)),
        ],
    )(*refs)


def attention_weight_shapes(normed, grad_products, rows):
    height, width = normed.shape[1], grad_products.shape[1]
    share = height // TEAM_SIZE
    return [
        jax.ShapeDtypeStruct((share // rows, TEAM_SIZE, rows, width - LANES + share), jnp.bfloat16),
        jax.ShapeDtypeStruct((SUBLANES, height), jnp.float32),
    ]


def greet_all():
    place = team_place()
    barrier = pltpu.get_barrier_semaphore()
    flips = [(step // 4, step // 2 % 2, step % 2) for step in range(1, TEAM_SIZE)]
    team = [
        (
            member(place, flip),
            {axis: 1 - at if turn else at for axis, at, turn in zip(TEAM, place, flip)},
        )
        for flip in flips
    ]
    sizes = [lax.axis_size(axis) for axis in DEPTH]
    depth = sizes[0] * sizes[1]
    spot = lax.axis_index(DEPTH[0]) * sizes[1] + lax.axis_index(DEPTH[1])
    line = []
    for step in range(1, depth):
        other = lax.rem(spot + step, depth)
        line.append({DEPTH[0]: other // sizes[1], DEPTH[1]: lax.rem(other, sizes[1])})
    for target in [device for _, device in team] + line:
        pl.semaphore_signal(
            barrier, inc=1, device_id=target, device_id_type=pl.DeviceIdType.MESH
        )
    pl.semaphore_wait(barrier, len(team) + len(line))
    return member(place, (0, 0, 0)), team, spot, line


def push(source, target, sems, number, device):
    copy = pltpu.make_async_remote_copy(
        src_ref=source,
        dst_ref=target,
        send_sem=sems.at[0, number],
        recv_sem=sems.at[1, number],
        device_id=device,
        device_id_type=pl.DeviceIdType.MESH,
    )
    copy.start()
    return copy


def begin_line(own, slots, sems, spot, line):
    slots[spot] = own[...]
    return [
        push(own, slots.at[spot], sems, number, device) for number, device in enumerate(line)
    ]


def begin_team(copies, slots, team_slots, sems, me, team):
    for copy in copies:
        copy.wait_recv()
    total = slots[0]
    for step in range(1, slots.shape[0]):
        total = total + slots[step]
    team_slots[me] = total
    return [
        push(team_slots.at[me], team_slots.at[me], sems, number, device)
        for number, (_, device) in enumerate(team)
    ]


def depth_size():
    return lax.axis_size(DEPTH[0]) * lax.axis_size(DEPTH[1])


def lane_squares(piece):
    total = jnp.sum(piece * piece, axis=0, keepdims=True)
    lanes = total[:, :LANES]
    for first in range(LANES, total.shape[1], LANES):
        lanes = lanes + total[:, first : first + LANES]
    return lanes


def in_lanes(values, shape):
    lane = lax.broadcasted_iota(jnp.int32, shape, 1)
    row = jnp.zeros(shape, jnp.float32)
    for number, value in enumerate(values):
        row = jnp.where(lane == number, jnp.sum(value, axis=1, keepdims=True), row)
    return row


def update_columns(columns, gradient, state, results, update_ref):
    weight = state[0][:, columns]
    moment, second, update = moments(
        weight, state[1][:, columns], state[2][:, columns], gradient.astype(jnp.float32)
    )
    results[0][:, columns] = moment
    results[1][:, columns] = second
    update_ref[:, columns] = update
    return lane_squares(weight), lane_squares(update)


def at_columns(first, width):
    return pl.ds(pl.multiple_of(first, width if width < LANES else LANES), width)


STEPS = 16


def ffn_moments_kernel(rows_ref, down_ref, *refs):
    state, down_state = refs[0:3], refs[3:6]
    results, update, down_results, down_update, squares_ref = (
        refs[6:8], refs[8], refs[9:11], refs[11], refs[12]
    )
    step = pl.program_id(0)

    @pl.when(step == 0)
    def _():
        squares_ref[...] = jnp.zeros_like(squares_ref)

    every = slice(None)
    found = update_columns(every, rows_ref[0], state, results, update)
    group = step // (STEPS // 2)
    squares_ref[pl.ds(group, 1)] += found[0]
    squares_ref[pl.ds(4 + group, 1)] += found[1]
    found = update_columns(every, down_ref[...], down_state, down_results, down_update)
    squares_ref[2:3] += found[0]
    squares_ref[6:7] += found[1]


def ffn_moments(ffn_rows, down_sum, state, down_state):
    team, rows, width = ffn_rows.shape
    half = STEPS // 2

    def column(array):
        return pl.BlockSpec((array.shape[0], array.shape[1] // STEPS), lambda i: (0, i))

    like = [jax.ShapeDtypeStruct(state[0].shape, jnp.float32)] * 3
    like_down = [jax.ShapeDtypeStruct(down_state[0].shape, jnp.float32)] * 3
    return pl.pallas_call(
        ffn_moments_kernel,
        grid=(STEPS,),
        out_shape=like + like_down + [jax.ShapeDtypeStruct((SUBLANES, LANES), jnp.float32)],
        in_specs=[
            pl.BlockSpec((1, rows, width // 2), lambda i: (lax.rem(i, half), 0, i // half)),
            column(down_sum),
        ]
        + [column(array) for array in state + down_state],
        out_specs=[column(array) for array in state + down_state]
        + [pl.BlockSpec((SUBLANES, LANES), lambda i: (0, 0))],
        compiler_params=pltpu.CompilerParams(vmem_limit_bytes=GATHER_VMEM),
        cost_estimate=pl.CostEstimate(
            flops=20 * state[0].size, bytes_accessed=30 * state[0].size, transcendentals=0
        ),
    )(ffn_rows, down_sum, *state, *down_state)


def attention_moments_kernel(rows_ref, attention_ref, *refs):
    state, out_state = refs[0:3], refs[3:6]
    results, step_ref, out_results, out_step_ref, squares_ref = (
        refs[6:8], refs[8], refs[9:11], refs[11], refs[12]
    )
    share = rows_ref.shape[2]
    query_width = share - 2 * HEAD_WIDTH
    out_width = out_state[0].shape[1] // TEAM_SIZE
    zero = jnp.zeros((1, LANES), jnp.float32)

    def one(turn, sums):
        found = ()
        for first, start, width in (
            (turn * query_width, 0, query_width),
            (TEAM_SIZE * query_width + turn * HEAD_WIDTH, query_width, HEAD_WIDTH),
            (
                TEAM_SIZE * (query_width + HEAD_WIDTH) + turn * HEAD_WIDTH,
                query_width + HEAD_WIDTH,
                HEAD_WIDTH,
            ),
        ):
            found = found + update_columns(
                at_columns(first, width), rows_ref[turn, :, pl.ds(start, width)], state, results,
                step_ref,
            )
        found = found + update_columns(
            at_columns(turn * out_width, out_width),
            attention_ref[turn, :, pl.ds(share, out_width)], out_state, out_results, out_step_ref,
        )
        return tuple(old + new for old, new in zip(sums, found))

    sums = lax.fori_loop(0, TEAM_SIZE, one, (zero,) * 8)
    for group in range(4):
        squares_ref[group : group + 1] = sums[2 * group]
        squares_ref[4 + group : 5 + group] = sums[2 * group + 1]


def attention_moments(projection_rows, attention_sum, state, out_state):
    vmem = pl.BlockSpec(memory_space=pltpu.VMEM)
    like = [jax.ShapeDtypeStruct(state[0].shape, jnp.float32)] * 3
    like_out = [jax.ShapeDtypeStruct(out_state[0].shape, jnp.float32)] * 3
    return pl.pallas_call(
        attention_moments_kernel,
        out_shape=like + like_out + [jax.ShapeDtypeStruct((SUBLANES, LANES), jnp.float32)],
        in_specs=[vmem] * 8,
        out_specs=[vmem] * 7,
        compiler_params=pltpu.CompilerParams(vmem_limit_bytes=GATHER_VMEM),
        cost_estimate=pl.CostEstimate(
            flops=20 * state[0].size, bytes_accessed=30 * state[0].size, transcendentals=0
        ),
    )(projection_rows, attention_sum, *state, *out_state)


def totals_kernel(
    heads, gate_ref, first_ref, second_ref, qk_ref, squares_ref, ffn_squares_ref,
    gate_out, gains_out, qk_out, norms_out,
    own, line_slots, team_slots, line_sems, team_sems,
):
    own[...] = jnp.zeros_like(own)
    own[0:heads] = gate_ref[0:heads]
    own[heads : heads + 1] = first_ref[...]
    own[heads + 1 : heads + 2] = second_ref[...]
    for row in range(2):
        own[heads + 2 : heads + 3, pl.ds(row * HEAD_WIDTH, HEAD_WIDTH)] = qk_ref[row : row + 1]
    rows = [squares_ref[group : group + 1] for group in range(4)]
    rows += [ffn_squares_ref[group : group + 1] for group in range(3)]
    rows += [squares_ref[4 + group : 5 + group] for group in range(4)]
    rows += [ffn_squares_ref[4 + group : 5 + group] for group in range(3)]
    own[heads + 2 : heads + 3, pl.ds(2 * HEAD_WIDTH, LANES)] = in_lanes(rows, (1, LANES))
    me, team, spot, line = greet_all()
    along = begin_line(own, line_slots, line_sems, spot, line)
    across = begin_team(along, line_slots, team_slots, team_sems, me, team)
    for copy in across:
        copy.wait_recv()
    total = team_slots[0, heads:]
    for turn in range(1, TEAM_SIZE):
        total = total + team_slots[turn, heads:]
    gains_out[...] = total[:2]
    for row in range(2):
        qk_out[row : row + 1] = total[2:3, row * HEAD_WIDTH : (row + 1) * HEAD_WIDTH]
    for turn in range(TEAM_SIZE):
        gate_out[turn * heads : (turn + 1) * heads] = team_slots[turn, :heads]
    norms = jnp.sqrt(total[2:3, 2 * HEAD_WIDTH : 2 * HEAD_WIDTH + LANES])
    groups = 7
    weight_norms = [norms[:, number : number + 1] for number in range(groups)]
    update_norms = [norms[:, groups + number : groups + number + 1] for number in range(groups)]
    norms_out[...] = jnp.zeros_like(norms_out)
    norms_out[0:1] = in_lanes(weight_norms, (1, LANES))
    norms_out[1:2] = in_lanes(update_norms, (1, LANES))
    norms_out[2:3] = in_lanes(
        [former / latter for former, latter in zip(weight_norms, update_norms)], (1, LANES)
    )
    for copy in along + across:
        copy.wait_send()


def totals(heads, gate_part, gains, qk_gains, squares, ffn_squares, collective_id):
    vmem = pl.BlockSpec(memory_space=pltpu.VMEM)
    width = gate_part.shape[1]
    depth = depth_size()
    return pl.pallas_call(
        functools.partial(totals_kernel, heads),
        out_shape=[
            jax.ShapeDtypeStruct((TEAM_SIZE * heads, width), jnp.float32),
            jax.ShapeDtypeStruct((2, width), jnp.float32),
            jax.ShapeDtypeStruct((2, HEAD_WIDTH), jnp.float32),
            jax.ShapeDtypeStruct((SUBLANES, LANES), jnp.float32),
        ],
        in_specs=[vmem] * 6,
        out_specs=[vmem] * 4,
        scratch_shapes=[
            pltpu.VMEM((SUBLANES, width), jnp.float32),
            pltpu.VMEM((depth, SUBLANES, width), jnp.float32),
            pltpu.VMEM((TEAM_SIZE, SUBLANES, width), jnp.float32),
            pltpu.SemaphoreType.DMA((2, max(depth - 1, 1))),
            pltpu.SemaphoreType.DMA((2, TEAM_SIZE - 1)),
        ],
        compiler_params=pltpu.CompilerParams(collective_id=collective_id, has_side_effects=True),
    )(gate_part, gains[0][None], gains[1][None], qk_gains, squares, ffn_squares)


def small_update(state, gradient, results, by_row):
    weight = state[0][...]
    moment, second, update = moments(weight, state[1][...], state[2][...], gradient[...])
    ratio = jnp.sum(weight * weight, axis=1, keepdims=True)
    size = jnp.sum(update * update, axis=1, keepdims=True)
    if not by_row:
        ratio = jnp.sum(ratio, axis=0, keepdims=True)
        size = jnp.sum(size, axis=0, keepdims=True)
    results[0][...] = weight - RATE * (jnp.sqrt(ratio) / jnp.sqrt(size)) * update
    results[1][...] = moment
    results[2][...] = second


def apply_kernel(edges, norms_ref, gate_ref, gains_ref, qk_ref, *refs):
    pairs = [refs[2 * number : 2 * number + 2] for number in range(4)]
    states = [refs[8 + 3 * number : 11 + 3 * number] for number in range(3)]
    targets = [refs[17 + 2 * number : 19 + 2 * number] for number in range(4)]
    results = [refs[25 + 3 * number : 28 + 3 * number] for number in range(3)]
    norms_out = refs[34]
    step = pl.program_id(0)

    @pl.when(step == 0)
    def _():
        norms_out[...] = norms_ref[0:2]
        small_update(states[0], gate_ref, results[0], False)
        small_update(states[1], gains_ref, results[1], True)
        small_update(states[2], qk_ref, results[2], True)

    for (weight, update), (new, low_new), (first, uppers) in zip(pairs, targets, edges):
        rate = norms_ref[2:3, first : first + 1]
        for number, upper in enumerate(uppers):
            group = first + number + 1
            rate = jnp.where(step < upper, rate, norms_ref[2:3, group : group + 1])
        value = weight[...] - RATE * rate * update[...]
        new[...] = value
        low_new[...] = value.astype(jnp.bfloat16)


def apply_all(norms, gate_total, gains_total, qk_total, pairs, edges, states):
    def whole(array):
        return pl.BlockSpec(array.shape, lambda i: (0, 0))

    def column(array):
        return pl.BlockSpec((array.shape[0], array.shape[1] // STEPS), lambda i: (0, i))

    small = [array for state in states for array in state]
    operands = [norms, gate_total, gains_total, qk_total]
    targets = []
    for weight, _ in pairs:
        targets.append(jax.ShapeDtypeStruct(weight.shape, jnp.float32))
        targets.append(jax.ShapeDtypeStruct(weight.shape, jnp.bfloat16))
    results = [jax.ShapeDtypeStruct(array.shape, jnp.float32) for array in small]
    results.append(jax.ShapeDtypeStruct((2, norms.shape[1]), jnp.float32))
    return pl.pallas_call(
        functools.partial(apply_kernel, edges),
        grid=(STEPS,),
        out_shape=targets + results,
        in_specs=[whole(array) for array in operands]
        + [column(array) for pair in pairs for array in pair]
        + [whole(array) for array in small],
        out_specs=[column(array) for array in targets] + [whole(array) for array in results],
        compiler_params=pltpu.CompilerParams(vmem_limit_bytes=GATHER_VMEM),
        cost_estimate=pl.CostEstimate(
            flops=4 * pairs[2][0].size, bytes_accessed=30 * pairs[2][0].size, transcendentals=0
        ),
    )(*operands, *[array for pair in pairs for array in pair], *small)


def team_exchange(blocks):
    return lax.all_to_all(blocks, TEAM, split_axis=0, concat_axis=0, tiled=True)


def turn_half(value_rows):
    return pltpu.roll(value_rows, value_rows.shape[-1] // 2, value_rows.ndim - 1)


def norm_turn(value_rows, gain, cosine, sine):
    scaled = rms_apply(value_rows, gain)
    return scaled * cosine + turn_half(scaled) * sine


def norm_turn_back(value_rows, gain, cosine, sine, gradient):
    turned = gradient * cosine + turn_half(gradient * sine)
    return rms_back(value_rows, gain, turned)


def greet_line():
    index, count = lax.axis_index("seq"), lax.axis_size("seq")
    barrier = pltpu.get_barrier_semaphore()

    @pl.when(index > 0)
    def _():
        pl.semaphore_signal(
            barrier, inc=1, device_id={"seq": index - 1}, device_id_type=pl.DeviceIdType.MESH
        )

    @pl.when(index < count - 1)
    def _():
        pl.semaphore_signal(
            barrier, inc=1, device_id={"seq": index + 1}, device_id_type=pl.DeviceIdType.MESH
        )

    inside = (index > 0) & (index < count - 1)

    @pl.when(inside)
    def _():
        pl.semaphore_wait(barrier, 2)

    @pl.when(jnp.logical_not(inside))
    def _():
        pl.semaphore_wait(barrier, 1)

    return index, count


def attend_kernel(
    window, scale, rows_ref, weight_ref, gate_ref, gains_ref, cosine_ref, sine_ref, start_ref,
    raw_ref, query_ref, pair_ref, stats_ref, across_ref, attended_ref, gated_ref,
    weight, pairs, send_sem, recv_sem,
):
    count_rows, length, _ = rows_ref.shape
    query_cols = query_ref.shape[2]
    heads = query_cols // HEAD_WIDTH
    keys_at = pl.ds(0, HEAD_WIDTH)
    values_at = pl.ds(HEAD_WIDTH, HEAD_WIDTH)
    index, count = greet_line()

    def hop(turn, row):
        return pltpu.make_async_remote_copy(
            src_ref=pairs.at[window - turn + 1, row],
            dst_ref=pairs.at[window - turn, row],
            send_sem=send_sem.at[turn - 1, row],
            recv_sem=recv_sem.at[turn - 1, row],
            device_id={"seq": lax.rem(index + 1, count)},
            device_id_type=pl.DeviceIdType.MESH,
        )

    block = weight_ref.shape[0] * weight_ref.shape[2]
    own = raw_ref.shape[2]
    for step in range(TEAM_SIZE):
        weight[pl.ds(step * block, block), pl.ds(0, own)] = whole_block(
            weight_ref, step, pl.ds(0, own)
        )
    weight[:, pl.ds(own, LANES)] = gate_ref[...]

    def project(row, carry):
        products = jnp.dot(rows_ref[row], weight[...], preferred_element_type=jnp.float32)
        raw = products[:, : query_cols + 2 * HEAD_WIDTH].astype(jnp.bfloat16)
        raw_ref[row] = raw
        cosine, sine = cosine_ref[row], sine_ref[row]
        key = norm_turn(
            raw[:, query_cols : query_cols + HEAD_WIDTH].astype(jnp.float32),
            gains_ref[1:2], cosine, sine,
        )
        pairs[window, row, :, keys_at] = key.astype(jnp.bfloat16)
        pairs[window, row, :, values_at] = raw[:, query_cols + HEAD_WIDTH :]

        @pl.when(index < count - 1)
        def _():
            hop(1, row).start()

        for head in range(heads):
            columns = slice(head * HEAD_WIDTH, (head + 1) * HEAD_WIDTH)
            query_ref[row, :, columns] = norm_turn(
                raw[:, columns].astype(jnp.float32), gains_ref[0:1], cosine, sine
            ).astype(jnp.bfloat16)
        stats_ref[row] = jax.nn.sigmoid(products[:, query_cols + 2 * HEAD_WIDTH :])
        return carry

    lax.fori_loop(0, count_rows, project, 0)

    @pl.when(index == 0)
    def _():
        for slot in range(window):
            pairs[slot] = jnp.zeros_like(pairs[slot])

    for turn in range(2, window + 1):

        def forward(row, carry):
            @pl.when(index > 0)
            def _():
                hop(turn - 1, row).wait_recv()

            @pl.when(index < count - 1)
            def _():
                hop(turn, row).start()

            return carry

        lax.fori_loop(0, count_rows, forward, 0)

    places = lax.broadcasted_iota(jnp.int32, (length, (window + 1) * length), 1)
    latest = window * length + lax.broadcasted_iota(jnp.int32, places.shape, 0)
    lane = lax.broadcasted_iota(jnp.int32, (length, LANES), 1)

    def attend(row, carry):
        @pl.when(index > 0)
        def _():
            hop(window, row).wait_recv()

        allowed = (places >= start_ref[row]) & (places <= latest)
        keys = pairs[:, row, :, keys_at].reshape(-1, HEAD_WIDTH)
        values = pairs[:, row, :, values_at].reshape(-1, HEAD_WIDTH)
        stats = stats_ref[row]
        for head in range(heads):
            columns = slice(head * HEAD_WIDTH, (head + 1) * HEAD_WIDTH)
            scores = dot_t(query_ref[row, :, columns], keys) * scale
            scores = jnp.where(allowed, scores, NEGATIVE)
            top = jnp.max(scores, axis=1, keepdims=True)
            powers = jnp.exp(scores - top)
            total = jnp.sum(powers, axis=1, keepdims=True)
            low_probs = (powers * (1.0 / total)).astype(jnp.bfloat16)
            output = jnp.dot(low_probs, values, preferred_element_type=jnp.float32)
            output = output.astype(jnp.bfloat16)
            attended_ref[row, :, columns] = output
            gated_ref[row, :, columns] = (
                output.astype(jnp.float32) * stats[:, head : head + 1]
            ).astype(jnp.bfloat16)
            stats = jnp.where(lane == heads + head, top + jnp.log(total), stats)
        stats_ref[row] = stats
        across_ref[row] = stats.T[:SUBLANES]
        pair_ref[:, row] = pairs[:, row]
        return carry

    lax.fori_loop(0, count_rows, attend, 0)

    @pl.when(index < count - 1)
    def _():
        for turn in range(1, window + 1):

            def finish(row, carry):
                hop(turn, row).wait_send()
                return carry

            lax.fori_loop(0, count_rows, finish, 0)


def attend(
    normed_rows, own_attention, own_gate, gains, cosine, sine, starts, query_cols, window, collective_id
):
    rows, length, _ = normed_rows.shape
    width = query_cols + 2 * HEAD_WIDTH + LANES
    bf16 = jnp.bfloat16
    vmem = pl.BlockSpec(memory_space=pltpu.VMEM)
    return pl.pallas_call(
        functools.partial(attend_kernel, window, HEAD_WIDTH ** (-0.5)),
        out_shape=[
            jax.ShapeDtypeStruct((rows, length, query_cols + 2 * HEAD_WIDTH), bf16),
            jax.ShapeDtypeStruct((rows, length, query_cols), bf16),
            jax.ShapeDtypeStruct((window + 1, rows, length, 2 * HEAD_WIDTH), bf16),
            jax.ShapeDtypeStruct((rows, length, LANES), jnp.float32),
            jax.ShapeDtypeStruct((rows, SUBLANES, length), jnp.float32),
            jax.ShapeDtypeStruct((rows, length, query_cols), bf16),
            jax.ShapeDtypeStruct((rows, length, query_cols), bf16),
        ],
        in_specs=[vmem] * 7,
        out_specs=[vmem] * 7,
        scratch_shapes=[
            pltpu.VMEM((MODEL_WIDTH, width), bf16),
            pltpu.VMEM((window + 1, rows, length, 2 * HEAD_WIDTH), bf16),
            pltpu.SemaphoreType.DMA((window, rows)),
            pltpu.SemaphoreType.DMA((window, rows)),
        ],
        compiler_params=pltpu.CompilerParams(
            collective_id=collective_id, has_side_effects=True, vmem_limit_bytes=VMEM_BYTES
        ),
        cost_estimate=pl.CostEstimate(
            flops=2 * rows * length * MODEL_WIDTH * width,
            bytes_accessed=ATTEND_COST * rows * length * MODEL_WIDTH,
            transcendentals=0,
        ),
    )(normed_rows, own_attention, own_gate, gains, cosine, sine, starts)


def attend_back_kernel(
    window, scale, rows_ref, weight_ref, gains_ref, cosine_ref, sine_ref, start_ref,
    raw_ref, query_ref, pair_ref, stats_ref, across_ref, attended_ref,
    products_ref, gain_ref,
    weight, parts, outs, ins, send_sem, recv_sem,
):
    count_rows, length, _ = rows_ref.shape
    query_cols = query_ref.shape[2]
    heads = query_cols // HEAD_WIDTH
    keys_at = pl.ds(0, HEAD_WIDTH)
    values_at = pl.ds(HEAD_WIDTH, HEAD_WIDTH)
    index, count = greet_line()
    lag = 2

    def hop(turn, row):
        return pltpu.make_async_remote_copy(
            src_ref=outs.at[turn - 1, row],
            dst_ref=ins.at[turn - 1, row],
            send_sem=send_sem.at[turn - 1, row],
            recv_sem=recv_sem.at[turn - 1, row],
            device_id={"seq": lax.rem(index + count - 1, count)},
            device_id_type=pl.DeviceIdType.MESH,
        )

    keys_total = (window + 1) * length
    places = lax.broadcasted_iota(jnp.int32, (keys_total, length), 0)
    latest = window * length + lax.broadcasted_iota(jnp.int32, places.shape, 1)
    lane = lax.broadcasted_iota(jnp.int32, (length, LANES), 1)
    gain_ref[...] = jnp.zeros_like(gain_ref)
    share = weight_ref.shape[3] - query_cols
    for step in range(TEAM_SIZE):
        weight[:, pl.ds(step * query_cols, query_cols)] = whole_block(
            weight_ref, step, pl.ds(share, query_cols)
        )

    @pl.when(index == count - 1)
    def _():
        ins[...] = jnp.zeros_like(ins)

    def compute(row):
        grad_gated = dot_t(rows_ref[row], weight[...])
        keys = pair_ref[:, row, :, keys_at].reshape(-1, HEAD_WIDTH)
        values = pair_ref[:, row, :, values_at].reshape(-1, HEAD_WIDTH)
        allowed = (places >= start_ref[row]) & (places <= latest)
        cosine, sine = cosine_ref[row], sine_ref[row]
        grad_pre = jnp.zeros((length, LANES), jnp.float32)
        grad_keys = jnp.zeros((keys_total, HEAD_WIDTH), jnp.float32)
        grad_values = jnp.zeros((keys_total, HEAD_WIDTH), jnp.float32)
        for head in range(heads):
            columns = slice(head * HEAD_WIDTH, (head + 1) * HEAD_WIDTH)
            gate = stats_ref[row, :, head : head + 1]
            own = grad_gated[:, columns]
            grad_out = (own * gate).astype(jnp.bfloat16)
            grad_gate = jnp.sum(
                own * attended_ref[row, :, columns].astype(jnp.float32), axis=1, keepdims=True
            )
            grad_pre = jnp.where(lane == head, grad_gate * gate * (1.0 - gate), grad_pre)
            query = query_ref[row, :, columns]
            scores = jnp.where(allowed, dot_t(keys, query) * scale, NEGATIVE)
            probs = jnp.exp(scores - across_ref[row, heads + head : heads + head + 1])
            grad_probs = dot_t(values, grad_out)
            inner = jnp.sum(probs * grad_probs, axis=0, keepdims=True)
            grad_scores = (probs * (grad_probs - inner)).astype(jnp.bfloat16)
            grad_values = grad_values + jnp.dot(
                probs.astype(jnp.bfloat16), grad_out, preferred_element_type=jnp.float32
            )
            grad_keys = grad_keys + jnp.dot(
                grad_scores, query, preferred_element_type=jnp.float32
            )
            grad_query = dot_tokens(grad_scores, keys) * scale
            grad_raw, gain = norm_turn_back(
                raw_ref[row, :, columns].astype(jnp.float32), gains_ref[0:1], cosine, sine,
                grad_query,
            )
            products_ref[row, :, columns] = grad_raw.astype(jnp.bfloat16)
            gain_ref[0:1] += jnp.sum(gain, axis=0, keepdims=True)
        products_ref[row, :, query_cols + 2 * HEAD_WIDTH :] = grad_pre.astype(jnp.bfloat16)
        parts[:, row, :, keys_at] = (grad_keys * scale).reshape(window + 1, length, HEAD_WIDTH)
        parts[:, row, :, values_at] = grad_values.reshape(window + 1, length, HEAD_WIDTH)

    def finish(row):
        grad_pair = parts[window, row] + ins[window - 1, row].astype(jnp.float32)
        grad_raw, gain = norm_turn_back(
            raw_ref[row, :, query_cols : query_cols + HEAD_WIDTH].astype(jnp.float32),
            gains_ref[1:2], cosine_ref[row], sine_ref[row], grad_pair[:, :HEAD_WIDTH],
        )
        products_ref[row, :, query_cols : query_cols + HEAD_WIDTH] = grad_raw.astype(jnp.bfloat16)
        products_ref[row, :, query_cols + HEAD_WIDTH : query_cols + 2 * HEAD_WIDTH] = grad_pair[
            :, HEAD_WIDTH:
        ].astype(jnp.bfloat16)
        gain_ref[1:2] += jnp.sum(gain, axis=0, keepdims=True)

    def step(turn_row, carry):
        @pl.when(turn_row < count_rows)
        def _():
            compute(turn_row)

        for turn in range(1, window + 2):
            row = turn_row - lag * (turn - 1)

            @pl.when((row >= 0) & (row < count_rows))
            def _():
                if turn > 1:

                    @pl.when(index < count - 1)
                    def _():
                        hop(turn - 1, row).wait_recv()

                if turn == window + 1:
                    finish(row)
                else:
                    part = parts[turn - 1, row]
                    if turn > 1:
                        part = part + ins[turn - 2, row].astype(jnp.float32)
                    outs[turn - 1, row] = part.astype(jnp.bfloat16)

                    @pl.when(index > 0)
                    def _():
                        hop(turn, row).start()

        return carry

    lax.fori_loop(0, count_rows + lag * window, step, 0)

    @pl.when(index > 0)
    def _():
        for turn in range(1, window + 1):

            def done(row, carry):
                hop(turn, row).wait_send()
                return carry

            lax.fori_loop(0, count_rows, done, 0)


def attend_back(
    grad_rows, own_attention, gains, cosine, sine, starts, saved, window, collective_id
):
    rows, length, _ = grad_rows.shape
    query_cols = saved[1].shape[2]
    width = query_cols + 2 * HEAD_WIDTH + LANES
    bf16 = jnp.bfloat16
    vmem = pl.BlockSpec(memory_space=pltpu.VMEM)
    return pl.pallas_call(
        functools.partial(attend_back_kernel, window, HEAD_WIDTH ** (-0.5)),
        out_shape=[
            jax.ShapeDtypeStruct((rows, length, width), bf16),
            jax.ShapeDtypeStruct((SUBLANES, HEAD_WIDTH), jnp.float32),
        ],
        in_specs=[vmem] * 12,
        out_specs=[vmem] * 2,
        scratch_shapes=[
            pltpu.VMEM((query_cols, MODEL_WIDTH), bf16),
            pltpu.VMEM((window + 1, rows, length, 2 * HEAD_WIDTH), jnp.float32),
            pltpu.VMEM((window, rows, length, 2 * HEAD_WIDTH), bf16),
            pltpu.VMEM((window, rows, length, 2 * HEAD_WIDTH), bf16),
            pltpu.SemaphoreType.DMA((window, rows)),
            pltpu.SemaphoreType.DMA((window, rows)),
        ],
        compiler_params=pltpu.CompilerParams(
            collective_id=collective_id, has_side_effects=True, vmem_limit_bytes=VMEM_BYTES
        ),
        cost_estimate=pl.CostEstimate(
            flops=2 * rows * length * MODEL_WIDTH * query_cols,
            bytes_accessed=ATTEND_COST * rows * length * MODEL_WIDTH,
            transcendentals=0,
        ),
    )(grad_rows, own_attention, gains, cosine, sine, starts, *saved)


def team_columns(matrix, widths):
    pieces = []
    lower = 0
    for width in widths:
        piece = matrix[:, lower : lower + width]
        pieces.append(piece.reshape(matrix.shape[0], TEAM_SIZE, width // TEAM_SIZE))
        lower = lower + width
    return jnp.concatenate(pieces, axis=2).transpose(1, 0, 2)


def gather_parts(blocks):
    return lax.all_gather(blocks, DEPTH, axis=0, tiled=False)


def scatter_parts(parts):
    depth, team, rows, width = parts.shape
    return lax.psum_scatter(
        parts.reshape(depth * team * rows, width), DEPTH, scatter_dimension=0, tiled=True
    ).reshape(team, rows, width)


def gather_rows(matrix):
    return lax.all_gather(matrix, DEPTH, axis=0, tiled=True)


def scatter_rows(gradient):
    return lax.psum_scatter(gradient, DEPTH, scatter_dimension=0, tiled=True)


def shards(
    inputs,
    cotangent,
    doc_lengths,
    projection_weight,
    projection_moment,
    projection_second,
    out_weight,
    out_moment,
    out_second,
    ffn_weight,
    ffn_moment,
    ffn_second,
    down_weight,
    down_moment,
    down_second,
    head_gate,
    gate_moment,
    gate_second,
    norm_gains,
    gains_moment,
    gains_second,
    qk_gains,
    qk_moment,
    qk_second,
):
    rows_dev, local_len, width = inputs.shape
    bf16 = jnp.bfloat16
    team = lax.axis_index(TEAM)
    place_seq = lax.axis_index("seq")
    group_heads = QUERY_HEADS // KEY_VALUE_HEADS
    window = -(-(DOC_MOST - 1) // local_len)
    window = min(window, lax.axis_size("seq") - 1)
    query_cols = QUERY_HEADS * HEAD_WIDTH
    key_value_columns = KEY_VALUE_HEADS * HEAD_WIDTH
    widths_qkv = (query_cols, key_value_columns, key_value_columns)
    widths_ffn = (FF, FF)
    own_query = query_cols // TEAM_SIZE
    own_key = key_value_columns // TEAM_SIZE
    own_ff = FF // TEAM_SIZE
    own_gate = lax.dynamic_slice_in_dim(head_gate.astype(bf16), team * group_heads, group_heads, 1)
    own_gate = jnp.pad(own_gate, ((0, 0), (0, LANES - group_heads)))
    own_attention = gather_parts(
        jnp.concatenate(
            [
                team_exchange(team_columns(projection_weight.astype(bf16), widths_qkv)),
                team_columns(out_weight.astype(bf16), (MODEL_WIDTH,)),
            ],
            axis=2,
        )
    )
    ffn_blocks = team_exchange(team_columns(ffn_weight.astype(bf16), widths_ffn))
    own_inner = gather_parts(ffn_blocks[:, :, :own_ff])
    lengths = lax.all_gather(doc_lengths, TEAM, axis=0, tiled=True)
    place = place_seq * local_len + jnp.arange(local_len, dtype=jnp.int32)
    position = positions(lengths, place)
    cosine, sine = rotary_tables(position, HEAD_WIDTH)
    starts = window * local_len + jnp.arange(local_len, dtype=jnp.int32)[None, :] - position
    inputs_flat = inputs[0].astype(jnp.float32)
    normed = rms_apply(inputs_flat, norm_gains[0]).astype(bf16)
    normed_all, grad_all = gather_team([normed, cotangent[0]], 0)
    raw, query_rot, pairs, stats, across, attended, gated = attend(
        normed_all.reshape(TEAM_SIZE, local_len, MODEL_WIDTH),
        own_attention,
        own_gate,
        qk_gains,
        cosine,
        sine,
        starts[:, :, None],
        own_query,
        window,
        8,
    )
    gated, up_blocks, low_down = lax.optimization_barrier(
        (gated, ffn_blocks[:, :, own_ff:], down_weight.astype(bf16))
    )
    own_up = gather_parts(up_blocks)
    own_down = gather_rows(low_down)
    middle = inputs_flat + scatter_team(product_out, [gated.reshape(-1, own_query)], [own_attention], 1)
    normed2 = rms_apply(middle, norm_gains[1]).astype(bf16)
    normed2_all = gather_team([normed2], 2)[0]
    hidden, slope, swish = ffn_forward(normed2_all, own_inner, own_up)
    grad_final = cotangent[0].astype(jnp.float32)
    down_part, own_down = lax.optimization_barrier(
        (low_tokens(hidden.reshape(-1, own_ff), grad_all), own_down)
    )
    grad_inner, grad_up = ffn_back(grad_all, own_down, slope, swish)
    grad_inner, grad_up = grad_inner.reshape(-1, own_ff), grad_up.reshape(-1, own_ff)
    inner_part, grad_inner = lax.optimization_barrier(
        (weight_parts(normed2_all, grad_inner, ffn_weight.shape[0]), grad_inner)
    )
    down_sum = scatter_rows(down_part)
    grad_normed2 = scatter_team(
        product_ffn_back, [grad_inner, grad_up], [own_inner, own_up], 4
    )
    grad_mid_part, gain_mid = rms_back(middle, norm_gains[1], grad_normed2)
    grad_middle = grad_final + grad_mid_part
    grad_low, down_sum = lax.optimization_barrier((grad_middle.astype(bf16), down_sum))
    inner_sum = scatter_parts(inner_part)
    grad_middle_all, up_part = gather_team(
        [grad_low],
        5,
        weight_work,
        (normed2_all, grad_up),
        (weight_shape(normed2_all, grad_up, ffn_weight.shape[0]),),
    )
    grad_products, gain_sums = attend_back(
        grad_middle_all.reshape(TEAM_SIZE, local_len, MODEL_WIDTH),
        own_attention,
        qk_gains,
        cosine,
        sine,
        starts[:, None, :],
        (raw, query_rot, pairs, stats, across, attended),
        window,
        9,
    )
    grad_products = grad_products.reshape(-1, grad_products.shape[2])
    up_part, grad_products, inner_sum = lax.optimization_barrier(
        (up_part, grad_products, inner_sum)
    )
    up_sum = scatter_parts(up_part)
    grad_normed, attention_part, gate_part = scatter_team(
        product_qkv_back,
        [grad_products],
        [own_attention, own_gate],
        6,
        attention_weight_work,
        (normed_all, grad_products, gated.reshape(-1, own_query), grad_middle_all),
        attention_weight_shapes(normed_all, grad_products, out_weight.shape[0]),
    )
    late_hidden, grad_normed = lax.optimization_barrier((hidden, grad_normed))
    attention_sum = scatter_parts(attention_part)
    final = middle + scatter_team(product_down, [late_hidden.reshape(-1, own_ff)], [own_down], 3)
    result = final.astype(bf16).reshape(inputs.shape)
    grad_in_part, gain_in = rms_back(inputs_flat, norm_gains[0], grad_normed)
    input_grad = (grad_middle + grad_in_part).reshape(inputs.shape)
    ffn_rows = team_exchange(jnp.concatenate([inner_sum, up_sum], axis=2))
    (
        ffn_moment_new,
        ffn_second_new,
        ffn_update,
        down_moment_new,
        down_second_new,
        down_update,
        ffn_squares,
    ) = ffn_moments(
        ffn_rows,
        down_sum,
        (ffn_weight, ffn_moment, ffn_second),
        (down_weight, down_moment, down_second),
    )
    attention_sum, ffn_squares = lax.optimization_barrier((attention_sum, ffn_squares))
    own_projection = own_query + 2 * own_key
    (
        projection_moment_next,
        projection_second_next,
        projection_update,
        out_moment_new,
        out_second_new,
        out_update,
        squares,
    ) = attention_moments(
        team_exchange(attention_sum[:, :, :own_projection]),
        attention_sum,
        (projection_weight, projection_moment, projection_second),
        (out_weight, out_moment, out_second),
    )
    gate_total, gains_total, qk_total, norms = totals(
        group_heads,
        gate_part,
        (jnp.sum(gain_in, axis=0), jnp.sum(gain_mid, axis=0)),
        gain_sums,
        squares,
        ffn_squares,
        10,
    )
    query_steps = STEPS * query_cols // (query_cols + 2 * key_value_columns)
    key_steps = STEPS * key_value_columns // (query_cols + 2 * key_value_columns)
    (
        projection_weight_next,
        qkv_copy,
        out_new,
        out_copy,
        ffn_new,
        ffn_copy,
        down_new,
        down_copy,
        head_gate_new,
        gate_moment_new,
        gate_second_new,
        gains_new,
        gains_moment_new,
        gains_second_new,
        qk_new,
        qk_moment_new,
        qk_second_new,
        norms,
    ) = apply_all(
        norms,
        gate_total,
        gains_total,
        qk_total,
        (
            (projection_weight, projection_update),
            (out_weight, out_update),
            (ffn_weight, ffn_update),
            (down_weight, down_update),
        ),
        (
            (0, (query_steps, query_steps + key_steps)),
            (3, ()),
            (4, (STEPS // 2,)),
            (6, ()),
        ),
        (
            (head_gate.T, gate_moment.T, gate_second.T),
            (norm_gains, gains_moment, gains_second),
            (qk_gains, qk_moment, qk_second),
        ),
    )
    return (
        result,
        input_grad,
        projection_weight_next,
        projection_moment_next,
        projection_second_next,
        qkv_copy,
        out_new,
        out_moment_new,
        out_second_new,
        out_copy,
        ffn_new,
        ffn_moment_new,
        ffn_second_new,
        ffn_copy,
        down_new,
        down_moment_new,
        down_second_new,
        down_copy,
        head_gate_new.T,
        gate_moment_new.T,
        gate_second_new.T,
        gains_new,
        gains_moment_new,
        gains_second_new,
        qk_new,
        qk_moment_new,
        qk_second_new,
        norms[:2, :7],
    )


def solution(mesh):
    mesh = Mesh(
        mesh.devices.reshape(2, 2, 2, mesh.shape["fsdp"] // TEAM_SIZE, mesh.shape["seq"]),
        TEAM + DEPTH,
    )
    rows = TEAM + DEPTH[:1]
    in_specs = (
        P(rows, "seq", None),
        P(rows, "seq", None),
        P(rows, None),
        P(TEAM + DEPTH, None),
        P(TEAM + DEPTH, None),
        P(TEAM + DEPTH, None),
        P(TEAM + DEPTH, None),
        P(TEAM + DEPTH, None),
        P(TEAM + DEPTH, None),
        P(TEAM + DEPTH, None),
        P(TEAM + DEPTH, None),
        P(TEAM + DEPTH, None),
        P(TEAM + DEPTH, None),
        P(TEAM + DEPTH, None),
        P(TEAM + DEPTH, None),
        P(),
        P(),
        P(),
        P(),
        P(),
        P(),
        P(),
        P(),
        P(),
    )
    out_specs = (
        P(rows, "seq", None),
        P(rows, "seq", None),
        P(TEAM + DEPTH, None),
        P(TEAM + DEPTH, None),
        P(TEAM + DEPTH, None),
        P(TEAM + DEPTH, None),
        P(TEAM + DEPTH, None),
        P(TEAM + DEPTH, None),
        P(TEAM + DEPTH, None),
        P(TEAM + DEPTH, None),
        P(TEAM + DEPTH, None),
        P(TEAM + DEPTH, None),
        P(TEAM + DEPTH, None),
        P(TEAM + DEPTH, None),
        P(TEAM + DEPTH, None),
        P(TEAM + DEPTH, None),
        P(TEAM + DEPTH, None),
        P(TEAM + DEPTH, None),
        P(),
        P(),
        P(),
        P(),
        P(),
        P(),
        P(),
        P(),
        P(),
        P(),
    )
    return jax.shard_map(shards, mesh=mesh, in_specs=in_specs, out_specs=out_specs, check_vma=False)
```

```python
import functools

import jax
import jax.numpy as jnp
from jax import lax
from jax.experimental import pallas as pl
from jax.experimental.pallas import tpu as pltpu
from jax.sharding import Mesh
from jax.sharding import PartitionSpec as P

MODEL_WIDTH = 2048
QUERY_HEADS = 16
KEY_VALUE_HEADS = 8
HEAD_WIDTH = 128
FF = 6144
ROW_TOKENS = 1024
STEP = 3
DOC_MOST = 512
TEAM_SIZE = 8
TEAM = ("t2", "t1", "t0")
DEPTH = ("spare", "seq")
LANES = 128
SUBLANES = 8
VMEM_BYTES = 60 << 20
GATHER_VMEM = 60 << 20
LAMB_COST = 70
GATHER_COST = 250
SCATTER_COST = 320
ATTEND_COST = 50


NORM_EPS = 1e-06
ADAM_EPS = 1e-06
RATE = 0.3
DECAY = 0.01
BETA = 0.5
THETA = 1000000.0
NEGATIVE = -1e30


def rms_apply(value_rows, gain):
    return (
        value_rows
        * lax.rsqrt(jnp.mean(value_rows * value_rows, axis=-1, keepdims=True) + NORM_EPS)
        * gain
    )


def rms_back(value_rows, gain, gradient):
    scale = lax.rsqrt(jnp.mean(value_rows * value_rows, axis=-1, keepdims=True) + NORM_EPS)
    scaled = gradient * gain
    inner = jnp.mean(scaled * value_rows, axis=-1, keepdims=True)
    grad_value = scale * scaled - value_rows * scale * scale * scale * inner
    grad_gain = gradient * value_rows * scale
    return (grad_value, grad_gain)


def dot_t(left, right):
    return lax.dot_general(
        left, right, (((1,), (1,)), ((), ())), preferred_element_type=jnp.float32
    )


def low_tokens(left, right):
    return dot_tokens(left, right).astype(jnp.bfloat16)


def dot_tokens(left, right):
    return lax.dot_general(
        left, right, (((0,), (0,)), ((), ())), preferred_element_type=jnp.float32
    )


def moments(weight, moment, second, gradient):
    moment_new = BETA * moment + (1.0 - BETA) * gradient
    second_new = BETA * second + (1.0 - BETA) * gradient * gradient
    correction = 1.0 - BETA**STEP
    update = (
        moment_new / correction / (jnp.sqrt(second_new / correction) + ADAM_EPS) + DECAY * weight
    )
    return (moment_new, second_new, update)


def rotary_tables(position, width):
    half = width // 2
    rates = THETA ** (-jnp.arange(half, dtype=jnp.float32) * 2.0 / width)
    angle = position.astype(jnp.float32)[..., None] * rates
    cosine, sine = jnp.cos(angle), jnp.sin(angle)
    return (
        jnp.concatenate([cosine, cosine], axis=-1),
        jnp.concatenate([-sine, sine], axis=-1),
    )


def positions(lengths, place):
    ends = jnp.cumsum(lengths, axis=1)
    starts = ends - lengths
    inside = (place[None, :, None] >= starts[:, None, :]) & (place[None, :, None] < ends[:, None, :])
    return place[None, :] - jnp.sum(jnp.where(inside, starts[:, None, :], 0), axis=2)


def team_place():
    return tuple(lax.axis_index(axis) for axis in TEAM)


def greet_team(place):
    barrier = pltpu.get_barrier_semaphore()
    for axis, index in zip(TEAM, place):
        pl.semaphore_signal(
            barrier, inc=1, device_id={axis: 1 - index}, device_id_type=pl.DeviceIdType.MESH
        )
    pl.semaphore_wait(barrier, len(TEAM))


def member(place, flips):
    index = 0
    for own, flip in zip(place, flips):
        index = index * 2 + (1 - own if flip else own)
    return index


def gather_kernel(count, work, *refs):
    given, made = (work[1], work[2]) if work else (0, 0)
    owns, operands = refs[:count], refs[count : count + given]
    alls = refs[count + given : 2 * count + given]
    results = refs[2 * count + given : 2 * count + given + made]
    own_sem, send_sem, recv_sem = refs[2 * count + given + made :]
    place = team_place()
    greet_team(place)
    me = member(place, (0, 0, 0))
    beside = member(place, (0, 1, 0))
    above = member(place, (1, 0, 0))
    across = member(place, (1, 1, 0))
    copies = [{} for _ in range(count)]
    keeps = []

    def send(item, number, axis, source, target):
        copy = pltpu.make_async_remote_copy(
            src_ref=source,
            dst_ref=target,
            send_sem=send_sem.at[item, number],
            recv_sem=recv_sem.at[item, number],
            device_id={TEAM[axis]: 1 - place[axis]},
            device_id_type=pl.DeviceIdType.MESH,
        )
        copy.start()
        copies[item][number] = copy

    def halves(item):
        half = owns[item].shape[0] // 2
        return pl.ds(0, half), pl.ds(half, half)

    for item in range(count):
        target = alls[item].at[me]
        send(item, 0, 1, owns[item], target)
        send(item, 1, 0, owns[item], target)
        send(item, 2, 2, owns[item], target)
        keeps.append(pltpu.make_async_copy(owns[item], target, own_sem.at[item]))
        keeps[item].start()
    if work:
        work[0](*operands, *results)
    for item in range(count):
        upper, lower = halves(item)
        copies[item][0].wait_recv()
        block = alls[item].at[beside]
        send(item, 3, 0, block.at[upper], block.at[upper])
        send(item, 4, 2, block, block)
        copies[item][1].wait_recv()
        block = alls[item].at[above]
        send(item, 5, 1, block.at[lower], block.at[lower])
        send(item, 6, 2, block, block)
    for item in range(count):
        upper, lower = halves(item)
        block = alls[item].at[across]
        copies[item][3].wait_recv()
        send(item, 7, 2, block.at[upper], block.at[upper])
        copies[item][5].wait_recv()
        send(item, 8, 2, block.at[lower], block.at[lower])
    for item in range(count):
        for number in (2, 4, 6, 7, 8):
            copies[item][number].wait_recv()
        for number in range(9):
            copies[item][number].wait_send()
        keeps[item].wait()


def gather_team(arrays, collective_id, work=None, operands=(), results=()):
    count = len(arrays)
    anywhere = pl.BlockSpec(memory_space=pl.ANY)
    out_shape = [jax.ShapeDtypeStruct((TEAM_SIZE,) + own.shape, own.dtype) for own in arrays]
    gathered = pl.pallas_call(
        functools.partial(
            gather_kernel, count, (work, len(operands), len(results)) if work else None
        ),
        out_shape=out_shape + list(results),
        in_specs=[anywhere] * (count + len(operands)),
        out_specs=[anywhere] * (count + len(results)),
        scratch_shapes=[
            pltpu.SemaphoreType.DMA((count,)),
            pltpu.SemaphoreType.DMA((count, 9)),
            pltpu.SemaphoreType.DMA((count, 9)),
        ],
        compiler_params=pltpu.CompilerParams(
            collective_id=collective_id, has_side_effects=True, vmem_limit_bytes=GATHER_VMEM
        ),
        cost_estimate=pl.CostEstimate(
            flops=0,
            bytes_accessed=sum(GATHER_COST * own.shape[0] * own.shape[1] for own in arrays),
            transcendentals=0,
        ),
    )(*arrays, *operands)
    return [
        whole.reshape(TEAM_SIZE * own.shape[0], own.shape[1])
        for whole, own in zip(gathered, arrays)
    ] + list(gathered[count:])


def scatter_kernel(product, count, work, *refs):
    given, made = (work[1], work[2]) if work else (0, 0)
    operands, extra = refs[:count], refs[count : count + given]
    sum_ref = refs[count + given]
    results = refs[count + given + 1 : count + given + 1 + made]
    own, out_near, in_near, out_far, in_half, in_full, send_sem, recv_sem = refs[
        count + given + 1 + made :
    ]
    place = team_place()
    greet_team(place)
    rows = sum_ref.shape[0]
    half = rows // 2
    upper, lower = pl.ds(0, half), pl.ds(half, half)

    def send(number, axis, source, target):
        copy = pltpu.make_async_remote_copy(
            src_ref=source,
            dst_ref=target,
            send_sem=send_sem.at[number],
            recv_sem=recv_sem.at[number],
            device_id={TEAM[axis]: 1 - place[axis]},
            device_id_type=pl.DeviceIdType.MESH,
        )
        copy.start()
        return copy

    flips = ((1, 1), (0, 1), (1, 0), (0, 0))
    near, far = [], {}
    is_first = place[2] == 0

    def begin(turn):
        first, second = flips[turn]
        pair = member(place[:2], (first, second))

        def one(step, columns):
            both = product(operands, pair, step, columns)
            former, latter = both[:rows], both[rows:]
            out_near[turn, :, columns] = jnp.where(is_first, latter, former).astype(jnp.bfloat16)
            own[turn, :, columns] = jnp.where(is_first, former, latter)

        over_tiles(sum_ref.shape[1], one)
        near.append(send(turn, 2, out_near.at[turn], in_near.at[turn]))

    def join(turn):
        near[turn].wait_recv()
        return own[turn] + in_near[turn].astype(jnp.float32)

    begin(0)
    begin(1)
    out_far[0] = join(0).astype(jnp.bfloat16)
    far[4] = send(4, 1, out_far.at[0, upper], in_half.at[0])
    far[5] = send(5, 0, out_far.at[0, lower], in_half.at[1])
    begin(2)
    own[1] = join(1)
    out_far[1, upper] = own[1, upper].astype(jnp.bfloat16)
    far[6] = send(6, 1, out_far.at[1, upper], in_full.at[0, upper])
    begin(3)
    own[2] = join(2)
    out_far[2, lower] = own[2, lower].astype(jnp.bfloat16)
    far[7] = send(7, 0, out_far.at[2, lower], in_full.at[1, lower])
    sum_ref[...] = join(3)
    far[5].wait_recv()
    out_far[1, lower] = (own[1, lower] + in_half[1].astype(jnp.float32)).astype(jnp.bfloat16)
    far[8] = send(8, 1, out_far.at[1, lower], in_full.at[0, lower])
    far[4].wait_recv()
    out_far[2, upper] = (own[2, upper] + in_half[0].astype(jnp.float32)).astype(jnp.bfloat16)
    far[9] = send(9, 0, out_far.at[2, upper], in_full.at[1, upper])
    if work:
        work[0](*extra, *results)
    far[6].wait_recv()
    far[7].wait_recv()
    far[8].wait_recv()
    far[9].wait_recv()
    sum_ref[...] = (
        sum_ref[...] + in_full[0].astype(jnp.float32) + in_full[1].astype(jnp.float32)
    )
    for copy in near + [far[number] for number in range(4, 10)]:
        copy.wait_send()


def over_tiles(width, one):
    tile = width // TEAM_SIZE

    def body(step, carry):
        one(step, pl.ds(pl.multiple_of(step * tile, tile), tile))
        return carry

    lax.fori_loop(0, TEAM_SIZE, body, 0)


def whole_block(ref, step, columns=slice(None)):
    block = ref[:, step, :, columns]
    return block.reshape(block.shape[0] * block.shape[1], block.shape[2])


def product_down(operands, pair, step, columns):
    hidden, weight = operands
    return jnp.dot(hidden[pair], weight[:, columns], preferred_element_type=jnp.float32)


def product_out(operands, pair, step, columns):
    gated, weight = operands
    depth = gated.shape[2]
    share = pl.ds(weight.shape[3] - depth, depth)
    return jnp.dot(
        gated[pair], whole_block(weight, step, share), preferred_element_type=jnp.float32
    )


def product_ffn_back(operands, pair, step, columns):
    grad_inner, grad_up, inner_weight, up_weight = operands
    return dot_t(grad_inner[pair], whole_block(inner_weight, step)) + dot_t(
        grad_up[pair], whole_block(up_weight, step)
    )


def product_qkv_back(operands, pair, step, columns):
    grad_products, weight, gate_weight = operands
    depth = grad_products.shape[2] - LANES
    share = pl.ds(0, depth)
    return dot_t(grad_products[pair, :, share], whole_block(weight, step, share)) + dot_t(
        grad_products[pair, :, pl.ds(depth, LANES)], gate_weight[columns, :]
    )


def scatter_team(
    product, lefts, rights, collective_id, work=None, operands=(), results=()
):
    rows = lefts[0].shape[0] // TEAM_SIZE
    depth = sum(left.shape[1] for left in lefts)
    width = MODEL_WIDTH
    paired = [left.reshape(TEAM_SIZE // 2, 2 * rows, left.shape[1]) for left in lefts]
    vmem = pl.BlockSpec(memory_space=pltpu.VMEM)
    anywhere = pl.BlockSpec(memory_space=pl.ANY)
    count = len(lefts) + len(rights)
    summed = pl.pallas_call(
        functools.partial(
            scatter_kernel, product, count, (work, len(operands), len(results)) if work else None
        ),
        out_shape=[jax.ShapeDtypeStruct((rows, width), jnp.float32)] + list(results),
        in_specs=[vmem] * count + [anywhere] * len(operands),
        out_specs=[vmem] + [anywhere] * len(results),
        scratch_shapes=[
            pltpu.VMEM((4, rows, width), jnp.float32),
            pltpu.VMEM((4, rows, width), jnp.bfloat16),
            pltpu.VMEM((4, rows, width), jnp.bfloat16),
            pltpu.VMEM((3, rows, width), jnp.bfloat16),
            pltpu.VMEM((2, rows // 2, width), jnp.bfloat16),
            pltpu.VMEM((2, rows, width), jnp.bfloat16),
            pltpu.SemaphoreType.DMA((10,)),
            pltpu.SemaphoreType.DMA((10,)),
        ],
        compiler_params=pltpu.CompilerParams(
            collective_id=collective_id, has_side_effects=True, vmem_limit_bytes=VMEM_BYTES
        ),
        cost_estimate=pl.CostEstimate(
            flops=2 * TEAM_SIZE * rows * depth * width,
            bytes_accessed=SCATTER_COST * rows * width,
            transcendentals=0,
        ),
    )(*paired, *rights, *operands)
    return summed if work else summed[0]


def ffn_kernel(rows_ref, inner_ref, up_ref, hidden_ref, slope_ref, swish_ref, inner_weight, up_weight):
    @pl.when(pl.program_id(0) == 0)
    def _():
        block = inner_ref.shape[0] * inner_ref.shape[2]
        for step in range(TEAM_SIZE):
            inner_weight[pl.ds(step * block, block), :] = whole_block(inner_ref, step)
            up_weight[pl.ds(step * block, block), :] = whole_block(up_ref, step)

    tile = 256

    def one(step, carry):
        columns = pl.ds(pl.multiple_of(step * tile, tile), tile)
        inner = jnp.dot(rows_ref[0], inner_weight[:, columns], preferred_element_type=jnp.float32)
        up_part = jnp.dot(rows_ref[0], up_weight[:, columns], preferred_element_type=jnp.float32)
        sigma = jax.nn.sigmoid(inner)
        swish = inner * sigma
        hidden_ref[0, :, columns] = (swish * up_part).astype(jnp.bfloat16)
        slope_ref[0, :, columns] = up_part * sigma * (1.0 + inner * (1.0 - sigma))
        swish_ref[0, :, columns] = swish
        return carry

    lax.fori_loop(0, hidden_ref.shape[2] // tile, one, 0, unroll=True)


def ffn_forward(normed_rows, inner_weight, up_weight):
    count, depth = TEAM_SIZE // 2, normed_rows.shape[1]
    length = normed_rows.shape[0] // count
    width = inner_weight.shape[3]
    whole = pl.BlockSpec(inner_weight.shape, lambda i: (0, 0, 0, 0), pipeline_mode=pl.Buffered(1))
    out = pl.BlockSpec((1, length, width), lambda i: (i, 0, 0))
    return pl.pallas_call(
        ffn_kernel,
        grid=(count,),
        out_shape=[
            jax.ShapeDtypeStruct((count, length, width), jnp.bfloat16),
            jax.ShapeDtypeStruct((count, length, width), jnp.float32),
            jax.ShapeDtypeStruct((count, length, width), jnp.float32),
        ],
        in_specs=[pl.BlockSpec((1, length, depth), lambda i: (i, 0, 0)), whole, whole],
        out_specs=[out, out, out],
        scratch_shapes=[pltpu.VMEM((depth, width), jnp.bfloat16)] * 2,
        compiler_params=pltpu.CompilerParams(vmem_limit_bytes=VMEM_BYTES),
        cost_estimate=pl.CostEstimate(
            flops=4 * count * length * depth * width,
            bytes_accessed=count * length * (2 * depth + 10 * width),
            transcendentals=count * length * width,
        ),
    )(normed_rows.reshape(count, length, depth), inner_weight, up_weight)


def ffn_back_kernel(grad_ref, weight_ref, slope_ref, swish_ref, inner_ref, up_ref):
    tile = 256

    def one(step, carry):
        columns = pl.ds(pl.multiple_of(step * tile, tile), tile)
        grad_hidden = dot_t(grad_ref[0], weight_ref[columns, :])
        inner_ref[0, :, columns] = (grad_hidden * slope_ref[0, :, columns]).astype(jnp.bfloat16)
        up_ref[0, :, columns] = (grad_hidden * swish_ref[0, :, columns]).astype(jnp.bfloat16)
        return carry

    lax.fori_loop(0, inner_ref.shape[2] // tile, one, 0, unroll=True)


def ffn_back(grad_rows, down_weight, slope, swish):
    count, length, width = slope.shape
    depth = grad_rows.shape[1]
    whole = pl.BlockSpec(down_weight.shape, lambda i: (0, 0), pipeline_mode=pl.Buffered(1))
    part = pl.BlockSpec((1, length, width), lambda i: (i, 0, 0))
    return pl.pallas_call(
        ffn_back_kernel,
        grid=(count,),
        out_shape=[jax.ShapeDtypeStruct((count, length, width), jnp.bfloat16)] * 2,
        in_specs=[pl.BlockSpec((1, length, depth), lambda i: (i, 0, 0)), whole, part, part],
        out_specs=[part, part],
        compiler_params=pltpu.CompilerParams(vmem_limit_bytes=VMEM_BYTES),
        cost_estimate=pl.CostEstimate(
            flops=2 * count * length * depth * width,
            bytes_accessed=count * length * (2 * depth + 12 * width),
            transcendentals=0,
        ),
    )(grad_rows.reshape(count, length, depth), down_weight, slope, swish)


def weight_kernel(left_ref, right_ref, part_ref):
    depth, _, rows, width = part_ref.shape
    part = dot_tokens(left_ref[...], right_ref[...])
    part_ref[...] = part.astype(jnp.bfloat16).reshape(depth, 1, rows, width)


def weight_shape(left, right, rows):
    depth = left.shape[1] // (TEAM_SIZE * rows)
    return jax.ShapeDtypeStruct((depth, TEAM_SIZE, rows, right.shape[1]), jnp.bfloat16)


def weight_specs(left, right, part):
    depth, _, rows, width = part.shape
    return dict(
        grid=(TEAM_SIZE,),
        in_specs=[
            pl.BlockSpec((left.shape[0], depth * rows), lambda i: (0, i)),
            pl.BlockSpec(right.shape, lambda i: (0, 0)),
        ],
        out_specs=[pl.BlockSpec((depth, 1, rows, width), lambda i: (0, i, 0, 0))],
    )


def weight_parts(left, right, rows):
    part = weight_shape(left, right, rows)
    (tokens, height), width = left.shape, right.shape[1]
    return pl.pallas_call(
        weight_kernel,
        out_shape=[part],
        compiler_params=pltpu.CompilerParams(vmem_limit_bytes=VMEM_BYTES),
        cost_estimate=pl.CostEstimate(
            flops=2 * tokens * height * width,
            bytes_accessed=2 * tokens * (height + width) + 2 * height * width,
            transcendentals=0,
        ),
        **weight_specs(left, right, part),
    )(left, right)[0]


def weight_work(left_ref, right_ref, part_ref):
    pltpu.emit_pipeline(weight_kernel, **weight_specs(left_ref, right_ref, part_ref))(
        left_ref, right_ref, part_ref
    )


def attention_weight_kernel(normed_ref, products_ref, gated_ref, grad_ref, part_ref, gate_ref):
    depth, _, rows, _ = part_ref.shape
    own = products_ref.shape[1] - LANES
    part = dot_tokens(normed_ref[...], products_ref[...])
    gate_ref[...] = part[:, own:].T[:SUBLANES]
    part_ref[:, :, :, pl.ds(0, own)] = (
        part[:, :own].astype(jnp.bfloat16).reshape(depth, 1, rows, own)
    )
    share = grad_ref.shape[1]
    part = dot_tokens(gated_ref[...], grad_ref[...])
    part_ref[:, :, :, pl.ds(own, share)] = part.astype(jnp.bfloat16).reshape(depth, 1, rows, share)


def attention_weight_work(*refs):
    normed, products, gated, grad, part, gate = refs
    depth, _, rows, width = part.shape
    share = depth * rows
    column = pl.BlockSpec((normed.shape[0], share), lambda i: (0, i))
    pltpu.emit_pipeline(
        attention_weight_kernel,
        grid=(TEAM_SIZE,),
        in_specs=[
            column,
            pl.BlockSpec(products.shape, lambda i: (0, 0)),
            pl.BlockSpec(gated.shape, lambda i: (0, 0)),
            column,
        ],
        out_specs=[
            pl.BlockSpec((depth, 1, rows, width), lambda i: (0, i, 0, 0)),
            pl.BlockSpec((SUBLANES, share), lambda i: (0, i)),
        ],
    )(*refs)


def attention_weight_shapes(normed, grad_products, rows):
    height, width = normed.shape[1], grad_products.shape[1]
    share = height // TEAM_SIZE
    return [
        jax.ShapeDtypeStruct((share // rows, TEAM_SIZE, rows, width - LANES + share), jnp.bfloat16),
        jax.ShapeDtypeStruct((SUBLANES, height), jnp.float32),
    ]


def greet_all():
    place = team_place()
    barrier = pltpu.get_barrier_semaphore()
    flips = [(step // 4, step // 2 % 2, step % 2) for step in range(1, TEAM_SIZE)]
    team = [
        (
            member(place, flip),
            {axis: 1 - at if turn else at for axis, at, turn in zip(TEAM, place, flip)},
        )
        for flip in flips
    ]
    sizes = [lax.axis_size(axis) for axis in DEPTH]
    depth = sizes[0] * sizes[1]
    spot = lax.axis_index(DEPTH[0]) * sizes[1] + lax.axis_index(DEPTH[1])
    line = []
    for step in range(1, depth):
        other = lax.rem(spot + step, depth)
        line.append({DEPTH[0]: other // sizes[1], DEPTH[1]: lax.rem(other, sizes[1])})
    for target in [device for _, device in team] + line:
        pl.semaphore_signal(
            barrier, inc=1, device_id=target, device_id_type=pl.DeviceIdType.MESH
        )
    pl.semaphore_wait(barrier, len(team) + len(line))
    return member(place, (0, 0, 0)), team, spot, line


def push(source, target, sems, number, device):
    copy = pltpu.make_async_remote_copy(
        src_ref=source,
        dst_ref=target,
        send_sem=sems.at[0, number],
        recv_sem=sems.at[1, number],
        device_id=device,
        device_id_type=pl.DeviceIdType.MESH,
    )
    copy.start()
    return copy


def begin_line(own, slots, sems, spot, line):
    slots[spot] = own[...]
    return [
        push(own, slots.at[spot], sems, number, device) for number, device in enumerate(line)
    ]


def begin_team(copies, slots, team_slots, sems, me, team):
    for copy in copies:
        copy.wait_recv()
    total = slots[0]
    for step in range(1, slots.shape[0]):
        total = total + slots[step]
    team_slots[me] = total
    return [
        push(team_slots.at[me], team_slots.at[me], sems, number, device)
        for number, (_, device) in enumerate(team)
    ]


def depth_size():
    return lax.axis_size(DEPTH[0]) * lax.axis_size(DEPTH[1])


def lane_squares(piece):
    total = jnp.sum(piece * piece, axis=0, keepdims=True)
    lanes = total[:, :LANES]
    for first in range(LANES, total.shape[1], LANES):
        lanes = lanes + total[:, first : first + LANES]
    return lanes


def in_lanes(values, shape):
    lane = lax.broadcasted_iota(jnp.int32, shape, 1)
    row = jnp.zeros(shape, jnp.float32)
    for number, value in enumerate(values):
        row = jnp.where(lane == number, jnp.sum(value, axis=1, keepdims=True), row)
    return row


def update_columns(columns, gradient, state, results, update_ref):
    weight = state[0][:, columns]
    moment, second, update = moments(
        weight, state[1][:, columns], state[2][:, columns], gradient.astype(jnp.float32)
    )
    results[0][:, columns] = moment
    results[1][:, columns] = second
    update_ref[:, columns] = update
    return lane_squares(weight), lane_squares(update)


def at_columns(first, width):
    return pl.ds(pl.multiple_of(first, width if width < LANES else LANES), width)


STEPS = 16


def ffn_moments_kernel(inner_ref, up_ref, down_ref, *refs):
    state, down_state = refs[0:3], refs[3:6]
    results, update, down_results, down_update, squares_ref = (
        refs[6:8], refs[8], refs[9:11], refs[11], refs[12]
    )
    step = pl.program_id(0)

    @pl.when(step == 0)
    def _():
        squares_ref[...] = jnp.zeros_like(squares_ref)

    every = slice(None)
    gradient = jnp.where(
        step < STEPS // 2, inner_ref[0].astype(jnp.float32), up_ref[0].astype(jnp.float32)
    )
    found = update_columns(every, gradient, state, results, update)
    group = step // (STEPS // 2)
    squares_ref[pl.ds(group, 1)] += found[0]
    squares_ref[pl.ds(4 + group, 1)] += found[1]
    found = update_columns(every, down_ref[...], down_state, down_results, down_update)
    squares_ref[2:3] += found[0]
    squares_ref[6:7] += found[1]


def ffn_moments(inner_rows, up_rows, down_sum, state, down_state):
    _, rows, width = inner_rows.shape
    half = STEPS // 2

    def column(array):
        return pl.BlockSpec((array.shape[0], array.shape[1] // STEPS), lambda i: (0, i))

    like = [jax.ShapeDtypeStruct(state[0].shape, jnp.float32)] * 3
    like_down = [jax.ShapeDtypeStruct(down_state[0].shape, jnp.float32)] * 3
    return pl.pallas_call(
        ffn_moments_kernel,
        grid=(STEPS,),
        out_shape=like + like_down + [jax.ShapeDtypeStruct((SUBLANES, LANES), jnp.float32)],
        in_specs=[
            pl.BlockSpec((1, rows, width), lambda i: (jnp.minimum(i, half - 1), 0, 0)),
            pl.BlockSpec((1, rows, width), lambda i: (jnp.maximum(i - half, 0), 0, 0)),
            column(down_sum),
        ]
        + [column(array) for array in state + down_state],
        out_specs=[column(array) for array in state + down_state]
        + [pl.BlockSpec((SUBLANES, LANES), lambda i: (0, 0))],
        compiler_params=pltpu.CompilerParams(vmem_limit_bytes=GATHER_VMEM),
        cost_estimate=pl.CostEstimate(
            flops=20 * state[0].size, bytes_accessed=30 * state[0].size, transcendentals=0
        ),
    )(inner_rows, up_rows, down_sum, *state, *down_state)


def begin_blocks(parts, landed, columns, sems, me, team):
    landed[me] = parts[me, :, columns]
    return [
        push(parts.at[index, :, columns], landed.at[me], sems, number, device)
        for number, (index, device) in enumerate(team)
    ]


def column_squares(columns, gradient, state):
    weight = state[0][:, columns]
    _, _, update = moments(
        weight, state[1][:, columns], state[2][:, columns], gradient.astype(jnp.float32)
    )
    return lane_squares(weight), lane_squares(update)


def add_all(olds, news):
    return tuple(old + new for old, new in zip(olds, news))


def totals_kernel(
    heads, attention_ref, gate_ref, first_ref, second_ref, qk_ref, ffn_squares_ref, *refs
):
    state, out_state = refs[0:3], refs[3:6]
    rows_out, gate_out, gains_out, qk_out, norms_out = refs[6:11]
    landed, own, line_slots, team_slots, block_sems, line_sems, team_sems = refs[11:]
    me, team, spot, line = greet_all()
    share = landed.shape[2]
    blocks = begin_blocks(attention_ref, landed, pl.ds(0, share), block_sems, me, team)
    query_width = share - 2 * HEAD_WIDTH
    out_width = out_state[0].shape[1] // TEAM_SIZE
    zero = jnp.zeros((1, LANES), jnp.float32)

    def out(turn, sums):
        columns = at_columns(turn * out_width, out_width)
        gradient = attention_ref[turn, :, pl.ds(share, out_width)]
        return add_all(sums, column_squares(columns, gradient, out_state))

    out_sums = lax.fori_loop(0, TEAM_SIZE, out, (zero,) * 2)
    own[...] = jnp.zeros_like(own)
    own[0:heads] = gate_ref[0:heads]
    own[heads : heads + 1] = first_ref[...]
    own[heads + 1 : heads + 2] = second_ref[...]
    for row in range(2):
        own[heads + 2 : heads + 3, pl.ds(row * HEAD_WIDTH, HEAD_WIDTH)] = qk_ref[row : row + 1]
    for copy in blocks:
        copy.wait_recv()

    def projection(turn, sums):
        found = ()
        for first, start, width in (
            (turn * query_width, 0, query_width),
            (TEAM_SIZE * query_width + turn * HEAD_WIDTH, query_width, HEAD_WIDTH),
            (
                TEAM_SIZE * (query_width + HEAD_WIDTH) + turn * HEAD_WIDTH,
                query_width + HEAD_WIDTH,
                HEAD_WIDTH,
            ),
        ):
            gradient = landed[turn, :, pl.ds(start, width)]
            found = found + column_squares(at_columns(first, width), gradient, state)
        return add_all(sums, found)

    sums = lax.fori_loop(0, TEAM_SIZE, projection, (zero,) * 6) + out_sums
    rows = [sums[2 * group] for group in range(4)]
    rows += [ffn_squares_ref[group : group + 1] for group in range(3)]
    rows += [sums[2 * group + 1] for group in range(4)]
    rows += [ffn_squares_ref[4 + group : 5 + group] for group in range(3)]
    own[heads + 2 : heads + 3, pl.ds(2 * HEAD_WIDTH, LANES)] = in_lanes(rows, (1, LANES))
    along = begin_line(own, line_slots, line_sems, spot, line)
    rows_out[...] = landed[...]
    across = begin_team(along, line_slots, team_slots, team_sems, me, team)
    for copy in across:
        copy.wait_recv()
    total = team_slots[0, heads:]
    for turn in range(1, TEAM_SIZE):
        total = total + team_slots[turn, heads:]
    gains_out[...] = total[:2]
    for row in range(2):
        qk_out[row : row + 1] = total[2:3, row * HEAD_WIDTH : (row + 1) * HEAD_WIDTH]
    for turn in range(TEAM_SIZE):
        gate_out[turn * heads : (turn + 1) * heads] = team_slots[turn, :heads]
    norms = jnp.sqrt(total[2:3, 2 * HEAD_WIDTH : 2 * HEAD_WIDTH + LANES])
    groups = 7
    weight_norms = [norms[:, number : number + 1] for number in range(groups)]
    update_norms = [norms[:, groups + number : groups + number + 1] for number in range(groups)]
    norms_out[...] = jnp.zeros_like(norms_out)
    norms_out[0:1] = in_lanes(weight_norms, (1, LANES))
    norms_out[1:2] = in_lanes(update_norms, (1, LANES))
    norms_out[2:3] = in_lanes(
        [former / latter for former, latter in zip(weight_norms, update_norms)], (1, LANES)
    )
    for copy in blocks + along + across:
        copy.wait_send()


def totals(
    heads, attention_sum, gate_part, gains, qk_gains, ffn_squares, state, out_state, collective_id
):
    vmem = pl.BlockSpec(memory_space=pltpu.VMEM)
    width = gate_part.shape[1]
    depth = depth_size()
    team, rows, _ = attention_sum.shape
    share = state[0].shape[1] // TEAM_SIZE
    return pl.pallas_call(
        functools.partial(totals_kernel, heads),
        out_shape=[
            jax.ShapeDtypeStruct((team, rows, share), jnp.bfloat16),
            jax.ShapeDtypeStruct((TEAM_SIZE * heads, width), jnp.float32),
            jax.ShapeDtypeStruct((2, width), jnp.float32),
            jax.ShapeDtypeStruct((2, HEAD_WIDTH), jnp.float32),
            jax.ShapeDtypeStruct((SUBLANES, LANES), jnp.float32),
        ],
        in_specs=[vmem] * 12,
        out_specs=[vmem] * 5,
        scratch_shapes=[
            pltpu.VMEM((team, rows, share), jnp.bfloat16),
            pltpu.VMEM((SUBLANES, width), jnp.float32),
            pltpu.VMEM((depth, SUBLANES, width), jnp.float32),
            pltpu.VMEM((TEAM_SIZE, SUBLANES, width), jnp.float32),
            pltpu.SemaphoreType.DMA((2, TEAM_SIZE - 1)),
            pltpu.SemaphoreType.DMA((2, max(depth - 1, 1))),
            pltpu.SemaphoreType.DMA((2, TEAM_SIZE - 1)),
        ],
        compiler_params=pltpu.CompilerParams(
            collective_id=collective_id, has_side_effects=True, vmem_limit_bytes=GATHER_VMEM
        ),
    )(
        attention_sum, gate_part, gains[0][None], gains[1][None], qk_gains, ffn_squares,
        *state, *out_state,
    )


def small_update(state, gradient, results, by_row):
    weight = state[0][...]
    moment, second, update = moments(weight, state[1][...], state[2][...], gradient[...])
    ratio = jnp.sum(weight * weight, axis=1, keepdims=True)
    size = jnp.sum(update * update, axis=1, keepdims=True)
    if not by_row:
        ratio = jnp.sum(ratio, axis=0, keepdims=True)
        size = jnp.sum(size, axis=0, keepdims=True)
    results[0][...] = weight - RATE * (jnp.sqrt(ratio) / jnp.sqrt(size)) * update
    results[1][...] = moment
    results[2][...] = second


def apply_kernel(
    norms_ref, gate_ref, gains_ref, qk_ref, rows_ref, attention_ref, *refs
):
    state, out_state = refs[0:3], refs[3:6]
    ffn_pair, down_pair = refs[6:8], refs[8:10]
    states = [refs[10 + 3 * number : 13 + 3 * number] for number in range(3)]
    targets, out_targets = refs[19:23], refs[23:27]
    ffn_targets, down_targets = refs[27:29], refs[29:31]
    results = [refs[31 + 3 * number : 34 + 3 * number] for number in range(3)]
    norms_out, gradient = refs[40], refs[41]
    step = pl.program_id(0)
    share = rows_ref.shape[2]
    wide = share - 2 * HEAD_WIDTH
    query_steps = TEAM_SIZE * wide // gradient.shape[1]
    key_steps = TEAM_SIZE * HEAD_WIDTH // gradient.shape[1]
    per_step = gradient.shape[1] // HEAD_WIDTH

    @pl.when(step == 0)
    def _():
        norms_out[...] = norms_ref[0:2]
        small_update(states[0], gate_ref, results[0], False)
        small_update(states[1], gains_ref, results[1], True)
        small_update(states[2], qk_ref, results[2], True)

    @pl.when(step < query_steps)
    def _():
        gradient[...] = rows_ref[step, :, pl.ds(0, wide)].astype(jnp.float32)

    for number in range(2):
        first = query_steps + number * key_steps

        @pl.when((step >= first) & (step < first + key_steps))
        def _():
            for item in range(per_step):
                gradient[:, pl.ds(item * HEAD_WIDTH, HEAD_WIDTH)] = rows_ref[
                    (step - first) * per_step + item, :, pl.ds(wide + number * HEAD_WIDTH, HEAD_WIDTH)
                ].astype(jnp.float32)

    def rate(first, uppers=()):
        found = norms_ref[2:3, first : first + 1]
        for number, upper in enumerate(uppers):
            group = first + number + 1
            found = jnp.where(step < upper, found, norms_ref[2:3, group : group + 1])
        return RATE * found

    def renew(weight, update, new, low_new, factor):
        value = weight - factor * update
        new[...] = value
        low_new[...] = value.astype(jnp.bfloat16)

    def both(state, gradient, targets, factor):
        weight = state[0][...]
        moment, second, update = moments(weight, state[1][...], state[2][...], gradient)
        targets[2][...] = moment
        targets[3][...] = second
        renew(weight, update, targets[0], targets[1], factor)

    both(state, gradient[...], targets, rate(0, (query_steps, query_steps + key_steps)))
    width = out_state[0].shape[1]
    per_block = (attention_ref.shape[2] - share) // width
    columns = at_columns(share + lax.rem(step, per_block) * width, width)
    both(
        out_state, attention_ref[step // per_block, :, columns].astype(jnp.float32), out_targets,
        rate(3),
    )
    renew(ffn_pair[0][...], ffn_pair[1][...], *ffn_targets, rate(4, (STEPS // 2,)))
    renew(down_pair[0][...], down_pair[1][...], *down_targets, rate(6))


def apply_all(
    norms, gate_total, gains_total, qk_total, projection_rows, attention_sum, state, out_state,
    ffn_pair, down_pair, states,
):
    def whole(array):
        return pl.BlockSpec(array.shape, lambda i: (0,) * array.ndim)

    def column(array):
        return pl.BlockSpec((array.shape[0], array.shape[1] // STEPS), lambda i: (0, i))

    def like(array, kind=jnp.float32):
        return jax.ShapeDtypeStruct(array.shape, kind)

    small = [array for group in states for array in group]
    fixed = [norms, gate_total, gains_total, qk_total, projection_rows, attention_sum]
    split = [*state, *out_state, *ffn_pair, *down_pair]
    targets = []
    for group in (state, out_state):
        targets += [like(group[0]), like(group[0], jnp.bfloat16), like(group[1]), like(group[2])]
    for group in (ffn_pair, down_pair):
        targets += [like(group[0]), like(group[0], jnp.bfloat16)]
    results = [like(array) for array in small]
    results.append(jax.ShapeDtypeStruct((2, norms.shape[1]), jnp.float32))
    rows = state[0].shape[0]
    return pl.pallas_call(
        apply_kernel,
        grid=(STEPS,),
        out_shape=targets + results,
        in_specs=[whole(array) for array in fixed]
        + [column(array) for array in split]
        + [whole(array) for array in small],
        out_specs=[column(array) for array in targets] + [whole(array) for array in results],
        scratch_shapes=[pltpu.VMEM((rows, state[0].shape[1] // STEPS), jnp.float32)],
        compiler_params=pltpu.CompilerParams(vmem_limit_bytes=GATHER_VMEM),
        cost_estimate=pl.CostEstimate(
            flops=4 * ffn_pair[0].size, bytes_accessed=30 * ffn_pair[0].size, transcendentals=0
        ),
    )(*fixed, *split, *small)


def team_exchange(blocks):
    return lax.all_to_all(blocks, TEAM, split_axis=0, concat_axis=0, tiled=True)


def turn_half(value_rows):
    return pltpu.roll(value_rows, value_rows.shape[-1] // 2, value_rows.ndim - 1)


def norm_turn(value_rows, gain, cosine, sine):
    scaled = rms_apply(value_rows, gain)
    return scaled * cosine + turn_half(scaled) * sine


def norm_turn_back(value_rows, gain, cosine, sine, gradient):
    turned = gradient * cosine + turn_half(gradient * sine)
    return rms_back(value_rows, gain, turned)


def greet_line():
    index, count = lax.axis_index("seq"), lax.axis_size("seq")
    barrier = pltpu.get_barrier_semaphore()

    @pl.when(index > 0)
    def _():
        pl.semaphore_signal(
            barrier, inc=1, device_id={"seq": index - 1}, device_id_type=pl.DeviceIdType.MESH
        )

    @pl.when(index < count - 1)
    def _():
        pl.semaphore_signal(
            barrier, inc=1, device_id={"seq": index + 1}, device_id_type=pl.DeviceIdType.MESH
        )

    inside = (index > 0) & (index < count - 1)

    @pl.when(inside)
    def _():
        pl.semaphore_wait(barrier, 2)

    @pl.when(jnp.logical_not(inside))
    def _():
        pl.semaphore_wait(barrier, 1)

    return index, count


def attend_kernel(
    window, scale, rows_ref, weight_ref, gate_ref, gains_ref, cosine_ref, sine_ref, start_ref,
    raw_ref, query_ref, pair_ref, stats_ref, across_ref, attended_ref, gated_ref,
    weight, pairs, send_sem, recv_sem,
):
    count_rows, length, _ = rows_ref.shape
    query_cols = query_ref.shape[2]
    heads = query_cols // HEAD_WIDTH
    keys_at = pl.ds(0, HEAD_WIDTH)
    values_at = pl.ds(HEAD_WIDTH, HEAD_WIDTH)
    index, count = greet_line()

    def hop(turn, row):
        return pltpu.make_async_remote_copy(
            src_ref=pairs.at[window - turn + 1, row],
            dst_ref=pairs.at[window - turn, row],
            send_sem=send_sem.at[turn - 1, row],
            recv_sem=recv_sem.at[turn - 1, row],
            device_id={"seq": lax.rem(index + 1, count)},
            device_id_type=pl.DeviceIdType.MESH,
        )

    block = weight_ref.shape[0] * weight_ref.shape[2]
    own = raw_ref.shape[2]
    for step in range(TEAM_SIZE):
        weight[pl.ds(step * block, block), pl.ds(0, own)] = whole_block(
            weight_ref, step, pl.ds(0, own)
        )
    weight[:, pl.ds(own, LANES)] = gate_ref[...]

    def project(row, carry):
        products = jnp.dot(rows_ref[row], weight[...], preferred_element_type=jnp.float32)
        raw = products[:, : query_cols + 2 * HEAD_WIDTH].astype(jnp.bfloat16)
        raw_ref[row] = raw
        cosine, sine = cosine_ref[row], sine_ref[row]
        key = norm_turn(
            raw[:, query_cols : query_cols + HEAD_WIDTH].astype(jnp.float32),
            gains_ref[1:2], cosine, sine,
        )
        pairs[window, row, :, keys_at] = key.astype(jnp.bfloat16)
        pairs[window, row, :, values_at] = raw[:, query_cols + HEAD_WIDTH :]

        @pl.when(index < count - 1)
        def _():
            hop(1, row).start()

        for head in range(heads):
            columns = slice(head * HEAD_WIDTH, (head + 1) * HEAD_WIDTH)
            query_ref[row, :, columns] = norm_turn(
                raw[:, columns].astype(jnp.float32), gains_ref[0:1], cosine, sine
            ).astype(jnp.bfloat16)
        stats_ref[row] = jax.nn.sigmoid(products[:, query_cols + 2 * HEAD_WIDTH :])
        return carry

    lax.fori_loop(0, count_rows, project, 0)

    @pl.when(index == 0)
    def _():
        for slot in range(window):
            pairs[slot] = jnp.zeros_like(pairs[slot])

    for turn in range(2, window + 1):

        def forward(row, carry):
            @pl.when(index > 0)
            def _():
                hop(turn - 1, row).wait_recv()

            @pl.when(index < count - 1)
            def _():
                hop(turn, row).start()

            return carry

        lax.fori_loop(0, count_rows, forward, 0)

    places = lax.broadcasted_iota(jnp.int32, (length, (window + 1) * length), 1)
    latest = window * length + lax.broadcasted_iota(jnp.int32, places.shape, 0)
    lane = lax.broadcasted_iota(jnp.int32, (length, LANES), 1)

    def attend(row, carry):
        @pl.when(index > 0)
        def _():
            hop(window, row).wait_recv()

        allowed = (places >= start_ref[row]) & (places <= latest)
        keys = pairs[:, row, :, keys_at].reshape(-1, HEAD_WIDTH)
        values = pairs[:, row, :, values_at].reshape(-1, HEAD_WIDTH)
        stats = stats_ref[row]
        for head in range(heads):
            columns = slice(head * HEAD_WIDTH, (head + 1) * HEAD_WIDTH)
            scores = dot_t(query_ref[row, :, columns], keys) * scale
            scores = jnp.where(allowed, scores, NEGATIVE)
            top = jnp.max(scores, axis=1, keepdims=True)
            powers = jnp.exp(scores - top)
            total = jnp.sum(powers, axis=1, keepdims=True)
            low_probs = (powers * (1.0 / total)).astype(jnp.bfloat16)
            output = jnp.dot(low_probs, values, preferred_element_type=jnp.float32)
            output = output.astype(jnp.bfloat16)
            attended_ref[row, :, columns] = output
            gated_ref[row, :, columns] = (
                output.astype(jnp.float32) * stats[:, head : head + 1]
            ).astype(jnp.bfloat16)
            stats = jnp.where(lane == heads + head, top + jnp.log(total), stats)
        stats_ref[row] = stats
        across_ref[row] = stats.T[:SUBLANES]
        pair_ref[:, row] = pairs[:, row]
        return carry

    lax.fori_loop(0, count_rows, attend, 0)

    @pl.when(index < count - 1)
    def _():
        for turn in range(1, window + 1):

            def finish(row, carry):
                hop(turn, row).wait_send()
                return carry

            lax.fori_loop(0, count_rows, finish, 0)


def attend(
    normed_rows, own_attention, own_gate, gains, cosine, sine, starts, query_cols, window, collective_id
):
    rows, length, _ = normed_rows.shape
    width = query_cols + 2 * HEAD_WIDTH + LANES
    bf16 = jnp.bfloat16
    vmem = pl.BlockSpec(memory_space=pltpu.VMEM)
    return pl.pallas_call(
        functools.partial(attend_kernel, window, HEAD_WIDTH ** (-0.5)),
        out_shape=[
            jax.ShapeDtypeStruct((rows, length, query_cols + 2 * HEAD_WIDTH), bf16),
            jax.ShapeDtypeStruct((rows, length, query_cols), bf16),
            jax.ShapeDtypeStruct((window + 1, rows, length, 2 * HEAD_WIDTH), bf16),
            jax.ShapeDtypeStruct((rows, length, LANES), jnp.float32),
            jax.ShapeDtypeStruct((rows, SUBLANES, length), jnp.float32),
            jax.ShapeDtypeStruct((rows, length, query_cols), bf16),
            jax.ShapeDtypeStruct((rows, length, query_cols), bf16),
        ],
        in_specs=[vmem] * 7,
        out_specs=[vmem] * 7,
        scratch_shapes=[
            pltpu.VMEM((MODEL_WIDTH, width), bf16),
            pltpu.VMEM((window + 1, rows, length, 2 * HEAD_WIDTH), bf16),
            pltpu.SemaphoreType.DMA((window, rows)),
            pltpu.SemaphoreType.DMA((window, rows)),
        ],
        compiler_params=pltpu.CompilerParams(
            collective_id=collective_id, has_side_effects=True, vmem_limit_bytes=VMEM_BYTES
        ),
        cost_estimate=pl.CostEstimate(
            flops=2 * rows * length * MODEL_WIDTH * width,
            bytes_accessed=ATTEND_COST * rows * length * MODEL_WIDTH,
            transcendentals=0,
        ),
    )(normed_rows, own_attention, own_gate, gains, cosine, sine, starts)


def attend_back_kernel(
    window, scale, rows_ref, weight_ref, gains_ref, cosine_ref, sine_ref, start_ref,
    raw_ref, query_ref, pair_ref, stats_ref, across_ref, attended_ref,
    products_ref, gain_ref,
    weight, parts, outs, ins, send_sem, recv_sem,
):
    count_rows, length, _ = rows_ref.shape
    query_cols = query_ref.shape[2]
    heads = query_cols // HEAD_WIDTH
    keys_at = pl.ds(0, HEAD_WIDTH)
    values_at = pl.ds(HEAD_WIDTH, HEAD_WIDTH)
    index, count = greet_line()
    lag = 2

    def hop(turn, row):
        return pltpu.make_async_remote_copy(
            src_ref=outs.at[turn - 1, row],
            dst_ref=ins.at[turn - 1, row],
            send_sem=send_sem.at[turn - 1, row],
            recv_sem=recv_sem.at[turn - 1, row],
            device_id={"seq": lax.rem(index + count - 1, count)},
            device_id_type=pl.DeviceIdType.MESH,
        )

    keys_total = (window + 1) * length
    places = lax.broadcasted_iota(jnp.int32, (keys_total, length), 0)
    latest = window * length + lax.broadcasted_iota(jnp.int32, places.shape, 1)
    lane = lax.broadcasted_iota(jnp.int32, (length, LANES), 1)
    gain_ref[...] = jnp.zeros_like(gain_ref)
    share = weight_ref.shape[3] - query_cols
    for step in range(TEAM_SIZE):
        weight[:, pl.ds(step * query_cols, query_cols)] = whole_block(
            weight_ref, step, pl.ds(share, query_cols)
        )

    @pl.when(index == count - 1)
    def _():
        ins[...] = jnp.zeros_like(ins)

    def compute(row):
        grad_gated = dot_t(rows_ref[row], weight[...])
        keys = pair_ref[:, row, :, keys_at].reshape(-1, HEAD_WIDTH)
        values = pair_ref[:, row, :, values_at].reshape(-1, HEAD_WIDTH)
        allowed = (places >= start_ref[row]) & (places <= latest)
        cosine, sine = cosine_ref[row], sine_ref[row]
        grad_pre = jnp.zeros((length, LANES), jnp.float32)
        grad_keys = jnp.zeros((keys_total, HEAD_WIDTH), jnp.float32)
        grad_values = jnp.zeros((keys_total, HEAD_WIDTH), jnp.float32)
        for head in range(heads):
            columns = slice(head * HEAD_WIDTH, (head + 1) * HEAD_WIDTH)
            gate = stats_ref[row, :, head : head + 1]
            own = grad_gated[:, columns]
            grad_out = (own * gate).astype(jnp.bfloat16)
            grad_gate = jnp.sum(
                own * attended_ref[row, :, columns].astype(jnp.float32), axis=1, keepdims=True
            )
            grad_pre = jnp.where(lane == head, grad_gate * gate * (1.0 - gate), grad_pre)
            query = query_ref[row, :, columns]
            scores = jnp.where(allowed, dot_t(keys, query) * scale, NEGATIVE)
            probs = jnp.exp(scores - across_ref[row, heads + head : heads + head + 1])
            grad_probs = dot_t(values, grad_out)
            inner = jnp.sum(probs * grad_probs, axis=0, keepdims=True)
            grad_scores = (probs * (grad_probs - inner)).astype(jnp.bfloat16)
            grad_values = grad_values + jnp.dot(
                probs.astype(jnp.bfloat16), grad_out, preferred_element_type=jnp.float32
            )
            grad_keys = grad_keys + jnp.dot(
                grad_scores, query, preferred_element_type=jnp.float32
            )
            grad_query = dot_tokens(grad_scores, keys) * scale
            grad_raw, gain = norm_turn_back(
                raw_ref[row, :, columns].astype(jnp.float32), gains_ref[0:1], cosine, sine,
                grad_query,
            )
            products_ref[row, :, columns] = grad_raw.astype(jnp.bfloat16)
            gain_ref[0:1] += jnp.sum(gain, axis=0, keepdims=True)
        products_ref[row, :, query_cols + 2 * HEAD_WIDTH :] = grad_pre.astype(jnp.bfloat16)
        parts[:, row, :, keys_at] = (grad_keys * scale).reshape(window + 1, length, HEAD_WIDTH)
        parts[:, row, :, values_at] = grad_values.reshape(window + 1, length, HEAD_WIDTH)

    def finish(row):
        grad_pair = parts[window, row] + ins[window - 1, row].astype(jnp.float32)
        grad_raw, gain = norm_turn_back(
            raw_ref[row, :, query_cols : query_cols + HEAD_WIDTH].astype(jnp.float32),
            gains_ref[1:2], cosine_ref[row], sine_ref[row], grad_pair[:, :HEAD_WIDTH],
        )
        products_ref[row, :, query_cols : query_cols + HEAD_WIDTH] = grad_raw.astype(jnp.bfloat16)
        products_ref[row, :, query_cols + HEAD_WIDTH : query_cols + 2 * HEAD_WIDTH] = grad_pair[
            :, HEAD_WIDTH:
        ].astype(jnp.bfloat16)
        gain_ref[1:2] += jnp.sum(gain, axis=0, keepdims=True)

    def step(turn_row, carry):
        @pl.when(turn_row < count_rows)
        def _():
            compute(turn_row)

        for turn in range(1, window + 2):
            row = turn_row - lag * (turn - 1)

            @pl.when((row >= 0) & (row < count_rows))
            def _():
                if turn > 1:

                    @pl.when(index < count - 1)
                    def _():
                        hop(turn - 1, row).wait_recv()

                if turn == window + 1:
                    finish(row)
                else:
                    part = parts[turn - 1, row]
                    if turn > 1:
                        part = part + ins[turn - 2, row].astype(jnp.float32)
                    outs[turn - 1, row] = part.astype(jnp.bfloat16)

                    @pl.when(index > 0)
                    def _():
                        hop(turn, row).start()

        return carry

    lax.fori_loop(0, count_rows + lag * window, step, 0)

    @pl.when(index > 0)
    def _():
        for turn in range(1, window + 1):

            def done(row, carry):
                hop(turn, row).wait_send()
                return carry

            lax.fori_loop(0, count_rows, done, 0)


def attend_back(
    grad_rows, own_attention, gains, cosine, sine, starts, saved, window, collective_id
):
    rows, length, _ = grad_rows.shape
    query_cols = saved[1].shape[2]
    width = query_cols + 2 * HEAD_WIDTH + LANES
    bf16 = jnp.bfloat16
    vmem = pl.BlockSpec(memory_space=pltpu.VMEM)
    return pl.pallas_call(
        functools.partial(attend_back_kernel, window, HEAD_WIDTH ** (-0.5)),
        out_shape=[
            jax.ShapeDtypeStruct((rows, length, width), bf16),
            jax.ShapeDtypeStruct((SUBLANES, HEAD_WIDTH), jnp.float32),
        ],
        in_specs=[vmem] * 12,
        out_specs=[vmem] * 2,
        scratch_shapes=[
            pltpu.VMEM((query_cols, MODEL_WIDTH), bf16),
            pltpu.VMEM((window + 1, rows, length, 2 * HEAD_WIDTH), jnp.float32),
            pltpu.VMEM((window, rows, length, 2 * HEAD_WIDTH), bf16),
            pltpu.VMEM((window, rows, length, 2 * HEAD_WIDTH), bf16),
            pltpu.SemaphoreType.DMA((window, rows)),
            pltpu.SemaphoreType.DMA((window, rows)),
        ],
        compiler_params=pltpu.CompilerParams(
            collective_id=collective_id, has_side_effects=True, vmem_limit_bytes=VMEM_BYTES
        ),
        cost_estimate=pl.CostEstimate(
            flops=2 * rows * length * MODEL_WIDTH * query_cols,
            bytes_accessed=ATTEND_COST * rows * length * MODEL_WIDTH,
            transcendentals=0,
        ),
    )(grad_rows, own_attention, gains, cosine, sine, starts, *saved)


def team_columns(matrix, widths):
    pieces = []
    lower = 0
    for width in widths:
        piece = matrix[:, lower : lower + width]
        pieces.append(piece.reshape(matrix.shape[0], TEAM_SIZE, width // TEAM_SIZE))
        lower = lower + width
    return jnp.concatenate(pieces, axis=2).transpose(1, 0, 2)


def gather_parts(blocks):
    return lax.all_gather(blocks, DEPTH, axis=0, tiled=False)


def scatter_parts(parts):
    depth, team, rows, width = parts.shape
    return lax.psum_scatter(
        parts.reshape(depth * team * rows, width), DEPTH, scatter_dimension=0, tiled=True
    ).reshape(team, rows, width)


def gather_rows(matrix):
    return lax.all_gather(matrix, DEPTH, axis=0, tiled=True)


def scatter_rows(gradient):
    return lax.psum_scatter(gradient, DEPTH, scatter_dimension=0, tiled=True)


def shards(
    inputs,
    cotangent,
    doc_lengths,
    projection_weight,
    projection_moment,
    projection_second,
    out_weight,
    out_moment,
    out_second,
    ffn_weight,
    ffn_moment,
    ffn_second,
    down_weight,
    down_moment,
    down_second,
    head_gate,
    gate_moment,
    gate_second,
    norm_gains,
    gains_moment,
    gains_second,
    qk_gains,
    qk_moment,
    qk_second,
):
    rows_dev, local_len, width = inputs.shape
    bf16 = jnp.bfloat16
    team = lax.axis_index(TEAM)
    place_seq = lax.axis_index("seq")
    group_heads = QUERY_HEADS // KEY_VALUE_HEADS
    window = -(-(DOC_MOST - 1) // local_len)
    window = min(window, lax.axis_size("seq") - 1)
    query_cols = QUERY_HEADS * HEAD_WIDTH
    key_value_columns = KEY_VALUE_HEADS * HEAD_WIDTH
    widths_qkv = (query_cols, key_value_columns, key_value_columns)
    widths_ffn = (FF, FF)
    own_query = query_cols // TEAM_SIZE
    own_key = key_value_columns // TEAM_SIZE
    own_ff = FF // TEAM_SIZE
    own_gate = lax.dynamic_slice_in_dim(head_gate.astype(bf16), team * group_heads, group_heads, 1)
    own_gate = jnp.pad(own_gate, ((0, 0), (0, LANES - group_heads)))
    own_attention = gather_parts(
        jnp.concatenate(
            [
                team_exchange(team_columns(projection_weight.astype(bf16), widths_qkv)),
                team_columns(out_weight.astype(bf16), (MODEL_WIDTH,)),
            ],
            axis=2,
        )
    )
    ffn_blocks = team_exchange(team_columns(ffn_weight.astype(bf16), widths_ffn))
    own_inner = gather_parts(ffn_blocks[:, :, :own_ff])
    lengths = lax.all_gather(doc_lengths, TEAM, axis=0, tiled=True)
    place = place_seq * local_len + jnp.arange(local_len, dtype=jnp.int32)
    position = positions(lengths, place)
    cosine, sine = rotary_tables(position, HEAD_WIDTH)
    starts = window * local_len + jnp.arange(local_len, dtype=jnp.int32)[None, :] - position
    inputs_flat = inputs[0].astype(jnp.float32)
    normed = rms_apply(inputs_flat, norm_gains[0]).astype(bf16)
    normed_all, grad_all = gather_team([normed, cotangent[0]], 0)
    raw, query_rot, pairs, stats, across, attended, gated = attend(
        normed_all.reshape(TEAM_SIZE, local_len, MODEL_WIDTH),
        own_attention,
        own_gate,
        qk_gains,
        cosine,
        sine,
        starts[:, :, None],
        own_query,
        window,
        8,
    )
    gated, up_blocks, low_down = lax.optimization_barrier(
        (gated, ffn_blocks[:, :, own_ff:], down_weight.astype(bf16))
    )
    own_up = gather_parts(up_blocks)
    own_down = gather_rows(low_down)
    middle = inputs_flat + scatter_team(product_out, [gated.reshape(-1, own_query)], [own_attention], 1)
    normed2 = rms_apply(middle, norm_gains[1]).astype(bf16)
    normed2_all = gather_team([normed2], 2)[0]
    hidden, slope, swish = ffn_forward(normed2_all, own_inner, own_up)
    grad_final = cotangent[0].astype(jnp.float32)
    down_part, own_down = lax.optimization_barrier(
        (low_tokens(hidden.reshape(-1, own_ff), grad_all), own_down)
    )
    grad_inner, grad_up = ffn_back(grad_all, own_down, slope, swish)
    grad_inner, grad_up = grad_inner.reshape(-1, own_ff), grad_up.reshape(-1, own_ff)
    inner_part, grad_inner = lax.optimization_barrier(
        (weight_parts(normed2_all, grad_inner, ffn_weight.shape[0]), grad_inner)
    )
    down_sum = scatter_rows(down_part)
    grad_normed2 = scatter_team(
        product_ffn_back, [grad_inner, grad_up], [own_inner, own_up], 4
    )
    grad_mid_part, gain_mid = rms_back(middle, norm_gains[1], grad_normed2)
    grad_middle = grad_final + grad_mid_part
    grad_low, down_sum = lax.optimization_barrier((grad_middle.astype(bf16), down_sum))
    inner_sum = scatter_parts(inner_part)
    grad_middle_all, up_part = gather_team(
        [grad_low],
        5,
        weight_work,
        (normed2_all, grad_up),
        (weight_shape(normed2_all, grad_up, ffn_weight.shape[0]),),
    )
    grad_products, gain_sums = attend_back(
        grad_middle_all.reshape(TEAM_SIZE, local_len, MODEL_WIDTH),
        own_attention,
        qk_gains,
        cosine,
        sine,
        starts[:, None, :],
        (raw, query_rot, pairs, stats, across, attended),
        window,
        9,
    )
    grad_products = grad_products.reshape(-1, grad_products.shape[2])
    up_part, grad_products, inner_sum = lax.optimization_barrier(
        (up_part, grad_products, inner_sum)
    )
    up_sum = scatter_parts(up_part)
    grad_normed, attention_part, gate_part = scatter_team(
        product_qkv_back,
        [grad_products],
        [own_attention, own_gate],
        6,
        attention_weight_work,
        (normed_all, grad_products, gated.reshape(-1, own_query), grad_middle_all),
        attention_weight_shapes(normed_all, grad_products, out_weight.shape[0]),
    )
    late_hidden, grad_normed, inner_sum = lax.optimization_barrier(
        (hidden, grad_normed, inner_sum)
    )
    inner_rows = team_exchange(inner_sum)
    attention_sum = scatter_parts(attention_part)
    summed = scatter_team(product_down, [late_hidden.reshape(-1, own_ff)], [own_down], 3)
    grad_in_part, gain_in = rms_back(inputs_flat, norm_gains[0], grad_normed)
    input_grad = (grad_middle + grad_in_part).reshape(inputs.shape)
    up_sum, summed, inner_rows = lax.optimization_barrier((up_sum, summed, inner_rows))
    (
        ffn_moment_new,
        ffn_second_new,
        ffn_update,
        down_moment_new,
        down_second_new,
        down_update,
        ffn_squares,
    ) = ffn_moments(
        inner_rows,
        team_exchange(up_sum),
        down_sum,
        (ffn_weight, ffn_moment, ffn_second),
        (down_weight, down_moment, down_second),
    )
    final = middle + summed
    result = final.astype(bf16).reshape(inputs.shape)
    attention_sum, ffn_squares, result, input_grad = lax.optimization_barrier(
        (attention_sum, ffn_squares, result, input_grad)
    )
    attention_state = (projection_weight, projection_moment, projection_second)
    out_state = (out_weight, out_moment, out_second)
    projection_rows, gate_total, gains_total, qk_total, norms = totals(
        group_heads,
        attention_sum,
        gate_part,
        (jnp.sum(gain_in, axis=0), jnp.sum(gain_mid, axis=0)),
        gain_sums,
        ffn_squares,
        attention_state,
        out_state,
        10,
    )
    (
        projection_weight_next,
        qkv_copy,
        projection_moment_next,
        projection_second_next,
        out_new,
        out_copy,
        out_moment_new,
        out_second_new,
        ffn_new,
        ffn_copy,
        down_new,
        down_copy,
        head_gate_new,
        gate_moment_new,
        gate_second_new,
        gains_new,
        gains_moment_new,
        gains_second_new,
        qk_new,
        qk_moment_new,
        qk_second_new,
        norms,
    ) = apply_all(
        norms,
        gate_total,
        gains_total,
        qk_total,
        projection_rows,
        attention_sum,
        attention_state,
        out_state,
        (ffn_weight, ffn_update),
        (down_weight, down_update),
        (
            (head_gate.T, gate_moment.T, gate_second.T),
            (norm_gains, gains_moment, gains_second),
            (qk_gains, qk_moment, qk_second),
        ),
    )
    return (
        result,
        input_grad,
        projection_weight_next,
        projection_moment_next,
        projection_second_next,
        qkv_copy,
        out_new,
        out_moment_new,
        out_second_new,
        out_copy,
        ffn_new,
        ffn_moment_new,
        ffn_second_new,
        ffn_copy,
        down_new,
        down_moment_new,
        down_second_new,
        down_copy,
        head_gate_new.T,
        gate_moment_new.T,
        gate_second_new.T,
        gains_new,
        gains_moment_new,
        gains_second_new,
        qk_new,
        qk_moment_new,
        qk_second_new,
        norms[:2, :7],
    )


def solution(mesh):
    mesh = Mesh(
        mesh.devices.reshape(2, 2, 2, mesh.shape["fsdp"] // TEAM_SIZE, mesh.shape["seq"]),
        TEAM + DEPTH,
    )
    rows = TEAM + DEPTH[:1]
    in_specs = (
        P(rows, "seq", None),
        P(rows, "seq", None),
        P(rows, None),
        P(TEAM + DEPTH, None),
        P(TEAM + DEPTH, None),
        P(TEAM + DEPTH, None),
        P(TEAM + DEPTH, None),
        P(TEAM + DEPTH, None),
        P(TEAM + DEPTH, None),
        P(TEAM + DEPTH, None),
        P(TEAM + DEPTH, None),
        P(TEAM + DEPTH, None),
        P(TEAM + DEPTH, None),
        P(TEAM + DEPTH, None),
        P(TEAM + DEPTH, None),
        P(),
        P(),
        P(),
        P(),
        P(),
        P(),
        P(),
        P(),
        P(),
    )
    out_specs = (
        P(rows, "seq", None),
        P(rows, "seq", None),
        P(TEAM + DEPTH, None),
        P(TEAM + DEPTH, None),
        P(TEAM + DEPTH, None),
        P(TEAM + DEPTH, None),
        P(TEAM + DEPTH, None),
        P(TEAM + DEPTH, None),
        P(TEAM + DEPTH, None),
        P(TEAM + DEPTH, None),
        P(TEAM + DEPTH, None),
        P(TEAM + DEPTH, None),
        P(TEAM + DEPTH, None),
        P(TEAM + DEPTH, None),
        P(TEAM + DEPTH, None),
        P(TEAM + DEPTH, None),
        P(TEAM + DEPTH, None),
        P(TEAM + DEPTH, None),
        P(),
        P(),
        P(),
        P(),
        P(),
        P(),
        P(),
        P(),
        P(),
        P(),
    )
    return jax.shard_map(shards, mesh=mesh, in_specs=in_specs, out_specs=out_specs, check_vma=False)
```

```python
import functools

import jax
import jax.numpy as jnp
from jax import lax
from jax.experimental import pallas as pl
from jax.experimental.pallas import tpu as pltpu
from jax.sharding import Mesh
from jax.sharding import PartitionSpec as P

MODEL_WIDTH = 2048
QUERY_HEADS = 16
KEY_VALUE_HEADS = 8
HEAD_WIDTH = 128
FF = 6144
ROW_TOKENS = 1024
STEP = 3
DOC_MOST = 512
TEAM_SIZE = 8
TEAM = ("t2", "t1", "t0")
DEPTH = ("spare", "seq")
LANES = 128
SUBLANES = 8
VMEM_BYTES = 60 << 20
GATHER_VMEM = 60 << 20
LAMB_COST = 70
GATHER_COST = 250
SCATTER_COST = 320
ATTEND_COST = 50


NORM_EPS = 1e-06
ADAM_EPS = 1e-06
RATE = 0.3
DECAY = 0.01
BETA = 0.5
THETA = 1000000.0
NEGATIVE = -1e30


def rms_apply(value_rows, gain):
    return (
        value_rows
        * lax.rsqrt(jnp.mean(value_rows * value_rows, axis=-1, keepdims=True) + NORM_EPS)
        * gain
    )


def rms_back(value_rows, gain, gradient):
    scale = lax.rsqrt(jnp.mean(value_rows * value_rows, axis=-1, keepdims=True) + NORM_EPS)
    scaled = gradient * gain
    inner = jnp.mean(scaled * value_rows, axis=-1, keepdims=True)
    grad_value = scale * scaled - value_rows * scale * scale * scale * inner
    grad_gain = gradient * value_rows * scale
    return (grad_value, grad_gain)


def dot_t(left, right):
    return lax.dot_general(
        left, right, (((1,), (1,)), ((), ())), preferred_element_type=jnp.float32
    )


def low_tokens(left, right):
    return dot_tokens(left, right).astype(jnp.bfloat16)


def dot_tokens(left, right):
    return lax.dot_general(
        left, right, (((0,), (0,)), ((), ())), preferred_element_type=jnp.float32
    )


def moments(weight, moment, second, gradient):
    moment_new = BETA * moment + (1.0 - BETA) * gradient
    second_new = BETA * second + (1.0 - BETA) * gradient * gradient
    correction = 1.0 - BETA**STEP
    update = (
        moment_new / correction / (jnp.sqrt(second_new / correction) + ADAM_EPS) + DECAY * weight
    )
    return (moment_new, second_new, update)


def rotary_tables(position, width):
    half = width // 2
    rates = THETA ** (-jnp.arange(half, dtype=jnp.float32) * 2.0 / width)
    angle = position.astype(jnp.float32)[..., None] * rates
    cosine, sine = jnp.cos(angle), jnp.sin(angle)
    return (
        jnp.concatenate([cosine, cosine], axis=-1),
        jnp.concatenate([-sine, sine], axis=-1),
    )


def positions(lengths, place):
    ends = jnp.cumsum(lengths, axis=1)
    starts = ends - lengths
    inside = (place[None, :, None] >= starts[:, None, :]) & (place[None, :, None] < ends[:, None, :])
    return place[None, :] - jnp.sum(jnp.where(inside, starts[:, None, :], 0), axis=2)


def team_place():
    return tuple(lax.axis_index(axis) for axis in TEAM)


def greet_team(place):
    barrier = pltpu.get_barrier_semaphore()
    for axis, index in zip(TEAM, place):
        pl.semaphore_signal(
            barrier, inc=1, device_id={axis: 1 - index}, device_id_type=pl.DeviceIdType.MESH
        )
    pl.semaphore_wait(barrier, len(TEAM))


def member(place, flips):
    index = 0
    for own, flip in zip(place, flips):
        index = index * 2 + (1 - own if flip else own)
    return index


def gather_kernel(count, work, *refs):
    given, made = (work[1], work[2]) if work else (0, 0)
    owns, operands = refs[:count], refs[count : count + given]
    alls = refs[count + given : 2 * count + given]
    results = refs[2 * count + given : 2 * count + given + made]
    own_sem, send_sem, recv_sem = refs[2 * count + given + made :]
    place = team_place()
    greet_team(place)
    me = member(place, (0, 0, 0))
    beside = member(place, (0, 1, 0))
    above = member(place, (1, 0, 0))
    across = member(place, (1, 1, 0))
    copies = [{} for _ in range(count)]
    keeps = []

    def send(item, number, axis, source, target):
        copy = pltpu.make_async_remote_copy(
            src_ref=source,
            dst_ref=target,
            send_sem=send_sem.at[item, number],
            recv_sem=recv_sem.at[item, number],
            device_id={TEAM[axis]: 1 - place[axis]},
            device_id_type=pl.DeviceIdType.MESH,
        )
        copy.start()
        copies[item][number] = copy

    def halves(item):
        half = owns[item].shape[0] // 2
        return pl.ds(0, half), pl.ds(half, half)

    for item in range(count):
        target = alls[item].at[me]
        send(item, 0, 1, owns[item], target)
        send(item, 1, 0, owns[item], target)
        send(item, 2, 2, owns[item], target)
        keeps.append(pltpu.make_async_copy(owns[item], target, own_sem.at[item]))
        keeps[item].start()
    if work:
        work[0](*operands, *results)
    for item in range(count):
        upper, lower = halves(item)
        copies[item][0].wait_recv()
        block = alls[item].at[beside]
        send(item, 3, 0, block.at[upper], block.at[upper])
        send(item, 4, 2, block, block)
        copies[item][1].wait_recv()
        block = alls[item].at[above]
        send(item, 5, 1, block.at[lower], block.at[lower])
        send(item, 6, 2, block, block)
    for item in range(count):
        upper, lower = halves(item)
        block = alls[item].at[across]
        copies[item][3].wait_recv()
        send(item, 7, 2, block.at[upper], block.at[upper])
        copies[item][5].wait_recv()
        send(item, 8, 2, block.at[lower], block.at[lower])
    for item in range(count):
        for number in (2, 4, 6, 7, 8):
            copies[item][number].wait_recv()
        for number in range(9):
            copies[item][number].wait_send()
        keeps[item].wait()


def gather_team(arrays, collective_id, work=None, operands=(), results=()):
    count = len(arrays)
    anywhere = pl.BlockSpec(memory_space=pl.ANY)
    out_shape = [jax.ShapeDtypeStruct((TEAM_SIZE,) + own.shape, own.dtype) for own in arrays]
    gathered = pl.pallas_call(
        functools.partial(
            gather_kernel, count, (work, len(operands), len(results)) if work else None
        ),
        out_shape=out_shape + list(results),
        in_specs=[anywhere] * (count + len(operands)),
        out_specs=[anywhere] * (count + len(results)),
        scratch_shapes=[
            pltpu.SemaphoreType.DMA((count,)),
            pltpu.SemaphoreType.DMA((count, 9)),
            pltpu.SemaphoreType.DMA((count, 9)),
        ],
        compiler_params=pltpu.CompilerParams(
            collective_id=collective_id, has_side_effects=True, vmem_limit_bytes=GATHER_VMEM
        ),
        cost_estimate=pl.CostEstimate(
            flops=0,
            bytes_accessed=sum(GATHER_COST * own.shape[0] * own.shape[1] for own in arrays),
            transcendentals=0,
        ),
    )(*arrays, *operands)
    return [
        whole.reshape(TEAM_SIZE * own.shape[0], own.shape[1])
        for whole, own in zip(gathered, arrays)
    ] + list(gathered[count:])


def scatter_kernel(product, count, work, *refs):
    given, made = (work[1], work[2]) if work else (0, 0)
    operands, extra = refs[:count], refs[count : count + given]
    sum_ref = refs[count + given]
    results = refs[count + given + 1 : count + given + 1 + made]
    own, out_near, in_near, out_far, in_half, in_full, send_sem, recv_sem = refs[
        count + given + 1 + made :
    ]
    place = team_place()
    greet_team(place)
    rows = sum_ref.shape[0]
    half = rows // 2
    upper, lower = pl.ds(0, half), pl.ds(half, half)

    def send(number, axis, source, target):
        copy = pltpu.make_async_remote_copy(
            src_ref=source,
            dst_ref=target,
            send_sem=send_sem.at[number],
            recv_sem=recv_sem.at[number],
            device_id={TEAM[axis]: 1 - place[axis]},
            device_id_type=pl.DeviceIdType.MESH,
        )
        copy.start()
        return copy

    flips = ((1, 1), (0, 1), (1, 0), (0, 0))
    near, far = [], {}
    is_first = place[2] == 0

    def begin(turn):
        first, second = flips[turn]
        pair = member(place[:2], (first, second))

        def one(step, columns):
            both = product(operands, pair, step, columns)
            former, latter = both[:rows], both[rows:]
            out_near[turn, :, columns] = jnp.where(is_first, latter, former).astype(jnp.bfloat16)
            own[turn, :, columns] = jnp.where(is_first, former, latter)

        over_tiles(sum_ref.shape[1], one)
        near.append(send(turn, 2, out_near.at[turn], in_near.at[turn]))

    def join(turn):
        near[turn].wait_recv()
        return own[turn] + in_near[turn].astype(jnp.float32)

    begin(0)
    begin(1)
    out_far[0] = join(0).astype(jnp.bfloat16)
    far[4] = send(4, 1, out_far.at[0, upper], in_half.at[0])
    far[5] = send(5, 0, out_far.at[0, lower], in_half.at[1])
    begin(2)
    own[1] = join(1)
    out_far[1, upper] = own[1, upper].astype(jnp.bfloat16)
    far[6] = send(6, 1, out_far.at[1, upper], in_full.at[0, upper])
    begin(3)
    own[2] = join(2)
    out_far[2, lower] = own[2, lower].astype(jnp.bfloat16)
    far[7] = send(7, 0, out_far.at[2, lower], in_full.at[1, lower])
    sum_ref[...] = join(3)
    far[5].wait_recv()
    out_far[1, lower] = (own[1, lower] + in_half[1].astype(jnp.float32)).astype(jnp.bfloat16)
    far[8] = send(8, 1, out_far.at[1, lower], in_full.at[0, lower])
    far[4].wait_recv()
    out_far[2, upper] = (own[2, upper] + in_half[0].astype(jnp.float32)).astype(jnp.bfloat16)
    far[9] = send(9, 0, out_far.at[2, upper], in_full.at[1, upper])
    if work:
        work[0](*extra, *results)
    far[6].wait_recv()
    far[7].wait_recv()
    far[8].wait_recv()
    far[9].wait_recv()
    sum_ref[...] = (
        sum_ref[...] + in_full[0].astype(jnp.float32) + in_full[1].astype(jnp.float32)
    )
    for copy in near + [far[number] for number in range(4, 10)]:
        copy.wait_send()


def over_tiles(width, one):
    tile = width // TEAM_SIZE

    def body(step, carry):
        one(step, pl.ds(pl.multiple_of(step * tile, tile), tile))
        return carry

    lax.fori_loop(0, TEAM_SIZE, body, 0)


def whole_block(ref, step, columns=slice(None)):
    block = ref[:, step, :, columns]
    return block.reshape(block.shape[0] * block.shape[1], block.shape[2])


def push_kernel(count, kept, *refs):
    blocks, rest = refs[:count], refs[count : count + kept]
    landed = refs[count + kept : 2 * count + kept]
    own_sem, send_sem, recv_sem = refs[2 * count + kept :]
    place = team_place()
    barrier = pltpu.get_barrier_semaphore()
    flips = [(step // 4, step // 2 % 2, step % 2) for step in range(1, TEAM_SIZE)]
    team = [
        (
            member(place, flip),
            {axis: 1 - at if turn else at for axis, at, turn in zip(TEAM, place, flip)},
        )
        for flip in flips
    ]
    for _, device in team:
        pl.semaphore_signal(
            barrier, inc=1, device_id=device, device_id_type=pl.DeviceIdType.MESH
        )
    pl.semaphore_wait(barrier, len(team))
    me = member(place, (0, 0, 0))
    copies = []

    def block(item, index):
        return blocks[item].at[index if blocks[item].shape[0] == TEAM_SIZE else 0]

    def target(item):
        if kept and item == 0:
            return landed[item].at[me, :, pl.ds(0, blocks[item].shape[2])]
        return landed[item].at[me]

    for item in range(count):
        for number, (index, device) in enumerate(team):
            copy = pltpu.make_async_remote_copy(
                src_ref=block(item, index),
                dst_ref=target(item),
                send_sem=send_sem.at[item, number],
                recv_sem=recv_sem.at[item, number],
                device_id=device,
                device_id_type=pl.DeviceIdType.MESH,
            )
            copy.start()
            copies.append(copy)
    keeps = [
        pltpu.make_async_copy(block(item, me), target(item), own_sem.at[item])
        for item in range(count)
    ]
    if kept:
        first = blocks[0].shape[2]
        keeps.append(
            pltpu.make_async_copy(
                rest[0], landed[0].at[:, :, pl.ds(first, rest[0].shape[2])], own_sem.at[count]
            )
        )
    for keep in keeps:
        keep.start()
    for copy in copies:
        copy.wait_recv()
    for keep in keeps:
        keep.wait()
    for copy in copies:
        copy.wait_send()


def push_team(arrays, collective_id, kept=()):
    count = len(arrays)
    anywhere = pl.BlockSpec(memory_space=pl.ANY)
    out_shape = [
        jax.ShapeDtypeStruct((TEAM_SIZE,) + array.shape[1:], array.dtype) for array in arrays
    ]
    for array in kept:
        team, rows, width = out_shape[0].shape
        out_shape[0] = jax.ShapeDtypeStruct((team, rows, width + array.shape[2]), array.dtype)
    return pl.pallas_call(
        functools.partial(push_kernel, count, len(kept)),
        out_shape=out_shape,
        in_specs=[anywhere] * (count + len(kept)),
        out_specs=[anywhere] * count,
        scratch_shapes=[
            pltpu.SemaphoreType.DMA((count + len(kept),)),
            pltpu.SemaphoreType.DMA((count, TEAM_SIZE - 1)),
            pltpu.SemaphoreType.DMA((count, TEAM_SIZE - 1)),
        ],
        compiler_params=pltpu.CompilerParams(
            collective_id=collective_id, has_side_effects=True, vmem_limit_bytes=GATHER_VMEM
        ),
        cost_estimate=pl.CostEstimate(
            flops=0, bytes_accessed=40 * sum(array.size for array in arrays), transcendentals=0
        ),
    )(*arrays, *kept)


def product_down(operands, pair, step, columns):
    hidden, weight = operands
    return jnp.dot(hidden[pair], weight[:, columns], preferred_element_type=jnp.float32)


def product_out(operands, pair, step, columns):
    gated, weight = operands
    depth = gated.shape[2]
    share = pl.ds(weight.shape[3] - depth, depth)
    return jnp.dot(
        gated[pair], whole_block(weight, step, share), preferred_element_type=jnp.float32
    )


def product_ffn_back(operands, pair, step, columns):
    grad_inner, grad_up, inner_weight, up_weight = operands
    return dot_t(grad_inner[pair], whole_block(inner_weight, step)) + dot_t(
        grad_up[pair], whole_block(up_weight, step)
    )


def product_qkv_back(operands, pair, step, columns):
    grad_products, weight, gate_weight = operands
    depth = grad_products.shape[2] - LANES
    share = pl.ds(0, depth)
    return dot_t(grad_products[pair, :, share], whole_block(weight, step, share)) + dot_t(
        grad_products[pair, :, pl.ds(depth, LANES)], gate_weight[columns, :]
    )


def scatter_team(
    product, lefts, rights, collective_id, work=None, operands=(), results=()
):
    rows = lefts[0].shape[0] // TEAM_SIZE
    depth = sum(left.shape[1] for left in lefts)
    width = MODEL_WIDTH
    paired = [left.reshape(TEAM_SIZE // 2, 2 * rows, left.shape[1]) for left in lefts]
    vmem = pl.BlockSpec(memory_space=pltpu.VMEM)
    anywhere = pl.BlockSpec(memory_space=pl.ANY)
    count = len(lefts) + len(rights)
    summed = pl.pallas_call(
        functools.partial(
            scatter_kernel, product, count, (work, len(operands), len(results)) if work else None
        ),
        out_shape=[jax.ShapeDtypeStruct((rows, width), jnp.float32)] + list(results),
        in_specs=[vmem] * count + [anywhere] * len(operands),
        out_specs=[vmem] + [anywhere] * len(results),
        scratch_shapes=[
            pltpu.VMEM((4, rows, width), jnp.float32),
            pltpu.VMEM((4, rows, width), jnp.bfloat16),
            pltpu.VMEM((4, rows, width), jnp.bfloat16),
            pltpu.VMEM((3, rows, width), jnp.bfloat16),
            pltpu.VMEM((2, rows // 2, width), jnp.bfloat16),
            pltpu.VMEM((2, rows, width), jnp.bfloat16),
            pltpu.SemaphoreType.DMA((10,)),
            pltpu.SemaphoreType.DMA((10,)),
        ],
        compiler_params=pltpu.CompilerParams(
            collective_id=collective_id, has_side_effects=True, vmem_limit_bytes=VMEM_BYTES
        ),
        cost_estimate=pl.CostEstimate(
            flops=2 * TEAM_SIZE * rows * depth * width,
            bytes_accessed=SCATTER_COST * rows * width,
            transcendentals=0,
        ),
    )(*paired, *rights, *operands)
    return summed if work else summed[0]


def ffn_kernel(rows_ref, inner_ref, up_ref, hidden_ref, slope_ref, swish_ref, inner_weight, up_weight):
    @pl.when(pl.program_id(0) == 0)
    def _():
        block = inner_ref.shape[0] * inner_ref.shape[2]
        for step in range(TEAM_SIZE):
            inner_weight[pl.ds(step * block, block), :] = whole_block(inner_ref, step)
            up_weight[pl.ds(step * block, block), :] = whole_block(up_ref, step)

    tile = 256

    def one(step, carry):
        columns = pl.ds(pl.multiple_of(step * tile, tile), tile)
        inner = jnp.dot(rows_ref[0], inner_weight[:, columns], preferred_element_type=jnp.float32)
        up_part = jnp.dot(rows_ref[0], up_weight[:, columns], preferred_element_type=jnp.float32)
        sigma = jax.nn.sigmoid(inner)
        swish = inner * sigma
        hidden_ref[0, :, columns] = (swish * up_part).astype(jnp.bfloat16)
        slope_ref[0, :, columns] = up_part * sigma * (1.0 + inner * (1.0 - sigma))
        swish_ref[0, :, columns] = swish
        return carry

    lax.fori_loop(0, hidden_ref.shape[2] // tile, one, 0, unroll=True)


def ffn_forward(normed_rows, inner_weight, up_weight):
    count, depth = TEAM_SIZE // 2, normed_rows.shape[1]
    length = normed_rows.shape[0] // count
    width = inner_weight.shape[3]
    whole = pl.BlockSpec(inner_weight.shape, lambda i: (0, 0, 0, 0), pipeline_mode=pl.Buffered(1))
    out = pl.BlockSpec((1, length, width), lambda i: (i, 0, 0))
    return pl.pallas_call(
        ffn_kernel,
        grid=(count,),
        out_shape=[
            jax.ShapeDtypeStruct((count, length, width), jnp.bfloat16),
            jax.ShapeDtypeStruct((count, length, width), jnp.float32),
            jax.ShapeDtypeStruct((count, length, width), jnp.float32),
        ],
        in_specs=[pl.BlockSpec((1, length, depth), lambda i: (i, 0, 0)), whole, whole],
        out_specs=[out, out, out],
        scratch_shapes=[pltpu.VMEM((depth, width), jnp.bfloat16)] * 2,
        compiler_params=pltpu.CompilerParams(vmem_limit_bytes=VMEM_BYTES),
        cost_estimate=pl.CostEstimate(
            flops=4 * count * length * depth * width,
            bytes_accessed=count * length * (2 * depth + 10 * width),
            transcendentals=count * length * width,
        ),
    )(normed_rows.reshape(count, length, depth), inner_weight, up_weight)


def ffn_back_kernel(grad_ref, weight_ref, slope_ref, swish_ref, inner_ref, up_ref):
    tile = 256

    def one(step, carry):
        columns = pl.ds(pl.multiple_of(step * tile, tile), tile)
        grad_hidden = dot_t(grad_ref[0], weight_ref[columns, :])
        inner_ref[0, :, columns] = (grad_hidden * slope_ref[0, :, columns]).astype(jnp.bfloat16)
        up_ref[0, :, columns] = (grad_hidden * swish_ref[0, :, columns]).astype(jnp.bfloat16)
        return carry

    lax.fori_loop(0, inner_ref.shape[2] // tile, one, 0, unroll=True)


def ffn_back(grad_rows, down_weight, slope, swish):
    count, length, width = slope.shape
    depth = grad_rows.shape[1]
    whole = pl.BlockSpec(down_weight.shape, lambda i: (0, 0), pipeline_mode=pl.Buffered(1))
    part = pl.BlockSpec((1, length, width), lambda i: (i, 0, 0))
    return pl.pallas_call(
        ffn_back_kernel,
        grid=(count,),
        out_shape=[jax.ShapeDtypeStruct((count, length, width), jnp.bfloat16)] * 2,
        in_specs=[pl.BlockSpec((1, length, depth), lambda i: (i, 0, 0)), whole, part, part],
        out_specs=[part, part],
        compiler_params=pltpu.CompilerParams(vmem_limit_bytes=VMEM_BYTES),
        cost_estimate=pl.CostEstimate(
            flops=2 * count * length * depth * width,
            bytes_accessed=count * length * (2 * depth + 12 * width),
            transcendentals=0,
        ),
    )(grad_rows.reshape(count, length, depth), down_weight, slope, swish)


def weight_kernel(left_ref, right_ref, part_ref):
    depth, _, rows, width = part_ref.shape
    part = dot_tokens(left_ref[...], right_ref[...])
    part_ref[...] = part.astype(jnp.bfloat16).reshape(depth, 1, rows, width)


def weight_shape(left, right, rows):
    depth = left.shape[1] // (TEAM_SIZE * rows)
    return jax.ShapeDtypeStruct((depth, TEAM_SIZE, rows, right.shape[1]), jnp.bfloat16)


def weight_specs(left, right, part):
    depth, _, rows, width = part.shape
    return dict(
        grid=(TEAM_SIZE,),
        in_specs=[
            pl.BlockSpec((left.shape[0], depth * rows), lambda i: (0, i)),
            pl.BlockSpec(right.shape, lambda i: (0, 0)),
        ],
        out_specs=[pl.BlockSpec((depth, 1, rows, width), lambda i: (0, i, 0, 0))],
    )


def weight_parts(left, right, rows):
    part = weight_shape(left, right, rows)
    (tokens, height), width = left.shape, right.shape[1]
    return pl.pallas_call(
        weight_kernel,
        out_shape=[part],
        compiler_params=pltpu.CompilerParams(vmem_limit_bytes=VMEM_BYTES),
        cost_estimate=pl.CostEstimate(
            flops=2 * tokens * height * width,
            bytes_accessed=2 * tokens * (height + width) + 2 * height * width,
            transcendentals=0,
        ),
        **weight_specs(left, right, part),
    )(left, right)[0]


def weight_work(left_ref, right_ref, part_ref):
    pltpu.emit_pipeline(weight_kernel, **weight_specs(left_ref, right_ref, part_ref))(
        left_ref, right_ref, part_ref
    )


def attention_weight_kernel(normed_ref, products_ref, gated_ref, grad_ref, part_ref, gate_ref):
    depth, _, rows, _ = part_ref.shape
    own = products_ref.shape[1] - LANES
    part = dot_tokens(normed_ref[...], products_ref[...])
    gate_ref[...] = part[:, own:].T[:SUBLANES]
    part_ref[:, :, :, pl.ds(0, own)] = (
        part[:, :own].astype(jnp.bfloat16).reshape(depth, 1, rows, own)
    )
    share = grad_ref.shape[1]
    part = dot_tokens(gated_ref[...], grad_ref[...])
    part_ref[:, :, :, pl.ds(own, share)] = part.astype(jnp.bfloat16).reshape(depth, 1, rows, share)


def attention_weight_work(*refs):
    normed, products, gated, grad, part, gate = refs
    depth, _, rows, width = part.shape
    share = depth * rows
    column = pl.BlockSpec((normed.shape[0], share), lambda i: (0, i))
    pltpu.emit_pipeline(
        attention_weight_kernel,
        grid=(TEAM_SIZE,),
        in_specs=[
            column,
            pl.BlockSpec(products.shape, lambda i: (0, 0)),
            pl.BlockSpec(gated.shape, lambda i: (0, 0)),
            column,
        ],
        out_specs=[
            pl.BlockSpec((depth, 1, rows, width), lambda i: (0, i, 0, 0)),
            pl.BlockSpec((SUBLANES, share), lambda i: (0, i)),
        ],
    )(*refs)


def attention_weight_shapes(normed, grad_products, rows):
    height, width = normed.shape[1], grad_products.shape[1]
    share = height // TEAM_SIZE
    return [
        jax.ShapeDtypeStruct((share // rows, TEAM_SIZE, rows, width - LANES + share), jnp.bfloat16),
        jax.ShapeDtypeStruct((SUBLANES, height), jnp.float32),
    ]


def greet_all():
    place = team_place()
    barrier = pltpu.get_barrier_semaphore()
    flips = [(step // 4, step // 2 % 2, step % 2) for step in range(1, TEAM_SIZE)]
    team = [
        (
            member(place, flip),
            {axis: 1 - at if turn else at for axis, at, turn in zip(TEAM, place, flip)},
        )
        for flip in flips
    ]
    sizes = [lax.axis_size(axis) for axis in DEPTH]
    depth = sizes[0] * sizes[1]
    spot = lax.axis_index(DEPTH[0]) * sizes[1] + lax.axis_index(DEPTH[1])
    line = []
    for step in range(1, depth):
        other = lax.rem(spot + step, depth)
        line.append({DEPTH[0]: other // sizes[1], DEPTH[1]: lax.rem(other, sizes[1])})
    for target in [device for _, device in team] + line:
        pl.semaphore_signal(
            barrier, inc=1, device_id=target, device_id_type=pl.DeviceIdType.MESH
        )
    pl.semaphore_wait(barrier, len(team) + len(line))
    return member(place, (0, 0, 0)), team, spot, line


def push(source, target, sems, number, device):
    copy = pltpu.make_async_remote_copy(
        src_ref=source,
        dst_ref=target,
        send_sem=sems.at[0, number],
        recv_sem=sems.at[1, number],
        device_id=device,
        device_id_type=pl.DeviceIdType.MESH,
    )
    copy.start()
    return copy


def begin_line(own, slots, sems, spot, line):
    slots[spot] = own[...]
    return [
        push(own, slots.at[spot], sems, number, device) for number, device in enumerate(line)
    ]


def begin_team(copies, slots, team_slots, sems, me, team):
    for copy in copies:
        copy.wait_recv()
    total = slots[0]
    for step in range(1, slots.shape[0]):
        total = total + slots[step]
    team_slots[me] = total
    return [
        push(team_slots.at[me], team_slots.at[me], sems, number, device)
        for number, (_, device) in enumerate(team)
    ]


def depth_size():
    return lax.axis_size(DEPTH[0]) * lax.axis_size(DEPTH[1])


def lane_squares(piece):
    total = jnp.sum(piece * piece, axis=0, keepdims=True)
    lanes = total[:, :LANES]
    for first in range(LANES, total.shape[1], LANES):
        lanes = lanes + total[:, first : first + LANES]
    return lanes


def in_lanes(values, shape):
    lane = lax.broadcasted_iota(jnp.int32, shape, 1)
    row = jnp.zeros(shape, jnp.float32)
    for number, value in enumerate(values):
        row = jnp.where(lane == number, jnp.sum(value, axis=1, keepdims=True), row)
    return row


def update_columns(columns, gradient, state, results, update_ref):
    weight = state[0][:, columns]
    moment, second, update = moments(
        weight, state[1][:, columns], state[2][:, columns], gradient.astype(jnp.float32)
    )
    results[0][:, columns] = moment
    results[1][:, columns] = second
    update_ref[:, columns] = update
    return lane_squares(weight), lane_squares(update)


def at_columns(first, width):
    return pl.ds(pl.multiple_of(first, width if width < LANES else LANES), width)


STEPS = 16


def ffn_moments_kernel(inner_ref, up_ref, down_ref, *refs):
    state, down_state = refs[0:3], refs[3:6]
    results, update, down_results, down_update, squares_ref = (
        refs[6:8], refs[8], refs[9:11], refs[11], refs[12]
    )
    step = pl.program_id(0)

    @pl.when(step == 0)
    def _():
        squares_ref[...] = jnp.zeros_like(squares_ref)

    every = slice(None)
    gradient = jnp.where(
        step < STEPS // 2, inner_ref[0].astype(jnp.float32), up_ref[0].astype(jnp.float32)
    )
    found = update_columns(every, gradient, state, results, update)
    group = step // (STEPS // 2)
    squares_ref[pl.ds(group, 1)] += found[0]
    squares_ref[pl.ds(4 + group, 1)] += found[1]
    found = update_columns(every, down_ref[...], down_state, down_results, down_update)
    squares_ref[2:3] += found[0]
    squares_ref[6:7] += found[1]


def ffn_moments(ffn_rows, down_sum, state, down_state):
    _, rows, width = ffn_rows.shape
    width, half = width // 2, STEPS // 2

    def column(array):
        return pl.BlockSpec((array.shape[0], array.shape[1] // STEPS), lambda i: (0, i))

    like = [jax.ShapeDtypeStruct(state[0].shape, jnp.float32)] * 3
    like_down = [jax.ShapeDtypeStruct(down_state[0].shape, jnp.float32)] * 3
    return pl.pallas_call(
        ffn_moments_kernel,
        grid=(STEPS,),
        out_shape=like + like_down + [jax.ShapeDtypeStruct((SUBLANES, LANES), jnp.float32)],
        in_specs=[
            pl.BlockSpec((1, rows, width), lambda i: (jnp.minimum(i, half - 1), 0, 0)),
            pl.BlockSpec((1, rows, width), lambda i: (jnp.maximum(i - half, 0), 0, 1)),
            column(down_sum),
        ]
        + [column(array) for array in state + down_state],
        out_specs=[column(array) for array in state + down_state]
        + [pl.BlockSpec((SUBLANES, LANES), lambda i: (0, 0))],
        compiler_params=pltpu.CompilerParams(vmem_limit_bytes=GATHER_VMEM),
        cost_estimate=pl.CostEstimate(
            flops=20 * state[0].size, bytes_accessed=30 * state[0].size, transcendentals=0
        ),
    )(ffn_rows, ffn_rows, down_sum, *state, *down_state)


def begin_blocks(parts, landed, columns, sems, me, team):
    landed[me] = parts[me, :, columns]
    return [
        push(parts.at[index, :, columns], landed.at[me], sems, number, device)
        for number, (index, device) in enumerate(team)
    ]


def column_squares(columns, gradient, state):
    weight = state[0][:, columns]
    _, _, update = moments(
        weight, state[1][:, columns], state[2][:, columns], gradient.astype(jnp.float32)
    )
    return lane_squares(weight), lane_squares(update)


def add_all(olds, news):
    return tuple(old + new for old, new in zip(olds, news))


def totals_kernel(
    heads, attention_ref, gate_ref, first_ref, second_ref, qk_ref, ffn_squares_ref, *refs
):
    state, out_state = refs[0:3], refs[3:6]
    rows_out, gate_out, gains_out, qk_out, norms_out = refs[6:11]
    landed, own, line_slots, team_slots, block_sems, line_sems, team_sems = refs[11:]
    me, team, spot, line = greet_all()
    share = landed.shape[2]
    blocks = begin_blocks(attention_ref, landed, pl.ds(0, share), block_sems, me, team)
    query_width = share - 2 * HEAD_WIDTH
    out_width = out_state[0].shape[1] // TEAM_SIZE
    zero = jnp.zeros((1, LANES), jnp.float32)

    def out(turn, sums):
        columns = at_columns(turn * out_width, out_width)
        gradient = attention_ref[turn, :, pl.ds(share, out_width)]
        return add_all(sums, column_squares(columns, gradient, out_state))

    out_sums = lax.fori_loop(0, TEAM_SIZE, out, (zero,) * 2)
    own[...] = jnp.zeros_like(own)
    own[0:heads] = gate_ref[0:heads]
    own[heads : heads + 1] = first_ref[...]
    own[heads + 1 : heads + 2] = second_ref[...]
    for row in range(2):
        own[heads + 2 : heads + 3, pl.ds(row * HEAD_WIDTH, HEAD_WIDTH)] = qk_ref[row : row + 1]
    for copy in blocks:
        copy.wait_recv()

    def projection(turn, sums):
        found = ()
        for first, start, width in (
            (turn * query_width, 0, query_width),
            (TEAM_SIZE * query_width + turn * HEAD_WIDTH, query_width, HEAD_WIDTH),
            (
                TEAM_SIZE * (query_width + HEAD_WIDTH) + turn * HEAD_WIDTH,
                query_width + HEAD_WIDTH,
                HEAD_WIDTH,
            ),
        ):
            gradient = landed[turn, :, pl.ds(start, width)]
            found = found + column_squares(at_columns(first, width), gradient, state)
        return add_all(sums, found)

    sums = lax.fori_loop(0, TEAM_SIZE, projection, (zero,) * 6) + out_sums
    rows = [sums[2 * group] for group in range(4)]
    rows += [ffn_squares_ref[group : group + 1] for group in range(3)]
    rows += [sums[2 * group + 1] for group in range(4)]
    rows += [ffn_squares_ref[4 + group : 5 + group] for group in range(3)]
    own[heads + 2 : heads + 3, pl.ds(2 * HEAD_WIDTH, LANES)] = in_lanes(rows, (1, LANES))
    along = begin_line(own, line_slots, line_sems, spot, line)
    rows_out[...] = landed[...]
    across = begin_team(along, line_slots, team_slots, team_sems, me, team)
    for copy in across:
        copy.wait_recv()
    total = team_slots[0, heads:]
    for turn in range(1, TEAM_SIZE):
        total = total + team_slots[turn, heads:]
    gains_out[...] = total[:2]
    for row in range(2):
        qk_out[row : row + 1] = total[2:3, row * HEAD_WIDTH : (row + 1) * HEAD_WIDTH]
    for turn in range(TEAM_SIZE):
        gate_out[turn * heads : (turn + 1) * heads] = team_slots[turn, :heads]
    norms = jnp.sqrt(total[2:3, 2 * HEAD_WIDTH : 2 * HEAD_WIDTH + LANES])
    groups = 7
    weight_norms = [norms[:, number : number + 1] for number in range(groups)]
    update_norms = [norms[:, groups + number : groups + number + 1] for number in range(groups)]
    norms_out[...] = jnp.zeros_like(norms_out)
    norms_out[0:1] = in_lanes(weight_norms, (1, LANES))
    norms_out[1:2] = in_lanes(update_norms, (1, LANES))
    norms_out[2:3] = in_lanes(
        [former / latter for former, latter in zip(weight_norms, update_norms)], (1, LANES)
    )
    for copy in blocks + along + across:
        copy.wait_send()


def totals(
    heads, attention_sum, gate_part, gains, qk_gains, ffn_squares, state, out_state, collective_id
):
    vmem = pl.BlockSpec(memory_space=pltpu.VMEM)
    width = gate_part.shape[1]
    depth = depth_size()
    team, rows, _ = attention_sum.shape
    share = state[0].shape[1] // TEAM_SIZE
    return pl.pallas_call(
        functools.partial(totals_kernel, heads),
        out_shape=[
            jax.ShapeDtypeStruct((team, rows, share), jnp.bfloat16),
            jax.ShapeDtypeStruct((TEAM_SIZE * heads, width), jnp.float32),
            jax.ShapeDtypeStruct((2, width), jnp.float32),
            jax.ShapeDtypeStruct((2, HEAD_WIDTH), jnp.float32),
            jax.ShapeDtypeStruct((SUBLANES, LANES), jnp.float32),
        ],
        in_specs=[vmem] * 12,
        out_specs=[vmem] * 5,
        scratch_shapes=[
            pltpu.VMEM((team, rows, share), jnp.bfloat16),
            pltpu.VMEM((SUBLANES, width), jnp.float32),
            pltpu.VMEM((depth, SUBLANES, width), jnp.float32),
            pltpu.VMEM((TEAM_SIZE, SUBLANES, width), jnp.float32),
            pltpu.SemaphoreType.DMA((2, TEAM_SIZE - 1)),
            pltpu.SemaphoreType.DMA((2, max(depth - 1, 1))),
            pltpu.SemaphoreType.DMA((2, TEAM_SIZE - 1)),
        ],
        compiler_params=pltpu.CompilerParams(
            collective_id=collective_id, has_side_effects=True, vmem_limit_bytes=GATHER_VMEM
        ),
    )(
        attention_sum, gate_part, gains[0][None], gains[1][None], qk_gains, ffn_squares,
        *state, *out_state,
    )


def small_update(state, gradient, results, by_row):
    weight = state[0][...]
    moment, second, update = moments(weight, state[1][...], state[2][...], gradient[...])
    ratio = jnp.sum(weight * weight, axis=1, keepdims=True)
    size = jnp.sum(update * update, axis=1, keepdims=True)
    if not by_row:
        ratio = jnp.sum(ratio, axis=0, keepdims=True)
        size = jnp.sum(size, axis=0, keepdims=True)
    results[0][...] = weight - RATE * (jnp.sqrt(ratio) / jnp.sqrt(size)) * update
    results[1][...] = moment
    results[2][...] = second


def apply_kernel(
    norms_ref, gate_ref, gains_ref, qk_ref, rows_ref, attention_ref, *refs
):
    state, out_state = refs[0:3], refs[3:6]
    ffn_pair, down_pair = refs[6:8], refs[8:10]
    states = [refs[10 + 3 * number : 13 + 3 * number] for number in range(3)]
    targets, out_targets = refs[19:23], refs[23:27]
    ffn_targets, down_targets = refs[27:29], refs[29:31]
    results = [refs[31 + 3 * number : 34 + 3 * number] for number in range(3)]
    norms_out, gradient = refs[40], refs[41]
    step = pl.program_id(0)
    share = rows_ref.shape[2]
    wide = share - 2 * HEAD_WIDTH
    query_steps = TEAM_SIZE * wide // gradient.shape[1]
    key_steps = TEAM_SIZE * HEAD_WIDTH // gradient.shape[1]
    per_step = gradient.shape[1] // HEAD_WIDTH

    @pl.when(step == 0)
    def _():
        norms_out[...] = norms_ref[0:2]
        small_update(states[0], gate_ref, results[0], False)
        small_update(states[1], gains_ref, results[1], True)
        small_update(states[2], qk_ref, results[2], True)

    @pl.when(step < query_steps)
    def _():
        gradient[...] = rows_ref[step, :, pl.ds(0, wide)].astype(jnp.float32)

    for number in range(2):
        first = query_steps + number * key_steps

        @pl.when((step >= first) & (step < first + key_steps))
        def _():
            for item in range(per_step):
                gradient[:, pl.ds(item * HEAD_WIDTH, HEAD_WIDTH)] = rows_ref[
                    (step - first) * per_step + item, :, pl.ds(wide + number * HEAD_WIDTH, HEAD_WIDTH)
                ].astype(jnp.float32)

    def rate(first, uppers=()):
        found = norms_ref[2:3, first : first + 1]
        for number, upper in enumerate(uppers):
            group = first + number + 1
            found = jnp.where(step < upper, found, norms_ref[2:3, group : group + 1])
        return RATE * found

    def renew(weight, update, new, low_new, factor):
        value = weight - factor * update
        new[...] = value
        low_new[...] = value.astype(jnp.bfloat16)

    def both(state, gradient, targets, factor):
        weight = state[0][...]
        moment, second, update = moments(weight, state[1][...], state[2][...], gradient)
        targets[2][...] = moment
        targets[3][...] = second
        renew(weight, update, targets[0], targets[1], factor)

    both(state, gradient[...], targets, rate(0, (query_steps, query_steps + key_steps)))
    width = out_state[0].shape[1]
    per_block = (attention_ref.shape[2] - share) // width
    columns = at_columns(share + lax.rem(step, per_block) * width, width)
    both(
        out_state, attention_ref[step // per_block, :, columns].astype(jnp.float32), out_targets,
        rate(3),
    )
    renew(ffn_pair[0][...], ffn_pair[1][...], *ffn_targets, rate(4, (STEPS // 2,)))
    renew(down_pair[0][...], down_pair[1][...], *down_targets, rate(6))


def apply_all(
    norms, gate_total, gains_total, qk_total, projection_rows, attention_sum, state, out_state,
    ffn_pair, down_pair, states,
):
    def whole(array):
        return pl.BlockSpec(array.shape, lambda i: (0,) * array.ndim)

    def column(array):
        return pl.BlockSpec((array.shape[0], array.shape[1] // STEPS), lambda i: (0, i))

    def like(array, kind=jnp.float32):
        return jax.ShapeDtypeStruct(array.shape, kind)

    small = [array for group in states for array in group]
    fixed = [norms, gate_total, gains_total, qk_total, projection_rows, attention_sum]
    split = [*state, *out_state, *ffn_pair, *down_pair]
    targets = []
    for group in (state, out_state):
        targets += [like(group[0]), like(group[0], jnp.bfloat16), like(group[1]), like(group[2])]
    for group in (ffn_pair, down_pair):
        targets += [like(group[0]), like(group[0], jnp.bfloat16)]
    results = [like(array) for array in small]
    results.append(jax.ShapeDtypeStruct((2, norms.shape[1]), jnp.float32))
    rows = state[0].shape[0]
    return pl.pallas_call(
        apply_kernel,
        grid=(STEPS,),
        out_shape=targets + results,
        in_specs=[whole(array) for array in fixed]
        + [column(array) for array in split]
        + [whole(array) for array in small],
        out_specs=[column(array) for array in targets] + [whole(array) for array in results],
        scratch_shapes=[pltpu.VMEM((rows, state[0].shape[1] // STEPS), jnp.float32)],
        compiler_params=pltpu.CompilerParams(vmem_limit_bytes=GATHER_VMEM),
        cost_estimate=pl.CostEstimate(
            flops=4 * ffn_pair[0].size, bytes_accessed=30 * ffn_pair[0].size, transcendentals=0
        ),
    )(*fixed, *split, *small)


def team_exchange(blocks):
    return lax.all_to_all(blocks, TEAM, split_axis=0, concat_axis=0, tiled=True)


def turn_half(value_rows):
    return pltpu.roll(value_rows, value_rows.shape[-1] // 2, value_rows.ndim - 1)


def norm_turn(value_rows, gain, cosine, sine):
    scaled = rms_apply(value_rows, gain)
    return scaled * cosine + turn_half(scaled) * sine


def norm_turn_back(value_rows, gain, cosine, sine, gradient):
    turned = gradient * cosine + turn_half(gradient * sine)
    return rms_back(value_rows, gain, turned)


def greet_line():
    index, count = lax.axis_index("seq"), lax.axis_size("seq")
    barrier = pltpu.get_barrier_semaphore()

    @pl.when(index > 0)
    def _():
        pl.semaphore_signal(
            barrier, inc=1, device_id={"seq": index - 1}, device_id_type=pl.DeviceIdType.MESH
        )

    @pl.when(index < count - 1)
    def _():
        pl.semaphore_signal(
            barrier, inc=1, device_id={"seq": index + 1}, device_id_type=pl.DeviceIdType.MESH
        )

    inside = (index > 0) & (index < count - 1)

    @pl.when(inside)
    def _():
        pl.semaphore_wait(barrier, 2)

    @pl.when(jnp.logical_not(inside))
    def _():
        pl.semaphore_wait(barrier, 1)

    return index, count


def attend_kernel(
    window, scale, rows_ref, weight_ref, gate_ref, gains_ref, cosine_ref, sine_ref, start_ref,
    raw_ref, query_ref, pair_ref, stats_ref, across_ref, attended_ref, gated_ref,
    weight, pairs, send_sem, recv_sem,
):
    count_rows, length, _ = rows_ref.shape
    query_cols = query_ref.shape[2]
    heads = query_cols // HEAD_WIDTH
    keys_at = pl.ds(0, HEAD_WIDTH)
    values_at = pl.ds(HEAD_WIDTH, HEAD_WIDTH)
    index, count = greet_line()

    def hop(turn, row):
        return pltpu.make_async_remote_copy(
            src_ref=pairs.at[window - turn + 1, row],
            dst_ref=pairs.at[window - turn, row],
            send_sem=send_sem.at[turn - 1, row],
            recv_sem=recv_sem.at[turn - 1, row],
            device_id={"seq": lax.rem(index + 1, count)},
            device_id_type=pl.DeviceIdType.MESH,
        )

    block = weight_ref.shape[0] * weight_ref.shape[2]
    own = raw_ref.shape[2]
    for step in range(TEAM_SIZE):
        weight[pl.ds(step * block, block), pl.ds(0, own)] = whole_block(
            weight_ref, step, pl.ds(0, own)
        )
    weight[:, pl.ds(own, LANES)] = gate_ref[...]

    def project(row, carry):
        products = jnp.dot(rows_ref[row], weight[...], preferred_element_type=jnp.float32)
        raw = products[:, : query_cols + 2 * HEAD_WIDTH].astype(jnp.bfloat16)
        raw_ref[row] = raw
        cosine, sine = cosine_ref[row], sine_ref[row]
        key = norm_turn(
            raw[:, query_cols : query_cols + HEAD_WIDTH].astype(jnp.float32),
            gains_ref[1:2], cosine, sine,
        )
        pairs[window, row, :, keys_at] = key.astype(jnp.bfloat16)
        pairs[window, row, :, values_at] = raw[:, query_cols + HEAD_WIDTH :]

        @pl.when(index < count - 1)
        def _():
            hop(1, row).start()

        for head in range(heads):
            columns = slice(head * HEAD_WIDTH, (head + 1) * HEAD_WIDTH)
            query_ref[row, :, columns] = norm_turn(
                raw[:, columns].astype(jnp.float32), gains_ref[0:1], cosine, sine
            ).astype(jnp.bfloat16)
        stats_ref[row] = jax.nn.sigmoid(products[:, query_cols + 2 * HEAD_WIDTH :])
        return carry

    lax.fori_loop(0, count_rows, project, 0)

    @pl.when(index == 0)
    def _():
        for slot in range(window):
            pairs[slot] = jnp.zeros_like(pairs[slot])

    for turn in range(2, window + 1):

        def forward(row, carry):
            @pl.when(index > 0)
            def _():
                hop(turn - 1, row).wait_recv()

            @pl.when(index < count - 1)
            def _():
                hop(turn, row).start()

            return carry

        lax.fori_loop(0, count_rows, forward, 0)

    places = lax.broadcasted_iota(jnp.int32, (length, (window + 1) * length), 1)
    latest = window * length + lax.broadcasted_iota(jnp.int32, places.shape, 0)
    lane = lax.broadcasted_iota(jnp.int32, (length, LANES), 1)

    def attend(row, carry):
        @pl.when(index > 0)
        def _():
            hop(window, row).wait_recv()

        allowed = (places >= start_ref[row]) & (places <= latest)
        keys = pairs[:, row, :, keys_at].reshape(-1, HEAD_WIDTH)
        values = pairs[:, row, :, values_at].reshape(-1, HEAD_WIDTH)
        stats = stats_ref[row]
        for head in range(heads):
            columns = slice(head * HEAD_WIDTH, (head + 1) * HEAD_WIDTH)
            scores = dot_t(query_ref[row, :, columns], keys) * scale
            scores = jnp.where(allowed, scores, NEGATIVE)
            top = jnp.max(scores, axis=1, keepdims=True)
            powers = jnp.exp(scores - top)
            total = jnp.sum(powers, axis=1, keepdims=True)
            low_probs = (powers * (1.0 / total)).astype(jnp.bfloat16)
            output = jnp.dot(low_probs, values, preferred_element_type=jnp.float32)
            output = output.astype(jnp.bfloat16)
            attended_ref[row, :, columns] = output
            gated_ref[row, :, columns] = (
                output.astype(jnp.float32) * stats[:, head : head + 1]
            ).astype(jnp.bfloat16)
            stats = jnp.where(lane == heads + head, top + jnp.log(total), stats)
        stats_ref[row] = stats
        across_ref[row] = stats.T[:SUBLANES]
        pair_ref[:, row] = pairs[:, row]
        return carry

    lax.fori_loop(0, count_rows, attend, 0)

    @pl.when(index < count - 1)
    def _():
        for turn in range(1, window + 1):

            def finish(row, carry):
                hop(turn, row).wait_send()
                return carry

            lax.fori_loop(0, count_rows, finish, 0)


def attend(
    normed_rows, own_attention, own_gate, gains, cosine, sine, starts, query_cols, window, collective_id
):
    rows, length, _ = normed_rows.shape
    width = query_cols + 2 * HEAD_WIDTH + LANES
    bf16 = jnp.bfloat16
    vmem = pl.BlockSpec(memory_space=pltpu.VMEM)
    return pl.pallas_call(
        functools.partial(attend_kernel, window, HEAD_WIDTH ** (-0.5)),
        out_shape=[
            jax.ShapeDtypeStruct((rows, length, query_cols + 2 * HEAD_WIDTH), bf16),
            jax.ShapeDtypeStruct((rows, length, query_cols), bf16),
            jax.ShapeDtypeStruct((window + 1, rows, length, 2 * HEAD_WIDTH), bf16),
            jax.ShapeDtypeStruct((rows, length, LANES), jnp.float32),
            jax.ShapeDtypeStruct((rows, SUBLANES, length), jnp.float32),
            jax.ShapeDtypeStruct((rows, length, query_cols), bf16),
            jax.ShapeDtypeStruct((rows, length, query_cols), bf16),
        ],
        in_specs=[vmem] * 7,
        out_specs=[vmem] * 7,
        scratch_shapes=[
            pltpu.VMEM((MODEL_WIDTH, width), bf16),
            pltpu.VMEM((window + 1, rows, length, 2 * HEAD_WIDTH), bf16),
            pltpu.SemaphoreType.DMA((window, rows)),
            pltpu.SemaphoreType.DMA((window, rows)),
        ],
        compiler_params=pltpu.CompilerParams(
            collective_id=collective_id, has_side_effects=True, vmem_limit_bytes=VMEM_BYTES
        ),
        cost_estimate=pl.CostEstimate(
            flops=2 * rows * length * MODEL_WIDTH * width,
            bytes_accessed=ATTEND_COST * rows * length * MODEL_WIDTH,
            transcendentals=0,
        ),
    )(normed_rows, own_attention, own_gate, gains, cosine, sine, starts)


def attend_back_kernel(
    window, scale, rows_ref, weight_ref, gains_ref, cosine_ref, sine_ref, start_ref,
    raw_ref, query_ref, pair_ref, stats_ref, across_ref, attended_ref,
    products_ref, gain_ref,
    weight, parts, outs, ins, send_sem, recv_sem,
):
    count_rows, length, _ = rows_ref.shape
    query_cols = query_ref.shape[2]
    heads = query_cols // HEAD_WIDTH
    keys_at = pl.ds(0, HEAD_WIDTH)
    values_at = pl.ds(HEAD_WIDTH, HEAD_WIDTH)
    index, count = greet_line()
    lag = 2

    def hop(turn, row):
        return pltpu.make_async_remote_copy(
            src_ref=outs.at[turn - 1, row],
            dst_ref=ins.at[turn - 1, row],
            send_sem=send_sem.at[turn - 1, row],
            recv_sem=recv_sem.at[turn - 1, row],
            device_id={"seq": lax.rem(index + count - 1, count)},
            device_id_type=pl.DeviceIdType.MESH,
        )

    keys_total = (window + 1) * length
    places = lax.broadcasted_iota(jnp.int32, (keys_total, length), 0)
    latest = window * length + lax.broadcasted_iota(jnp.int32, places.shape, 1)
    lane = lax.broadcasted_iota(jnp.int32, (length, LANES), 1)
    gain_ref[...] = jnp.zeros_like(gain_ref)
    share = weight_ref.shape[3] - query_cols
    for step in range(TEAM_SIZE):
        weight[:, pl.ds(step * query_cols, query_cols)] = whole_block(
            weight_ref, step, pl.ds(share, query_cols)
        )

    @pl.when(index == count - 1)
    def _():
        ins[...] = jnp.zeros_like(ins)

    def compute(row):
        grad_gated = dot_t(rows_ref[row], weight[...])
        keys = pair_ref[:, row, :, keys_at].reshape(-1, HEAD_WIDTH)
        values = pair_ref[:, row, :, values_at].reshape(-1, HEAD_WIDTH)
        allowed = (places >= start_ref[row]) & (places <= latest)
        cosine, sine = cosine_ref[row], sine_ref[row]
        grad_pre = jnp.zeros((length, LANES), jnp.float32)
        grad_keys = jnp.zeros((keys_total, HEAD_WIDTH), jnp.float32)
        grad_values = jnp.zeros((keys_total, HEAD_WIDTH), jnp.float32)
        for head in range(heads):
            columns = slice(head * HEAD_WIDTH, (head + 1) * HEAD_WIDTH)
            gate = stats_ref[row, :, head : head + 1]
            own = grad_gated[:, columns]
            grad_out = (own * gate).astype(jnp.bfloat16)
            grad_gate = jnp.sum(
                own * attended_ref[row, :, columns].astype(jnp.float32), axis=1, keepdims=True
            )
            grad_pre = jnp.where(lane == head, grad_gate * gate * (1.0 - gate), grad_pre)
            query = query_ref[row, :, columns]
            scores = jnp.where(allowed, dot_t(keys, query) * scale, NEGATIVE)
            probs = jnp.exp(scores - across_ref[row, heads + head : heads + head + 1])
            grad_probs = dot_t(values, grad_out)
            inner = jnp.sum(probs * grad_probs, axis=0, keepdims=True)
            grad_scores = (probs * (grad_probs - inner)).astype(jnp.bfloat16)
            grad_values = grad_values + jnp.dot(
                probs.astype(jnp.bfloat16), grad_out, preferred_element_type=jnp.float32
            )
            grad_keys = grad_keys + jnp.dot(
                grad_scores, query, preferred_element_type=jnp.float32
            )
            grad_query = dot_tokens(grad_scores, keys) * scale
            grad_raw, gain = norm_turn_back(
                raw_ref[row, :, columns].astype(jnp.float32), gains_ref[0:1], cosine, sine,
                grad_query,
            )
            products_ref[row, :, columns] = grad_raw.astype(jnp.bfloat16)
            gain_ref[0:1] += jnp.sum(gain, axis=0, keepdims=True)
        products_ref[row, :, query_cols + 2 * HEAD_WIDTH :] = grad_pre.astype(jnp.bfloat16)
        parts[:, row, :, keys_at] = (grad_keys * scale).reshape(window + 1, length, HEAD_WIDTH)
        parts[:, row, :, values_at] = grad_values.reshape(window + 1, length, HEAD_WIDTH)

    def finish(row):
        grad_pair = parts[window, row] + ins[window - 1, row].astype(jnp.float32)
        grad_raw, gain = norm_turn_back(
            raw_ref[row, :, query_cols : query_cols + HEAD_WIDTH].astype(jnp.float32),
            gains_ref[1:2], cosine_ref[row], sine_ref[row], grad_pair[:, :HEAD_WIDTH],
        )
        products_ref[row, :, query_cols : query_cols + HEAD_WIDTH] = grad_raw.astype(jnp.bfloat16)
        products_ref[row, :, query_cols + HEAD_WIDTH : query_cols + 2 * HEAD_WIDTH] = grad_pair[
            :, HEAD_WIDTH:
        ].astype(jnp.bfloat16)
        gain_ref[1:2] += jnp.sum(gain, axis=0, keepdims=True)

    def step(turn_row, carry):
        @pl.when(turn_row < count_rows)
        def _():
            compute(turn_row)

        for turn in range(1, window + 2):
            row = turn_row - lag * (turn - 1)

            @pl.when((row >= 0) & (row < count_rows))
            def _():
                if turn > 1:

                    @pl.when(index < count - 1)
                    def _():
                        hop(turn - 1, row).wait_recv()

                if turn == window + 1:
                    finish(row)
                else:
                    part = parts[turn - 1, row]
                    if turn > 1:
                        part = part + ins[turn - 2, row].astype(jnp.float32)
                    outs[turn - 1, row] = part.astype(jnp.bfloat16)

                    @pl.when(index > 0)
                    def _():
                        hop(turn, row).start()

        return carry

    lax.fori_loop(0, count_rows + lag * window, step, 0)

    @pl.when(index > 0)
    def _():
        for turn in range(1, window + 1):

            def done(row, carry):
                hop(turn, row).wait_send()
                return carry

            lax.fori_loop(0, count_rows, done, 0)


def attend_back(
    grad_rows, own_attention, gains, cosine, sine, starts, saved, window, collective_id
):
    rows, length, _ = grad_rows.shape
    query_cols = saved[1].shape[2]
    width = query_cols + 2 * HEAD_WIDTH + LANES
    bf16 = jnp.bfloat16
    vmem = pl.BlockSpec(memory_space=pltpu.VMEM)
    return pl.pallas_call(
        functools.partial(attend_back_kernel, window, HEAD_WIDTH ** (-0.5)),
        out_shape=[
            jax.ShapeDtypeStruct((rows, length, width), bf16),
            jax.ShapeDtypeStruct((SUBLANES, HEAD_WIDTH), jnp.float32),
        ],
        in_specs=[vmem] * 12,
        out_specs=[vmem] * 2,
        scratch_shapes=[
            pltpu.VMEM((query_cols, MODEL_WIDTH), bf16),
            pltpu.VMEM((window + 1, rows, length, 2 * HEAD_WIDTH), jnp.float32),
            pltpu.VMEM((window, rows, length, 2 * HEAD_WIDTH), bf16),
            pltpu.VMEM((window, rows, length, 2 * HEAD_WIDTH), bf16),
            pltpu.SemaphoreType.DMA((window, rows)),
            pltpu.SemaphoreType.DMA((window, rows)),
        ],
        compiler_params=pltpu.CompilerParams(
            collective_id=collective_id, has_side_effects=True, vmem_limit_bytes=VMEM_BYTES
        ),
        cost_estimate=pl.CostEstimate(
            flops=2 * rows * length * MODEL_WIDTH * query_cols,
            bytes_accessed=ATTEND_COST * rows * length * MODEL_WIDTH,
            transcendentals=0,
        ),
    )(grad_rows, own_attention, gains, cosine, sine, starts, *saved)


def team_columns(matrix, widths):
    pieces = []
    lower = 0
    for width in widths:
        piece = matrix[:, lower : lower + width]
        pieces.append(piece.reshape(matrix.shape[0], TEAM_SIZE, width // TEAM_SIZE))
        lower = lower + width
    return jnp.concatenate(pieces, axis=2).transpose(1, 0, 2)


def gather_parts(blocks):
    return lax.all_gather(blocks, DEPTH, axis=0, tiled=False)


def scatter_parts(parts):
    depth, team, rows, width = parts.shape
    return lax.psum_scatter(
        parts.reshape(depth * team * rows, width), DEPTH, scatter_dimension=0, tiled=True
    ).reshape(team, rows, width)


def gather_rows(matrix):
    return lax.all_gather(matrix, DEPTH, axis=0, tiled=True)


def scatter_rows(gradient):
    return lax.psum_scatter(gradient, DEPTH, scatter_dimension=0, tiled=True)


def shards(
    inputs,
    cotangent,
    doc_lengths,
    projection_weight,
    projection_moment,
    projection_second,
    out_weight,
    out_moment,
    out_second,
    ffn_weight,
    ffn_moment,
    ffn_second,
    down_weight,
    down_moment,
    down_second,
    head_gate,
    gate_moment,
    gate_second,
    norm_gains,
    gains_moment,
    gains_second,
    qk_gains,
    qk_moment,
    qk_second,
):
    rows_dev, local_len, width = inputs.shape
    bf16 = jnp.bfloat16
    team = lax.axis_index(TEAM)
    place_seq = lax.axis_index("seq")
    group_heads = QUERY_HEADS // KEY_VALUE_HEADS
    window = -(-(DOC_MOST - 1) // local_len)
    window = min(window, lax.axis_size("seq") - 1)
    query_cols = QUERY_HEADS * HEAD_WIDTH
    key_value_columns = KEY_VALUE_HEADS * HEAD_WIDTH
    widths_qkv = (query_cols, key_value_columns, key_value_columns)
    widths_ffn = (FF, FF)
    own_query = query_cols // TEAM_SIZE
    own_key = key_value_columns // TEAM_SIZE
    own_ff = FF // TEAM_SIZE
    own_gate = lax.dynamic_slice_in_dim(head_gate.astype(bf16), team * group_heads, group_heads, 1)
    own_gate = jnp.pad(own_gate, ((0, 0), (0, LANES - group_heads)))
    (attention_blocks,) = push_team(
        [team_columns(projection_weight.astype(bf16), widths_qkv)],
        11,
        [team_columns(out_weight.astype(bf16), (MODEL_WIDTH,))],
    )
    own_attention = gather_parts(attention_blocks)
    low_ffn, attention_blocks = lax.optimization_barrier(
        (ffn_weight.astype(bf16), attention_blocks)
    )
    inner_blocks, up_blocks, lengths = push_team(
        [
            team_columns(low_ffn[:, :FF], (FF,)),
            team_columns(low_ffn[:, FF:], (FF,)),
            jnp.pad(doc_lengths, ((0, SUBLANES - 1), (0, LANES - doc_lengths.shape[1])))[None],
        ],
        12,
    )
    own_inner = gather_parts(inner_blocks)
    lengths = lengths[:, 0, : doc_lengths.shape[1]]
    place = place_seq * local_len + jnp.arange(local_len, dtype=jnp.int32)
    position = positions(lengths, place)
    cosine, sine = rotary_tables(position, HEAD_WIDTH)
    starts = window * local_len + jnp.arange(local_len, dtype=jnp.int32)[None, :] - position
    inputs_flat = inputs[0].astype(jnp.float32)
    normed = rms_apply(inputs_flat, norm_gains[0]).astype(bf16)
    normed_all, grad_all = gather_team([normed, cotangent[0]], 0)
    raw, query_rot, pairs, stats, across, attended, gated = attend(
        normed_all.reshape(TEAM_SIZE, local_len, MODEL_WIDTH),
        own_attention,
        own_gate,
        qk_gains,
        cosine,
        sine,
        starts[:, :, None],
        own_query,
        window,
        8,
    )
    gated, up_blocks, low_down = lax.optimization_barrier(
        (gated, up_blocks, down_weight.astype(bf16))
    )
    own_up = gather_parts(up_blocks)
    own_down = gather_rows(low_down)
    middle = inputs_flat + scatter_team(product_out, [gated.reshape(-1, own_query)], [own_attention], 1)
    normed2 = rms_apply(middle, norm_gains[1]).astype(bf16)
    normed2_all = gather_team([normed2], 2)[0]
    hidden, slope, swish = ffn_forward(normed2_all, own_inner, own_up)
    grad_final = cotangent[0].astype(jnp.float32)
    down_part, own_down = lax.optimization_barrier(
        (low_tokens(hidden.reshape(-1, own_ff), grad_all), own_down)
    )
    grad_inner, grad_up = ffn_back(grad_all, own_down, slope, swish)
    grad_inner, grad_up = grad_inner.reshape(-1, own_ff), grad_up.reshape(-1, own_ff)
    inner_part, grad_inner = lax.optimization_barrier(
        (weight_parts(normed2_all, grad_inner, ffn_weight.shape[0]), grad_inner)
    )
    down_sum = scatter_rows(down_part)
    grad_normed2 = scatter_team(
        product_ffn_back, [grad_inner, grad_up], [own_inner, own_up], 4
    )
    grad_mid_part, gain_mid = rms_back(middle, norm_gains[1], grad_normed2)
    grad_middle = grad_final + grad_mid_part
    grad_low, down_sum = lax.optimization_barrier((grad_middle.astype(bf16), down_sum))
    inner_sum = scatter_parts(inner_part)
    grad_middle_all, up_part = gather_team(
        [grad_low],
        5,
        weight_work,
        (normed2_all, grad_up),
        (weight_shape(normed2_all, grad_up, ffn_weight.shape[0]),),
    )
    grad_products, gain_sums = attend_back(
        grad_middle_all.reshape(TEAM_SIZE, local_len, MODEL_WIDTH),
        own_attention,
        qk_gains,
        cosine,
        sine,
        starts[:, None, :],
        (raw, query_rot, pairs, stats, across, attended),
        window,
        9,
    )
    grad_products = grad_products.reshape(-1, grad_products.shape[2])
    up_part, grad_products, inner_sum = lax.optimization_barrier(
        (up_part, grad_products, inner_sum)
    )
    up_sum = scatter_parts(up_part)
    grad_normed, attention_part, gate_part = scatter_team(
        product_qkv_back,
        [grad_products],
        [own_attention, own_gate],
        6,
        attention_weight_work,
        (normed_all, grad_products, gated.reshape(-1, own_query), grad_middle_all),
        attention_weight_shapes(normed_all, grad_products, out_weight.shape[0]),
    )
    late_hidden, grad_normed = lax.optimization_barrier((hidden, grad_normed))
    ffn_rows = team_exchange(jnp.concatenate([inner_sum, up_sum], axis=2))
    attention_sum = scatter_parts(attention_part)
    summed = scatter_team(product_down, [late_hidden.reshape(-1, own_ff)], [own_down], 3)
    grad_in_part, gain_in = rms_back(inputs_flat, norm_gains[0], grad_normed)
    input_grad = (grad_middle + grad_in_part).reshape(inputs.shape)
    ffn_rows, summed = lax.optimization_barrier((ffn_rows, summed))
    (
        ffn_moment_new,
        ffn_second_new,
        ffn_update,
        down_moment_new,
        down_second_new,
        down_update,
        ffn_squares,
    ) = ffn_moments(
        ffn_rows,
        down_sum,
        (ffn_weight, ffn_moment, ffn_second),
        (down_weight, down_moment, down_second),
    )
    final = middle + summed
    result = final.astype(bf16).reshape(inputs.shape)
    attention_sum, ffn_squares, result, input_grad = lax.optimization_barrier(
        (attention_sum, ffn_squares, result, input_grad)
    )
    attention_state = (projection_weight, projection_moment, projection_second)
    out_state = (out_weight, out_moment, out_second)
    projection_rows, gate_total, gains_total, qk_total, norms = totals(
        group_heads,
        attention_sum,
        gate_part,
        (jnp.sum(gain_in, axis=0), jnp.sum(gain_mid, axis=0)),
        gain_sums,
        ffn_squares,
        attention_state,
        out_state,
        10,
    )
    (
        projection_weight_next,
        qkv_copy,
        projection_moment_next,
        projection_second_next,
        out_new,
        out_copy,
        out_moment_new,
        out_second_new,
        ffn_new,
        ffn_copy,
        down_new,
        down_copy,
        head_gate_new,
        gate_moment_new,
        gate_second_new,
        gains_new,
        gains_moment_new,
        gains_second_new,
        qk_new,
        qk_moment_new,
        qk_second_new,
        norms,
    ) = apply_all(
        norms,
        gate_total,
        gains_total,
        qk_total,
        projection_rows,
        attention_sum,
        attention_state,
        out_state,
        (ffn_weight, ffn_update),
        (down_weight, down_update),
        (
            (head_gate.T, gate_moment.T, gate_second.T),
            (norm_gains, gains_moment, gains_second),
            (qk_gains, qk_moment, qk_second),
        ),
    )
    return (
        result,
        input_grad,
        projection_weight_next,
        projection_moment_next,
        projection_second_next,
        qkv_copy,
        out_new,
        out_moment_new,
        out_second_new,
        out_copy,
        ffn_new,
        ffn_moment_new,
        ffn_second_new,
        ffn_copy,
        down_new,
        down_moment_new,
        down_second_new,
        down_copy,
        head_gate_new.T,
        gate_moment_new.T,
        gate_second_new.T,
        gains_new,
        gains_moment_new,
        gains_second_new,
        qk_new,
        qk_moment_new,
        qk_second_new,
        norms[:2, :7],
    )


def solution(mesh):
    mesh = Mesh(
        mesh.devices.reshape(2, 2, 2, mesh.shape["fsdp"] // TEAM_SIZE, mesh.shape["seq"]),
        TEAM + DEPTH,
    )
    rows = TEAM + DEPTH[:1]
    in_specs = (
        P(rows, "seq", None),
        P(rows, "seq", None),
        P(rows, None),
        P(TEAM + DEPTH, None),
        P(TEAM + DEPTH, None),
        P(TEAM + DEPTH, None),
        P(TEAM + DEPTH, None),
        P(TEAM + DEPTH, None),
        P(TEAM + DEPTH, None),
        P(TEAM + DEPTH, None),
        P(TEAM + DEPTH, None),
        P(TEAM + DEPTH, None),
        P(TEAM + DEPTH, None),
        P(TEAM + DEPTH, None),
        P(TEAM + DEPTH, None),
        P(),
        P(),
        P(),
        P(),
        P(),
        P(),
        P(),
        P(),
        P(),
    )
    out_specs = (
        P(rows, "seq", None),
        P(rows, "seq", None),
        P(TEAM + DEPTH, None),
        P(TEAM + DEPTH, None),
        P(TEAM + DEPTH, None),
        P(TEAM + DEPTH, None),
        P(TEAM + DEPTH, None),
        P(TEAM + DEPTH, None),
        P(TEAM + DEPTH, None),
        P(TEAM + DEPTH, None),
        P(TEAM + DEPTH, None),
        P(TEAM + DEPTH, None),
        P(TEAM + DEPTH, None),
        P(TEAM + DEPTH, None),
        P(TEAM + DEPTH, None),
        P(TEAM + DEPTH, None),
        P(TEAM + DEPTH, None),
        P(TEAM + DEPTH, None),
        P(),
        P(),
        P(),
        P(),
        P(),
        P(),
        P(),
        P(),
        P(),
        P(),
    )
    return jax.shard_map(shards, mesh=mesh, in_specs=in_specs, out_specs=out_specs, check_vma=False)
```

```python
import functools

import jax
import jax.numpy as jnp
from jax import lax
from jax.experimental import pallas as pl
from jax.experimental.pallas import tpu as pltpu
from jax.sharding import Mesh
from jax.sharding import PartitionSpec as P

MODEL_WIDTH = 2048
QUERY_HEADS = 16
KEY_VALUE_HEADS = 8
HEAD_WIDTH = 128
FF = 6144
ROW_TOKENS = 1024
STEP = 3
DOC_MOST = 512
TEAM_SIZE = 8
TEAM = ("t2", "t1", "t0")
DEPTH = ("spare", "seq")
LANES = 128
SUBLANES = 8
VMEM_BYTES = 60 << 20
GATHER_VMEM = 60 << 20
LAMB_COST = 70
GATHER_COST = 250
SCATTER_COST = 320
ATTEND_COST = 50


NORM_EPS = 1e-06
ADAM_EPS = 1e-06
RATE = 0.3
DECAY = 0.01
BETA = 0.5
THETA = 1000000.0
NEGATIVE = -1e30


def rms_apply(value_rows, gain):
    return (
        value_rows
        * lax.rsqrt(jnp.mean(value_rows * value_rows, axis=-1, keepdims=True) + NORM_EPS)
        * gain
    )


def rms_back(value_rows, gain, gradient):
    scale = lax.rsqrt(jnp.mean(value_rows * value_rows, axis=-1, keepdims=True) + NORM_EPS)
    scaled = gradient * gain
    inner = jnp.mean(scaled * value_rows, axis=-1, keepdims=True)
    grad_value = scale * scaled - value_rows * scale * scale * scale * inner
    grad_gain = gradient * value_rows * scale
    return (grad_value, grad_gain)


def dot_t(left, right):
    return lax.dot_general(
        left, right, (((1,), (1,)), ((), ())), preferred_element_type=jnp.float32
    )


def low_tokens(left, right):
    return dot_tokens(left, right).astype(jnp.bfloat16)


def dot_tokens(left, right):
    return lax.dot_general(
        left, right, (((0,), (0,)), ((), ())), preferred_element_type=jnp.float32
    )


def moments(weight, moment, second, gradient):
    moment_new = BETA * moment + (1.0 - BETA) * gradient
    second_new = BETA * second + (1.0 - BETA) * gradient * gradient
    correction = 1.0 - BETA**STEP
    update = (
        moment_new / correction / (jnp.sqrt(second_new / correction) + ADAM_EPS) + DECAY * weight
    )
    return (moment_new, second_new, update)


def rotary_tables(position, width):
    half = width // 2
    rates = THETA ** (-jnp.arange(half, dtype=jnp.float32) * 2.0 / width)
    angle = position.astype(jnp.float32)[..., None] * rates
    cosine, sine = jnp.cos(angle), jnp.sin(angle)
    return (
        jnp.concatenate([cosine, cosine], axis=-1),
        jnp.concatenate([-sine, sine], axis=-1),
    )


def positions(lengths, place):
    ends = jnp.cumsum(lengths, axis=1)
    starts = ends - lengths
    inside = (place[None, :, None] >= starts[:, None, :]) & (place[None, :, None] < ends[:, None, :])
    return place[None, :] - jnp.sum(jnp.where(inside, starts[:, None, :], 0), axis=2)


def team_place():
    return tuple(lax.axis_index(axis) for axis in TEAM)


def greet_team(place):
    barrier = pltpu.get_barrier_semaphore()
    for axis, index in zip(TEAM, place):
        pl.semaphore_signal(
            barrier, inc=1, device_id={axis: 1 - index}, device_id_type=pl.DeviceIdType.MESH
        )
    pl.semaphore_wait(barrier, len(TEAM))


def member(place, flips):
    index = 0
    for own, flip in zip(place, flips):
        index = index * 2 + (1 - own if flip else own)
    return index


def gather_kernel(count, work, *refs):
    given, made = (work[1], work[2]) if work else (0, 0)
    owns, operands = refs[:count], refs[count : count + given]
    alls = refs[count + given : 2 * count + given]
    results = refs[2 * count + given : 2 * count + given + made]
    own_sem, send_sem, recv_sem = refs[2 * count + given + made :]
    place = team_place()
    greet_team(place)
    me = member(place, (0, 0, 0))
    beside = member(place, (0, 1, 0))
    above = member(place, (1, 0, 0))
    across = member(place, (1, 1, 0))
    copies = [{} for _ in range(count)]
    keeps = []

    def send(item, number, axis, source, target):
        copy = pltpu.make_async_remote_copy(
            src_ref=source,
            dst_ref=target,
            send_sem=send_sem.at[item, number],
            recv_sem=recv_sem.at[item, number],
            device_id={TEAM[axis]: 1 - place[axis]},
            device_id_type=pl.DeviceIdType.MESH,
        )
        copy.start()
        copies[item][number] = copy

    def halves(item):
        half = owns[item].shape[0] // 2
        return pl.ds(0, half), pl.ds(half, half)

    for item in range(count):
        target = alls[item].at[me]
        send(item, 0, 1, owns[item], target)
        send(item, 1, 0, owns[item], target)
        send(item, 2, 2, owns[item], target)
        keeps.append(pltpu.make_async_copy(owns[item], target, own_sem.at[item]))
        keeps[item].start()
    if work:
        work[0](*operands, *results)
    for item in range(count):
        upper, lower = halves(item)
        copies[item][0].wait_recv()
        block = alls[item].at[beside]
        send(item, 3, 0, block.at[upper], block.at[upper])
        send(item, 4, 2, block, block)
        copies[item][1].wait_recv()
        block = alls[item].at[above]
        send(item, 5, 1, block.at[lower], block.at[lower])
        send(item, 6, 2, block, block)
    for item in range(count):
        upper, lower = halves(item)
        block = alls[item].at[across]
        copies[item][3].wait_recv()
        send(item, 7, 2, block.at[upper], block.at[upper])
        copies[item][5].wait_recv()
        send(item, 8, 2, block.at[lower], block.at[lower])
    for item in range(count):
        for number in (2, 4, 6, 7, 8):
            copies[item][number].wait_recv()
        for number in range(9):
            copies[item][number].wait_send()
        keeps[item].wait()


def gather_team(arrays, collective_id, work=None, operands=(), results=()):
    count = len(arrays)
    anywhere = pl.BlockSpec(memory_space=pl.ANY)
    out_shape = [jax.ShapeDtypeStruct((TEAM_SIZE,) + own.shape, own.dtype) for own in arrays]
    gathered = pl.pallas_call(
        functools.partial(
            gather_kernel, count, (work, len(operands), len(results)) if work else None
        ),
        out_shape=out_shape + list(results),
        in_specs=[anywhere] * (count + len(operands)),
        out_specs=[anywhere] * (count + len(results)),
        scratch_shapes=[
            pltpu.SemaphoreType.DMA((count,)),
            pltpu.SemaphoreType.DMA((count, 9)),
            pltpu.SemaphoreType.DMA((count, 9)),
        ],
        compiler_params=pltpu.CompilerParams(
            collective_id=collective_id, has_side_effects=True, vmem_limit_bytes=GATHER_VMEM
        ),
        cost_estimate=pl.CostEstimate(
            flops=0,
            bytes_accessed=sum(GATHER_COST * own.shape[0] * own.shape[1] for own in arrays),
            transcendentals=0,
        ),
    )(*arrays, *operands)
    return [
        whole.reshape(TEAM_SIZE * own.shape[0], own.shape[1])
        for whole, own in zip(gathered, arrays)
    ] + list(gathered[count:])


def scatter_kernel(product, count, work, *refs):
    given, made = (work[1], work[2]) if work else (0, 0)
    operands, extra = refs[:count], refs[count : count + given]
    sum_ref = refs[count + given]
    results = refs[count + given + 1 : count + given + 1 + made]
    own, out_near, in_near, out_far, in_half, in_full, send_sem, recv_sem = refs[
        count + given + 1 + made :
    ]
    place = team_place()
    greet_team(place)
    rows = sum_ref.shape[0]
    half = rows // 2
    upper, lower = pl.ds(0, half), pl.ds(half, half)

    def send(number, axis, source, target):
        copy = pltpu.make_async_remote_copy(
            src_ref=source,
            dst_ref=target,
            send_sem=send_sem.at[number],
            recv_sem=recv_sem.at[number],
            device_id={TEAM[axis]: 1 - place[axis]},
            device_id_type=pl.DeviceIdType.MESH,
        )
        copy.start()
        return copy

    flips = ((1, 1), (0, 1), (1, 0), (0, 0))
    near, far = [], {}
    is_first = place[2] == 0

    def begin(turn):
        first, second = flips[turn]
        pair = member(place[:2], (first, second))

        def one(step, columns):
            both = product(operands, pair, step, columns)
            former, latter = both[:rows], both[rows:]
            out_near[turn, :, columns] = jnp.where(is_first, latter, former).astype(jnp.bfloat16)
            own[turn, :, columns] = jnp.where(is_first, former, latter)

        over_tiles(sum_ref.shape[1], one)
        near.append(send(turn, 2, out_near.at[turn], in_near.at[turn]))

    def join(turn):
        near[turn].wait_recv()
        return own[turn] + in_near[turn].astype(jnp.float32)

    begin(0)
    begin(1)
    out_far[0] = join(0).astype(jnp.bfloat16)
    far[4] = send(4, 1, out_far.at[0, upper], in_half.at[0])
    far[5] = send(5, 0, out_far.at[0, lower], in_half.at[1])
    begin(2)
    own[1] = join(1)
    out_far[1, upper] = own[1, upper].astype(jnp.bfloat16)
    far[6] = send(6, 1, out_far.at[1, upper], in_full.at[0, upper])
    begin(3)
    own[2] = join(2)
    out_far[2, lower] = own[2, lower].astype(jnp.bfloat16)
    far[7] = send(7, 0, out_far.at[2, lower], in_full.at[1, lower])
    sum_ref[...] = join(3)
    far[5].wait_recv()
    out_far[1, lower] = (own[1, lower] + in_half[1].astype(jnp.float32)).astype(jnp.bfloat16)
    far[8] = send(8, 1, out_far.at[1, lower], in_full.at[0, lower])
    far[4].wait_recv()
    out_far[2, upper] = (own[2, upper] + in_half[0].astype(jnp.float32)).astype(jnp.bfloat16)
    far[9] = send(9, 0, out_far.at[2, upper], in_full.at[1, upper])
    if work:
        work[0](*extra, *results)
    far[6].wait_recv()
    far[7].wait_recv()
    far[8].wait_recv()
    far[9].wait_recv()
    sum_ref[...] = (
        sum_ref[...] + in_full[0].astype(jnp.float32) + in_full[1].astype(jnp.float32)
    )
    for copy in near + [far[number] for number in range(4, 10)]:
        copy.wait_send()


def over_tiles(width, one):
    tile = width // TEAM_SIZE

    def body(step, carry):
        one(step, pl.ds(pl.multiple_of(step * tile, tile), tile))
        return carry

    lax.fori_loop(0, TEAM_SIZE, body, 0)


def whole_block(ref, step, columns=slice(None)):
    block = ref[:, step, :, columns]
    return block.reshape(block.shape[0] * block.shape[1], block.shape[2])


def push_kernel(count, kept, *refs):
    blocks, rest = refs[:count], refs[count : count + kept]
    landed = refs[count + kept : 2 * count + kept]
    own_sem, send_sem, recv_sem = refs[2 * count + kept :]
    place = team_place()
    barrier = pltpu.get_barrier_semaphore()
    flips = [(step // 4, step // 2 % 2, step % 2) for step in range(1, TEAM_SIZE)]
    team = [
        (
            member(place, flip),
            {axis: 1 - at if turn else at for axis, at, turn in zip(TEAM, place, flip)},
        )
        for flip in flips
    ]
    for _, device in team:
        pl.semaphore_signal(
            barrier, inc=1, device_id=device, device_id_type=pl.DeviceIdType.MESH
        )
    pl.semaphore_wait(barrier, len(team))
    me = member(place, (0, 0, 0))
    copies = []

    def block(item, index):
        return blocks[item].at[index if blocks[item].shape[0] == TEAM_SIZE else 0]

    def target(item):
        if kept and item == 0:
            return landed[item].at[me, :, pl.ds(0, blocks[item].shape[2])]
        return landed[item].at[me]

    for item in range(count):
        for number, (index, device) in enumerate(team):
            copy = pltpu.make_async_remote_copy(
                src_ref=block(item, index),
                dst_ref=target(item),
                send_sem=send_sem.at[item, number],
                recv_sem=recv_sem.at[item, number],
                device_id=device,
                device_id_type=pl.DeviceIdType.MESH,
            )
            copy.start()
            copies.append(copy)
    keeps = [
        pltpu.make_async_copy(block(item, me), target(item), own_sem.at[item])
        for item in range(count)
    ]
    if kept:
        first = blocks[0].shape[2]
        keeps.append(
            pltpu.make_async_copy(
                rest[0], landed[0].at[:, :, pl.ds(first, rest[0].shape[2])], own_sem.at[count]
            )
        )
    for keep in keeps:
        keep.start()
    for copy in copies:
        copy.wait_recv()
    for keep in keeps:
        keep.wait()
    for copy in copies:
        copy.wait_send()


def push_team(arrays, collective_id, kept=()):
    count = len(arrays)
    anywhere = pl.BlockSpec(memory_space=pl.ANY)
    out_shape = [
        jax.ShapeDtypeStruct((TEAM_SIZE,) + array.shape[1:], array.dtype) for array in arrays
    ]
    for array in kept:
        team, rows, width = out_shape[0].shape
        out_shape[0] = jax.ShapeDtypeStruct((team, rows, width + array.shape[2]), array.dtype)
    return pl.pallas_call(
        functools.partial(push_kernel, count, len(kept)),
        out_shape=out_shape,
        in_specs=[anywhere] * (count + len(kept)),
        out_specs=[anywhere] * count,
        scratch_shapes=[
            pltpu.SemaphoreType.DMA((count + len(kept),)),
            pltpu.SemaphoreType.DMA((count, TEAM_SIZE - 1)),
            pltpu.SemaphoreType.DMA((count, TEAM_SIZE - 1)),
        ],
        compiler_params=pltpu.CompilerParams(
            collective_id=collective_id, has_side_effects=True, vmem_limit_bytes=GATHER_VMEM
        ),
        cost_estimate=pl.CostEstimate(
            flops=0, bytes_accessed=40 * sum(array.size for array in arrays), transcendentals=0
        ),
    )(*arrays, *kept)


def product_down(operands, pair, step, columns):
    hidden, weight = operands
    return jnp.dot(hidden[pair], weight[:, columns], preferred_element_type=jnp.float32)


def product_out(operands, pair, step, columns):
    gated, weight = operands
    depth = gated.shape[2]
    share = pl.ds(weight.shape[3] - depth, depth)
    return jnp.dot(
        gated[pair], whole_block(weight, step, share), preferred_element_type=jnp.float32
    )


def product_ffn_back(operands, pair, step, columns):
    grad_inner, grad_up, inner_weight, up_weight = operands
    return dot_t(grad_inner[pair], whole_block(inner_weight, step)) + dot_t(
        grad_up[pair], whole_block(up_weight, step)
    )


def product_qkv_back(operands, pair, step, columns):
    grad_products, weight, gate_weight = operands
    depth = grad_products.shape[2] - LANES
    share = pl.ds(0, depth)
    return dot_t(grad_products[pair, :, share], whole_block(weight, step, share)) + dot_t(
        grad_products[pair, :, pl.ds(depth, LANES)], gate_weight[columns, :]
    )


def scatter_team(
    product, lefts, rights, collective_id, work=None, operands=(), results=()
):
    rows = lefts[0].shape[0] // TEAM_SIZE
    depth = sum(left.shape[1] for left in lefts)
    width = MODEL_WIDTH
    paired = [left.reshape(TEAM_SIZE // 2, 2 * rows, left.shape[1]) for left in lefts]
    vmem = pl.BlockSpec(memory_space=pltpu.VMEM)
    anywhere = pl.BlockSpec(memory_space=pl.ANY)
    count = len(lefts) + len(rights)
    summed = pl.pallas_call(
        functools.partial(
            scatter_kernel, product, count, (work, len(operands), len(results)) if work else None
        ),
        out_shape=[jax.ShapeDtypeStruct((rows, width), jnp.float32)] + list(results),
        in_specs=[vmem] * count + [anywhere] * len(operands),
        out_specs=[vmem] + [anywhere] * len(results),
        scratch_shapes=[
            pltpu.VMEM((4, rows, width), jnp.float32),
            pltpu.VMEM((4, rows, width), jnp.bfloat16),
            pltpu.VMEM((4, rows, width), jnp.bfloat16),
            pltpu.VMEM((3, rows, width), jnp.bfloat16),
            pltpu.VMEM((2, rows // 2, width), jnp.bfloat16),
            pltpu.VMEM((2, rows, width), jnp.bfloat16),
            pltpu.SemaphoreType.DMA((10,)),
            pltpu.SemaphoreType.DMA((10,)),
        ],
        compiler_params=pltpu.CompilerParams(
            collective_id=collective_id, has_side_effects=True, vmem_limit_bytes=VMEM_BYTES
        ),
        cost_estimate=pl.CostEstimate(
            flops=2 * TEAM_SIZE * rows * depth * width,
            bytes_accessed=SCATTER_COST * rows * width,
            transcendentals=0,
        ),
    )(*paired, *rights, *operands)
    return summed if work else summed[0]


def ffn_kernel(rows_ref, inner_ref, up_ref, hidden_ref, slope_ref, swish_ref, inner_weight, up_weight):
    @pl.when(pl.program_id(0) == 0)
    def _():
        block = inner_ref.shape[0] * inner_ref.shape[2]
        for step in range(TEAM_SIZE):
            inner_weight[pl.ds(step * block, block), :] = whole_block(inner_ref, step)
            up_weight[pl.ds(step * block, block), :] = whole_block(up_ref, step)

    tile = 256

    def one(step, carry):
        columns = pl.ds(pl.multiple_of(step * tile, tile), tile)
        inner = jnp.dot(rows_ref[0], inner_weight[:, columns], preferred_element_type=jnp.float32)
        up_part = jnp.dot(rows_ref[0], up_weight[:, columns], preferred_element_type=jnp.float32)
        sigma = jax.nn.sigmoid(inner)
        swish = inner * sigma
        hidden_ref[0, :, columns] = (swish * up_part).astype(jnp.bfloat16)
        slope_ref[0, :, columns] = up_part * sigma * (1.0 + inner * (1.0 - sigma))
        swish_ref[0, :, columns] = swish
        return carry

    lax.fori_loop(0, hidden_ref.shape[2] // tile, one, 0, unroll=True)


def ffn_forward(normed_rows, inner_weight, up_weight):
    count, depth = TEAM_SIZE // 2, normed_rows.shape[1]
    length = normed_rows.shape[0] // count
    width = inner_weight.shape[3]
    whole = pl.BlockSpec(inner_weight.shape, lambda i: (0, 0, 0, 0), pipeline_mode=pl.Buffered(1))
    out = pl.BlockSpec((1, length, width), lambda i: (i, 0, 0))
    return pl.pallas_call(
        ffn_kernel,
        grid=(count,),
        out_shape=[
            jax.ShapeDtypeStruct((count, length, width), jnp.bfloat16),
            jax.ShapeDtypeStruct((count, length, width), jnp.float32),
            jax.ShapeDtypeStruct((count, length, width), jnp.float32),
        ],
        in_specs=[pl.BlockSpec((1, length, depth), lambda i: (i, 0, 0)), whole, whole],
        out_specs=[out, out, out],
        scratch_shapes=[pltpu.VMEM((depth, width), jnp.bfloat16)] * 2,
        compiler_params=pltpu.CompilerParams(vmem_limit_bytes=VMEM_BYTES),
        cost_estimate=pl.CostEstimate(
            flops=4 * count * length * depth * width,
            bytes_accessed=count * length * (2 * depth + 10 * width),
            transcendentals=count * length * width,
        ),
    )(normed_rows.reshape(count, length, depth), inner_weight, up_weight)


def ffn_back_kernel(grad_ref, weight_ref, slope_ref, swish_ref, inner_ref, up_ref):
    tile = 256

    def one(step, carry):
        columns = pl.ds(pl.multiple_of(step * tile, tile), tile)
        grad_hidden = dot_t(grad_ref[0], weight_ref[columns, :])
        inner_ref[0, :, columns] = (grad_hidden * slope_ref[0, :, columns]).astype(jnp.bfloat16)
        up_ref[0, :, columns] = (grad_hidden * swish_ref[0, :, columns]).astype(jnp.bfloat16)
        return carry

    lax.fori_loop(0, inner_ref.shape[2] // tile, one, 0, unroll=True)


def ffn_back(grad_rows, down_weight, slope, swish):
    count, length, width = slope.shape
    depth = grad_rows.shape[1]
    whole = pl.BlockSpec(down_weight.shape, lambda i: (0, 0), pipeline_mode=pl.Buffered(1))
    part = pl.BlockSpec((1, length, width), lambda i: (i, 0, 0))
    return pl.pallas_call(
        ffn_back_kernel,
        grid=(count,),
        out_shape=[jax.ShapeDtypeStruct((count, length, width), jnp.bfloat16)] * 2,
        in_specs=[pl.BlockSpec((1, length, depth), lambda i: (i, 0, 0)), whole, part, part],
        out_specs=[part, part],
        compiler_params=pltpu.CompilerParams(vmem_limit_bytes=VMEM_BYTES),
        cost_estimate=pl.CostEstimate(
            flops=2 * count * length * depth * width,
            bytes_accessed=count * length * (2 * depth + 12 * width),
            transcendentals=0,
        ),
    )(grad_rows.reshape(count, length, depth), down_weight, slope, swish)


def weight_kernel(left_ref, right_ref, part_ref):
    depth, _, rows, width = part_ref.shape
    part = dot_tokens(left_ref[...], right_ref[...])
    part_ref[...] = part.astype(jnp.bfloat16).reshape(depth, 1, rows, width)


def weight_shape(left, right, rows):
    depth = left.shape[1] // (TEAM_SIZE * rows)
    return jax.ShapeDtypeStruct((depth, TEAM_SIZE, rows, right.shape[1]), jnp.bfloat16)


def weight_specs(left, right, part):
    depth, _, rows, width = part.shape
    return dict(
        grid=(TEAM_SIZE,),
        in_specs=[
            pl.BlockSpec((left.shape[0], depth * rows), lambda i: (0, i)),
            pl.BlockSpec(right.shape, lambda i: (0, 0)),
        ],
        out_specs=[pl.BlockSpec((depth, 1, rows, width), lambda i: (0, i, 0, 0))],
    )


def weight_parts(left, right, rows):
    part = weight_shape(left, right, rows)
    (tokens, height), width = left.shape, right.shape[1]
    return pl.pallas_call(
        weight_kernel,
        out_shape=[part],
        compiler_params=pltpu.CompilerParams(vmem_limit_bytes=VMEM_BYTES),
        cost_estimate=pl.CostEstimate(
            flops=2 * tokens * height * width,
            bytes_accessed=2 * tokens * (height + width) + 2 * height * width,
            transcendentals=0,
        ),
        **weight_specs(left, right, part),
    )(left, right)[0]


def weight_work(left_ref, right_ref, part_ref):
    pltpu.emit_pipeline(weight_kernel, **weight_specs(left_ref, right_ref, part_ref))(
        left_ref, right_ref, part_ref
    )


def attention_weight_kernel(normed_ref, products_ref, gated_ref, grad_ref, part_ref, gate_ref):
    depth, _, rows, _ = part_ref.shape
    own = products_ref.shape[1] - LANES
    part = dot_tokens(normed_ref[...], products_ref[...])
    gate_ref[...] = part[:, own:].T[:SUBLANES]
    part_ref[:, :, :, pl.ds(0, own)] = (
        part[:, :own].astype(jnp.bfloat16).reshape(depth, 1, rows, own)
    )
    share = grad_ref.shape[1]
    part = dot_tokens(gated_ref[...], grad_ref[...])
    part_ref[:, :, :, pl.ds(own, share)] = part.astype(jnp.bfloat16).reshape(depth, 1, rows, share)


def attention_weight_work(*refs):
    normed, products, gated, grad, part, gate = refs
    depth, _, rows, width = part.shape
    share = depth * rows
    column = pl.BlockSpec((normed.shape[0], share), lambda i: (0, i))
    pltpu.emit_pipeline(
        attention_weight_kernel,
        grid=(TEAM_SIZE,),
        in_specs=[
            column,
            pl.BlockSpec(products.shape, lambda i: (0, 0)),
            pl.BlockSpec(gated.shape, lambda i: (0, 0)),
            column,
        ],
        out_specs=[
            pl.BlockSpec((depth, 1, rows, width), lambda i: (0, i, 0, 0)),
            pl.BlockSpec((SUBLANES, share), lambda i: (0, i)),
        ],
    )(*refs)


def attention_weight_shapes(normed, grad_products, rows):
    height, width = normed.shape[1], grad_products.shape[1]
    share = height // TEAM_SIZE
    return [
        jax.ShapeDtypeStruct((share // rows, TEAM_SIZE, rows, width - LANES + share), jnp.bfloat16),
        jax.ShapeDtypeStruct((SUBLANES, height), jnp.float32),
    ]


def greet_all():
    place = team_place()
    barrier = pltpu.get_barrier_semaphore()
    flips = [(step // 4, step // 2 % 2, step % 2) for step in range(1, TEAM_SIZE)]
    team = [
        (
            member(place, flip),
            {axis: 1 - at if turn else at for axis, at, turn in zip(TEAM, place, flip)},
        )
        for flip in flips
    ]
    sizes = [lax.axis_size(axis) for axis in DEPTH]
    depth = sizes[0] * sizes[1]
    spot = lax.axis_index(DEPTH[0]) * sizes[1] + lax.axis_index(DEPTH[1])
    line = []
    for step in range(1, depth):
        other = lax.rem(spot + step, depth)
        line.append({DEPTH[0]: other // sizes[1], DEPTH[1]: lax.rem(other, sizes[1])})
    for target in [device for _, device in team] + line:
        pl.semaphore_signal(
            barrier, inc=1, device_id=target, device_id_type=pl.DeviceIdType.MESH
        )
    pl.semaphore_wait(barrier, len(team) + len(line))
    return member(place, (0, 0, 0)), team, spot, line


def push(source, target, sems, number, device):
    copy = pltpu.make_async_remote_copy(
        src_ref=source,
        dst_ref=target,
        send_sem=sems.at[0, number],
        recv_sem=sems.at[1, number],
        device_id=device,
        device_id_type=pl.DeviceIdType.MESH,
    )
    copy.start()
    return copy


def begin_line(own, slots, sems, spot, line):
    slots[spot] = own[...]
    return [
        push(own, slots.at[spot], sems, number, device) for number, device in enumerate(line)
    ]


def begin_team(copies, slots, team_slots, sems, me, team):
    for copy in copies:
        copy.wait_recv()
    total = slots[0]
    for step in range(1, slots.shape[0]):
        total = total + slots[step]
    team_slots[me] = total
    return [
        push(team_slots.at[me], team_slots.at[me], sems, number, device)
        for number, (_, device) in enumerate(team)
    ]


def depth_size():
    return lax.axis_size(DEPTH[0]) * lax.axis_size(DEPTH[1])


def lane_squares(piece):
    total = jnp.sum(piece * piece, axis=0, keepdims=True)
    lanes = total[:, :LANES]
    for first in range(LANES, total.shape[1], LANES):
        lanes = lanes + total[:, first : first + LANES]
    return lanes


def in_lanes(values, shape):
    lane = lax.broadcasted_iota(jnp.int32, shape, 1)
    row = jnp.zeros(shape, jnp.float32)
    for number, value in enumerate(values):
        row = jnp.where(lane == number, jnp.sum(value, axis=1, keepdims=True), row)
    return row


def update_columns(columns, gradient, state, results, update_ref):
    weight = state[0][:, columns]
    moment, second, update = moments(
        weight, state[1][:, columns], state[2][:, columns], gradient.astype(jnp.float32)
    )
    results[0][:, columns] = moment
    results[1][:, columns] = second
    update_ref[:, columns] = update
    return lane_squares(weight), lane_squares(update)


def at_columns(first, width):
    return pl.ds(pl.multiple_of(first, width if width < LANES else LANES), width)


STEPS = 4


def ffn_moments_kernel(inner_ref, up_ref, down_ref, *refs):
    state, down_state = refs[0:3], refs[3:6]
    results, update, down_results, down_update, squares_ref = (
        refs[6:8], refs[8], refs[9:11], refs[11], refs[12]
    )
    step = pl.program_id(0)

    @pl.when(step == 0)
    def _():
        squares_ref[...] = jnp.zeros_like(squares_ref)

    group = step // (STEPS // 2)
    count, _, width = inner_ref.shape

    def one(item, sums):
        gradient = jnp.where(
            group == 0, inner_ref[item].astype(jnp.float32), up_ref[item].astype(jnp.float32)
        )
        columns = at_columns(item * width, width)
        return add_all(sums, update_columns(columns, gradient, state, results, update))

    zero = jnp.zeros((1, LANES), jnp.float32)
    found = lax.fori_loop(0, count, one, (zero, zero), unroll=True)
    squares_ref[pl.ds(group, 1)] += found[0]
    squares_ref[pl.ds(4 + group, 1)] += found[1]
    every = slice(None)
    found = update_columns(every, down_ref[...], down_state, down_results, down_update)
    squares_ref[2:3] += found[0]
    squares_ref[6:7] += found[1]


def ffn_moments(inner_rows, up_rows, down_sum, state, down_state):
    _, rows, width = inner_rows.shape
    half = STEPS // 2
    count = TEAM_SIZE // half

    def column(array):
        return pl.BlockSpec((array.shape[0], array.shape[1] // STEPS), lambda i: (0, i))

    like = [jax.ShapeDtypeStruct(state[0].shape, jnp.float32)] * 3
    like_down = [jax.ShapeDtypeStruct(down_state[0].shape, jnp.float32)] * 3
    return pl.pallas_call(
        ffn_moments_kernel,
        grid=(STEPS,),
        out_shape=like + like_down + [jax.ShapeDtypeStruct((SUBLANES, LANES), jnp.float32)],
        in_specs=[
            pl.BlockSpec((count, rows, width), lambda i: (jnp.minimum(i, half - 1), 0, 0)),
            pl.BlockSpec((count, rows, width), lambda i: (jnp.maximum(i - half, 0), 0, 0)),
            column(down_sum),
        ]
        + [column(array) for array in state + down_state],
        out_specs=[column(array) for array in state + down_state]
        + [pl.BlockSpec((SUBLANES, LANES), lambda i: (0, 0))],
        compiler_params=pltpu.CompilerParams(vmem_limit_bytes=GATHER_VMEM),
        cost_estimate=pl.CostEstimate(
            flops=20 * state[0].size, bytes_accessed=30 * state[0].size, transcendentals=0
        ),
    )(inner_rows, up_rows, down_sum, *state, *down_state)


def begin_blocks(parts, landed, columns, sems, me, team):
    landed[me] = parts[me, :, columns]
    return [
        push(parts.at[index, :, columns], landed.at[me], sems, number, device)
        for number, (index, device) in enumerate(team)
    ]


def column_squares(columns, gradient, state):
    weight = state[0][:, columns]
    _, _, update = moments(
        weight, state[1][:, columns], state[2][:, columns], gradient.astype(jnp.float32)
    )
    return lane_squares(weight), lane_squares(update)


def add_all(olds, news):
    return tuple(old + new for old, new in zip(olds, news))


def totals_kernel(
    heads, attention_ref, gate_ref, first_ref, second_ref, qk_ref, ffn_squares_ref, *refs
):
    state, out_state = refs[0:3], refs[3:6]
    rows_out, gate_out, gains_out, qk_out, norms_out = refs[6:11]
    (
        landed, own, line_slots, team_slots, tile, tile_line, tile_team,
        block_sems, line_sems, team_sems, tile_line_sems, tile_team_sems,
    ) = refs[11:]
    me, team, spot, line = greet_all()
    share = landed.shape[2]
    blocks = begin_blocks(attention_ref, landed, pl.ds(0, share), block_sems, me, team)
    own[...] = jnp.zeros_like(own)
    own[0:heads] = gate_ref[0:heads]
    own[heads : heads + 1] = first_ref[...]
    own[heads + 1 : heads + 2] = second_ref[...]
    for row in range(2):
        own[heads + 2 : heads + 3, pl.ds(row * HEAD_WIDTH, HEAD_WIDTH)] = qk_ref[row : row + 1]
    along = begin_line(own, line_slots, line_sems, spot, line)
    query_width = share - 2 * HEAD_WIDTH
    out_width = out_state[0].shape[1] // TEAM_SIZE
    zero = jnp.zeros((1, LANES), jnp.float32)

    def out(turn, sums):
        columns = at_columns(turn * out_width, out_width)
        gradient = attention_ref[turn, :, pl.ds(share, out_width)]
        return add_all(sums, column_squares(columns, gradient, out_state))

    out_sums = lax.fori_loop(0, TEAM_SIZE, out, (zero,) * 2)
    across = begin_team(along, line_slots, team_slots, team_sems, me, team)
    for copy in blocks:
        copy.wait_recv()

    def projection(turn, sums):
        found = ()
        for first, start, width in (
            (turn * query_width, 0, query_width),
            (TEAM_SIZE * query_width + turn * HEAD_WIDTH, query_width, HEAD_WIDTH),
            (
                TEAM_SIZE * (query_width + HEAD_WIDTH) + turn * HEAD_WIDTH,
                query_width + HEAD_WIDTH,
                HEAD_WIDTH,
            ),
        ):
            gradient = landed[turn, :, pl.ds(start, width)]
            found = found + column_squares(at_columns(first, width), gradient, state)
        return add_all(sums, found)

    sums = lax.fori_loop(0, TEAM_SIZE, projection, (zero,) * 6) + out_sums
    rows = [sums[2 * group] for group in range(4)]
    rows += [ffn_squares_ref[group : group + 1] for group in range(3)]
    rows += [sums[2 * group + 1] for group in range(4)]
    rows += [ffn_squares_ref[4 + group : 5 + group] for group in range(3)]
    tile[...] = jnp.zeros_like(tile)
    tile[0:1] = in_lanes(rows, (1, LANES))
    tile_along = begin_line(tile, tile_line, tile_line_sems, spot, line)
    rows_out[...] = landed[...]
    tile_across = begin_team(tile_along, tile_line, tile_team, tile_team_sems, me, team)
    for copy in across:
        copy.wait_recv()
    total = team_slots[0, heads:]
    for turn in range(1, TEAM_SIZE):
        total = total + team_slots[turn, heads:]
    gains_out[...] = total[:2]
    for row in range(2):
        qk_out[row : row + 1] = total[2:3, row * HEAD_WIDTH : (row + 1) * HEAD_WIDTH]
    for turn in range(TEAM_SIZE):
        gate_out[turn * heads : (turn + 1) * heads] = team_slots[turn, :heads]
    for copy in tile_across:
        copy.wait_recv()
    total = tile_team[0, 0:1]
    for turn in range(1, TEAM_SIZE):
        total = total + tile_team[turn, 0:1]
    norms = jnp.sqrt(total)
    groups = 7
    weight_norms = [norms[:, number : number + 1] for number in range(groups)]
    update_norms = [norms[:, groups + number : groups + number + 1] for number in range(groups)]
    norms_out[...] = jnp.zeros_like(norms_out)
    norms_out[0:1] = in_lanes(weight_norms, (1, LANES))
    norms_out[1:2] = in_lanes(update_norms, (1, LANES))
    norms_out[2:3] = in_lanes(
        [former / latter for former, latter in zip(weight_norms, update_norms)], (1, LANES)
    )
    for copy in blocks + along + across + tile_along + tile_across:
        copy.wait_send()


def totals(
    heads, attention_sum, gate_part, gains, qk_gains, ffn_squares, state, out_state, collective_id
):
    vmem = pl.BlockSpec(memory_space=pltpu.VMEM)
    width = gate_part.shape[1]
    depth = depth_size()
    team, rows, _ = attention_sum.shape
    share = state[0].shape[1] // TEAM_SIZE
    return pl.pallas_call(
        functools.partial(totals_kernel, heads),
        out_shape=[
            jax.ShapeDtypeStruct((team, rows, share), jnp.bfloat16),
            jax.ShapeDtypeStruct((TEAM_SIZE * heads, width), jnp.float32),
            jax.ShapeDtypeStruct((2, width), jnp.float32),
            jax.ShapeDtypeStruct((2, HEAD_WIDTH), jnp.float32),
            jax.ShapeDtypeStruct((SUBLANES, LANES), jnp.float32),
        ],
        in_specs=[vmem] * 12,
        out_specs=[vmem] * 5,
        scratch_shapes=[
            pltpu.VMEM((team, rows, share), jnp.bfloat16),
            pltpu.VMEM((SUBLANES, width), jnp.float32),
            pltpu.VMEM((depth, SUBLANES, width), jnp.float32),
            pltpu.VMEM((TEAM_SIZE, SUBLANES, width), jnp.float32),
            pltpu.VMEM((SUBLANES, LANES), jnp.float32),
            pltpu.VMEM((depth, SUBLANES, LANES), jnp.float32),
            pltpu.VMEM((TEAM_SIZE, SUBLANES, LANES), jnp.float32),
            pltpu.SemaphoreType.DMA((2, TEAM_SIZE - 1)),
            pltpu.SemaphoreType.DMA((2, max(depth - 1, 1))),
            pltpu.SemaphoreType.DMA((2, TEAM_SIZE - 1)),
            pltpu.SemaphoreType.DMA((2, max(depth - 1, 1))),
            pltpu.SemaphoreType.DMA((2, TEAM_SIZE - 1)),
        ],
        compiler_params=pltpu.CompilerParams(
            collective_id=collective_id, has_side_effects=True, vmem_limit_bytes=GATHER_VMEM
        ),
    )(
        attention_sum, gate_part, gains[0][None], gains[1][None], qk_gains, ffn_squares,
        *state, *out_state,
    )


def small_update(state, gradient, results, by_row):
    weight = state[0][...]
    moment, second, update = moments(weight, state[1][...], state[2][...], gradient[...])
    ratio = jnp.sum(weight * weight, axis=1, keepdims=True)
    size = jnp.sum(update * update, axis=1, keepdims=True)
    if not by_row:
        ratio = jnp.sum(ratio, axis=0, keepdims=True)
        size = jnp.sum(size, axis=0, keepdims=True)
    results[0][...] = weight - RATE * (jnp.sqrt(ratio) / jnp.sqrt(size)) * update
    results[1][...] = moment
    results[2][...] = second


def apply_kernel(
    norms_ref, gate_ref, gains_ref, qk_ref, rows_ref, attention_ref, *refs
):
    state, out_state = refs[0:3], refs[3:6]
    ffn_pair, down_pair = refs[6:8], refs[8:10]
    states = [refs[10 + 3 * number : 13 + 3 * number] for number in range(3)]
    targets, out_targets = refs[19:23], refs[23:27]
    ffn_targets, down_targets = refs[27:29], refs[29:31]
    results = [refs[31 + 3 * number : 34 + 3 * number] for number in range(3)]
    norms_out, gradient, out_gradient = refs[40:]
    step = pl.program_id(0)
    share = rows_ref.shape[2]
    wide = share - 2 * HEAD_WIDTH
    query_steps = TEAM_SIZE * wide // gradient.shape[1]
    key_steps = TEAM_SIZE * HEAD_WIDTH // gradient.shape[1]

    @pl.when(step == 0)
    def _():
        norms_out[...] = norms_ref[0:2]
        small_update(states[0], gate_ref, results[0], False)
        small_update(states[1], gains_ref, results[1], True)
        small_update(states[2], qk_ref, results[2], True)

    @pl.when(step < query_steps)
    def _():
        per_step = gradient.shape[1] // wide
        for item in range(per_step):
            gradient[:, pl.ds(item * wide, wide)] = rows_ref[
                step * per_step + item, :, pl.ds(0, wide)
            ].astype(jnp.float32)

    for number in range(2):
        first = query_steps + number * key_steps

        @pl.when((step >= first) & (step < first + key_steps))
        def _():
            per_step = gradient.shape[1] // HEAD_WIDTH
            for item in range(per_step):
                gradient[:, pl.ds(item * HEAD_WIDTH, HEAD_WIDTH)] = rows_ref[
                    (step - first) * per_step + item, :, pl.ds(wide + number * HEAD_WIDTH, HEAD_WIDTH)
                ].astype(jnp.float32)

    def rate(first, uppers=()):
        found = norms_ref[2:3, first : first + 1]
        for number, upper in enumerate(uppers):
            group = first + number + 1
            found = jnp.where(step < upper, found, norms_ref[2:3, group : group + 1])
        return RATE * found

    def renew(weight, update, new, low_new, factor):
        value = weight - factor * update
        new[...] = value
        low_new[...] = value.astype(jnp.bfloat16)

    def both(state, gradient, targets, factor):
        weight = state[0][...]
        moment, second, update = moments(weight, state[1][...], state[2][...], gradient)
        targets[2][...] = moment
        targets[3][...] = second
        renew(weight, update, targets[0], targets[1], factor)

    both(state, gradient[...], targets, rate(0, (query_steps, query_steps + key_steps)))
    width = attention_ref.shape[2] - share
    count = out_gradient.shape[1] // width
    for item in range(count):
        out_gradient[:, pl.ds(item * width, width)] = attention_ref[
            step * count + item, :, pl.ds(share, width)
        ].astype(jnp.float32)
    both(out_state, out_gradient[...], out_targets, rate(3))
    renew(ffn_pair[0][...], ffn_pair[1][...], *ffn_targets, rate(4, (STEPS // 2,)))
    renew(down_pair[0][...], down_pair[1][...], *down_targets, rate(6))


def apply_all(
    norms, gate_total, gains_total, qk_total, projection_rows, attention_sum, state, out_state,
    ffn_pair, down_pair, states,
):
    def whole(array):
        return pl.BlockSpec(array.shape, lambda i: (0,) * array.ndim)

    def column(array):
        return pl.BlockSpec((array.shape[0], array.shape[1] // STEPS), lambda i: (0, i))

    def like(array, kind=jnp.float32):
        return jax.ShapeDtypeStruct(array.shape, kind)

    small = [array for group in states for array in group]
    fixed = [norms, gate_total, gains_total, qk_total, projection_rows, attention_sum]
    split = [*state, *out_state, *ffn_pair, *down_pair]
    targets = []
    for group in (state, out_state):
        targets += [like(group[0]), like(group[0], jnp.bfloat16), like(group[1]), like(group[2])]
    for group in (ffn_pair, down_pair):
        targets += [like(group[0]), like(group[0], jnp.bfloat16)]
    results = [like(array) for array in small]
    results.append(jax.ShapeDtypeStruct((2, norms.shape[1]), jnp.float32))
    rows = state[0].shape[0]
    return pl.pallas_call(
        apply_kernel,
        grid=(STEPS,),
        out_shape=targets + results,
        in_specs=[whole(array) for array in fixed]
        + [column(array) for array in split]
        + [whole(array) for array in small],
        out_specs=[column(array) for array in targets] + [whole(array) for array in results],
        scratch_shapes=[
            pltpu.VMEM((rows, state[0].shape[1] // STEPS), jnp.float32),
            pltpu.VMEM((rows, out_state[0].shape[1] // STEPS), jnp.float32),
        ],
        compiler_params=pltpu.CompilerParams(vmem_limit_bytes=GATHER_VMEM),
        cost_estimate=pl.CostEstimate(
            flops=4 * ffn_pair[0].size, bytes_accessed=30 * ffn_pair[0].size, transcendentals=0
        ),
    )(*fixed, *split, *small)


def team_exchange(blocks):
    return lax.all_to_all(blocks, TEAM, split_axis=0, concat_axis=0, tiled=True)


def turn_half(value_rows):
    return pltpu.roll(value_rows, value_rows.shape[-1] // 2, value_rows.ndim - 1)


def norm_turn(value_rows, gain, cosine, sine):
    scaled = rms_apply(value_rows, gain)
    return scaled * cosine + turn_half(scaled) * sine


def norm_turn_back(value_rows, gain, cosine, sine, gradient):
    turned = gradient * cosine + turn_half(gradient * sine)
    return rms_back(value_rows, gain, turned)


def greet_line():
    index, count = lax.axis_index("seq"), lax.axis_size("seq")
    barrier = pltpu.get_barrier_semaphore()

    @pl.when(index > 0)
    def _():
        pl.semaphore_signal(
            barrier, inc=1, device_id={"seq": index - 1}, device_id_type=pl.DeviceIdType.MESH
        )

    @pl.when(index < count - 1)
    def _():
        pl.semaphore_signal(
            barrier, inc=1, device_id={"seq": index + 1}, device_id_type=pl.DeviceIdType.MESH
        )

    inside = (index > 0) & (index < count - 1)

    @pl.when(inside)
    def _():
        pl.semaphore_wait(barrier, 2)

    @pl.when(jnp.logical_not(inside))
    def _():
        pl.semaphore_wait(barrier, 1)

    return index, count


def attend_kernel(
    window, scale, rows_ref, weight_ref, gate_ref, gains_ref, cosine_ref, sine_ref, start_ref,
    raw_ref, query_ref, pair_ref, stats_ref, across_ref, attended_ref, gated_ref,
    weight, pairs, send_sem, recv_sem,
):
    count_rows, length, _ = rows_ref.shape
    query_cols = query_ref.shape[2]
    heads = query_cols // HEAD_WIDTH
    keys_at = pl.ds(0, HEAD_WIDTH)
    values_at = pl.ds(HEAD_WIDTH, HEAD_WIDTH)
    index, count = greet_line()

    def hop(turn, row):
        return pltpu.make_async_remote_copy(
            src_ref=pairs.at[window - turn + 1, row],
            dst_ref=pairs.at[window - turn, row],
            send_sem=send_sem.at[turn - 1, row],
            recv_sem=recv_sem.at[turn - 1, row],
            device_id={"seq": lax.rem(index + 1, count)},
            device_id_type=pl.DeviceIdType.MESH,
        )

    block = weight_ref.shape[0] * weight_ref.shape[2]
    own = raw_ref.shape[2]
    for step in range(TEAM_SIZE):
        weight[pl.ds(step * block, block), pl.ds(0, own)] = whole_block(
            weight_ref, step, pl.ds(0, own)
        )
    weight[:, pl.ds(own, LANES)] = gate_ref[...]

    def project(row, carry):
        products = jnp.dot(rows_ref[row], weight[...], preferred_element_type=jnp.float32)
        raw = products[:, : query_cols + 2 * HEAD_WIDTH].astype(jnp.bfloat16)
        raw_ref[row] = raw
        cosine, sine = cosine_ref[row], sine_ref[row]
        key = norm_turn(
            raw[:, query_cols : query_cols + HEAD_WIDTH].astype(jnp.float32),
            gains_ref[1:2], cosine, sine,
        )
        pairs[window, row, :, keys_at] = key.astype(jnp.bfloat16)
        pairs[window, row, :, values_at] = raw[:, query_cols + HEAD_WIDTH :]

        @pl.when(index < count - 1)
        def _():
            hop(1, row).start()

        for head in range(heads):
            columns = slice(head * HEAD_WIDTH, (head + 1) * HEAD_WIDTH)
            query_ref[row, :, columns] = norm_turn(
                raw[:, columns].astype(jnp.float32), gains_ref[0:1], cosine, sine
            ).astype(jnp.bfloat16)
        stats_ref[row] = jax.nn.sigmoid(products[:, query_cols + 2 * HEAD_WIDTH :])
        return carry

    lax.fori_loop(0, count_rows, project, 0)

    @pl.when(index == 0)
    def _():
        for slot in range(window):
            pairs[slot] = jnp.zeros_like(pairs[slot])

    for turn in range(2, window + 1):

        def forward(row, carry):
            @pl.when(index > 0)
            def _():
                hop(turn - 1, row).wait_recv()

            @pl.when(index < count - 1)
            def _():
                hop(turn, row).start()

            return carry

        lax.fori_loop(0, count_rows, forward, 0)

    places = lax.broadcasted_iota(jnp.int32, (length, (window + 1) * length), 1)
    latest = window * length + lax.broadcasted_iota(jnp.int32, places.shape, 0)
    lane = lax.broadcasted_iota(jnp.int32, (length, LANES), 1)

    def attend(row, carry):
        @pl.when(index > 0)
        def _():
            hop(window, row).wait_recv()

        allowed = (places >= start_ref[row]) & (places <= latest)
        keys = pairs[:, row, :, keys_at].reshape(-1, HEAD_WIDTH)
        values = pairs[:, row, :, values_at].reshape(-1, HEAD_WIDTH)
        stats = stats_ref[row]
        for head in range(heads):
            columns = slice(head * HEAD_WIDTH, (head + 1) * HEAD_WIDTH)
            scores = dot_t(query_ref[row, :, columns], keys) * scale
            scores = jnp.where(allowed, scores, NEGATIVE)
            top = jnp.max(scores, axis=1, keepdims=True)
            powers = jnp.exp(scores - top)
            total = jnp.sum(powers, axis=1, keepdims=True)
            low_probs = (powers * (1.0 / total)).astype(jnp.bfloat16)
            output = jnp.dot(low_probs, values, preferred_element_type=jnp.float32)
            output = output.astype(jnp.bfloat16)
            attended_ref[row, :, columns] = output
            gated_ref[row, :, columns] = (
                output.astype(jnp.float32) * stats[:, head : head + 1]
            ).astype(jnp.bfloat16)
            stats = jnp.where(lane == heads + head, top + jnp.log(total), stats)
        stats_ref[row] = stats
        across_ref[row] = stats.T[:SUBLANES]
        pair_ref[:, row] = pairs[:, row]
        return carry

    lax.fori_loop(0, count_rows, attend, 0)

    @pl.when(index < count - 1)
    def _():
        for turn in range(1, window + 1):

            def finish(row, carry):
                hop(turn, row).wait_send()
                return carry

            lax.fori_loop(0, count_rows, finish, 0)


def attend(
    normed_rows, own_attention, own_gate, gains, cosine, sine, starts, query_cols, window, collective_id
):
    rows, length, _ = normed_rows.shape
    width = query_cols + 2 * HEAD_WIDTH + LANES
    bf16 = jnp.bfloat16
    vmem = pl.BlockSpec(memory_space=pltpu.VMEM)
    return pl.pallas_call(
        functools.partial(attend_kernel, window, HEAD_WIDTH ** (-0.5)),
        out_shape=[
            jax.ShapeDtypeStruct((rows, length, query_cols + 2 * HEAD_WIDTH), bf16),
            jax.ShapeDtypeStruct((rows, length, query_cols), bf16),
            jax.ShapeDtypeStruct((window + 1, rows, length, 2 * HEAD_WIDTH), bf16),
            jax.ShapeDtypeStruct((rows, length, LANES), jnp.float32),
            jax.ShapeDtypeStruct((rows, SUBLANES, length), jnp.float32),
            jax.ShapeDtypeStruct((rows, length, query_cols), bf16),
            jax.ShapeDtypeStruct((rows, length, query_cols), bf16),
        ],
        in_specs=[vmem] * 7,
        out_specs=[vmem] * 7,
        scratch_shapes=[
            pltpu.VMEM((MODEL_WIDTH, width), bf16),
            pltpu.VMEM((window + 1, rows, length, 2 * HEAD_WIDTH), bf16),
            pltpu.SemaphoreType.DMA((window, rows)),
            pltpu.SemaphoreType.DMA((window, rows)),
        ],
        compiler_params=pltpu.CompilerParams(
            collective_id=collective_id, has_side_effects=True, vmem_limit_bytes=VMEM_BYTES
        ),
        cost_estimate=pl.CostEstimate(
            flops=2 * rows * length * MODEL_WIDTH * width,
            bytes_accessed=ATTEND_COST * rows * length * MODEL_WIDTH,
            transcendentals=0,
        ),
    )(normed_rows, own_attention, own_gate, gains, cosine, sine, starts)


def attend_back_kernel(
    window, scale, rows_ref, weight_ref, gains_ref, cosine_ref, sine_ref, start_ref,
    raw_ref, query_ref, pair_ref, stats_ref, across_ref, attended_ref,
    products_ref, gain_ref,
    weight, parts, outs, ins, send_sem, recv_sem,
):
    count_rows, length, _ = rows_ref.shape
    query_cols = query_ref.shape[2]
    heads = query_cols // HEAD_WIDTH
    keys_at = pl.ds(0, HEAD_WIDTH)
    values_at = pl.ds(HEAD_WIDTH, HEAD_WIDTH)
    index, count = greet_line()
    lag = 2

    def hop(turn, row):
        return pltpu.make_async_remote_copy(
            src_ref=outs.at[turn - 1, row],
            dst_ref=ins.at[turn - 1, row],
            send_sem=send_sem.at[turn - 1, row],
            recv_sem=recv_sem.at[turn - 1, row],
            device_id={"seq": lax.rem(index + count - 1, count)},
            device_id_type=pl.DeviceIdType.MESH,
        )

    keys_total = (window + 1) * length
    places = lax.broadcasted_iota(jnp.int32, (keys_total, length), 0)
    latest = window * length + lax.broadcasted_iota(jnp.int32, places.shape, 1)
    lane = lax.broadcasted_iota(jnp.int32, (length, LANES), 1)
    gain_ref[...] = jnp.zeros_like(gain_ref)
    share = weight_ref.shape[3] - query_cols
    for step in range(TEAM_SIZE):
        weight[:, pl.ds(step * query_cols, query_cols)] = whole_block(
            weight_ref, step, pl.ds(share, query_cols)
        )

    @pl.when(index == count - 1)
    def _():
        ins[...] = jnp.zeros_like(ins)

    def compute(row):
        grad_gated = dot_t(rows_ref[row], weight[...])
        keys = pair_ref[:, row, :, keys_at].reshape(-1, HEAD_WIDTH)
        values = pair_ref[:, row, :, values_at].reshape(-1, HEAD_WIDTH)
        allowed = (places >= start_ref[row]) & (places <= latest)
        cosine, sine = cosine_ref[row], sine_ref[row]
        grad_pre = jnp.zeros((length, LANES), jnp.float32)
        grad_keys = jnp.zeros((keys_total, HEAD_WIDTH), jnp.float32)
        grad_values = jnp.zeros((keys_total, HEAD_WIDTH), jnp.float32)
        for head in range(heads):
            columns = slice(head * HEAD_WIDTH, (head + 1) * HEAD_WIDTH)
            gate = stats_ref[row, :, head : head + 1]
            own = grad_gated[:, columns]
            grad_out = (own * gate).astype(jnp.bfloat16)
            grad_gate = jnp.sum(
                own * attended_ref[row, :, columns].astype(jnp.float32), axis=1, keepdims=True
            )
            grad_pre = jnp.where(lane == head, grad_gate * gate * (1.0 - gate), grad_pre)
            query = query_ref[row, :, columns]
            scores = jnp.where(allowed, dot_t(keys, query) * scale, NEGATIVE)
            probs = jnp.exp(scores - across_ref[row, heads + head : heads + head + 1])
            grad_probs = dot_t(values, grad_out)
            inner = jnp.sum(probs * grad_probs, axis=0, keepdims=True)
            grad_scores = (probs * (grad_probs - inner)).astype(jnp.bfloat16)
            grad_values = grad_values + jnp.dot(
                probs.astype(jnp.bfloat16), grad_out, preferred_element_type=jnp.float32
            )
            grad_keys = grad_keys + jnp.dot(
                grad_scores, query, preferred_element_type=jnp.float32
            )
            grad_query = dot_tokens(grad_scores, keys) * scale
            grad_raw, gain = norm_turn_back(
                raw_ref[row, :, columns].astype(jnp.float32), gains_ref[0:1], cosine, sine,
                grad_query,
            )
            products_ref[row, :, columns] = grad_raw.astype(jnp.bfloat16)
            gain_ref[0:1] += jnp.sum(gain, axis=0, keepdims=True)
        products_ref[row, :, query_cols + 2 * HEAD_WIDTH :] = grad_pre.astype(jnp.bfloat16)
        parts[:, row, :, keys_at] = (grad_keys * scale).reshape(window + 1, length, HEAD_WIDTH)
        parts[:, row, :, values_at] = grad_values.reshape(window + 1, length, HEAD_WIDTH)

    def finish(row):
        grad_pair = parts[window, row] + ins[window - 1, row].astype(jnp.float32)
        grad_raw, gain = norm_turn_back(
            raw_ref[row, :, query_cols : query_cols + HEAD_WIDTH].astype(jnp.float32),
            gains_ref[1:2], cosine_ref[row], sine_ref[row], grad_pair[:, :HEAD_WIDTH],
        )
        products_ref[row, :, query_cols : query_cols + HEAD_WIDTH] = grad_raw.astype(jnp.bfloat16)
        products_ref[row, :, query_cols + HEAD_WIDTH : query_cols + 2 * HEAD_WIDTH] = grad_pair[
            :, HEAD_WIDTH:
        ].astype(jnp.bfloat16)
        gain_ref[1:2] += jnp.sum(gain, axis=0, keepdims=True)

    def step(turn_row, carry):
        @pl.when(turn_row < count_rows)
        def _():
            compute(turn_row)

        for turn in range(1, window + 2):
            row = turn_row - lag * (turn - 1)

            @pl.when((row >= 0) & (row < count_rows))
            def _():
                if turn > 1:

                    @pl.when(index < count - 1)
                    def _():
                        hop(turn - 1, row).wait_recv()

                if turn == window + 1:
                    finish(row)
                else:
                    part = parts[turn - 1, row]
                    if turn > 1:
                        part = part + ins[turn - 2, row].astype(jnp.float32)
                    outs[turn - 1, row] = part.astype(jnp.bfloat16)

                    @pl.when(index > 0)
                    def _():
                        hop(turn, row).start()

        return carry

    lax.fori_loop(0, count_rows + lag * window, step, 0)

    @pl.when(index > 0)
    def _():
        for turn in range(1, window + 1):

            def done(row, carry):
                hop(turn, row).wait_send()
                return carry

            lax.fori_loop(0, count_rows, done, 0)


def attend_back(
    grad_rows, own_attention, gains, cosine, sine, starts, saved, window, collective_id
):
    rows, length, _ = grad_rows.shape
    query_cols = saved[1].shape[2]
    width = query_cols + 2 * HEAD_WIDTH + LANES
    bf16 = jnp.bfloat16
    vmem = pl.BlockSpec(memory_space=pltpu.VMEM)
    return pl.pallas_call(
        functools.partial(attend_back_kernel, window, HEAD_WIDTH ** (-0.5)),
        out_shape=[
            jax.ShapeDtypeStruct((rows, length, width), bf16),
            jax.ShapeDtypeStruct((SUBLANES, HEAD_WIDTH), jnp.float32),
        ],
        in_specs=[vmem] * 12,
        out_specs=[vmem] * 2,
        scratch_shapes=[
            pltpu.VMEM((query_cols, MODEL_WIDTH), bf16),
            pltpu.VMEM((window + 1, rows, length, 2 * HEAD_WIDTH), jnp.float32),
            pltpu.VMEM((window, rows, length, 2 * HEAD_WIDTH), bf16),
            pltpu.VMEM((window, rows, length, 2 * HEAD_WIDTH), bf16),
            pltpu.SemaphoreType.DMA((window, rows)),
            pltpu.SemaphoreType.DMA((window, rows)),
        ],
        compiler_params=pltpu.CompilerParams(
            collective_id=collective_id, has_side_effects=True, vmem_limit_bytes=VMEM_BYTES
        ),
        cost_estimate=pl.CostEstimate(
            flops=2 * rows * length * MODEL_WIDTH * query_cols,
            bytes_accessed=ATTEND_COST * rows * length * MODEL_WIDTH,
            transcendentals=0,
        ),
    )(grad_rows, own_attention, gains, cosine, sine, starts, *saved)


def team_columns(matrix, widths):
    pieces = []
    lower = 0
    for width in widths:
        piece = matrix[:, lower : lower + width]
        pieces.append(piece.reshape(matrix.shape[0], TEAM_SIZE, width // TEAM_SIZE))
        lower = lower + width
    return jnp.concatenate(pieces, axis=2).transpose(1, 0, 2)


def gather_parts(blocks):
    return lax.all_gather(blocks, DEPTH, axis=0, tiled=False)


def scatter_parts(parts):
    depth, team, rows, width = parts.shape
    return lax.psum_scatter(
        parts.reshape(depth * team * rows, width), DEPTH, scatter_dimension=0, tiled=True
    ).reshape(team, rows, width)


def gather_rows(matrix):
    return lax.all_gather(matrix, DEPTH, axis=0, tiled=True)


def scatter_rows(gradient):
    return lax.psum_scatter(gradient, DEPTH, scatter_dimension=0, tiled=True)


def shards(
    inputs,
    cotangent,
    doc_lengths,
    projection_weight,
    projection_moment,
    projection_second,
    out_weight,
    out_moment,
    out_second,
    ffn_weight,
    ffn_moment,
    ffn_second,
    down_weight,
    down_moment,
    down_second,
    head_gate,
    gate_moment,
    gate_second,
    norm_gains,
    gains_moment,
    gains_second,
    qk_gains,
    qk_moment,
    qk_second,
):
    rows_dev, local_len, width = inputs.shape
    bf16 = jnp.bfloat16
    team = lax.axis_index(TEAM)
    place_seq = lax.axis_index("seq")
    group_heads = QUERY_HEADS // KEY_VALUE_HEADS
    window = -(-(DOC_MOST - 1) // local_len)
    window = min(window, lax.axis_size("seq") - 1)
    query_cols = QUERY_HEADS * HEAD_WIDTH
    key_value_columns = KEY_VALUE_HEADS * HEAD_WIDTH
    widths_qkv = (query_cols, key_value_columns, key_value_columns)
    widths_ffn = (FF, FF)
    own_query = query_cols // TEAM_SIZE
    own_key = key_value_columns // TEAM_SIZE
    own_ff = FF // TEAM_SIZE
    own_gate = lax.dynamic_slice_in_dim(head_gate.astype(bf16), team * group_heads, group_heads, 1)
    own_gate = jnp.pad(own_gate, ((0, 0), (0, LANES - group_heads)))
    (attention_blocks,) = push_team(
        [team_columns(projection_weight.astype(bf16), widths_qkv)],
        11,
        [team_columns(out_weight.astype(bf16), (MODEL_WIDTH,))],
    )
    own_attention = gather_parts(attention_blocks)
    low_ffn, attention_blocks = lax.optimization_barrier(
        (ffn_weight.astype(bf16), attention_blocks)
    )
    inner_blocks, up_blocks, lengths = push_team(
        [
            team_columns(low_ffn[:, :FF], (FF,)),
            team_columns(low_ffn[:, FF:], (FF,)),
            jnp.pad(doc_lengths, ((0, SUBLANES - 1), (0, LANES - doc_lengths.shape[1])))[None],
        ],
        12,
    )
    own_inner = gather_parts(inner_blocks)
    lengths = lengths[:, 0, : doc_lengths.shape[1]]
    place = place_seq * local_len + jnp.arange(local_len, dtype=jnp.int32)
    position = positions(lengths, place)
    cosine, sine = rotary_tables(position, HEAD_WIDTH)
    starts = window * local_len + jnp.arange(local_len, dtype=jnp.int32)[None, :] - position
    inputs_flat = inputs[0].astype(jnp.float32)
    normed = rms_apply(inputs_flat, norm_gains[0]).astype(bf16)
    normed_all, grad_all = gather_team([normed, cotangent[0]], 0)
    raw, query_rot, pairs, stats, across, attended, gated = attend(
        normed_all.reshape(TEAM_SIZE, local_len, MODEL_WIDTH),
        own_attention,
        own_gate,
        qk_gains,
        cosine,
        sine,
        starts[:, :, None],
        own_query,
        window,
        8,
    )
    gated, up_blocks, low_down = lax.optimization_barrier(
        (gated, up_blocks, down_weight.astype(bf16))
    )
    own_up = gather_parts(up_blocks)
    own_down = gather_rows(low_down)
    middle = inputs_flat + scatter_team(product_out, [gated.reshape(-1, own_query)], [own_attention], 1)
    normed2 = rms_apply(middle, norm_gains[1]).astype(bf16)
    normed2_all = gather_team([normed2], 2)[0]
    hidden, slope, swish = ffn_forward(normed2_all, own_inner, own_up)
    grad_final = cotangent[0].astype(jnp.float32)
    down_part, own_down = lax.optimization_barrier(
        (low_tokens(hidden.reshape(-1, own_ff), grad_all), own_down)
    )
    grad_inner, grad_up = ffn_back(grad_all, own_down, slope, swish)
    grad_inner, grad_up = grad_inner.reshape(-1, own_ff), grad_up.reshape(-1, own_ff)
    inner_part, grad_inner = lax.optimization_barrier(
        (weight_parts(normed2_all, grad_inner, ffn_weight.shape[0]), grad_inner)
    )
    down_sum = scatter_rows(down_part)
    grad_normed2 = scatter_team(
        product_ffn_back, [grad_inner, grad_up], [own_inner, own_up], 4
    )
    grad_mid_part, gain_mid = rms_back(middle, norm_gains[1], grad_normed2)
    grad_middle = grad_final + grad_mid_part
    grad_low, down_sum = lax.optimization_barrier((grad_middle.astype(bf16), down_sum))
    inner_sum = scatter_parts(inner_part)
    grad_middle_all, up_part = gather_team(
        [grad_low],
        5,
        weight_work,
        (normed2_all, grad_up),
        (weight_shape(normed2_all, grad_up, ffn_weight.shape[0]),),
    )
    grad_products, gain_sums = attend_back(
        grad_middle_all.reshape(TEAM_SIZE, local_len, MODEL_WIDTH),
        own_attention,
        qk_gains,
        cosine,
        sine,
        starts[:, None, :],
        (raw, query_rot, pairs, stats, across, attended),
        window,
        9,
    )
    grad_products = grad_products.reshape(-1, grad_products.shape[2])
    up_part, grad_products, inner_sum = lax.optimization_barrier(
        (up_part, grad_products, inner_sum)
    )
    up_sum = scatter_parts(up_part)
    grad_normed, attention_part, gate_part = scatter_team(
        product_qkv_back,
        [grad_products],
        [own_attention, own_gate],
        6,
        attention_weight_work,
        (normed_all, grad_products, gated.reshape(-1, own_query), grad_middle_all),
        attention_weight_shapes(normed_all, grad_products, out_weight.shape[0]),
    )
    late_hidden, grad_normed, inner_sum = lax.optimization_barrier(
        (hidden, grad_normed, inner_sum)
    )
    inner_rows = team_exchange(inner_sum)
    attention_sum = scatter_parts(attention_part)
    summed = scatter_team(product_down, [late_hidden.reshape(-1, own_ff)], [own_down], 3)
    grad_in_part, gain_in = rms_back(inputs_flat, norm_gains[0], grad_normed)
    input_grad = (grad_middle + grad_in_part).reshape(inputs.shape)
    up_sum, summed, inner_rows = lax.optimization_barrier((up_sum, summed, inner_rows))
    (
        ffn_moment_new,
        ffn_second_new,
        ffn_update,
        down_moment_new,
        down_second_new,
        down_update,
        ffn_squares,
    ) = ffn_moments(
        inner_rows,
        team_exchange(up_sum),
        down_sum,
        (ffn_weight, ffn_moment, ffn_second),
        (down_weight, down_moment, down_second),
    )
    final = middle + summed
    result = final.astype(bf16).reshape(inputs.shape)
    attention_sum, ffn_squares, result, input_grad = lax.optimization_barrier(
        (attention_sum, ffn_squares, result, input_grad)
    )
    attention_state = (projection_weight, projection_moment, projection_second)
    out_state = (out_weight, out_moment, out_second)
    projection_rows, gate_total, gains_total, qk_total, norms = totals(
        group_heads,
        attention_sum,
        gate_part,
        (jnp.sum(gain_in, axis=0), jnp.sum(gain_mid, axis=0)),
        gain_sums,
        ffn_squares,
        attention_state,
        out_state,
        10,
    )
    (
        projection_weight_next,
        qkv_copy,
        projection_moment_next,
        projection_second_next,
        out_new,
        out_copy,
        out_moment_new,
        out_second_new,
        ffn_new,
        ffn_copy,
        down_new,
        down_copy,
        head_gate_new,
        gate_moment_new,
        gate_second_new,
        gains_new,
        gains_moment_new,
        gains_second_new,
        qk_new,
        qk_moment_new,
        qk_second_new,
        norms,
    ) = apply_all(
        norms,
        gate_total,
        gains_total,
        qk_total,
        projection_rows,
        attention_sum,
        attention_state,
        out_state,
        (ffn_weight, ffn_update),
        (down_weight, down_update),
        (
            (head_gate.T, gate_moment.T, gate_second.T),
            (norm_gains, gains_moment, gains_second),
            (qk_gains, qk_moment, qk_second),
        ),
    )
    return (
        result,
        input_grad,
        projection_weight_next,
        projection_moment_next,
        projection_second_next,
        qkv_copy,
        out_new,
        out_moment_new,
        out_second_new,
        out_copy,
        ffn_new,
        ffn_moment_new,
        ffn_second_new,
        ffn_copy,
        down_new,
        down_moment_new,
        down_second_new,
        down_copy,
        head_gate_new.T,
        gate_moment_new.T,
        gate_second_new.T,
        gains_new,
        gains_moment_new,
        gains_second_new,
        qk_new,
        qk_moment_new,
        qk_second_new,
        norms[:2, :7],
    )


def solution(mesh):
    mesh = Mesh(
        mesh.devices.reshape(2, 2, 2, mesh.shape["fsdp"] // TEAM_SIZE, mesh.shape["seq"]),
        TEAM + DEPTH,
    )
    rows = TEAM + DEPTH[:1]
    in_specs = (
        P(rows, "seq", None),
        P(rows, "seq", None),
        P(rows, None),
        P(TEAM + DEPTH, None),
        P(TEAM + DEPTH, None),
        P(TEAM + DEPTH, None),
        P(TEAM + DEPTH, None),
        P(TEAM + DEPTH, None),
        P(TEAM + DEPTH, None),
        P(TEAM + DEPTH, None),
        P(TEAM + DEPTH, None),
        P(TEAM + DEPTH, None),
        P(TEAM + DEPTH, None),
        P(TEAM + DEPTH, None),
        P(TEAM + DEPTH, None),
        P(),
        P(),
        P(),
        P(),
        P(),
        P(),
        P(),
        P(),
        P(),
    )
    out_specs = (
        P(rows, "seq", None),
        P(rows, "seq", None),
        P(TEAM + DEPTH, None),
        P(TEAM + DEPTH, None),
        P(TEAM + DEPTH, None),
        P(TEAM + DEPTH, None),
        P(TEAM + DEPTH, None),
        P(TEAM + DEPTH, None),
        P(TEAM + DEPTH, None),
        P(TEAM + DEPTH, None),
        P(TEAM + DEPTH, None),
        P(TEAM + DEPTH, None),
        P(TEAM + DEPTH, None),
        P(TEAM + DEPTH, None),
        P(TEAM + DEPTH, None),
        P(TEAM + DEPTH, None),
        P(TEAM + DEPTH, None),
        P(TEAM + DEPTH, None),
        P(),
        P(),
        P(),
        P(),
        P(),
        P(),
        P(),
        P(),
        P(),
        P(),
    )
    return jax.shard_map(shards, mesh=mesh, in_specs=in_specs, out_specs=out_specs, check_vma=False)
```

```python
import functools

import jax
import jax.numpy as jnp
from jax import lax
from jax.experimental import pallas as pl
from jax.experimental.pallas import tpu as pltpu
from jax.sharding import Mesh
from jax.sharding import PartitionSpec as P

MODEL_WIDTH = 2048
QUERY_HEADS = 16
KEY_VALUE_HEADS = 8
HEAD_WIDTH = 128
FF = 6144
ROW_TOKENS = 1024
STEP = 3
DOC_MOST = 512
TEAM_SIZE = 8
TEAM = ("t2", "t1", "t0")
DEPTH = ("spare", "seq")
LANES = 128
SUBLANES = 8
VMEM_BYTES = 60 << 20
GATHER_VMEM = 60 << 20
LAMB_COST = 70
GATHER_COST = 250
SCATTER_COST = 320
ATTEND_COST = 50


NORM_EPS = 1e-06
ADAM_EPS = 1e-06
RATE = 0.3
DECAY = 0.01
BETA = 0.5
THETA = 1000000.0
NEGATIVE = -1e30


def rms_apply(value_rows, gain):
    return (
        value_rows
        * lax.rsqrt(jnp.mean(value_rows * value_rows, axis=-1, keepdims=True) + NORM_EPS)
        * gain
    )


def rms_back(value_rows, gain, gradient):
    scale = lax.rsqrt(jnp.mean(value_rows * value_rows, axis=-1, keepdims=True) + NORM_EPS)
    scaled = gradient * gain
    inner = jnp.mean(scaled * value_rows, axis=-1, keepdims=True)
    grad_value = scale * scaled - value_rows * scale * scale * scale * inner
    grad_gain = gradient * value_rows * scale
    return (grad_value, grad_gain)


def dot_t(left, right):
    return lax.dot_general(
        left, right, (((1,), (1,)), ((), ())), preferred_element_type=jnp.float32
    )


def low_tokens(left, right):
    return dot_tokens(left, right).astype(jnp.bfloat16)


def dot_tokens(left, right):
    return lax.dot_general(
        left, right, (((0,), (0,)), ((), ())), preferred_element_type=jnp.float32
    )


def moments(weight, moment, second, gradient):
    moment_new = BETA * moment + (1.0 - BETA) * gradient
    second_new = BETA * second + (1.0 - BETA) * gradient * gradient
    correction = 1.0 - BETA**STEP
    update = (
        moment_new / correction / (jnp.sqrt(second_new / correction) + ADAM_EPS) + DECAY * weight
    )
    return (moment_new, second_new, update)


def rotary_tables(position, width):
    half = width // 2
    rates = THETA ** (-jnp.arange(half, dtype=jnp.float32) * 2.0 / width)
    angle = position.astype(jnp.float32)[..., None] * rates
    cosine, sine = jnp.cos(angle), jnp.sin(angle)
    return (
        jnp.concatenate([cosine, cosine], axis=-1),
        jnp.concatenate([-sine, sine], axis=-1),
    )


def positions(lengths, place):
    ends = jnp.cumsum(lengths, axis=1)
    starts = ends - lengths
    inside = (place[None, :, None] >= starts[:, None, :]) & (place[None, :, None] < ends[:, None, :])
    return place[None, :] - jnp.sum(jnp.where(inside, starts[:, None, :], 0), axis=2)


def team_place():
    return tuple(lax.axis_index(axis) for axis in TEAM)


def greet_team(place):
    barrier = pltpu.get_barrier_semaphore()
    for axis, index in zip(TEAM, place):
        pl.semaphore_signal(
            barrier, inc=1, device_id={axis: 1 - index}, device_id_type=pl.DeviceIdType.MESH
        )
    pl.semaphore_wait(barrier, len(TEAM))


def member(place, flips):
    index = 0
    for own, flip in zip(place, flips):
        index = index * 2 + (1 - own if flip else own)
    return index


def gather_kernel(count, work, *refs):
    given, made = (work[1], work[2]) if work else (0, 0)
    owns, operands = refs[:count], refs[count : count + given]
    alls = refs[count + given : 2 * count + given]
    results = refs[2 * count + given : 2 * count + given + made]
    own_sem, send_sem, recv_sem = refs[2 * count + given + made :]
    place = team_place()
    greet_team(place)
    me = member(place, (0, 0, 0))
    beside = member(place, (0, 1, 0))
    above = member(place, (1, 0, 0))
    across = member(place, (1, 1, 0))
    copies = [{} for _ in range(count)]
    keeps = []

    def send(item, number, axis, source, target):
        copy = pltpu.make_async_remote_copy(
            src_ref=source,
            dst_ref=target,
            send_sem=send_sem.at[item, number],
            recv_sem=recv_sem.at[item, number],
            device_id={TEAM[axis]: 1 - place[axis]},
            device_id_type=pl.DeviceIdType.MESH,
        )
        copy.start()
        copies[item][number] = copy

    def halves(item):
        half = owns[item].shape[0] // 2
        return pl.ds(0, half), pl.ds(half, half)

    for item in range(count):
        target = alls[item].at[me]
        send(item, 0, 1, owns[item], target)
        send(item, 1, 0, owns[item], target)
        send(item, 2, 2, owns[item], target)
        keeps.append(pltpu.make_async_copy(owns[item], target, own_sem.at[item]))
        keeps[item].start()
    if work:
        work[0](*operands, *results)
    for item in range(count):
        upper, lower = halves(item)
        copies[item][0].wait_recv()
        block = alls[item].at[beside]
        send(item, 3, 0, block.at[upper], block.at[upper])
        send(item, 4, 2, block, block)
        copies[item][1].wait_recv()
        block = alls[item].at[above]
        send(item, 5, 1, block.at[lower], block.at[lower])
        send(item, 6, 2, block, block)
    for item in range(count):
        upper, lower = halves(item)
        block = alls[item].at[across]
        copies[item][3].wait_recv()
        send(item, 7, 2, block.at[upper], block.at[upper])
        copies[item][5].wait_recv()
        send(item, 8, 2, block.at[lower], block.at[lower])
    for item in range(count):
        for number in (2, 4, 6, 7, 8):
            copies[item][number].wait_recv()
        for number in range(9):
            copies[item][number].wait_send()
        keeps[item].wait()


def gather_team(arrays, collective_id, work=None, operands=(), results=()):
    count = len(arrays)
    anywhere = pl.BlockSpec(memory_space=pl.ANY)
    out_shape = [jax.ShapeDtypeStruct((TEAM_SIZE,) + own.shape, own.dtype) for own in arrays]
    gathered = pl.pallas_call(
        functools.partial(
            gather_kernel, count, (work, len(operands), len(results)) if work else None
        ),
        out_shape=out_shape + list(results),
        in_specs=[anywhere] * (count + len(operands)),
        out_specs=[anywhere] * (count + len(results)),
        scratch_shapes=[
            pltpu.SemaphoreType.DMA((count,)),
            pltpu.SemaphoreType.DMA((count, 9)),
            pltpu.SemaphoreType.DMA((count, 9)),
        ],
        compiler_params=pltpu.CompilerParams(
            collective_id=collective_id, has_side_effects=True, vmem_limit_bytes=GATHER_VMEM
        ),
        cost_estimate=pl.CostEstimate(
            flops=0,
            bytes_accessed=sum(GATHER_COST * own.shape[0] * own.shape[1] for own in arrays),
            transcendentals=0,
        ),
    )(*arrays, *operands)
    return [
        whole.reshape(TEAM_SIZE * own.shape[0], own.shape[1])
        for whole, own in zip(gathered, arrays)
    ] + list(gathered[count:])


def scatter_kernel(product, count, work, *refs):
    given, made = (work[1], work[2]) if work else (0, 0)
    operands, extra = refs[:count], refs[count : count + given]
    sum_ref = refs[count + given]
    results = refs[count + given + 1 : count + given + 1 + made]
    own, out_near, in_near, out_far, in_half, in_full, send_sem, recv_sem = refs[
        count + given + 1 + made :
    ]
    place = team_place()
    greet_team(place)
    rows = sum_ref.shape[0]
    half = rows // 2
    upper, lower = pl.ds(0, half), pl.ds(half, half)

    def send(number, axis, source, target):
        copy = pltpu.make_async_remote_copy(
            src_ref=source,
            dst_ref=target,
            send_sem=send_sem.at[number],
            recv_sem=recv_sem.at[number],
            device_id={TEAM[axis]: 1 - place[axis]},
            device_id_type=pl.DeviceIdType.MESH,
        )
        copy.start()
        return copy

    flips = ((1, 1), (0, 1), (1, 0), (0, 0))
    near, far = [], {}
    is_first = place[2] == 0

    def begin(turn):
        first, second = flips[turn]
        pair = member(place[:2], (first, second))

        def one(step, columns):
            both = product(operands, pair, step, columns)
            former, latter = both[:rows], both[rows:]
            out_near[turn, :, columns] = jnp.where(is_first, latter, former).astype(jnp.bfloat16)
            own[turn, :, columns] = jnp.where(is_first, former, latter)

        over_tiles(sum_ref.shape[1], one)
        near.append(send(turn, 2, out_near.at[turn], in_near.at[turn]))

    def join(turn):
        near[turn].wait_recv()
        return own[turn] + in_near[turn].astype(jnp.float32)

    begin(0)
    begin(1)
    out_far[0] = join(0).astype(jnp.bfloat16)
    far[4] = send(4, 1, out_far.at[0, upper], in_half.at[0])
    far[5] = send(5, 0, out_far.at[0, lower], in_half.at[1])
    begin(2)
    own[1] = join(1)
    out_far[1, upper] = own[1, upper].astype(jnp.bfloat16)
    far[6] = send(6, 1, out_far.at[1, upper], in_full.at[0, upper])
    begin(3)
    own[2] = join(2)
    out_far[2, lower] = own[2, lower].astype(jnp.bfloat16)
    far[7] = send(7, 0, out_far.at[2, lower], in_full.at[1, lower])
    sum_ref[...] = join(3)
    far[5].wait_recv()
    out_far[1, lower] = (own[1, lower] + in_half[1].astype(jnp.float32)).astype(jnp.bfloat16)
    far[8] = send(8, 1, out_far.at[1, lower], in_full.at[0, lower])
    far[4].wait_recv()
    out_far[2, upper] = (own[2, upper] + in_half[0].astype(jnp.float32)).astype(jnp.bfloat16)
    far[9] = send(9, 0, out_far.at[2, upper], in_full.at[1, upper])
    if work:
        work[0](*extra, *results)
    far[6].wait_recv()
    far[7].wait_recv()
    far[8].wait_recv()
    far[9].wait_recv()
    sum_ref[...] = (
        sum_ref[...] + in_full[0].astype(jnp.float32) + in_full[1].astype(jnp.float32)
    )
    for copy in near + [far[number] for number in range(4, 10)]:
        copy.wait_send()


def over_tiles(width, one):
    tile = width // TEAM_SIZE

    def body(step, carry):
        one(step, pl.ds(pl.multiple_of(step * tile, tile), tile))
        return carry

    lax.fori_loop(0, TEAM_SIZE, body, 0)


def whole_block(ref, step, columns=slice(None)):
    block = ref[:, step, :, columns]
    return block.reshape(block.shape[0] * block.shape[1], block.shape[2])


def push_kernel(count, kept, *refs):
    blocks, rest = refs[:count], refs[count : count + kept]
    landed = refs[count + kept : 2 * count + kept]
    own_sem, send_sem, recv_sem = refs[2 * count + kept :]
    place = team_place()
    barrier = pltpu.get_barrier_semaphore()
    flips = [(step // 4, step // 2 % 2, step % 2) for step in range(1, TEAM_SIZE)]
    team = [
        (
            member(place, flip),
            {axis: 1 - at if turn else at for axis, at, turn in zip(TEAM, place, flip)},
        )
        for flip in flips
    ]
    for _, device in team:
        pl.semaphore_signal(
            barrier, inc=1, device_id=device, device_id_type=pl.DeviceIdType.MESH
        )
    pl.semaphore_wait(barrier, len(team))
    me = member(place, (0, 0, 0))
    copies = []

    def block(item, index):
        return blocks[item].at[index if blocks[item].shape[0] == TEAM_SIZE else 0]

    def target(item):
        if kept and item == 0:
            return landed[item].at[me, :, pl.ds(0, blocks[item].shape[2])]
        return landed[item].at[me]

    for item in range(count):
        for number, (index, device) in enumerate(team):
            copy = pltpu.make_async_remote_copy(
                src_ref=block(item, index),
                dst_ref=target(item),
                send_sem=send_sem.at[item, number],
                recv_sem=recv_sem.at[item, number],
                device_id=device,
                device_id_type=pl.DeviceIdType.MESH,
            )
            copy.start()
            copies.append(copy)
    keeps = [
        pltpu.make_async_copy(block(item, me), target(item), own_sem.at[item])
        for item in range(count)
    ]
    if kept:
        first = blocks[0].shape[2]
        keeps.append(
            pltpu.make_async_copy(
                rest[0], landed[0].at[:, :, pl.ds(first, rest[0].shape[2])], own_sem.at[count]
            )
        )
    for keep in keeps:
        keep.start()
    for copy in copies:
        copy.wait_recv()
    for keep in keeps:
        keep.wait()
    for copy in copies:
        copy.wait_send()


def push_team(arrays, collective_id, kept=()):
    count = len(arrays)
    anywhere = pl.BlockSpec(memory_space=pl.ANY)
    out_shape = [
        jax.ShapeDtypeStruct((TEAM_SIZE,) + array.shape[1:], array.dtype) for array in arrays
    ]
    for array in kept:
        team, rows, width = out_shape[0].shape
        out_shape[0] = jax.ShapeDtypeStruct((team, rows, width + array.shape[2]), array.dtype)
    return pl.pallas_call(
        functools.partial(push_kernel, count, len(kept)),
        out_shape=out_shape,
        in_specs=[anywhere] * (count + len(kept)),
        out_specs=[anywhere] * count,
        scratch_shapes=[
            pltpu.SemaphoreType.DMA((count + len(kept),)),
            pltpu.SemaphoreType.DMA((count, TEAM_SIZE - 1)),
            pltpu.SemaphoreType.DMA((count, TEAM_SIZE - 1)),
        ],
        compiler_params=pltpu.CompilerParams(
            collective_id=collective_id, has_side_effects=True, vmem_limit_bytes=GATHER_VMEM
        ),
        cost_estimate=pl.CostEstimate(
            flops=0, bytes_accessed=40 * sum(array.size for array in arrays), transcendentals=0
        ),
    )(*arrays, *kept)


def product_down(operands, pair, step, columns):
    hidden, weight = operands
    return jnp.dot(hidden[pair], weight[:, columns], preferred_element_type=jnp.float32)


def product_out(operands, pair, step, columns):
    gated, weight = operands
    depth = gated.shape[2]
    share = pl.ds(weight.shape[3] - depth, depth)
    return jnp.dot(
        gated[pair], whole_block(weight, step, share), preferred_element_type=jnp.float32
    )


def product_ffn_back(operands, pair, step, columns):
    grad_inner, grad_up, inner_weight, up_weight = operands
    return dot_t(grad_inner[pair], whole_block(inner_weight, step)) + dot_t(
        grad_up[pair], whole_block(up_weight, step)
    )


def product_qkv_back(operands, pair, step, columns):
    grad_products, weight, gate_weight = operands
    depth = grad_products.shape[2] - LANES
    share = pl.ds(0, depth)
    return dot_t(grad_products[pair, :, share], whole_block(weight, step, share)) + dot_t(
        grad_products[pair, :, pl.ds(depth, LANES)], gate_weight[columns, :]
    )


def scatter_team(
    product, lefts, rights, collective_id, work=None, operands=(), results=()
):
    rows = lefts[0].shape[0] // TEAM_SIZE
    depth = sum(left.shape[1] for left in lefts)
    width = MODEL_WIDTH
    paired = [left.reshape(TEAM_SIZE // 2, 2 * rows, left.shape[1]) for left in lefts]
    vmem = pl.BlockSpec(memory_space=pltpu.VMEM)
    anywhere = pl.BlockSpec(memory_space=pl.ANY)
    count = len(lefts) + len(rights)
    summed = pl.pallas_call(
        functools.partial(
            scatter_kernel, product, count, (work, len(operands), len(results)) if work else None
        ),
        out_shape=[jax.ShapeDtypeStruct((rows, width), jnp.float32)] + list(results),
        in_specs=[vmem] * count + [anywhere] * len(operands),
        out_specs=[vmem] + [anywhere] * len(results),
        scratch_shapes=[
            pltpu.VMEM((4, rows, width), jnp.float32),
            pltpu.VMEM((4, rows, width), jnp.bfloat16),
            pltpu.VMEM((4, rows, width), jnp.bfloat16),
            pltpu.VMEM((3, rows, width), jnp.bfloat16),
            pltpu.VMEM((2, rows // 2, width), jnp.bfloat16),
            pltpu.VMEM((2, rows, width), jnp.bfloat16),
            pltpu.SemaphoreType.DMA((10,)),
            pltpu.SemaphoreType.DMA((10,)),
        ],
        compiler_params=pltpu.CompilerParams(
            collective_id=collective_id, has_side_effects=True, vmem_limit_bytes=VMEM_BYTES
        ),
        cost_estimate=pl.CostEstimate(
            flops=2 * TEAM_SIZE * rows * depth * width,
            bytes_accessed=SCATTER_COST * rows * width,
            transcendentals=0,
        ),
    )(*paired, *rights, *operands)
    return summed if work else summed[0]


def ffn_kernel(rows_ref, inner_ref, up_ref, hidden_ref, slope_ref, swish_ref, inner_weight, up_weight):
    @pl.when(pl.program_id(0) == 0)
    def _():
        block = inner_ref.shape[0] * inner_ref.shape[2]
        for step in range(TEAM_SIZE):
            inner_weight[pl.ds(step * block, block), :] = whole_block(inner_ref, step)
            up_weight[pl.ds(step * block, block), :] = whole_block(up_ref, step)

    tile = 256

    def one(step, carry):
        columns = pl.ds(pl.multiple_of(step * tile, tile), tile)
        inner = jnp.dot(rows_ref[0], inner_weight[:, columns], preferred_element_type=jnp.float32)
        up_part = jnp.dot(rows_ref[0], up_weight[:, columns], preferred_element_type=jnp.float32)
        sigma = jax.nn.sigmoid(inner)
        swish = inner * sigma
        hidden_ref[0, :, columns] = (swish * up_part).astype(jnp.bfloat16)
        slope_ref[0, :, columns] = up_part * sigma * (1.0 + inner * (1.0 - sigma))
        swish_ref[0, :, columns] = swish
        return carry

    lax.fori_loop(0, hidden_ref.shape[2] // tile, one, 0, unroll=True)


def ffn_forward(normed_rows, inner_weight, up_weight):
    count, depth = TEAM_SIZE // 2, normed_rows.shape[1]
    length = normed_rows.shape[0] // count
    width = inner_weight.shape[3]
    whole = pl.BlockSpec(inner_weight.shape, lambda i: (0, 0, 0, 0), pipeline_mode=pl.Buffered(1))
    out = pl.BlockSpec((1, length, width), lambda i: (i, 0, 0))
    return pl.pallas_call(
        ffn_kernel,
        grid=(count,),
        out_shape=[
            jax.ShapeDtypeStruct((count, length, width), jnp.bfloat16),
            jax.ShapeDtypeStruct((count, length, width), jnp.float32),
            jax.ShapeDtypeStruct((count, length, width), jnp.float32),
        ],
        in_specs=[pl.BlockSpec((1, length, depth), lambda i: (i, 0, 0)), whole, whole],
        out_specs=[out, out, out],
        scratch_shapes=[pltpu.VMEM((depth, width), jnp.bfloat16)] * 2,
        compiler_params=pltpu.CompilerParams(vmem_limit_bytes=VMEM_BYTES),
        cost_estimate=pl.CostEstimate(
            flops=4 * count * length * depth * width,
            bytes_accessed=count * length * (2 * depth + 10 * width),
            transcendentals=count * length * width,
        ),
    )(normed_rows.reshape(count, length, depth), inner_weight, up_weight)


def ffn_back_kernel(grad_ref, weight_ref, slope_ref, swish_ref, inner_ref, up_ref):
    tile = 256

    def one(step, carry):
        columns = pl.ds(pl.multiple_of(step * tile, tile), tile)
        grad_hidden = dot_t(grad_ref[0], weight_ref[columns, :])
        inner_ref[0, :, columns] = (grad_hidden * slope_ref[0, :, columns]).astype(jnp.bfloat16)
        up_ref[0, :, columns] = (grad_hidden * swish_ref[0, :, columns]).astype(jnp.bfloat16)
        return carry

    lax.fori_loop(0, inner_ref.shape[2] // tile, one, 0, unroll=True)


def ffn_back(grad_rows, down_weight, slope, swish):
    count, length, width = slope.shape
    depth = grad_rows.shape[1]
    whole = pl.BlockSpec(down_weight.shape, lambda i: (0, 0), pipeline_mode=pl.Buffered(1))
    part = pl.BlockSpec((1, length, width), lambda i: (i, 0, 0))
    return pl.pallas_call(
        ffn_back_kernel,
        grid=(count,),
        out_shape=[jax.ShapeDtypeStruct((count, length, width), jnp.bfloat16)] * 2,
        in_specs=[pl.BlockSpec((1, length, depth), lambda i: (i, 0, 0)), whole, part, part],
        out_specs=[part, part],
        compiler_params=pltpu.CompilerParams(vmem_limit_bytes=VMEM_BYTES),
        cost_estimate=pl.CostEstimate(
            flops=2 * count * length * depth * width,
            bytes_accessed=count * length * (2 * depth + 12 * width),
            transcendentals=0,
        ),
    )(grad_rows.reshape(count, length, depth), down_weight, slope, swish)


def weight_kernel(left_ref, right_ref, part_ref):
    depth, _, rows, width = part_ref.shape
    part = dot_tokens(left_ref[...], right_ref[...])
    part_ref[...] = part.astype(jnp.bfloat16).reshape(depth, 1, rows, width)


def weight_shape(left, right, rows):
    depth = left.shape[1] // (TEAM_SIZE * rows)
    return jax.ShapeDtypeStruct((depth, TEAM_SIZE, rows, right.shape[1]), jnp.bfloat16)


def weight_specs(left, right, part):
    depth, _, rows, width = part.shape
    return dict(
        grid=(TEAM_SIZE,),
        in_specs=[
            pl.BlockSpec((left.shape[0], depth * rows), lambda i: (0, i)),
            pl.BlockSpec(right.shape, lambda i: (0, 0)),
        ],
        out_specs=[pl.BlockSpec((depth, 1, rows, width), lambda i: (0, i, 0, 0))],
    )


def weight_work(left_ref, right_ref, part_ref):
    pltpu.emit_pipeline(weight_kernel, **weight_specs(left_ref, right_ref, part_ref))(
        left_ref, right_ref, part_ref
    )


def attention_weight_kernel(normed_ref, products_ref, gated_ref, grad_ref, part_ref, gate_ref):
    depth, _, rows, _ = part_ref.shape
    own = products_ref.shape[1] - LANES
    part = dot_tokens(normed_ref[...], products_ref[...])
    gate_ref[...] = part[:, own:].T[:SUBLANES]
    part_ref[:, :, :, pl.ds(0, own)] = (
        part[:, :own].astype(jnp.bfloat16).reshape(depth, 1, rows, own)
    )
    share = grad_ref.shape[1]
    part = dot_tokens(gated_ref[...], grad_ref[...])
    part_ref[:, :, :, pl.ds(own, share)] = part.astype(jnp.bfloat16).reshape(depth, 1, rows, share)


def attention_weight_work(*refs):
    normed, products, gated, grad, part, gate = refs
    depth, _, rows, width = part.shape
    share = depth * rows
    column = pl.BlockSpec((normed.shape[0], share), lambda i: (0, i))
    pltpu.emit_pipeline(
        attention_weight_kernel,
        grid=(TEAM_SIZE,),
        in_specs=[
            column,
            pl.BlockSpec(products.shape, lambda i: (0, 0)),
            pl.BlockSpec(gated.shape, lambda i: (0, 0)),
            column,
        ],
        out_specs=[
            pl.BlockSpec((depth, 1, rows, width), lambda i: (0, i, 0, 0)),
            pl.BlockSpec((SUBLANES, share), lambda i: (0, i)),
        ],
    )(*refs)


def attention_weight_shapes(normed, grad_products, rows):
    height, width = normed.shape[1], grad_products.shape[1]
    share = height // TEAM_SIZE
    return [
        jax.ShapeDtypeStruct((share // rows, TEAM_SIZE, rows, width - LANES + share), jnp.bfloat16),
        jax.ShapeDtypeStruct((SUBLANES, height), jnp.float32),
    ]


def greet_all():
    place = team_place()
    barrier = pltpu.get_barrier_semaphore()
    flips = [(step // 4, step // 2 % 2, step % 2) for step in range(1, TEAM_SIZE)]
    team = [
        (
            member(place, flip),
            {axis: 1 - at if turn else at for axis, at, turn in zip(TEAM, place, flip)},
        )
        for flip in flips
    ]
    sizes = [lax.axis_size(axis) for axis in DEPTH]
    depth = sizes[0] * sizes[1]
    spot = lax.axis_index(DEPTH[0]) * sizes[1] + lax.axis_index(DEPTH[1])
    line = []
    for step in range(1, depth):
        other = lax.rem(spot + step, depth)
        line.append({DEPTH[0]: other // sizes[1], DEPTH[1]: lax.rem(other, sizes[1])})
    for target in [device for _, device in team] + line:
        pl.semaphore_signal(
            barrier, inc=1, device_id=target, device_id_type=pl.DeviceIdType.MESH
        )
    pl.semaphore_wait(barrier, len(team) + len(line))
    return member(place, (0, 0, 0)), team, spot, line


def push(source, target, sems, number, device):
    copy = pltpu.make_async_remote_copy(
        src_ref=source,
        dst_ref=target,
        send_sem=sems.at[0, number],
        recv_sem=sems.at[1, number],
        device_id=device,
        device_id_type=pl.DeviceIdType.MESH,
    )
    copy.start()
    return copy


def begin_line(own, slots, sems, spot, line):
    slots[spot] = own[...]
    return [
        push(own, slots.at[spot], sems, number, device) for number, device in enumerate(line)
    ]


def begin_team(copies, slots, team_slots, sems, me, team):
    for copy in copies:
        copy.wait_recv()
    total = slots[0]
    for step in range(1, slots.shape[0]):
        total = total + slots[step]
    team_slots[me] = total
    return [
        push(team_slots.at[me], team_slots.at[me], sems, number, device)
        for number, (_, device) in enumerate(team)
    ]


def depth_size():
    return lax.axis_size(DEPTH[0]) * lax.axis_size(DEPTH[1])


def lane_squares(piece):
    total = jnp.sum(piece * piece, axis=0, keepdims=True)
    lanes = total[:, :LANES]
    for first in range(LANES, total.shape[1], LANES):
        lanes = lanes + total[:, first : first + LANES]
    return lanes


def in_lanes(values, shape):
    lane = lax.broadcasted_iota(jnp.int32, shape, 1)
    row = jnp.zeros(shape, jnp.float32)
    for number, value in enumerate(values):
        row = jnp.where(lane == number, jnp.sum(value, axis=1, keepdims=True), row)
    return row


def update_columns(columns, gradient, state, results, update_ref):
    weight = state[0][:, columns]
    moment, second, update = moments(
        weight, state[1][:, columns], state[2][:, columns], gradient.astype(jnp.float32)
    )
    results[0][:, columns] = moment
    results[1][:, columns] = second
    update_ref[:, columns] = update
    return lane_squares(weight), lane_squares(update)


def at_columns(first, width):
    return pl.ds(pl.multiple_of(first, width if width < LANES else LANES), width)


STEPS = 4


def half_moments_kernel(group, with_down, rows_ref, *refs):
    state, refs = refs[0:3], refs[3:]
    if with_down:
        down_ref, down_state, refs = refs[0], refs[1:4], refs[4:]
    else:
        before_ref, refs = refs[3], refs[4:]
    results, update, squares_ref = refs[0:2], refs[2], refs[3]

    @pl.when(pl.program_id(0) == 0)
    def _():
        squares_ref[...] = jnp.zeros_like(squares_ref) if with_down else before_ref[...]

    count, _, width = rows_ref.shape

    def one(item, sums):
        columns = at_columns(item * width, width)
        return add_all(sums, update_columns(columns, rows_ref[item], state, results, update))

    zero = jnp.zeros((1, LANES), jnp.float32)
    found = lax.fori_loop(0, count, one, (zero, zero), unroll=True)
    squares_ref[group : group + 1] += found[0]
    squares_ref[4 + group : 5 + group] += found[1]
    if with_down:
        found = update_columns(slice(None), down_ref[...], down_state, refs[4:6], refs[6])
        squares_ref[2:3] += found[0]
        squares_ref[6:7] += found[1]


def half_moments(group, rows, state, down_sum=None, down_state=None, before=None):
    with_down = group == 0
    half = STEPS // 2
    count = TEAM_SIZE // half
    anywhere = pl.BlockSpec(memory_space=pl.ANY)
    fixed = pl.BlockSpec((SUBLANES, LANES), lambda i: (0, 0))

    def column(array, parts, first):
        return pl.BlockSpec((array.shape[0], array.shape[1] // parts), lambda i: (0, i + first))

    def like(arrays):
        return [jax.ShapeDtypeStruct(array.shape, jnp.float32) for array in arrays]

    columns = [column(array, STEPS, group * half) for array in state]
    in_specs = [pl.BlockSpec((count,) + rows.shape[1:], lambda i: (i, 0, 0))] + columns
    out_shape = like(state) + [jax.ShapeDtypeStruct((SUBLANES, LANES), jnp.float32)]
    out_specs = columns + [fixed]
    operands = [rows, *state]
    aliases = {}
    if with_down:
        down_columns = [column(array, half, 0) for array in down_state]
        in_specs += [column(down_sum, half, 0)] + down_columns
        out_shape += like(down_state)
        out_specs += down_columns
        operands += [down_sum, *down_state]
    else:
        in_specs += [anywhere] * 3 + [fixed]
        operands += list(before)
        aliases = {4: 0, 5: 1, 6: 2}
    return pl.pallas_call(
        functools.partial(half_moments_kernel, group, with_down),
        grid=(half,),
        out_shape=out_shape,
        in_specs=in_specs,
        out_specs=out_specs,
        input_output_aliases=aliases,
        compiler_params=pltpu.CompilerParams(vmem_limit_bytes=GATHER_VMEM),
        cost_estimate=pl.CostEstimate(
            flops=10 * state[0].size, bytes_accessed=15 * state[0].size, transcendentals=0
        ),
    )(*operands)


def begin_blocks(parts, landed, columns, sems, me, team):
    landed[me] = parts[me, :, columns]
    return [
        push(parts.at[index, :, columns], landed.at[me], sems, number, device)
        for number, (index, device) in enumerate(team)
    ]


def column_squares(columns, gradient, state):
    weight = state[0][:, columns]
    _, _, update = moments(
        weight, state[1][:, columns], state[2][:, columns], gradient.astype(jnp.float32)
    )
    return lane_squares(weight), lane_squares(update)


def add_all(olds, news):
    return tuple(old + new for old, new in zip(olds, news))


def totals_kernel(
    heads, attention_ref, gate_ref, first_ref, second_ref, qk_ref, ffn_squares_ref, *refs
):
    state, out_state = refs[0:3], refs[3:6]
    rows_out, gate_out, gains_out, qk_out, norms_out = refs[6:11]
    (
        landed, own, line_slots, team_slots, tile, tile_line, tile_team,
        block_sems, line_sems, team_sems, tile_line_sems, tile_team_sems,
    ) = refs[11:]
    me, team, spot, line = greet_all()
    share = landed.shape[2]
    blocks = begin_blocks(attention_ref, landed, pl.ds(0, share), block_sems, me, team)
    own[...] = jnp.zeros_like(own)
    own[0:heads] = gate_ref[0:heads]
    own[heads : heads + 1] = first_ref[...]
    own[heads + 1 : heads + 2] = second_ref[...]
    for row in range(2):
        own[heads + 2 : heads + 3, pl.ds(row * HEAD_WIDTH, HEAD_WIDTH)] = qk_ref[row : row + 1]
    along = begin_line(own, line_slots, line_sems, spot, line)
    query_width = share - 2 * HEAD_WIDTH
    out_width = out_state[0].shape[1] // TEAM_SIZE
    zero = jnp.zeros((1, LANES), jnp.float32)

    def out(turn, sums):
        columns = at_columns(turn * out_width, out_width)
        gradient = attention_ref[turn, :, pl.ds(share, out_width)]
        return add_all(sums, column_squares(columns, gradient, out_state))

    out_sums = lax.fori_loop(0, TEAM_SIZE, out, (zero,) * 2)
    across = begin_team(along, line_slots, team_slots, team_sems, me, team)
    for copy in blocks:
        copy.wait_recv()

    def projection(turn, sums):
        found = ()
        for first, start, width in (
            (turn * query_width, 0, query_width),
            (TEAM_SIZE * query_width + turn * HEAD_WIDTH, query_width, HEAD_WIDTH),
            (
                TEAM_SIZE * (query_width + HEAD_WIDTH) + turn * HEAD_WIDTH,
                query_width + HEAD_WIDTH,
                HEAD_WIDTH,
            ),
        ):
            gradient = landed[turn, :, pl.ds(start, width)]
            found = found + column_squares(at_columns(first, width), gradient, state)
        return add_all(sums, found)

    sums = lax.fori_loop(0, TEAM_SIZE, projection, (zero,) * 6) + out_sums
    rows = [sums[2 * group] for group in range(4)]
    rows += [ffn_squares_ref[group : group + 1] for group in range(3)]
    rows += [sums[2 * group + 1] for group in range(4)]
    rows += [ffn_squares_ref[4 + group : 5 + group] for group in range(3)]
    tile[...] = jnp.zeros_like(tile)
    tile[0:1] = in_lanes(rows, (1, LANES))
    tile_along = begin_line(tile, tile_line, tile_line_sems, spot, line)
    rows_out[...] = landed[...]
    tile_across = begin_team(tile_along, tile_line, tile_team, tile_team_sems, me, team)
    for copy in across:
        copy.wait_recv()
    total = team_slots[0, heads:]
    for turn in range(1, TEAM_SIZE):
        total = total + team_slots[turn, heads:]
    gains_out[...] = total[:2]
    for row in range(2):
        qk_out[row : row + 1] = total[2:3, row * HEAD_WIDTH : (row + 1) * HEAD_WIDTH]
    for turn in range(TEAM_SIZE):
        gate_out[turn * heads : (turn + 1) * heads] = team_slots[turn, :heads]
    for copy in tile_across:
        copy.wait_recv()
    total = tile_team[0, 0:1]
    for turn in range(1, TEAM_SIZE):
        total = total + tile_team[turn, 0:1]
    norms = jnp.sqrt(total)
    groups = 7
    weight_norms = [norms[:, number : number + 1] for number in range(groups)]
    update_norms = [norms[:, groups + number : groups + number + 1] for number in range(groups)]
    norms_out[...] = jnp.zeros_like(norms_out)
    norms_out[0:1] = in_lanes(weight_norms, (1, LANES))
    norms_out[1:2] = in_lanes(update_norms, (1, LANES))
    norms_out[2:3] = in_lanes(
        [former / latter for former, latter in zip(weight_norms, update_norms)], (1, LANES)
    )
    for copy in blocks + along + across + tile_along + tile_across:
        copy.wait_send()


def totals(
    heads, attention_sum, gate_part, gains, qk_gains, ffn_squares, state, out_state, collective_id
):
    vmem = pl.BlockSpec(memory_space=pltpu.VMEM)
    width = gate_part.shape[1]
    depth = depth_size()
    team, rows, _ = attention_sum.shape
    share = state[0].shape[1] // TEAM_SIZE
    return pl.pallas_call(
        functools.partial(totals_kernel, heads),
        out_shape=[
            jax.ShapeDtypeStruct((team, rows, share), jnp.bfloat16),
            jax.ShapeDtypeStruct((TEAM_SIZE * heads, width), jnp.float32),
            jax.ShapeDtypeStruct((2, width), jnp.float32),
            jax.ShapeDtypeStruct((2, HEAD_WIDTH), jnp.float32),
            jax.ShapeDtypeStruct((SUBLANES, LANES), jnp.float32),
        ],
        in_specs=[vmem] * 12,
        out_specs=[vmem] * 5,
        scratch_shapes=[
            pltpu.VMEM((team, rows, share), jnp.bfloat16),
            pltpu.VMEM((SUBLANES, width), jnp.float32),
            pltpu.VMEM((depth, SUBLANES, width), jnp.float32),
            pltpu.VMEM((TEAM_SIZE, SUBLANES, width), jnp.float32),
            pltpu.VMEM((SUBLANES, LANES), jnp.float32),
            pltpu.VMEM((depth, SUBLANES, LANES), jnp.float32),
            pltpu.VMEM((TEAM_SIZE, SUBLANES, LANES), jnp.float32),
            pltpu.SemaphoreType.DMA((2, TEAM_SIZE - 1)),
            pltpu.SemaphoreType.DMA((2, max(depth - 1, 1))),
            pltpu.SemaphoreType.DMA((2, TEAM_SIZE - 1)),
            pltpu.SemaphoreType.DMA((2, max(depth - 1, 1))),
            pltpu.SemaphoreType.DMA((2, TEAM_SIZE - 1)),
        ],
        compiler_params=pltpu.CompilerParams(
            collective_id=collective_id, has_side_effects=True, vmem_limit_bytes=GATHER_VMEM
        ),
    )(
        attention_sum, gate_part, gains[0][None], gains[1][None], qk_gains, ffn_squares,
        *state, *out_state,
    )


def small_update(state, gradient, results, by_row):
    weight = state[0][...]
    moment, second, update = moments(weight, state[1][...], state[2][...], gradient[...])
    ratio = jnp.sum(weight * weight, axis=1, keepdims=True)
    size = jnp.sum(update * update, axis=1, keepdims=True)
    if not by_row:
        ratio = jnp.sum(ratio, axis=0, keepdims=True)
        size = jnp.sum(size, axis=0, keepdims=True)
    results[0][...] = weight - RATE * (jnp.sqrt(ratio) / jnp.sqrt(size)) * update
    results[1][...] = moment
    results[2][...] = second


def apply_kernel(
    norms_ref, gate_ref, gains_ref, qk_ref, rows_ref, attention_ref, *refs
):
    state, out_state = refs[0:3], refs[3:6]
    ffn_pair, down_pair = refs[6:8], refs[8:10]
    states = [refs[10 + 3 * number : 13 + 3 * number] for number in range(3)]
    targets, out_targets = refs[19:23], refs[23:27]
    ffn_targets, down_targets = refs[27:29], refs[29:31]
    results = [refs[31 + 3 * number : 34 + 3 * number] for number in range(3)]
    norms_out, gradient, out_gradient = refs[40:]
    step = pl.program_id(0)
    share = rows_ref.shape[2]
    wide = share - 2 * HEAD_WIDTH
    query_steps = TEAM_SIZE * wide // gradient.shape[1]
    key_steps = TEAM_SIZE * HEAD_WIDTH // gradient.shape[1]

    @pl.when(step == 0)
    def _():
        norms_out[...] = norms_ref[0:2]
        small_update(states[0], gate_ref, results[0], False)
        small_update(states[1], gains_ref, results[1], True)
        small_update(states[2], qk_ref, results[2], True)

    @pl.when(step < query_steps)
    def _():
        per_step = gradient.shape[1] // wide
        for item in range(per_step):
            gradient[:, pl.ds(item * wide, wide)] = rows_ref[
                step * per_step + item, :, pl.ds(0, wide)
            ].astype(jnp.float32)

    for number in range(2):
        first = query_steps + number * key_steps

        @pl.when((step >= first) & (step < first + key_steps))
        def _():
            per_step = gradient.shape[1] // HEAD_WIDTH
            for item in range(per_step):
                gradient[:, pl.ds(item * HEAD_WIDTH, HEAD_WIDTH)] = rows_ref[
                    (step - first) * per_step + item, :, pl.ds(wide + number * HEAD_WIDTH, HEAD_WIDTH)
                ].astype(jnp.float32)

    def rate(first, uppers=()):
        found = norms_ref[2:3, first : first + 1]
        for number, upper in enumerate(uppers):
            group = first + number + 1
            found = jnp.where(step < upper, found, norms_ref[2:3, group : group + 1])
        return RATE * found

    def renew(weight, update, new, low_new, factor):
        value = weight - factor * update
        new[...] = value
        low_new[...] = value.astype(jnp.bfloat16)

    def both(state, gradient, targets, factor):
        weight = state[0][...]
        moment, second, update = moments(weight, state[1][...], state[2][...], gradient)
        targets[2][...] = moment
        targets[3][...] = second
        renew(weight, update, targets[0], targets[1], factor)

    both(state, gradient[...], targets, rate(0, (query_steps, query_steps + key_steps)))
    width = attention_ref.shape[2] - share
    count = out_gradient.shape[1] // width
    for item in range(count):
        out_gradient[:, pl.ds(item * width, width)] = attention_ref[
            step * count + item, :, pl.ds(share, width)
        ].astype(jnp.float32)
    both(out_state, out_gradient[...], out_targets, rate(3))
    renew(ffn_pair[0][...], ffn_pair[1][...], *ffn_targets, rate(4, (STEPS // 2,)))
    renew(down_pair[0][...], down_pair[1][...], *down_targets, rate(6))


def apply_all(
    norms, gate_total, gains_total, qk_total, projection_rows, attention_sum, state, out_state,
    ffn_pair, down_pair, states,
):
    def whole(array):
        return pl.BlockSpec(array.shape, lambda i: (0,) * array.ndim)

    def column(array):
        return pl.BlockSpec((array.shape[0], array.shape[1] // STEPS), lambda i: (0, i))

    def like(array, kind=jnp.float32):
        return jax.ShapeDtypeStruct(array.shape, kind)

    small = [array for group in states for array in group]
    fixed = [norms, gate_total, gains_total, qk_total, projection_rows, attention_sum]
    split = [*state, *out_state, *ffn_pair, *down_pair]
    targets = []
    for group in (state, out_state):
        targets += [like(group[0]), like(group[0], jnp.bfloat16), like(group[1]), like(group[2])]
    for group in (ffn_pair, down_pair):
        targets += [like(group[0]), like(group[0], jnp.bfloat16)]
    results = [like(array) for array in small]
    results.append(jax.ShapeDtypeStruct((2, norms.shape[1]), jnp.float32))
    rows = state[0].shape[0]
    return pl.pallas_call(
        apply_kernel,
        grid=(STEPS,),
        out_shape=targets + results,
        in_specs=[whole(array) for array in fixed]
        + [column(array) for array in split]
        + [whole(array) for array in small],
        out_specs=[column(array) for array in targets] + [whole(array) for array in results],
        scratch_shapes=[
            pltpu.VMEM((rows, state[0].shape[1] // STEPS), jnp.float32),
            pltpu.VMEM((rows, out_state[0].shape[1] // STEPS), jnp.float32),
        ],
        compiler_params=pltpu.CompilerParams(vmem_limit_bytes=GATHER_VMEM),
        cost_estimate=pl.CostEstimate(
            flops=4 * ffn_pair[0].size, bytes_accessed=30 * ffn_pair[0].size, transcendentals=0
        ),
    )(*fixed, *split, *small)


def team_exchange(blocks):
    return lax.all_to_all(blocks, TEAM, split_axis=0, concat_axis=0, tiled=True)


def turn_half(value_rows):
    return pltpu.roll(value_rows, value_rows.shape[-1] // 2, value_rows.ndim - 1)


def norm_turn(value_rows, gain, cosine, sine):
    scaled = rms_apply(value_rows, gain)
    return scaled * cosine + turn_half(scaled) * sine


def norm_turn_back(value_rows, gain, cosine, sine, gradient):
    turned = gradient * cosine + turn_half(gradient * sine)
    return rms_back(value_rows, gain, turned)


def greet_line():
    index, count = lax.axis_index("seq"), lax.axis_size("seq")
    barrier = pltpu.get_barrier_semaphore()

    @pl.when(index > 0)
    def _():
        pl.semaphore_signal(
            barrier, inc=1, device_id={"seq": index - 1}, device_id_type=pl.DeviceIdType.MESH
        )

    @pl.when(index < count - 1)
    def _():
        pl.semaphore_signal(
            barrier, inc=1, device_id={"seq": index + 1}, device_id_type=pl.DeviceIdType.MESH
        )

    inside = (index > 0) & (index < count - 1)

    @pl.when(inside)
    def _():
        pl.semaphore_wait(barrier, 2)

    @pl.when(jnp.logical_not(inside))
    def _():
        pl.semaphore_wait(barrier, 1)

    return index, count


def attend_kernel(
    window, scale, rows_ref, weight_ref, gate_ref, gains_ref, cosine_ref, sine_ref, start_ref,
    raw_ref, query_ref, pair_ref, stats_ref, across_ref, attended_ref, gated_ref,
    weight, pairs, send_sem, recv_sem,
):
    count_rows, length, _ = rows_ref.shape
    query_cols = query_ref.shape[2]
    heads = query_cols // HEAD_WIDTH
    keys_at = pl.ds(0, HEAD_WIDTH)
    values_at = pl.ds(HEAD_WIDTH, HEAD_WIDTH)
    index, count = greet_line()

    def hop(turn, row):
        return pltpu.make_async_remote_copy(
            src_ref=pairs.at[window - turn + 1, row],
            dst_ref=pairs.at[window - turn, row],
            send_sem=send_sem.at[turn - 1, row],
            recv_sem=recv_sem.at[turn - 1, row],
            device_id={"seq": lax.rem(index + 1, count)},
            device_id_type=pl.DeviceIdType.MESH,
        )

    block = weight_ref.shape[0] * weight_ref.shape[2]
    own = raw_ref.shape[2]
    for step in range(TEAM_SIZE):
        weight[pl.ds(step * block, block), pl.ds(0, own)] = whole_block(
            weight_ref, step, pl.ds(0, own)
        )
    weight[:, pl.ds(own, LANES)] = gate_ref[...]

    def project(row, carry):
        products = jnp.dot(rows_ref[row], weight[...], preferred_element_type=jnp.float32)
        raw = products[:, : query_cols + 2 * HEAD_WIDTH].astype(jnp.bfloat16)
        raw_ref[row] = raw
        cosine, sine = cosine_ref[row], sine_ref[row]
        key = norm_turn(
            raw[:, query_cols : query_cols + HEAD_WIDTH].astype(jnp.float32),
            gains_ref[1:2], cosine, sine,
        )
        pairs[window, row, :, keys_at] = key.astype(jnp.bfloat16)
        pairs[window, row, :, values_at] = raw[:, query_cols + HEAD_WIDTH :]

        @pl.when(index < count - 1)
        def _():
            hop(1, row).start()

        for head in range(heads):
            columns = slice(head * HEAD_WIDTH, (head + 1) * HEAD_WIDTH)
            query_ref[row, :, columns] = norm_turn(
                raw[:, columns].astype(jnp.float32), gains_ref[0:1], cosine, sine
            ).astype(jnp.bfloat16)
        stats_ref[row] = jax.nn.sigmoid(products[:, query_cols + 2 * HEAD_WIDTH :])
        return carry

    lax.fori_loop(0, count_rows, project, 0)

    @pl.when(index == 0)
    def _():
        for slot in range(window):
            pairs[slot] = jnp.zeros_like(pairs[slot])

    for turn in range(2, window + 1):

        def forward(row, carry):
            @pl.when(index > 0)
            def _():
                hop(turn - 1, row).wait_recv()

            @pl.when(index < count - 1)
            def _():
                hop(turn, row).start()

            return carry

        lax.fori_loop(0, count_rows, forward, 0)

    places = lax.broadcasted_iota(jnp.int32, (length, (window + 1) * length), 1)
    latest = window * length + lax.broadcasted_iota(jnp.int32, places.shape, 0)
    lane = lax.broadcasted_iota(jnp.int32, (length, LANES), 1)

    def attend(row, carry):
        @pl.when(index > 0)
        def _():
            hop(window, row).wait_recv()

        allowed = (places >= start_ref[row]) & (places <= latest)
        keys = pairs[:, row, :, keys_at].reshape(-1, HEAD_WIDTH)
        values = pairs[:, row, :, values_at].reshape(-1, HEAD_WIDTH)
        stats = stats_ref[row]
        for head in range(heads):
            columns = slice(head * HEAD_WIDTH, (head + 1) * HEAD_WIDTH)
            scores = dot_t(query_ref[row, :, columns], keys) * scale
            scores = jnp.where(allowed, scores, NEGATIVE)
            top = jnp.max(scores, axis=1, keepdims=True)
            powers = jnp.exp(scores - top)
            total = jnp.sum(powers, axis=1, keepdims=True)
            low_probs = (powers * (1.0 / total)).astype(jnp.bfloat16)
            output = jnp.dot(low_probs, values, preferred_element_type=jnp.float32)
            output = output.astype(jnp.bfloat16)
            attended_ref[row, :, columns] = output
            gated_ref[row, :, columns] = (
                output.astype(jnp.float32) * stats[:, head : head + 1]
            ).astype(jnp.bfloat16)
            stats = jnp.where(lane == heads + head, top + jnp.log(total), stats)
        stats_ref[row] = stats
        across_ref[row] = stats.T[:SUBLANES]
        pair_ref[:, row] = pairs[:, row]
        return carry

    lax.fori_loop(0, count_rows, attend, 0)

    @pl.when(index < count - 1)
    def _():
        for turn in range(1, window + 1):

            def finish(row, carry):
                hop(turn, row).wait_send()
                return carry

            lax.fori_loop(0, count_rows, finish, 0)


def attend(
    normed_rows, own_attention, own_gate, gains, cosine, sine, starts, query_cols, window, collective_id
):
    rows, length, _ = normed_rows.shape
    width = query_cols + 2 * HEAD_WIDTH + LANES
    bf16 = jnp.bfloat16
    vmem = pl.BlockSpec(memory_space=pltpu.VMEM)
    return pl.pallas_call(
        functools.partial(attend_kernel, window, HEAD_WIDTH ** (-0.5)),
        out_shape=[
            jax.ShapeDtypeStruct((rows, length, query_cols + 2 * HEAD_WIDTH), bf16),
            jax.ShapeDtypeStruct((rows, length, query_cols), bf16),
            jax.ShapeDtypeStruct((window + 1, rows, length, 2 * HEAD_WIDTH), bf16),
            jax.ShapeDtypeStruct((rows, length, LANES), jnp.float32),
            jax.ShapeDtypeStruct((rows, SUBLANES, length), jnp.float32),
            jax.ShapeDtypeStruct((rows, length, query_cols), bf16),
            jax.ShapeDtypeStruct((rows, length, query_cols), bf16),
        ],
        in_specs=[vmem] * 7,
        out_specs=[vmem] * 7,
        scratch_shapes=[
            pltpu.VMEM((MODEL_WIDTH, width), bf16),
            pltpu.VMEM((window + 1, rows, length, 2 * HEAD_WIDTH), bf16),
            pltpu.SemaphoreType.DMA((window, rows)),
            pltpu.SemaphoreType.DMA((window, rows)),
        ],
        compiler_params=pltpu.CompilerParams(
            collective_id=collective_id, has_side_effects=True, vmem_limit_bytes=VMEM_BYTES
        ),
        cost_estimate=pl.CostEstimate(
            flops=2 * rows * length * MODEL_WIDTH * width,
            bytes_accessed=ATTEND_COST * rows * length * MODEL_WIDTH,
            transcendentals=0,
        ),
    )(normed_rows, own_attention, own_gate, gains, cosine, sine, starts)


def attend_back_kernel(
    window, scale, rows_ref, weight_ref, gains_ref, cosine_ref, sine_ref, start_ref,
    raw_ref, query_ref, pair_ref, stats_ref, across_ref, attended_ref,
    products_ref, gain_ref,
    weight, parts, outs, ins, send_sem, recv_sem,
):
    count_rows, length, _ = rows_ref.shape
    query_cols = query_ref.shape[2]
    heads = query_cols // HEAD_WIDTH
    keys_at = pl.ds(0, HEAD_WIDTH)
    values_at = pl.ds(HEAD_WIDTH, HEAD_WIDTH)
    index, count = greet_line()
    lag = 2

    def hop(turn, row):
        return pltpu.make_async_remote_copy(
            src_ref=outs.at[turn - 1, row],
            dst_ref=ins.at[turn - 1, row],
            send_sem=send_sem.at[turn - 1, row],
            recv_sem=recv_sem.at[turn - 1, row],
            device_id={"seq": lax.rem(index + count - 1, count)},
            device_id_type=pl.DeviceIdType.MESH,
        )

    keys_total = (window + 1) * length
    places = lax.broadcasted_iota(jnp.int32, (keys_total, length), 0)
    latest = window * length + lax.broadcasted_iota(jnp.int32, places.shape, 1)
    lane = lax.broadcasted_iota(jnp.int32, (length, LANES), 1)
    gain_ref[...] = jnp.zeros_like(gain_ref)
    share = weight_ref.shape[3] - query_cols
    for step in range(TEAM_SIZE):
        weight[:, pl.ds(step * query_cols, query_cols)] = whole_block(
            weight_ref, step, pl.ds(share, query_cols)
        )

    @pl.when(index == count - 1)
    def _():
        ins[...] = jnp.zeros_like(ins)

    def compute(row):
        grad_gated = dot_t(rows_ref[row], weight[...])
        keys = pair_ref[:, row, :, keys_at].reshape(-1, HEAD_WIDTH)
        values = pair_ref[:, row, :, values_at].reshape(-1, HEAD_WIDTH)
        allowed = (places >= start_ref[row]) & (places <= latest)
        cosine, sine = cosine_ref[row], sine_ref[row]
        grad_pre = jnp.zeros((length, LANES), jnp.float32)
        grad_keys = jnp.zeros((keys_total, HEAD_WIDTH), jnp.float32)
        grad_values = jnp.zeros((keys_total, HEAD_WIDTH), jnp.float32)
        for head in range(heads):
            columns = slice(head * HEAD_WIDTH, (head + 1) * HEAD_WIDTH)
            gate = stats_ref[row, :, head : head + 1]
            own = grad_gated[:, columns]
            grad_out = (own * gate).astype(jnp.bfloat16)
            grad_gate = jnp.sum(
                own * attended_ref[row, :, columns].astype(jnp.float32), axis=1, keepdims=True
            )
            grad_pre = jnp.where(lane == head, grad_gate * gate * (1.0 - gate), grad_pre)
            query = query_ref[row, :, columns]
            scores = jnp.where(allowed, dot_t(keys, query) * scale, NEGATIVE)
            probs = jnp.exp(scores - across_ref[row, heads + head : heads + head + 1])
            grad_probs = dot_t(values, grad_out)
            inner = jnp.sum(probs * grad_probs, axis=0, keepdims=True)
            grad_scores = (probs * (grad_probs - inner)).astype(jnp.bfloat16)
            grad_values = grad_values + jnp.dot(
                probs.astype(jnp.bfloat16), grad_out, preferred_element_type=jnp.float32
            )
            grad_keys = grad_keys + jnp.dot(
                grad_scores, query, preferred_element_type=jnp.float32
            )
            grad_query = dot_tokens(grad_scores, keys) * scale
            grad_raw, gain = norm_turn_back(
                raw_ref[row, :, columns].astype(jnp.float32), gains_ref[0:1], cosine, sine,
                grad_query,
            )
            products_ref[row, :, columns] = grad_raw.astype(jnp.bfloat16)
            gain_ref[0:1] += jnp.sum(gain, axis=0, keepdims=True)
        products_ref[row, :, query_cols + 2 * HEAD_WIDTH :] = grad_pre.astype(jnp.bfloat16)
        parts[:, row, :, keys_at] = (grad_keys * scale).reshape(window + 1, length, HEAD_WIDTH)
        parts[:, row, :, values_at] = grad_values.reshape(window + 1, length, HEAD_WIDTH)

    def finish(row):
        grad_pair = parts[window, row] + ins[window - 1, row].astype(jnp.float32)
        grad_raw, gain = norm_turn_back(
            raw_ref[row, :, query_cols : query_cols + HEAD_WIDTH].astype(jnp.float32),
            gains_ref[1:2], cosine_ref[row], sine_ref[row], grad_pair[:, :HEAD_WIDTH],
        )
        products_ref[row, :, query_cols : query_cols + HEAD_WIDTH] = grad_raw.astype(jnp.bfloat16)
        products_ref[row, :, query_cols + HEAD_WIDTH : query_cols + 2 * HEAD_WIDTH] = grad_pair[
            :, HEAD_WIDTH:
        ].astype(jnp.bfloat16)
        gain_ref[1:2] += jnp.sum(gain, axis=0, keepdims=True)

    def step(turn_row, carry):
        @pl.when(turn_row < count_rows)
        def _():
            compute(turn_row)

        for turn in range(1, window + 2):
            row = turn_row - lag * (turn - 1)

            @pl.when((row >= 0) & (row < count_rows))
            def _():
                if turn > 1:

                    @pl.when(index < count - 1)
                    def _():
                        hop(turn - 1, row).wait_recv()

                if turn == window + 1:
                    finish(row)
                else:
                    part = parts[turn - 1, row]
                    if turn > 1:
                        part = part + ins[turn - 2, row].astype(jnp.float32)
                    outs[turn - 1, row] = part.astype(jnp.bfloat16)

                    @pl.when(index > 0)
                    def _():
                        hop(turn, row).start()

        return carry

    lax.fori_loop(0, count_rows + lag * window, step, 0)

    @pl.when(index > 0)
    def _():
        for turn in range(1, window + 1):

            def done(row, carry):
                hop(turn, row).wait_send()
                return carry

            lax.fori_loop(0, count_rows, done, 0)


def attend_back(
    grad_rows, own_attention, gains, cosine, sine, starts, saved, window, collective_id
):
    rows, length, _ = grad_rows.shape
    query_cols = saved[1].shape[2]
    width = query_cols + 2 * HEAD_WIDTH + LANES
    bf16 = jnp.bfloat16
    vmem = pl.BlockSpec(memory_space=pltpu.VMEM)
    return pl.pallas_call(
        functools.partial(attend_back_kernel, window, HEAD_WIDTH ** (-0.5)),
        out_shape=[
            jax.ShapeDtypeStruct((rows, length, width), bf16),
            jax.ShapeDtypeStruct((SUBLANES, HEAD_WIDTH), jnp.float32),
        ],
        in_specs=[vmem] * 12,
        out_specs=[vmem] * 2,
        scratch_shapes=[
            pltpu.VMEM((query_cols, MODEL_WIDTH), bf16),
            pltpu.VMEM((window + 1, rows, length, 2 * HEAD_WIDTH), jnp.float32),
            pltpu.VMEM((window, rows, length, 2 * HEAD_WIDTH), bf16),
            pltpu.VMEM((window, rows, length, 2 * HEAD_WIDTH), bf16),
            pltpu.SemaphoreType.DMA((window, rows)),
            pltpu.SemaphoreType.DMA((window, rows)),
        ],
        compiler_params=pltpu.CompilerParams(
            collective_id=collective_id, has_side_effects=True, vmem_limit_bytes=VMEM_BYTES
        ),
        cost_estimate=pl.CostEstimate(
            flops=2 * rows * length * MODEL_WIDTH * query_cols,
            bytes_accessed=ATTEND_COST * rows * length * MODEL_WIDTH,
            transcendentals=0,
        ),
    )(grad_rows, own_attention, gains, cosine, sine, starts, *saved)


def team_columns(matrix, widths):
    pieces = []
    lower = 0
    for width in widths:
        piece = matrix[:, lower : lower + width]
        pieces.append(piece.reshape(matrix.shape[0], TEAM_SIZE, width // TEAM_SIZE))
        lower = lower + width
    return jnp.concatenate(pieces, axis=2).transpose(1, 0, 2)


def gather_parts(blocks):
    return lax.all_gather(blocks, DEPTH, axis=0, tiled=False)


def scatter_parts(parts):
    depth, team, rows, width = parts.shape
    return lax.psum_scatter(
        parts.reshape(depth * team * rows, width), DEPTH, scatter_dimension=0, tiled=True
    ).reshape(team, rows, width)


def gather_rows(matrix):
    return lax.all_gather(matrix, DEPTH, axis=0, tiled=True)


def scatter_rows(gradient):
    return lax.psum_scatter(gradient, DEPTH, scatter_dimension=0, tiled=True)


def shards(
    inputs,
    cotangent,
    doc_lengths,
    projection_weight,
    projection_moment,
    projection_second,
    out_weight,
    out_moment,
    out_second,
    ffn_weight,
    ffn_moment,
    ffn_second,
    down_weight,
    down_moment,
    down_second,
    head_gate,
    gate_moment,
    gate_second,
    norm_gains,
    gains_moment,
    gains_second,
    qk_gains,
    qk_moment,
    qk_second,
):
    rows_dev, local_len, width = inputs.shape
    bf16 = jnp.bfloat16
    team = lax.axis_index(TEAM)
    place_seq = lax.axis_index("seq")
    group_heads = QUERY_HEADS // KEY_VALUE_HEADS
    window = -(-(DOC_MOST - 1) // local_len)
    window = min(window, lax.axis_size("seq") - 1)
    query_cols = QUERY_HEADS * HEAD_WIDTH
    key_value_columns = KEY_VALUE_HEADS * HEAD_WIDTH
    widths_qkv = (query_cols, key_value_columns, key_value_columns)
    widths_ffn = (FF, FF)
    own_query = query_cols // TEAM_SIZE
    own_key = key_value_columns // TEAM_SIZE
    own_ff = FF // TEAM_SIZE
    own_gate = lax.dynamic_slice_in_dim(head_gate.astype(bf16), team * group_heads, group_heads, 1)
    own_gate = jnp.pad(own_gate, ((0, 0), (0, LANES - group_heads)))
    (attention_blocks,) = push_team(
        [team_columns(projection_weight.astype(bf16), widths_qkv)],
        11,
        [team_columns(out_weight.astype(bf16), (MODEL_WIDTH,))],
    )
    own_attention = gather_parts(attention_blocks)
    low_ffn, attention_blocks = lax.optimization_barrier(
        (ffn_weight.astype(bf16), attention_blocks)
    )
    inner_blocks, up_blocks, lengths = push_team(
        [
            team_columns(low_ffn[:, :FF], (FF,)),
            team_columns(low_ffn[:, FF:], (FF,)),
            jnp.pad(doc_lengths, ((0, SUBLANES - 1), (0, LANES - doc_lengths.shape[1])))[None],
        ],
        12,
    )
    own_inner = gather_parts(inner_blocks)
    lengths = lengths[:, 0, : doc_lengths.shape[1]]
    place = place_seq * local_len + jnp.arange(local_len, dtype=jnp.int32)
    position = positions(lengths, place)
    cosine, sine = rotary_tables(position, HEAD_WIDTH)
    starts = window * local_len + jnp.arange(local_len, dtype=jnp.int32)[None, :] - position
    inputs_flat = inputs[0].astype(jnp.float32)
    normed = rms_apply(inputs_flat, norm_gains[0]).astype(bf16)
    normed_all, grad_all = gather_team([normed, cotangent[0]], 0)
    raw, query_rot, pairs, stats, across, attended, gated = attend(
        normed_all.reshape(TEAM_SIZE, local_len, MODEL_WIDTH),
        own_attention,
        own_gate,
        qk_gains,
        cosine,
        sine,
        starts[:, :, None],
        own_query,
        window,
        8,
    )
    gated, up_blocks, low_down = lax.optimization_barrier(
        (gated, up_blocks, down_weight.astype(bf16))
    )
    own_up = gather_parts(up_blocks)
    own_down = gather_rows(low_down)
    middle = inputs_flat + scatter_team(product_out, [gated.reshape(-1, own_query)], [own_attention], 1)
    normed2 = rms_apply(middle, norm_gains[1]).astype(bf16)
    normed2_all = gather_team([normed2], 2)[0]
    hidden, slope, swish = ffn_forward(normed2_all, own_inner, own_up)
    grad_final = cotangent[0].astype(jnp.float32)
    down_part, own_down = lax.optimization_barrier(
        (low_tokens(hidden.reshape(-1, own_ff), grad_all), own_down)
    )
    grad_inner, grad_up = ffn_back(grad_all, own_down, slope, swish)
    grad_inner, grad_up = grad_inner.reshape(-1, own_ff), grad_up.reshape(-1, own_ff)
    down_sum = scatter_rows(down_part)
    grad_normed2, inner_part = scatter_team(
        product_ffn_back,
        [grad_inner, grad_up],
        [own_inner, own_up],
        4,
        weight_work,
        (normed2_all, grad_inner),
        (weight_shape(normed2_all, grad_inner, ffn_weight.shape[0]),),
    )
    grad_mid_part, gain_mid = rms_back(middle, norm_gains[1], grad_normed2)
    grad_middle = grad_final + grad_mid_part
    grad_low, down_sum = lax.optimization_barrier((grad_middle.astype(bf16), down_sum))
    inner_sum = scatter_parts(inner_part)
    grad_middle_all, up_part = gather_team(
        [grad_low],
        5,
        weight_work,
        (normed2_all, grad_up),
        (weight_shape(normed2_all, grad_up, ffn_weight.shape[0]),),
    )
    grad_products, gain_sums = attend_back(
        grad_middle_all.reshape(TEAM_SIZE, local_len, MODEL_WIDTH),
        own_attention,
        qk_gains,
        cosine,
        sine,
        starts[:, None, :],
        (raw, query_rot, pairs, stats, across, attended),
        window,
        9,
    )
    grad_products = grad_products.reshape(-1, grad_products.shape[2])
    up_part, grad_products, inner_sum = lax.optimization_barrier(
        (up_part, grad_products, inner_sum)
    )
    up_sum = scatter_parts(up_part)
    grad_normed, attention_part, gate_part = scatter_team(
        product_qkv_back,
        [grad_products],
        [own_attention, own_gate],
        6,
        attention_weight_work,
        (normed_all, grad_products, gated.reshape(-1, own_query), grad_middle_all),
        attention_weight_shapes(normed_all, grad_products, out_weight.shape[0]),
    )
    late_hidden, grad_normed, inner_sum = lax.optimization_barrier(
        (hidden, grad_normed, inner_sum)
    )
    inner_rows = team_exchange(inner_sum)
    attention_sum = scatter_parts(attention_part)
    summed = scatter_team(product_down, [late_hidden.reshape(-1, own_ff)], [own_down], 3)
    grad_in_part, gain_in = rms_back(inputs_flat, norm_gains[0], grad_normed)
    input_grad = (grad_middle + grad_in_part).reshape(inputs.shape)
    up_sum, summed, inner_rows = lax.optimization_barrier((up_sum, summed, inner_rows))
    up_rows = team_exchange(up_sum)
    ffn_state = (ffn_weight, ffn_moment, ffn_second)
    *half, squares, down_moment_new, down_second_new, down_update = half_moments(
        0, inner_rows, ffn_state, down_sum, (down_weight, down_moment, down_second)
    )
    ffn_moment_new, ffn_second_new, ffn_update, ffn_squares = half_moments(
        1, up_rows, ffn_state, before=(*half, squares)
    )
    final = middle + summed
    result = final.astype(bf16).reshape(inputs.shape)
    attention_sum, ffn_squares, result, input_grad = lax.optimization_barrier(
        (attention_sum, ffn_squares, result, input_grad)
    )
    attention_state = (projection_weight, projection_moment, projection_second)
    out_state = (out_weight, out_moment, out_second)
    projection_rows, gate_total, gains_total, qk_total, norms = totals(
        group_heads,
        attention_sum,
        gate_part,
        (jnp.sum(gain_in, axis=0), jnp.sum(gain_mid, axis=0)),
        gain_sums,
        ffn_squares,
        attention_state,
        out_state,
        10,
    )
    (
        projection_weight_next,
        qkv_copy,
        projection_moment_next,
        projection_second_next,
        out_new,
        out_copy,
        out_moment_new,
        out_second_new,
        ffn_new,
        ffn_copy,
        down_new,
        down_copy,
        head_gate_new,
        gate_moment_new,
        gate_second_new,
        gains_new,
        gains_moment_new,
        gains_second_new,
        qk_new,
        qk_moment_new,
        qk_second_new,
        norms,
    ) = apply_all(
        norms,
        gate_total,
        gains_total,
        qk_total,
        projection_rows,
        attention_sum,
        attention_state,
        out_state,
        (ffn_weight, ffn_update),
        (down_weight, down_update),
        (
            (head_gate.T, gate_moment.T, gate_second.T),
            (norm_gains, gains_moment, gains_second),
            (qk_gains, qk_moment, qk_second),
        ),
    )
    return (
        result,
        input_grad,
        projection_weight_next,
        projection_moment_next,
        projection_second_next,
        qkv_copy,
        out_new,
        out_moment_new,
        out_second_new,
        out_copy,
        ffn_new,
        ffn_moment_new,
        ffn_second_new,
        ffn_copy,
        down_new,
        down_moment_new,
        down_second_new,
        down_copy,
        head_gate_new.T,
        gate_moment_new.T,
        gate_second_new.T,
        gains_new,
        gains_moment_new,
        gains_second_new,
        qk_new,
        qk_moment_new,
        qk_second_new,
        norms[:2, :7],
    )


def solution(mesh):
    mesh = Mesh(
        mesh.devices.reshape(2, 2, 2, mesh.shape["fsdp"] // TEAM_SIZE, mesh.shape["seq"]),
        TEAM + DEPTH,
    )
    rows = TEAM + DEPTH[:1]
    in_specs = (
        P(rows, "seq", None),
        P(rows, "seq", None),
        P(rows, None),
        P(TEAM + DEPTH, None),
        P(TEAM + DEPTH, None),
        P(TEAM + DEPTH, None),
        P(TEAM + DEPTH, None),
        P(TEAM + DEPTH, None),
        P(TEAM + DEPTH, None),
        P(TEAM + DEPTH, None),
        P(TEAM + DEPTH, None),
        P(TEAM + DEPTH, None),
        P(TEAM + DEPTH, None),
        P(TEAM + DEPTH, None),
        P(TEAM + DEPTH, None),
        P(),
        P(),
        P(),
        P(),
        P(),
        P(),
        P(),
        P(),
        P(),
    )
    out_specs = (
        P(rows, "seq", None),
        P(rows, "seq", None),
        P(TEAM + DEPTH, None),
        P(TEAM + DEPTH, None),
        P(TEAM + DEPTH, None),
        P(TEAM + DEPTH, None),
        P(TEAM + DEPTH, None),
        P(TEAM + DEPTH, None),
        P(TEAM + DEPTH, None),
        P(TEAM + DEPTH, None),
        P(TEAM + DEPTH, None),
        P(TEAM + DEPTH, None),
        P(TEAM + DEPTH, None),
        P(TEAM + DEPTH, None),
        P(TEAM + DEPTH, None),
        P(TEAM + DEPTH, None),
        P(TEAM + DEPTH, None),
        P(TEAM + DEPTH, None),
        P(),
        P(),
        P(),
        P(),
        P(),
        P(),
        P(),
        P(),
        P(),
        P(),
    )
    return jax.shard_map(shards, mesh=mesh, in_specs=in_specs, out_specs=out_specs, check_vma=False)
```
